32 devices in a mesh: dp: 4 (over z), lat: 4 (over x, core), lon: 2 (over y).
Axes of the slice: x: 2, y: 2, z: 4, core: 2. Of those that a mesh axis runs over, the one named last changes fastest.
Arguments:
- inputs: bfloat16 [8, 8, 24, 24, 192], P('dp', None, 'lat', 'lon'), may hold values from -6 to 6
- cotangent: bfloat16 [8, 8, 24, 24, 192], P('dp', None, 'lat', 'lon'), may hold values from -6 to 6
- lead_counts: int32 [2], replicated, may hold values from 1 to 4
- home_slots: int32 [64], replicated, may hold values from 0 to 127, as said below
- master: float32 [128, 9728], P(('dp', 'lat', 'lon'))
- moment_one: float32 [128, 9728], P(('dp', 'lat', 'lon'))
- moment_two: float32 [128, 9728], P(('dp', 'lat', 'lon')), as said below
- step_count: int32 [1], replicated, may hold values from 2 to 20
Outputs:
- result: bfloat16 [8, 8, 24, 24, 192], P('dp', None, 'lat', 'lon')
- grad_inputs: float32 [8, 8, 24, 24, 192], P('dp', None, 'lat', 'lon')
- grad_vectors: float32 [9, 192], replicated
- new_master: float32 [128, 9728], P(('dp', 'lat', 'lon'))
- new_moment_one: float32 [128, 9728], P(('dp', 'lat', 'lon'))
- new_moment_two: float32 [128, 9728], P(('dp', 'lat', 'lon'))
The draws below stay inside these ranges and needn't reach their ends.
Inputs may be any that keep to these rules, and one draw needn't show every extreme that they name: The 64 values are distinct; bucket b lives on device home_slots[b] // 4 in its slot home_slots[b] mod 4; some device holds 4 buckets. `moment_two`: entries are positive.
All inputs are finite; a program needn't handle non-finite values.
Results may differ from the reference program's by a relative error of at most 0.017.
The reference program's roundings to bfloat16 on the way count: a program that leaves them out, or rounds other values in their place, can miss the bound.
Values may be sent and summed in bfloat16 or wider, within the bound.
A program may use at most 256 MiB of HBM per device.

```python
import math
import jax
import jax.numpy as jnp
from jax import lax

D = 192
FF = 768
HEADS = 6
HEAD_DIM = 32
LEVELS = 8
WIN_LAT = 6
WIN_LON = 12
LEADS = 4
CAPACITY = 4
SLOTS = 8
SAMPLES = 2
NLAT = 24
NLON = 24
LAT_GROUPS = 5
PARAMS = 616392
BUCKETS = 64
BUCKET = 9728
HOMES = 128


def offsets_drawn(groups):
    sizes_list = [3 * D * D, D * D, 3 * D * D, D * D, D * FF, FF * D, groups * HEADS * WIN_LAT * WIN_LAT * (2 * WIN_LON - 1), 9 * D]
    segment_marks = [0]
    for amount in sizes_list:
        segment_marks.append(segment_marks[-1] + amount)
    return segment_marks


def layout(key):
    base_key = jax.random.fold_in(key, 7)
    key_scores, key_device, key_order = jax.random.split(base_key, 3)
    slot_ids = jnp.arange(HOMES, dtype=jnp.int32)
    scores = jax.random.randint(key_scores, (HOMES,), 0, 1 << 20, dtype=jnp.int32)
    chosen_device = jax.random.randint(key_device, (), 0, HOMES // CAPACITY, dtype=jnp.int32)
    forced = (slot_ids // CAPACITY == chosen_device) | (slot_ids == 0) | (slot_ids == HOMES - 1)
    scores = jnp.where(forced, -1, scores)
    slot_order = jnp.argsort(scores, stable=True)
    chosen = slot_order[:BUCKETS]
    shuffle = jax.random.permutation(key_order, BUCKETS)
    return chosen[shuffle].astype(jnp.int32)


def slot_index(key):
    home_slots = layout(key)
    owner_bucket = jnp.full((HOMES,), -1, jnp.int32).at[home_slots].set(jnp.arange(BUCKETS, dtype=jnp.int32))
    columns = jnp.arange(BUCKET, dtype=jnp.int32)[None, :]
    return jnp.where(owner_bucket[:, None] >= 0, owner_bucket[:, None] * BUCKET + columns, PARAMS)


def per_segment(flat_index, value_list, rest):
    segment_marks = offsets_drawn(LAT_GROUPS)
    result = jnp.full(flat_index.shape, rest, jnp.float32)
    for number in range(8):
        inside = (flat_index >= segment_marks[number]) & (flat_index < segment_marks[number + 1])
        result = jnp.where(inside, value_list[number], result)
    return result


def draw_noise(key, salt):
    sub_key = jax.random.fold_in(key, salt)
    return jax.random.normal(sub_key, (HOMES, BUCKET), jnp.float32)


def grad_scales(flat_index):
    grad_root = math.sqrt(SLOTS * LEVELS * NLAT * NLON / 2.0)
    factors = [0.2, 0.3, 0.3, 0.3, 0.4, 0.4, 0.02, 0.5]
    return per_segment(flat_index, [grad_root * factor for factor in factors], 1.0)


def draw_home_slots(key, part):
    return layout(key)


def draw_master(key, part):
    flat_index = slot_index(key)
    noise_draw = draw_noise(key, 11)
    spread_table = per_segment(flat_index, [1.3 / math.sqrt(D), 4.0 / math.sqrt(D), 1.3 / math.sqrt(D), 2.0 / math.sqrt(D), 1.0 / math.sqrt(D), 1.5 / math.sqrt(FF), 0.5, 0.3], 0.05)
    segment_marks = offsets_drawn(LAT_GROUPS)
    vector_row = (flat_index - segment_marks[7]) // D
    gain_entry = (flat_index >= segment_marks[7]) & (flat_index < segment_marks[8]) & (vector_row % 3 == 0)
    return jnp.where(gain_entry, 1.0 + 0.1 * noise_draw, spread_table * noise_draw)


def draw_moment_one(key, part):
    flat_index = slot_index(key)
    return grad_scales(flat_index) * 0.67 * draw_noise(key, 13)


def draw_moment_two(key, part):
    flat_index = slot_index(key)
    scale_table = grad_scales(flat_index)
    sub_key = jax.random.fold_in(key, 17)
    factor = jnp.exp(jax.random.uniform(sub_key, (HOMES, BUCKET), jnp.float32, 0.0, math.log(4.0)))
    return scale_table * scale_table * 1.22 * factor


def levels(own_key, shape, cuts, least, largest):
    gain, own = 1.0, jax.random.fold_in(own_key, 6)
    for dim, parts in cuts:
        steps = jnp.exp(jax.random.uniform(jax.random.fold_in(own, dim), (parts,), jnp.float32, least / len(cuts), largest / len(cuts)))
        gain = gain * jnp.repeat(steps, shape[dim] // parts).reshape([-1 if axis == dim else 1 for axis in range(len(shape))])
    return gain


def gaussian(stream_key, dims, scale, bound, shards=(), held_as=jnp.bfloat16):
    entries = scale * jax.random.normal(stream_key, dims, jnp.float32)
    if shards:
        entries = entries * levels(stream_key, dims, shards, -0.22, 0.18)
    return jnp.clip(entries, -bound, bound).astype(held_as)


def setup_inputs(seed: int = 0) -> dict:
    key_of = jax.random.split(jax.random.key(seed), 9)
    inputs = gaussian(key_of[0], (SLOTS, LEVELS, NLAT, NLON, D), 1.0, 6.0, ((0, 4), (2, 4), (3, 2)))
    cotangent = gaussian(key_of[1], (SLOTS, LEVELS, NLAT, NLON, D), 1.0, 6.0, ((0, 4), (2, 4), (3, 2)))
    lead_counts = jax.random.randint(key_of[2], (SAMPLES,), 1, 5).astype(jnp.int32)
    home_slots = draw_home_slots(jax.random.fold_in(key_of[8], 71), 0)
    master = draw_master(jax.random.fold_in(key_of[8], 71), 0)
    moment_one = draw_moment_one(jax.random.fold_in(key_of[8], 71), 0)
    moment_two = draw_moment_two(jax.random.fold_in(key_of[8], 71), 0)
    step_count = jax.random.randint(key_of[7], (1,), 2, 21).astype(jnp.int32)
    return dict(inputs=inputs, cotangent=cotangent, lead_counts=lead_counts, home_slots=home_slots, master=master, moment_one=moment_one, moment_two=moment_two, step_count=step_count)


@jax.custom_vjp
def low(v):
    return lax.optimization_barrier(v.astype(jnp.bfloat16)).astype(jnp.float32)

@jax.custom_vjp
def low_back(v):
    return v

def low_keep(v):
    return (low(v), None)

def low_pass(kept, grad):
    return (grad,)

def back_keep(v):
    return (v, None)

def back_low(kept, grad):
    return (low(grad),)
low.defvjp(low_keep, low_pass)
low_back.defvjp(back_keep, back_low)
precise = lax.Precision.HIGHEST
eps_norm = 1e-05
beta_one = 0.6
beta_two = 0.45
eps_adam = 1e-08
decay_rate = 0.1
penalty_value = -1000000000.0

def offsets(groups):
    sizes_list = [3 * D * D, D * D, 3 * D * D, D * D, D * FF, FF * D, groups * HEADS * WIN_LAT * WIN_LAT * (2 * WIN_LON - 1), 9 * D]
    segment_marks = [0]
    for amount in sizes_list:
        segment_marks.append(segment_marks[-1] + amount)
    return segment_marks

def unpack(flat_params, groups):
    segment_marks = offsets(groups)
    shapes_list = [(D, 3 * D), (D, D), (D, 3 * D), (D, D), (D, FF), (FF, D), (groups, HEADS, WIN_LAT, WIN_LAT, 2 * WIN_LON - 1), (9, D)]
    return [flat_params[segment_marks[number]:segment_marks[number + 1]].reshape(shapes_list[number]) for number in range(8)]

def step_rates(flat_index, segment_marks):
    rate_list = [2.6 / math.sqrt(D), 8.0 / math.sqrt(D), 2.6 / math.sqrt(D), 4.0 / math.sqrt(D), 2.0 / math.sqrt(D), 3.0 / math.sqrt(FF), 1.0, 0.6]
    result = jnp.full(flat_index.shape, 0.1, jnp.float32)
    for number in range(8):
        inside = (flat_index >= segment_marks[number]) & (flat_index < segment_marks[number + 1])
        result = jnp.where(inside, rate_list[number], result)
    return result

def adam_step(weights, first_moment, second_moment, grad_rows, flat_index, step_value, segment_marks):
    lr_values = step_rates(flat_index, segment_marks)
    steps_float = step_value.astype(jnp.float32)
    first_new = beta_one * first_moment + (1.0 - beta_one) * grad_rows
    second_new = beta_two * second_moment + (1.0 - beta_two) * grad_rows * grad_rows
    fix_one = 1.0 - beta_one ** steps_float
    fix_two = 1.0 - beta_two ** steps_float
    update = first_new / fix_one / (jnp.sqrt(second_new / fix_two) + eps_adam) + decay_rate * weights
    return (weights - lr_values * update, first_new, second_new)

def norm_layer(values, gain_vec, shift_vec):
    center = lax.optimization_barrier(jnp.mean(values, axis=-1, keepdims=True))
    spread = lax.optimization_barrier(jnp.mean(jnp.square(values - center), axis=-1, keepdims=True))
    return (values - center) * lax.rsqrt(spread + eps_norm) * gain_vec + shift_vec

def softmax_rows(scores):
    row_max = lax.optimization_barrier(jnp.max(scores, axis=-1, keepdims=True))
    exp_scores = jnp.exp(scores - row_max)
    return exp_scores / lax.optimization_barrier(jnp.sum(exp_scores, axis=-1, keepdims=True))

def lon_table():
    query_col = jnp.arange(WIN_LON, dtype=jnp.int32)[:, None, None]
    key_col = jnp.arange(WIN_LON, dtype=jnp.int32)[None, :, None]
    offset_col = jnp.arange(2 * WIN_LON - 1, dtype=jnp.int32)[None, None, :]
    return (offset_col == query_col - key_col + WIN_LON - 1).astype(jnp.float32)

def earth_bias(earth_table):
    full_bias = jnp.einsum('ghabd,ced->ghacbe', earth_table, lon_table(), precision=precise)
    window_area = WIN_LAT * WIN_LON
    lat_pad = jnp.arange(LAT_GROUPS, dtype=jnp.int32)[:, None] * WIN_LAT + jnp.arange(window_area, dtype=jnp.int32)[None, :] // WIN_LON
    outside = (lat_pad < WIN_LAT // 2) | (lat_pad >= NLAT + WIN_LAT // 2)
    penalty = jnp.where(outside, penalty_value, 0.0)
    return full_bias.reshape(LAT_GROUPS, HEADS, window_area, window_area) + penalty[:, None, None, :]

def window_split(field_in):
    padded = jnp.pad(field_in, ((0, 0), (WIN_LAT // 2, WIN_LAT // 2), (0, 0), (0, 0)))
    rolled = jnp.roll(padded, -(WIN_LON // 2), axis=2)
    shaped = rolled.reshape(LEVELS, LAT_GROUPS, WIN_LAT, NLON // WIN_LON, WIN_LON, HEADS, HEAD_DIM)
    return shaped.transpose(0, 1, 3, 5, 2, 4, 6).reshape(LEVELS, LAT_GROUPS, NLON // WIN_LON, HEADS, WIN_LAT * WIN_LON, HEAD_DIM)

def window_join(field_in):
    shaped = field_in.reshape(LEVELS, LAT_GROUPS, NLON // WIN_LON, HEADS, WIN_LAT, WIN_LON, HEAD_DIM)
    rows_all = shaped.transpose(0, 1, 4, 2, 5, 3, 6).reshape(LEVELS, LAT_GROUPS * WIN_LAT, NLON, D)
    cropped = rows_all[:, WIN_LAT // 2:WIN_LAT // 2 + NLAT]
    return jnp.roll(cropped, WIN_LON // 2, axis=2)

def slot_block(params, tokens, gate_value):
    qkv_one, out_one, qkv_two, out_two, up_weight, down_weight, earth_table, vectors = params
    score_scale = 1.0 / math.sqrt(HEAD_DIM)
    normed = low(norm_layer(tokens, vectors[0], vectors[1]))
    mixed_rows = low_back(low(jnp.dot(normed, qkv_one, precision=precise)))
    query_win = window_split(mixed_rows[..., :D])
    key_win = window_split(mixed_rows[..., D:2 * D])
    value_win = window_split(mixed_rows[..., 2 * D:])
    scores = jnp.einsum('lgwhqe,lgwhke->lgwhqk', query_win, key_win, precision=precise) * score_scale
    scores = low_back(scores + earth_bias(earth_table)[:, None])
    attn_probs = low(softmax_rows(scores))
    attended = jnp.einsum('lgwhqk,lgwhke->lgwhqe', attn_probs, value_win, precision=precise)
    attended = low_back(low(window_join(attended)))
    branch = low_back(jnp.dot(attended, out_one, precision=precise) + vectors[2])
    tokens_one = tokens + gate_value * branch
    normed = low(norm_layer(tokens_one, vectors[3], vectors[4]))
    mixed_rows = low_back(low(jnp.dot(normed, qkv_two, precision=precise)))
    split_heads = mixed_rows.reshape(LEVELS, NLAT, NLON, 3, HEADS, HEAD_DIM)
    scores = jnp.einsum('lijhe,mijhe->ijhlm', split_heads[:, :, :, 0], split_heads[:, :, :, 1], precision=precise) * score_scale
    attn_probs = low(softmax_rows(low_back(scores)))
    attended = jnp.einsum('ijhlm,mijhe->lijhe', attn_probs, split_heads[:, :, :, 2], precision=precise).reshape(LEVELS, NLAT, NLON, D)
    attended = low_back(low(attended))
    branch = low_back(jnp.dot(attended, out_two, precision=precise) + vectors[5])
    tokens_two = tokens_one + gate_value * branch
    normed = low(norm_layer(tokens_two, vectors[6], vectors[7]))
    hidden = low_back(jnp.dot(normed, up_weight, precision=precise))
    active = low(jax.nn.gelu(hidden))
    branch = low_back(jnp.dot(active, down_weight, precision=precise) + vectors[8])
    return tokens_two + gate_value * branch

def forward(flat_params, inputs_float, slot_gates):
    params = unpack(low(flat_params), LAT_GROUPS)

    def one_slot(slot_pair):
        return slot_block(params, slot_pair[0], slot_pair[1])
    return lax.map(jax.checkpoint(one_slot), (inputs_float, slot_gates))

def reference(inputs, cotangent, lead_counts, home_slots, master, moment_one, moment_two, step_count):
    slot_ids = jnp.arange(SLOTS, dtype=jnp.int32)
    slot_gates = (slot_ids % LEADS < lead_counts[slot_ids // LEADS]).astype(jnp.float32)
    flat_params = master[home_slots].reshape(-1)
    outputs, pullback = jax.vjp(lambda weights, values: forward(weights, values, slot_gates), flat_params, inputs.astype(jnp.float32))
    grad_flat, grad_inputs = pullback(cotangent.astype(jnp.float32))
    segment_marks = offsets(LAT_GROUPS)
    grad_vectors = grad_flat[segment_marks[7]:segment_marks[8]].reshape(9, D)
    slot_grads = jnp.zeros(master.shape, jnp.float32).at[home_slots].set(grad_flat.reshape(BUCKETS, BUCKET))
    owner_bucket = jnp.full((HOMES,), -1, jnp.int32).at[home_slots].set(jnp.arange(BUCKETS, dtype=jnp.int32))
    columns = jnp.arange(BUCKET, dtype=jnp.int32)[None, :]
    flat_index = jnp.where(owner_bucket[:, None] >= 0, owner_bucket[:, None] * BUCKET + columns, PARAMS)
    new_master, new_one, new_two = adam_step(master, moment_one, moment_two, slot_grads, flat_index, step_count[0], segment_marks)
    return (outputs.astype(jnp.bfloat16), grad_inputs, grad_vectors, new_master, new_one, new_two)
```

```python
import functools
import math

import jax
import jax.numpy as jnp
from jax import lax
from jax.experimental import pallas as pl
from jax.experimental.pallas import tpu as pltpu
from jax.sharding import PartitionSpec as P

D = 192
FF = 768
HEADS = 6
HEAD_DIM = 32
LEVELS = 8
WIN_LAT = 6
WIN_LON = 12
LEADS = 4
HALF_LAT = WIN_LAT // 2
HALF_LON = WIN_LON // 2
QUAD = HALF_LAT * HALF_LON
AREA = WIN_LAT * WIN_LON
LANES = HEADS * AREA
WIDE = 256
SCALE = 1.0 / math.sqrt(HEAD_DIM)

beta_one = 0.6
beta_two = 0.45
eps_norm = 1e-05
eps_adam = 1e-08
decay_rate = 0.1
penalty_value = -1000000000.0
bf16 = jnp.bfloat16
f32 = jnp.float32


def offsets(groups):
    sizes_list = [
        3 * D * D,
        D * D,
        3 * D * D,
        D * D,
        D * FF,
        FF * D,
        groups * HEADS * WIN_LAT * WIN_LAT * (2 * WIN_LON - 1),
        9 * D,
    ]
    segment_marks = [0]
    for amount in sizes_list:
        segment_marks.append(segment_marks[-1] + amount)
    return segment_marks


def unpack(flat_params, groups):
    segment_marks = offsets(groups)
    shapes_list = [
        (D, 3 * D),
        (D, D),
        (D, 3 * D),
        (D, D),
        (D, FF),
        (FF, D),
        (groups, HEADS, WIN_LAT, WIN_LAT, 2 * WIN_LON - 1),
        (9, D),
    ]
    return [
        flat_params[segment_marks[number] : segment_marks[number + 1]].reshape(shapes_list[number])
        for number in range(8)
    ]


def step_rates(flat_index, segment_marks):
    rate_list = [
        2.6 / math.sqrt(D),
        8.0 / math.sqrt(D),
        2.6 / math.sqrt(D),
        4.0 / math.sqrt(D),
        2.0 / math.sqrt(D),
        3.0 / math.sqrt(FF),
        1.0,
        0.6,
    ]
    result = jnp.full(flat_index.shape, 0.1, jnp.float32)
    for number in range(8):
        inside = (flat_index >= segment_marks[number]) & (flat_index < segment_marks[number + 1])
        result = jnp.where(inside, rate_list[number], result)
    return result


def adam_step(
    weights, first_moment, second_moment, grad_rows, flat_index, step_value, segment_marks
):
    lr_values = step_rates(flat_index, segment_marks)
    steps_float = step_value.astype(jnp.float32)
    first_new = beta_one * first_moment + (1.0 - beta_one) * grad_rows
    second_new = beta_two * second_moment + (1.0 - beta_two) * grad_rows * grad_rows
    fix_one = 1.0 - beta_one**steps_float
    fix_two = 1.0 - beta_two**steps_float
    update = (
        first_new / fix_one / (jnp.sqrt(second_new / fix_two) + eps_adam) + decay_rate * weights
    )
    return (weights - lr_values * update, first_new, second_new)


def lon_table():
    query_col = jnp.arange(WIN_LON, dtype=jnp.int32)[:, None, None]
    key_col = jnp.arange(WIN_LON, dtype=jnp.int32)[None, :, None]
    offset_col = jnp.arange(2 * WIN_LON - 1, dtype=jnp.int32)[None, None, :]
    return (offset_col == query_col - key_col + WIN_LON - 1).astype(jnp.float32)


def nn(left, right):
    return jnp.dot(left, right, preferred_element_type=f32)


def nt(left, right):
    return lax.dot_general(left, right, (((1,), (1,)), ((), ())), preferred_element_type=f32)


def tn(left, right):
    return lax.dot_general(left, right, (((0,), (0,)), ((), ())), preferred_element_type=f32)


def normed(values):
    center = values - jnp.sum(values, axis=-1, keepdims=True) * (1.0 / D)
    spread = jnp.sum(center * center, axis=-1, keepdims=True) * (1.0 / D)
    inverse = lax.rsqrt(spread + eps_norm)
    return center * inverse, inverse


def norm_back(grad, hat, inverse, gain):
    scaled = grad * gain
    mean_one = jnp.sum(scaled, axis=-1, keepdims=True) * (1.0 / D)
    mean_two = jnp.sum(scaled * hat, axis=-1, keepdims=True) * (1.0 / D)
    return inverse * (scaled - mean_one - hat * mean_two)


def row_fold(values):
    return jnp.sum(values.reshape(values.shape[0] // 8, 8, values.shape[1]), axis=0)


def head_masks(dtype):
    lane = lax.broadcasted_iota(jnp.int32, (1, WIDE), 1) // HEAD_DIM
    return [jnp.where(lane == head, 1.0, 0.0).astype(dtype) for head in range(HEADS)]


def spread_heads(values, masks):
    return jnp.concatenate([values * mask for mask in masks], axis=0)


def fold_heads(big, count):
    parts = [big[head * count : (head + 1) * count] for head in range(HEADS)]
    lane = lax.broadcasted_iota(jnp.int32, (count, 128), 1)
    low = parts[3][:, :128]
    for head in (2, 1, 0):
        low = jnp.where(lane < HEAD_DIM * (head + 1), parts[head][:, :128], low)
    high = jnp.where(lane < HEAD_DIM, parts[4][:, 128:], parts[5][:, 128:])
    return jnp.concatenate([low, high], axis=1)


def rounded(values):
    return values.astype(bf16).astype(f32)


GROUP = 64
GLANES = HEADS * GROUP
CHUNK = 288


def block_kernel(
    levels_here,
    x_ref,
    cot_ref,
    gate_ref,
    bias_ref,
    w1_ref,
    o1_ref,
    w2_ref,
    o2_ref,
    up_ref,
    down_ref,
    vec_ref,
    res_ref,
    gin_ref,
    dw1_ref,
    do1_ref,
    dw2_ref,
    do2_ref,
    dup_ref,
    ddown_ref,
    dbias_ref,
    dvec_ref,
    n1_ref,
    hat1_ref,
    inv1_ref,
    qkv_ref,
    probs_ref,
    att_ref,
    att1_ref,
    tok1_ref,
    n2_ref,
    hat2_ref,
    inv2_ref,
    mix2_ref,
    cprobs_ref,
    att2_ref,
    n3_ref,
    act_ref,
    gh_ref,
    delta3_ref,
    delta2_ref,
    delta1_ref,
    gmid_ref,
    glow_ref,
    gatt2_ref,
    gm2_ref,
    gm1_ref,
    vacc_ref,
):
    tokens = x_ref.shape[0]
    count = tokens // AREA
    chunks = tokens // CHUNK

    def part(index):
        return pl.ds(pl.multiple_of(index * CHUNK, CHUNK), CHUNK)

    def vec(index):
        return vec_ref[index : index + 1, :]

    def gate_rows():
        gate = gate_ref[...]
        return jnp.broadcast_to(gate[None], (CHUNK // count, count, D)).reshape(CHUNK, D)

    vacc_ref[...] = jnp.zeros_like(vacc_ref)

    def note(index, values):
        vacc_ref[index] += row_fold(values)

    @pl.loop(0, chunks)
    def _(c):
        rows = part(c)
        hat, inverse = normed(x_ref[rows, :].astype(f32))
        hat1_ref[rows, :] = hat
        inv1_ref[rows, :] = jnp.broadcast_to(inverse, (CHUNK, 128))
        low = (hat * vec(0) + vec(1)).astype(bf16)
        n1_ref[rows, :] = low
        mixed = rounded(nn(low, w1_ref[...]))
        for tile in range(6):
            qkv_ref[tile, rows, :] = mixed[:, 128 * tile : 128 * (tile + 1)]

    def window(ref, first, s):
        rows = pl.ds(s, AREA, stride=count)
        return jnp.concatenate([ref[first, rows, :], ref[first + 1, rows, :]], axis=1)

    def window_store(ref, first, s, values):
        rows = pl.ds(s, AREA, stride=count)
        ref[first, rows, :] = values[:, :128]
        ref[first + 1, rows, :] = values[:, 128:]

    @pl.loop(0, count)
    def _(s):
        masks = head_masks(f32)
        query = spread_heads(window(qkv_ref, 0, s), masks).astype(bf16)
        key = window(qkv_ref, 2, s).astype(bf16)
        value = window(qkv_ref, 4, s).astype(bf16)
        scores = nt(key, query) * SCALE + bias_ref[...]
        top = jnp.max(scores, axis=0, keepdims=True)
        exps = jnp.exp(scores - top)
        probs = exps * (1.0 / jnp.sum(exps, axis=0, keepdims=True))
        probs_ref[s] = probs
        out = fold_heads(tn(probs.astype(bf16), value), AREA)
        window_store(att_ref, 0, s, out)

    @pl.loop(0, chunks)
    def _(c):
        rows = part(c)
        att = jnp.concatenate([att_ref[0, rows, :], att_ref[1, rows, :]], axis=1).astype(bf16)
        att1_ref[rows, :] = att
        branch = nn(att, o1_ref[...]) + vec(2)
        tok = x_ref[rows, :].astype(f32) + gate_rows() * branch
        tok1_ref[rows, :] = tok
        hat, inverse = normed(tok)
        hat2_ref[rows, :] = hat
        inv2_ref[rows, :] = jnp.broadcast_to(inverse, (CHUNK, 128))
        low = (hat * vec(3) + vec(4)).astype(bf16)
        n2_ref[rows, :] = low
        mix2_ref[rows, :] = nn(low, w2_ref[...]).astype(bf16)

    def column_masks():
        lane = lax.broadcasted_iota(jnp.int32, (8, GLANES), 1)
        place = (lane % GROUP) // 8
        return [place == index for index in range(GROUP // 8)]

    def squeeze_column(values, masks):
        out = values[:8]
        for index in range(1, GROUP // 8):
            out = jnp.where(masks[index], values[8 * index : 8 * index + 8], out)
        return out

    def widen_column(values, masks):
        return jnp.concatenate([jnp.where(mask, values, 0.0) for mask in masks], axis=0).astype(bf16)

    def group_rows(g):
        return pl.ds(pl.multiple_of(g * GROUP, GROUP), GROUP)

    @pl.loop(0, tokens // GROUP)
    def _(g):
        rows = group_rows(g)
        heads = head_masks(bf16)
        columns = column_masks()
        query = spread_heads(mix2_ref[rows, 0:WIDE], heads)
        key = mix2_ref[rows, WIDE : 2 * WIDE]
        value = mix2_ref[rows, 2 * WIDE : 3 * WIDE]
        scores = squeeze_column(nt(key, query), columns) * SCALE
        top = jnp.max(scores, axis=0, keepdims=True)
        exps = jnp.exp(scores - top)
        probs = exps * (1.0 / jnp.sum(exps, axis=0, keepdims=True))
        cprobs_ref[g] = probs
        out = fold_heads(tn(widen_column(probs, columns), value), GROUP)
        att2_ref[rows, :] = out.astype(bf16)

    root = math.sqrt(2.0 / math.pi)

    @pl.loop(0, chunks)
    def _(c):
        rows = part(c)
        gate = gate_rows()
        tok = tok1_ref[rows, :] + gate * (nn(att2_ref[rows, :], o2_ref[...]) + vec(5))
        hat, inverse = normed(tok)
        low = (hat * vec(6) + vec(7)).astype(bf16)
        n3_ref[rows, :] = low
        hidden = nn(low, up_ref[...])
        square = hidden * hidden
        bend = jnp.tanh(root * (hidden + 0.044715 * square * hidden))
        half = 0.5 * (1.0 + bend)
        act = (hidden * half).astype(bf16)
        act_ref[rows, :] = act
        res_ref[rows, :] = (tok + gate * (nn(act, down_ref[...]) + vec(8))).astype(bf16)
        slope = half + (0.5 * root) * hidden * (1.0 - bend * bend) * (
            1.0 + (3.0 * 0.044715) * square
        )
        after = cot_ref[rows, :].astype(f32)
        delta3 = (gate * after).astype(bf16)
        delta3_ref[rows, :] = delta3
        note(8, delta3.astype(f32))
        gh = (nt(delta3, down_ref[...]) * slope).astype(bf16)
        gh_ref[rows, :] = gh
        grad = nt(gh, up_ref[...])
        note(6, grad * hat)
        note(7, grad)
        mid = after + norm_back(grad, hat, inverse, vec(6))
        gmid_ref[rows, :] = mid
        delta2 = (gate * mid).astype(bf16)
        delta2_ref[rows, :] = delta2
        note(5, delta2.astype(f32))
        gatt2_ref[rows, :] = nt(delta2, o2_ref[...]).astype(bf16)

    @pl.loop(0, tokens // GROUP)
    def _(g):
        rows = group_rows(g)
        heads = head_masks(bf16)
        columns = column_masks()
        query = spread_heads(mix2_ref[rows, 0:WIDE], heads)
        key = mix2_ref[rows, WIDE : 2 * WIDE]
        value = mix2_ref[rows, 2 * WIDE : 3 * WIDE]
        grad = spread_heads(gatt2_ref[rows, :], heads)
        probs = cprobs_ref[g]
        slopes = squeeze_column(nt(value, grad), columns)
        slopes = probs * (slopes - jnp.sum(probs * slopes, axis=0, keepdims=True))
        wide = widen_column(slopes, columns)
        dquery = fold_heads(tn(wide, key), GROUP) * SCALE
        dkey = nn(wide, query) * SCALE
        dvalue = nn(widen_column(probs, columns), grad)
        gm2_ref[rows, 0:WIDE] = dquery.astype(bf16)
        gm2_ref[rows, WIDE : 2 * WIDE] = dkey.astype(bf16)
        gm2_ref[rows, 2 * WIDE : 3 * WIDE] = dvalue.astype(bf16)

    @pl.loop(0, chunks)
    def _(c):
        rows = part(c)
        grad = nt(gm2_ref[rows, :], w2_ref[...])
        hat = hat2_ref[rows, :]
        inverse = inv2_ref[rows, :][:, :1]
        note(3, grad * hat)
        note(4, grad)
        low = gmid_ref[rows, :] + norm_back(grad, hat, inverse, vec(3))
        glow_ref[rows, :] = low
        delta1 = (gate_rows() * low).astype(bf16)
        delta1_ref[rows, :] = delta1
        note(2, delta1.astype(f32))
        gatt = rounded(nt(delta1, o1_ref[...]))
        att_ref[0, rows, :] = gatt[:, :128]
        att_ref[1, rows, :] = gatt[:, 128:]

    dbias_ref[...] = jnp.zeros_like(dbias_ref)

    @pl.loop(0, count)
    def _(s):
        masks = head_masks(f32)
        query = spread_heads(window(qkv_ref, 0, s), masks).astype(bf16)
        key = window(qkv_ref, 2, s).astype(bf16)
        value = window(qkv_ref, 4, s).astype(bf16)
        grad = spread_heads(window(att_ref, 0, s), masks).astype(bf16)
        probs = probs_ref[s]
        slopes = nt(value, grad)
        slopes = probs * (slopes - jnp.sum(probs * slopes, axis=0, keepdims=True))
        low = slopes.astype(bf16)
        dbias_ref[...] += low.astype(f32)
        window_store(qkv_ref, 0, s, rounded(fold_heads(tn(low, key), AREA) * SCALE))
        window_store(qkv_ref, 2, s, rounded(nn(low, query) * SCALE))
        window_store(qkv_ref, 4, s, rounded(nn(probs.astype(bf16), grad)))

    @pl.loop(0, chunks)
    def _(c):
        rows = part(c)
        mixed = jnp.concatenate([qkv_ref[tile, rows, :] for tile in range(6)], axis=1).astype(bf16)
        gm1_ref[rows, :] = mixed
        grad = nt(mixed, w1_ref[...])
        hat = hat1_ref[rows, :]
        inverse = inv1_ref[rows, :][:, :1]
        note(0, grad * hat)
        note(1, grad)
        gin_ref[rows, :] = glow_ref[rows, :] + norm_back(grad, hat, inverse, vec(0))

    dw1_ref[...] = tn(n1_ref[...], gm1_ref[...])
    do1_ref[...] = tn(att1_ref[...], delta1_ref[...])
    dw2_ref[...] = tn(n2_ref[...], gm2_ref[...])
    do2_ref[...] = tn(att2_ref[...], delta2_ref[...])
    dup_ref[...] = tn(n3_ref[...], gh_ref[...])
    ddown_ref[...] = tn(act_ref[...], delta3_ref[...])
    for index in range(9):
        dvec_ref[index : index + 1, :] = jnp.sum(vacc_ref[index], axis=0, keepdims=True)


def block_call(x, cot, gate, bias, w1, o1, w2, o2, up, down, vec):
    tokens = x.shape[0]
    count = tokens // AREA
    shape = jax.ShapeDtypeStruct
    outs = [
        shape((tokens, D), bf16),
        shape((tokens, D), f32),
        shape((D, 3 * WIDE), f32),
        shape((WIDE, D), f32),
        shape((D, 3 * WIDE), f32),
        shape((WIDE, D), f32),
        shape((D, FF), f32),
        shape((FF, D), f32),
        shape((AREA, LANES), f32),
        shape((9, D), f32),
    ]
    vmem = pltpu.VMEM
    scratch = [
        vmem((tokens, D), bf16),
        vmem((tokens, D), f32),
        vmem((tokens, 128), f32),
        vmem((6, tokens, 128), f32),
        vmem((count, AREA, LANES), f32),
        vmem((2, tokens, 128), f32),
        vmem((tokens, WIDE), bf16),
        vmem((tokens, D), f32),
        vmem((tokens, D), bf16),
        vmem((tokens, D), f32),
        vmem((tokens, 128), f32),
        vmem((tokens, 3 * WIDE), bf16),
        vmem((tokens // GROUP, 8, GLANES), f32),
        vmem((tokens, WIDE), bf16),
        vmem((tokens, D), bf16),
        vmem((tokens, FF), bf16),
        vmem((tokens, FF), bf16),
        vmem((tokens, D), bf16),
        vmem((tokens, D), bf16),
        vmem((tokens, D), bf16),
        vmem((tokens, D), f32),
        vmem((tokens, D), f32),
        vmem((tokens, WIDE), bf16),
        vmem((tokens, 3 * WIDE), bf16),
        vmem((tokens, 3 * WIDE), bf16),
        vmem((9, 8, D), f32),
    ]
    spec = pl.BlockSpec(memory_space=pltpu.VMEM)
    return pl.pallas_call(
        functools.partial(block_kernel, count),
        out_shape=outs,
        in_specs=[spec] * 11,
        out_specs=[spec] * len(outs),
        scratch_shapes=scratch,
        compiler_params=pltpu.CompilerParams(vmem_limit_bytes=60 * 1024 * 1024),
        name="block",
    )(x, cot, gate, bias, w1, o1, w2, o2, up, down, vec)


def from_next(block, axis):
    count = lax.axis_size(axis)
    return lax.ppermute(block, axis, [((i + 1) % count, i) for i in range(count)])


def to_next(block, axis):
    count = lax.axis_size(axis)
    return lax.ppermute(block, axis, [(i, (i + 1) % count) for i in range(count)])


def shift_in(block):
    slots, levels = block.shape[:2]
    moved = block.reshape(slots * levels, WIN_LAT, WIN_LON, D).transpose(1, 2, 0, 3)
    right = from_next(moved[:, :HALF_LON], "lon")
    pair = jnp.stack([moved[:, HALF_LON:], right])
    below = from_next(pair[:, :HALF_LAT], "lat")
    return jnp.stack([pair[:, HALF_LAT:], below]).reshape(-1, D)


def shift_out(values, slots, levels):
    quads = values.reshape(2, 2, HALF_LAT, HALF_LON, slots * levels, D)
    above = to_next(quads[1], "lat")
    rows = jnp.concatenate([above, quads[0]], axis=1)
    left = to_next(rows[1], "lon")
    grid = jnp.concatenate([left, rows[0]], axis=1)
    return grid.transpose(2, 0, 1, 3).reshape(slots, levels, WIN_LAT, WIN_LON, D)


def pad_qkv(weight):
    return jnp.pad(weight.reshape(D, 3, D), ((0, 0), (0, 0), (0, WIDE - D))).reshape(D, 3 * WIDE)


def cut_qkv(weight):
    return weight.reshape(D, 3, WIDE)[:, :, :D].reshape(D, 3 * D)


def per_device(
    inputs, cotangent, lead_counts, home_slots, master, moment_one, moment_two, step_count
):
    slots_here = inputs.shape[0]
    levels = inputs.shape[1]
    lat_size = lax.axis_size("lat")
    lat_place = lax.axis_index("lat")
    groups = lat_size + 1
    segment_marks = offsets(groups)
    copies = lax.all_gather(master.astype(bf16), ("dp", "lat", "lon"), axis=0, tiled=True)
    bucket_rows = jnp.take(copies, home_slots, axis=0)
    qkv_one, out_one, qkv_two, out_two, up_weight, down_weight, earth_table, vectors = unpack(
        bucket_rows.reshape(-1), groups
    )
    earth_table = earth_table.astype(f32)
    vectors = vectors.astype(f32)
    slot_global = lax.axis_index("dp") * slots_here + jnp.arange(slots_here, dtype=jnp.int32)
    sample_match = (slot_global // LEADS)[:, None] == jnp.arange(
        lead_counts.shape[0], dtype=jnp.int32
    )[None, :]
    slot_counts = jnp.sum(jnp.where(sample_match, lead_counts[None, :], 0), axis=1)
    slot_gates = (slot_global % LEADS < slot_counts).astype(f32)
    gate = jnp.broadcast_to(slot_gates[:, None, None], (slots_here, levels, D)).reshape(-1, D)

    last = lat_place == lat_size - 1
    second = jnp.where(last, 0, lat_place + 1)
    halves = jnp.stack(
        [
            lax.dynamic_index_in_dim(earth_table, lat_place + 1, 0, keepdims=False)[:, :HALF_LAT],
            lax.dynamic_index_in_dim(earth_table, second, 0, keepdims=False)[:, HALF_LAT:],
        ]
    )
    full = jnp.einsum("uhabd,ced->behuac", halves, lon_table(), precision=lax.Precision.HIGHEST)
    full = full.reshape(2, HALF_LAT, 2, HALF_LON, HEADS, 2, HALF_LAT, 2, HALF_LON)
    full = full.transpose(0, 2, 1, 3, 4, 5, 7, 6, 8)
    sides = jnp.arange(2, dtype=jnp.int32)
    cross = (sides[:, None] != sides[None, :]) & last
    penalty = jnp.where(cross, penalty_value, 0.0)
    bias = (full + penalty[:, None, None, None, None, :, None, None, None]).reshape(AREA, LANES)

    x = shift_in(inputs)
    cot = shift_in(cotangent)
    pad_rows = ((0, WIDE - D), (0, 0))
    res, gin, dw1, do1, dw2, do2, dup, ddown, dbias, dvec = block_call(
        x,
        cot,
        gate,
        bias,
        pad_qkv(qkv_one),
        jnp.pad(out_one, pad_rows),
        pad_qkv(qkv_two),
        jnp.pad(out_two, pad_rows),
        up_weight,
        down_weight,
        vectors,
    )
    result = shift_out(res, slots_here, levels)
    grad_inputs = shift_out(gin.astype(bf16), slots_here, levels).astype(f32)

    dfull = dbias.reshape(2, 2, HALF_LAT, HALF_LON, HEADS, 2, 2, HALF_LAT, HALF_LON)
    dfull = dfull.transpose(0, 2, 1, 3, 4, 5, 7, 6, 8)
    dfull = dfull.reshape(WIN_LAT, WIN_LON, HEADS, 2, HALF_LAT, WIN_LON)
    dhalves = jnp.einsum("behuac,ced->uhabd", dfull, lon_table(), precision=lax.Precision.HIGHEST)
    group_ids = jnp.arange(groups, dtype=jnp.int32)[:, None, None, None, None]
    grad_earth = jnp.concatenate(
        [
            jnp.where(group_ids == lat_place + 1, dhalves[0][None], 0.0),
            jnp.where(group_ids == second, dhalves[1][None], 0.0),
        ],
        axis=2,
    )
    grad_members = [
        cut_qkv(dw1),
        do1[:D],
        cut_qkv(dw2),
        do2[:D],
        dup,
        ddown,
        grad_earth,
        dvec,
    ]
    grad_flat = jnp.concatenate([member.reshape(-1) for member in grad_members])
    bucket_total = home_slots.shape[0]
    bucket_width = master.shape[1]
    slots_mine = master.shape[0]
    grad_flat = jnp.pad(grad_flat, (0, bucket_total * bucket_width - grad_flat.shape[0]))
    grad_rows = grad_flat.reshape(bucket_total, bucket_width)
    device_place = lax.axis_index(("dp", "lat", "lon"))
    slot_ids = device_place * slots_mine + jnp.arange(slots_mine, dtype=jnp.int32)
    owner_match = home_slots[None, :] == slot_ids[:, None]
    spread_rows = (
        jnp.zeros((lax.axis_size(("dp", "lat", "lon")) * slots_mine, bucket_width), f32)
        .at[home_slots]
        .set(grad_rows)
    )
    my_grads = lax.psum_scatter(spread_rows, ("dp", "lat", "lon"), scatter_dimension=0, tiled=True)
    grad_vectors = lax.psum(dvec, ("dp", "lat", "lon"))
    bucket_ids = jnp.sum(
        jnp.where(owner_match, jnp.arange(bucket_total, dtype=jnp.int32)[None, :], 0), axis=1
    )
    present = jnp.any(owner_match, axis=1)
    columns = jnp.arange(bucket_width, dtype=jnp.int32)[None, :]
    flat_index = jnp.where(
        present[:, None], bucket_ids[:, None] * bucket_width + columns, segment_marks[8]
    )
    new_master, new_one, new_two = adam_step(
        master, moment_one, moment_two, my_grads, flat_index, step_count[0], segment_marks
    )
    return (result, grad_inputs, grad_vectors, new_master, new_one, new_two)


def solution(mesh):
    in_specs = (
        P("dp", None, "lat", "lon", None),
        P("dp", None, "lat", "lon", None),
        P(),
        P(),
        P(("dp", "lat", "lon"), None),
        P(("dp", "lat", "lon"), None),
        P(("dp", "lat", "lon"), None),
        P(),
    )
    out_specs = (
        P("dp", None, "lat", "lon", None),
        P("dp", None, "lat", "lon", None),
        P(),
        P(("dp", "lat", "lon"), None),
        P(("dp", "lat", "lon"), None),
        P(("dp", "lat", "lon"), None),
    )
    return jax.shard_map(
        per_device, mesh=mesh, in_specs=in_specs, out_specs=out_specs, check_vma=False
    )
```

```python
import functools
import math

import jax
import jax.numpy as jnp
from jax import lax
from jax.experimental import pallas as pl
from jax.experimental.pallas import tpu as pltpu
from jax.sharding import PartitionSpec as P

D = 192
FF = 768
HEADS = 6
HEAD_DIM = 32
LEVELS = 8
WIN_LAT = 6
WIN_LON = 12
LEADS = 4
HALF_LAT = WIN_LAT // 2
HALF_LON = WIN_LON // 2
QUAD = HALF_LAT * HALF_LON
AREA = WIN_LAT * WIN_LON
LANES = HEADS * AREA
WIDE = 256
SCALE = 1.0 / math.sqrt(HEAD_DIM)

beta_one = 0.6
beta_two = 0.45
eps_norm = 1e-05
eps_adam = 1e-08
decay_rate = 0.1
penalty_value = -1000000000.0
bf16 = jnp.bfloat16
f32 = jnp.float32


def offsets(groups):
    sizes_list = [
        3 * D * D,
        D * D,
        3 * D * D,
        D * D,
        D * FF,
        FF * D,
        groups * HEADS * WIN_LAT * WIN_LAT * (2 * WIN_LON - 1),
        9 * D,
    ]
    segment_marks = [0]
    for amount in sizes_list:
        segment_marks.append(segment_marks[-1] + amount)
    return segment_marks


def unpack(flat_params, groups):
    segment_marks = offsets(groups)
    shapes_list = [
        (D, 3 * D),
        (D, D),
        (D, 3 * D),
        (D, D),
        (D, FF),
        (FF, D),
        (groups, HEADS, WIN_LAT, WIN_LAT, 2 * WIN_LON - 1),
        (9, D),
    ]
    return [
        flat_params[segment_marks[number] : segment_marks[number + 1]].reshape(shapes_list[number])
        for number in range(8)
    ]


def lon_table():
    query_col = jnp.arange(WIN_LON, dtype=jnp.int32)[:, None, None]
    key_col = jnp.arange(WIN_LON, dtype=jnp.int32)[None, :, None]
    offset_col = jnp.arange(2 * WIN_LON - 1, dtype=jnp.int32)[None, None, :]
    return (offset_col == query_col - key_col + WIN_LON - 1).astype(jnp.float32)


def nn(left, right):
    return jnp.dot(left, right, preferred_element_type=f32)


def nt(left, right):
    return lax.dot_general(left, right, (((1,), (1,)), ((), ())), preferred_element_type=f32)


def tn(left, right):
    return lax.dot_general(left, right, (((0,), (0,)), ((), ())), preferred_element_type=f32)


def normed(values):
    center = values - jnp.sum(values, axis=-1, keepdims=True) * (1.0 / D)
    spread = jnp.sum(center * center, axis=-1, keepdims=True) * (1.0 / D)
    inverse = lax.rsqrt(spread + eps_norm)
    return center * inverse, inverse


def norm_back(grad, hat, inverse, gain):
    scaled = grad * gain
    mean_one = jnp.sum(scaled, axis=-1, keepdims=True) * (1.0 / D)
    mean_two = jnp.sum(scaled * hat, axis=-1, keepdims=True) * (1.0 / D)
    return inverse * (scaled - mean_one - hat * mean_two)


def row_fold(values):
    return jnp.sum(values.reshape(values.shape[0] // 8, 8, values.shape[1]), axis=0)


def head_masks(dtype):
    lane = lax.broadcasted_iota(jnp.int32, (1, WIDE), 1) // HEAD_DIM
    return [jnp.where(lane == head, 1.0, 0.0).astype(dtype) for head in range(HEADS)]


def spread_heads(values, masks):
    return jnp.concatenate([values * mask for mask in masks], axis=0)


def fold_heads(big, count):
    parts = [big[head * count : (head + 1) * count] for head in range(HEADS)]
    lane = lax.broadcasted_iota(jnp.int32, (count, 128), 1)
    low = parts[3][:, :128]
    for head in (2, 1, 0):
        low = jnp.where(lane < HEAD_DIM * (head + 1), parts[head][:, :128], low)
    high = jnp.where(lane < HEAD_DIM, parts[4][:, 128:], parts[5][:, 128:])
    return jnp.concatenate([low, high], axis=1)


def rounded(values):
    return values.astype(bf16).astype(f32)


GROUP = 64
GLANES = HEADS * GROUP
CHUNK = 288


def block_kernel(
    levels_here,
    tok_ref,
    gate_ref,
    bias_ref,
    w1_ref,
    o1_ref,
    w2_ref,
    o2_ref,
    up_ref,
    down_ref,
    vec_ref,
    out_ref,
    dw1_ref,
    do1_ref,
    dw2_ref,
    do2_ref,
    dup_ref,
    ddown_ref,
    dbias_ref,
    dvec_ref,
    n1_ref,
    hat1_ref,
    inv1_ref,
    qkv_ref,
    probs_ref,
    att_ref,
    att1_ref,
    tok1_ref,
    n2_ref,
    hat2_ref,
    inv2_ref,
    mix2_ref,
    cprobs_ref,
    att2_ref,
    n3_ref,
    act_ref,
    gh_ref,
    delta3_ref,
    delta2_ref,
    delta1_ref,
    gmid_ref,
    glow_ref,
    gatt2_ref,
    gm2_ref,
    gm1_ref,
    vacc_ref,
):
    tokens = 4 * tok_ref.shape[2]
    count = tokens // AREA
    chunks = 4

    def part(index):
        return pl.ds(pl.multiple_of(index * CHUNK, CHUNK), CHUNK)

    def vec(index):
        return vec_ref[index : index + 1, :]

    def gate_rows():
        gate = gate_ref[...]
        return jnp.broadcast_to(gate[None], (CHUNK // count, count, D)).reshape(CHUNK, D)

    vacc_ref[...] = jnp.zeros_like(vacc_ref)

    def note(index, values):
        vacc_ref[index] += row_fold(values)

    @pl.loop(0, chunks)
    def _(c):
        rows = part(c)
        hat, inverse = normed(tok_ref[c, 0].astype(f32))
        hat1_ref[rows, :] = hat
        inv1_ref[rows, :] = jnp.broadcast_to(inverse, (CHUNK, 128))
        low = (hat * vec(0) + vec(1)).astype(bf16)
        n1_ref[rows, :] = low
        mixed = rounded(nn(low, w1_ref[...]))
        for tile in range(6):
            qkv_ref[tile, rows, :] = mixed[:, 128 * tile : 128 * (tile + 1)]

    def window(ref, first, s):
        rows = pl.ds(s, AREA, stride=count)
        return jnp.concatenate([ref[first, rows, :], ref[first + 1, rows, :]], axis=1)

    def window_store(ref, first, s, values):
        rows = pl.ds(s, AREA, stride=count)
        ref[first, rows, :] = values[:, :128]
        ref[first + 1, rows, :] = values[:, 128:]

    @pl.loop(0, count)
    def _(s):
        masks = head_masks(f32)
        query = spread_heads(window(qkv_ref, 0, s), masks).astype(bf16)
        key = window(qkv_ref, 2, s).astype(bf16)
        value = window(qkv_ref, 4, s).astype(bf16)
        scores = nt(key, query) * SCALE + bias_ref[...]
        top = jnp.max(scores, axis=0, keepdims=True)
        exps = jnp.exp(scores - top)
        probs = exps * (1.0 / jnp.sum(exps, axis=0, keepdims=True))
        probs_ref[s] = probs
        out = fold_heads(tn(probs.astype(bf16), value), AREA)
        window_store(att_ref, 0, s, out)

    @pl.loop(0, chunks)
    def _(c):
        rows = part(c)
        att = jnp.concatenate([att_ref[0, rows, :], att_ref[1, rows, :]], axis=1).astype(bf16)
        att1_ref[rows, :] = att
        branch = nn(att, o1_ref[...]) + vec(2)
        tok = tok_ref[c, 0].astype(f32) + gate_rows() * branch
        tok1_ref[rows, :] = tok
        hat, inverse = normed(tok)
        hat2_ref[rows, :] = hat
        inv2_ref[rows, :] = jnp.broadcast_to(inverse, (CHUNK, 128))
        low = (hat * vec(3) + vec(4)).astype(bf16)
        n2_ref[rows, :] = low
        mix2_ref[rows, :] = nn(low, w2_ref[...]).astype(bf16)

    def column_masks():
        lane = lax.broadcasted_iota(jnp.int32, (8, GLANES), 1)
        place = (lane % GROUP) // 8
        return [place == index for index in range(GROUP // 8)]

    def squeeze_column(values, masks):
        out = values[:8]
        for index in range(1, GROUP // 8):
            out = jnp.where(masks[index], values[8 * index : 8 * index + 8], out)
        return out

    def widen_column(values, masks):
        return jnp.concatenate([jnp.where(mask, values, 0.0) for mask in masks], axis=0).astype(bf16)

    def group_rows(g):
        return pl.ds(pl.multiple_of(g * GROUP, GROUP), GROUP)

    @pl.loop(0, tokens // GROUP)
    def _(g):
        rows = group_rows(g)
        heads = head_masks(bf16)
        columns = column_masks()
        query = spread_heads(mix2_ref[rows, 0:WIDE], heads)
        key = mix2_ref[rows, WIDE : 2 * WIDE]
        value = mix2_ref[rows, 2 * WIDE : 3 * WIDE]
        scores = squeeze_column(nt(key, query), columns) * SCALE
        top = jnp.max(scores, axis=0, keepdims=True)
        exps = jnp.exp(scores - top)
        probs = exps * (1.0 / jnp.sum(exps, axis=0, keepdims=True))
        cprobs_ref[g] = probs
        out = fold_heads(tn(widen_column(probs, columns), value), GROUP)
        att2_ref[rows, :] = out.astype(bf16)

    root = math.sqrt(2.0 / math.pi)

    @pl.loop(0, chunks)
    def _(c):
        rows = part(c)
        gate = gate_rows()
        tok = tok1_ref[rows, :] + gate * (nn(att2_ref[rows, :], o2_ref[...]) + vec(5))
        hat, inverse = normed(tok)
        low = (hat * vec(6) + vec(7)).astype(bf16)
        n3_ref[rows, :] = low
        hidden = nn(low, up_ref[...])
        square = hidden * hidden
        bend = jnp.tanh(root * (hidden + 0.044715 * square * hidden))
        half = 0.5 * (1.0 + bend)
        act = (hidden * half).astype(bf16)
        act_ref[rows, :] = act
        out_ref[c, 0] = (tok + gate * (nn(act, down_ref[...]) + vec(8))).astype(bf16)
        slope = half + (0.5 * root) * hidden * (1.0 - bend * bend) * (
            1.0 + (3.0 * 0.044715) * square
        )
        after = tok_ref[c, 1].astype(f32)
        delta3 = (gate * after).astype(bf16)
        delta3_ref[rows, :] = delta3
        note(8, delta3.astype(f32))
        gh = (nt(delta3, down_ref[...]) * slope).astype(bf16)
        gh_ref[rows, :] = gh
        grad = nt(gh, up_ref[...])
        note(6, grad * hat)
        note(7, grad)
        mid = after + norm_back(grad, hat, inverse, vec(6))
        gmid_ref[rows, :] = mid
        delta2 = (gate * mid).astype(bf16)
        delta2_ref[rows, :] = delta2
        note(5, delta2.astype(f32))
        gatt2_ref[rows, :] = nt(delta2, o2_ref[...]).astype(bf16)

    @pl.loop(0, tokens // GROUP)
    def _(g):
        rows = group_rows(g)
        heads = head_masks(bf16)
        columns = column_masks()
        query = spread_heads(mix2_ref[rows, 0:WIDE], heads)
        key = mix2_ref[rows, WIDE : 2 * WIDE]
        value = mix2_ref[rows, 2 * WIDE : 3 * WIDE]
        grad = spread_heads(gatt2_ref[rows, :], heads)
        probs = cprobs_ref[g]
        slopes = squeeze_column(nt(value, grad), columns)
        slopes = probs * (slopes - jnp.sum(probs * slopes, axis=0, keepdims=True))
        wide = widen_column(slopes, columns)
        dquery = fold_heads(tn(wide, key), GROUP) * SCALE
        dkey = nn(wide, query) * SCALE
        dvalue = nn(widen_column(probs, columns), grad)
        gm2_ref[rows, 0:WIDE] = dquery.astype(bf16)
        gm2_ref[rows, WIDE : 2 * WIDE] = dkey.astype(bf16)
        gm2_ref[rows, 2 * WIDE : 3 * WIDE] = dvalue.astype(bf16)

    @pl.loop(0, chunks)
    def _(c):
        rows = part(c)
        grad = nt(gm2_ref[rows, :], w2_ref[...])
        hat = hat2_ref[rows, :]
        inverse = inv2_ref[rows, :][:, :1]
        note(3, grad * hat)
        note(4, grad)
        low = gmid_ref[rows, :] + norm_back(grad, hat, inverse, vec(3))
        glow_ref[rows, :] = low
        delta1 = (gate_rows() * low).astype(bf16)
        delta1_ref[rows, :] = delta1
        note(2, delta1.astype(f32))
        gatt = rounded(nt(delta1, o1_ref[...]))
        att_ref[0, rows, :] = gatt[:, :128]
        att_ref[1, rows, :] = gatt[:, 128:]

    dbias_ref[...] = jnp.zeros_like(dbias_ref)

    @pl.loop(0, count)
    def _(s):
        masks = head_masks(f32)
        query = spread_heads(window(qkv_ref, 0, s), masks).astype(bf16)
        key = window(qkv_ref, 2, s).astype(bf16)
        value = window(qkv_ref, 4, s).astype(bf16)
        grad = spread_heads(window(att_ref, 0, s), masks).astype(bf16)
        probs = probs_ref[s]
        slopes = nt(value, grad)
        slopes = probs * (slopes - jnp.sum(probs * slopes, axis=0, keepdims=True))
        low = slopes.astype(bf16)
        dbias_ref[...] += low.astype(f32)
        window_store(qkv_ref, 0, s, rounded(fold_heads(tn(low, key), AREA) * SCALE))
        window_store(qkv_ref, 2, s, rounded(nn(low, query) * SCALE))
        window_store(qkv_ref, 4, s, rounded(nn(probs.astype(bf16), grad)))

    @pl.loop(0, chunks)
    def _(c):
        rows = part(c)
        mixed = jnp.concatenate([qkv_ref[tile, rows, :] for tile in range(6)], axis=1).astype(bf16)
        gm1_ref[rows, :] = mixed
        grad = nt(mixed, w1_ref[...])
        hat = hat1_ref[rows, :]
        inverse = inv1_ref[rows, :][:, :1]
        note(0, grad * hat)
        note(1, grad)
        grad_in = glow_ref[rows, :] + norm_back(grad, hat, inverse, vec(0))
        out_ref[c, 1] = grad_in.astype(bf16)

    dw1_ref[...] = tn(n1_ref[...], gm1_ref[...])
    do1_ref[...] = tn(att1_ref[...], delta1_ref[...])
    dw2_ref[...] = tn(n2_ref[...], gm2_ref[...])
    do2_ref[...] = tn(att2_ref[...], delta2_ref[...])
    dup_ref[...] = tn(n3_ref[...], gh_ref[...])
    ddown_ref[...] = tn(act_ref[...], delta3_ref[...])
    for index in range(9):
        dvec_ref[index : index + 1, :] = jnp.sum(vacc_ref[index], axis=0, keepdims=True)


def block_call(tok, gate, bias, w1, o1, w2, o2, up, down, vec):
    tokens = 4 * tok.shape[2]
    count = tokens // AREA
    shape = jax.ShapeDtypeStruct
    outs = [
        shape(tok.shape, bf16),
        shape((D, 3 * WIDE), f32),
        shape((WIDE, D), f32),
        shape((D, 3 * WIDE), f32),
        shape((WIDE, D), f32),
        shape((D, FF), f32),
        shape((FF, D), f32),
        shape((AREA, LANES), f32),
        shape((9, D), f32),
    ]
    vmem = pltpu.VMEM
    scratch = [
        vmem((tokens, D), bf16),
        vmem((tokens, D), f32),
        vmem((tokens, 128), f32),
        vmem((6, tokens, 128), f32),
        vmem((count, AREA, LANES), f32),
        vmem((2, tokens, 128), f32),
        vmem((tokens, WIDE), bf16),
        vmem((tokens, D), f32),
        vmem((tokens, D), bf16),
        vmem((tokens, D), f32),
        vmem((tokens, 128), f32),
        vmem((tokens, 3 * WIDE), bf16),
        vmem((tokens // GROUP, 8, GLANES), f32),
        vmem((tokens, WIDE), bf16),
        vmem((tokens, D), bf16),
        vmem((tokens, FF), bf16),
        vmem((tokens, FF), bf16),
        vmem((tokens, D), bf16),
        vmem((tokens, D), bf16),
        vmem((tokens, D), bf16),
        vmem((tokens, D), f32),
        vmem((tokens, D), f32),
        vmem((tokens, WIDE), bf16),
        vmem((tokens, 3 * WIDE), bf16),
        vmem((tokens, 3 * WIDE), bf16),
        vmem((9, 8, D), f32),
    ]
    spec = pl.BlockSpec(memory_space=pltpu.VMEM)
    return pl.pallas_call(
        functools.partial(block_kernel, count),
        out_shape=outs,
        in_specs=[spec] * 10,
        out_specs=[spec] * len(outs),
        scratch_shapes=scratch,
        compiler_params=pltpu.CompilerParams(vmem_limit_bytes=60 * 1024 * 1024),
        name="block",
    )(tok, gate, bias, w1, o1, w2, o2, up, down, vec)


MESH = pl.DeviceIdType.MESH


def places():
    lat_size, lon_size, dp_size = lax.axis_size("lat"), lax.axis_size("lon"), lax.axis_size("dp")
    return (
        lax.axis_index("dp"),
        lax.axis_index("lat"),
        lax.axis_index("lon"),
        dp_size,
        lat_size,
        lon_size,
    )


def greet(targets):
    barrier = pltpu.get_barrier_semaphore()
    for target in targets:
        pl.semaphore_signal(barrier, inc=1, device_id=target, device_id_type=MESH)
    pl.semaphore_wait(barrier, len(targets))


def around(place, step, size):
    return lax.rem(place + step, size)


def neighbours(whole_plane):
    dp, lat, lon, dp_size, lat_size, lon_size = places()
    if whole_plane:
        steps = {(i, j) for i in range(lat_size) for j in range(lon_size)}
    else:
        steps = {(1, 0), (lat_size - 1, 0), (1, 1 % lon_size), (lat_size - 1, lon_size - 1)}
        steps |= {(2 * i, 0) for i in range(1, lat_size // 2)} | {(0, j) for j in range(lon_size)}
    steps.discard((0, 0))
    found = [(around(dp, step, dp_size), lat, lon) for step in range(1, dp_size)]
    return found + [
        (dp, around(lat, i, lat_size), around(lon, j, lon_size)) for i, j in sorted(steps)
    ]


def pairing(src, dst, sends, receives, send_slot, receive_slot, target):
    return pltpu.make_async_remote_copy(
        src_ref=src,
        dst_ref=dst,
        send_sem=sends.at[send_slot],
        recv_sem=receives.at[receive_slot],
        device_id=target,
        device_id_type=MESH,
    )


def gather_kernel(
    sizes, own_ref, quads_ref, all_ref, tokens_ref, sends, receives, keeps
):
    dp_size, lat_size, lon_size = sizes
    chips = lat_size // 2
    dp, lat, lon = lax.axis_index("dp"), lax.axis_index("lat"), lax.axis_index("lon")
    core, chip = lax.rem(lat, 2), lat // 2
    greet(neighbours(False))
    line = 0
    first = dp_size
    second = first + dp_size * max(chips, lon_size)
    cross = second + dp_size * max(chips, lon_size)
    moves = cross + dp_size

    def chip_at(step):
        return (dp, around(chip, step, chips) * 2 + core, lon)

    def lon_at(step):
        return (dp, lat, around(lon, step, lon_size))

    def run(mine):
        unit = lon * chips + chip if mine == 0 else chip * lon_size + lon
        one, two = (chips, lon_size) if mine == 0 else (lon_size, chips)
        one_at, two_at = (chip_at, lon_at) if mine == 0 else (lon_at, chip_at)
        place_two = lon if mine == 0 else chip
        begun = []

        def send(src, dst, slot, back, target):
            copy = pairing(src, dst, sends, receives, slot, back, target)
            copy.start()
            begun.append(copy)

        def await_arrival(dst, slot):
            pairing(dst, dst, sends, receives, slot, slot, chip_at(0)).wait_recv()

        own_copy = pltpu.make_async_copy(own_ref, all_ref.at[dp, mine, unit], keeps.at[0])
        own_copy.start()
        for step in range(1, dp_size):
            send(
                own_ref,
                all_ref.at[dp, mine, unit],
                line + step,
                line + dp_size - step,
                (around(dp, step, dp_size), lat, lon),
            )
        order = sorted(range(dp_size), key=lambda step: min(step, dp_size - step))
        chunk = [around(dp, step, dp_size) for step in order]
        for turn in range(dp_size + 2):
            if turn < dp_size:
                here = all_ref.at[chunk[turn], mine, unit]
                if turn:
                    await_arrival(here, line + order[turn])
                for step in range(1, one):
                    send(
                        here if turn else own_ref,
                        here,
                        first + order[turn] * one + step,
                        first + order[turn] * one + one - step,
                        one_at(step),
                    )
            if turn == 0:
                move_starts(send)
                own_copy.wait()
            if 0 <= turn - 1 < dp_size:
                back = turn - 1
                for step in range(1, one):
                    await_arrival(
                        all_ref.at[chunk[back], mine, unit], first + order[back] * one + step
                    )
                group = all_ref.at[chunk[back], mine, pl.ds(place_two * one, one)]
                for step in range(1, two):
                    send(
                        group,
                        group,
                        second + order[back] * two + step,
                        second + order[back] * two + two - step,
                        two_at(step),
                    )
            if 0 <= turn - 2 < dp_size:
                back = turn - 2
                group = all_ref.at[chunk[back], mine, pl.ds(place_two * one, one)]
                for step in range(1, two):
                    await_arrival(group, second + order[back] * two + step)
                whole = all_ref.at[chunk[back], mine]
                send(
                    whole, whole, cross + order[back], cross + order[back], (dp, chip * 2 + 1 - mine, lon)
                )
        for turn in range(dp_size):
            await_arrival(all_ref.at[chunk[turn], 1 - mine], cross + order[turn])
        for quad in range(1, 4):
            await_arrival(tokens_ref.at[quad], moves + quad)
        for copy in begun:
            copy.wait_send()

    def move_starts(send):
        for quad in range(1, 4):
            up, left = quad // 2, quad % 2
            target = (dp, around(lat, lat_size - up, lat_size), around(lon, lon_size - left, lon_size))
            send(quads_ref.at[quad], tokens_ref.at[quad], moves + quad, moves + quad, target)

    keep = pltpu.make_async_copy(quads_ref.at[0], tokens_ref.at[0], keeps.at[1])
    keep.start()
    for mine in range(2):

        @pl.when(core == mine)
        def _():
            run(mine)

    keep.wait()


def gather_call(own, quads, sizes):
    dp_size, lat_size, lon_size = sizes
    chips = lat_size // 2
    count = dp_size * (2 + 2 * max(chips, lon_size)) + 4
    return pl.pallas_call(
        functools.partial(gather_kernel, sizes),
        out_shape=[
            jax.ShapeDtypeStruct((dp_size, 2, chips * lon_size) + own.shape, own.dtype),
            jax.ShapeDtypeStruct(quads.shape, quads.dtype),
        ],
        in_specs=[pl.BlockSpec(memory_space=pltpu.VMEM)] * 2,
        out_specs=[pl.BlockSpec(memory_space=pltpu.VMEM)] * 2,
        scratch_shapes=[
            pltpu.SemaphoreType.DMA((count,)),
            pltpu.SemaphoreType.DMA((count,)),
            pltpu.SemaphoreType.DMA((2,)),
        ],
        compiler_params=pltpu.CompilerParams(
            collective_id=0, has_side_effects=True, vmem_limit_bytes=40 * 1024 * 1024
        ),
        name="gather",
    )(own, quads)


def reduce_kernel(
    sizes,
    grads_ref,
    vecs_ref,
    quads_ref,
    homes_ref,
    mine_ref,
    total_ref,
    tokens_ref,
    half_in,
    half,
    one_in,
    one,
    two_in,
    line_out,
    line_in,
    plane_out,
    plane_in,
    vec_in,
    vec_now,
    sends,
    receives,
    keeps,
):
    dp_size, lat_size, lon_size = sizes
    chips = lat_size // 2
    dp, lat, lon = lax.axis_index("dp"), lax.axis_index("lat"), lax.axis_index("lon")
    core, chip = lax.rem(lat, 2), lat // 2
    rows, buckets = grads_ref.shape[:2]
    n_half, n_side = rows // 2, rows // 4
    n_chip, n_lon, n_last = n_side // chips, n_side // lon_size, n_side // (chips * lon_size)
    plane = lat_size * lon_size
    per_home = plane_out.shape[2]
    greet(neighbours(True))
    begun = []

    def send(src, dst, slot, back, target):
        copy = pairing(src, dst, sends, receives, slot, back, target)
        copy.start()
        begun.append(copy)

    def await_arrival(dst, slot):
        pairing(dst, dst, sends, receives, slot, slot, (dp, lat, lon)).wait_recv()

    def chip_at(step):
        return (dp, around(chip, step, chips) * 2 + core, lon)

    def lon_at(step):
        return (dp, lat, around(lon, step, lon_size))

    cross = 0
    chip_one = 2
    lon_one = chip_one + 2 * chips
    lon_two = lon_one + lon_size
    chip_two = lon_two + 2 * lon_size
    line = chip_two + chips
    last = line + 2 * dp_size
    moves = last + 2 * plane

    partner = (dp, chip * 2 + 1 - core, lon)
    keep = pltpu.make_async_copy(quads_ref.at[0], tokens_ref.at[0], keeps.at[0])
    keep.start()
    send(grads_ref.at[pl.ds((1 - core) * n_half, n_half)], half_in, cross, cross, partner)
    send(vecs_ref, vec_in.at[0], cross + 1, cross + 1, partner)

    def move(kind):
        for quad in range(1, 4):
            down, right = quad // 2, quad % 2
            target = (dp, around(lat, down, lat_size), around(lon, right, lon_size))
            slot = moves + 4 * kind + quad
            send(quads_ref.at[quad, kind], tokens_ref.at[quad, kind], slot, slot, target)

    move(0)
    await_arrival(half_in, cross)
    half[...] = (grads_ref[pl.ds(core * n_half, n_half)].astype(f32) + half_in[...].astype(f32)).astype(bf16)
    await_arrival(vec_in.at[0], cross + 1)
    vec_now[0] = vecs_ref[...] + vec_in[0]

    for step in range(1, chips):
        there = around(chip, step, chips)
        back = chips - step
        send(half.at[pl.ds(there * n_chip, n_chip)], one_in.at[pl.ds(back * n_chip, n_chip)], chip_one + step, chip_one + back, chip_at(step))
        send(vec_now.at[0], vec_in.at[back], chip_one + chips + step, chip_one + chips + back, chip_at(step))
    for step in range(1, lon_size):
        there = around(lon, step, lon_size)
        back = lon_size - step
        send(
            half.at[pl.ds(n_side + there * n_lon, n_lon)],
            one_in.at[pl.ds(n_side + back * n_lon, n_lon)],
            lon_one + step,
            lon_one + back,
            lon_at(step),
        )
    total = half[pl.ds(chip * n_chip, n_chip)].astype(f32)
    vec_total = vec_now[0]
    for step in range(1, chips):
        await_arrival(one_in.at[pl.ds(step * n_chip, n_chip)], chip_one + step)
        total = total + one_in[pl.ds(step * n_chip, n_chip)].astype(f32)
        await_arrival(vec_in.at[step], chip_one + chips + step)
        vec_total = vec_total + vec_in[step]
    one[pl.ds(0, n_chip)] = total.astype(bf16)
    vec_now[1] = vec_total
    for step in range(1, lon_size):
        there = around(lon, step, lon_size)
        back = lon_size - step
        send(one.at[pl.ds(there * n_last, n_last)], two_in.at[0, pl.ds(back * n_last, n_last)], lon_two + step, lon_two + back, lon_at(step))
        send(vec_now.at[1], vec_in.at[chips + back], lon_two + lon_size + step, lon_two + lon_size + back, lon_at(step))
    total = half[pl.ds(n_side + lon * n_lon, n_lon)].astype(f32)
    for step in range(1, lon_size):
        await_arrival(one_in.at[pl.ds(n_side + step * n_lon, n_lon)], lon_one + step)
        total = total + one_in[pl.ds(n_side + step * n_lon, n_lon)].astype(f32)
    one[pl.ds(n_chip, n_lon)] = total.astype(bf16)
    for step in range(1, chips):
        there = around(chip, step, chips)
        back = chips - step
        send(
            one.at[pl.ds(n_chip + there * n_last, n_last)],
            two_in.at[1, pl.ds(back * n_last, n_last)],
            chip_two + step,
            chip_two + back,
            chip_at(step),
        )
    final_a = one[pl.ds(lon * n_last, n_last)].astype(f32)
    vec_total = vec_now[1]
    for step in range(1, lon_size):
        await_arrival(two_in.at[0, pl.ds(step * n_last, n_last)], lon_two + step)
        final_a = final_a + two_in[0, pl.ds(step * n_last, n_last)].astype(f32)
        await_arrival(vec_in.at[chips + step], lon_two + lon_size + step)
        vec_total = vec_total + vec_in[chips + step]
    vec_now[2] = vec_total
    final_b = one[pl.ds(n_chip + chip * n_last, n_last)].astype(f32)
    for step in range(1, chips):
        await_arrival(two_in.at[1, pl.ds(step * n_last, n_last)], chip_two + step)
        final_b = final_b + two_in[1, pl.ds(step * n_last, n_last)].astype(f32)
    final = jnp.concatenate([final_a, final_b], axis=0).astype(bf16)

    width = plane * per_home
    homes = homes_ref[...]
    place = lax.broadcasted_iota(jnp.int32, (dp_size * width, buckets), 0)
    turn = lax.rem(place // width + dp, dp_size)
    pick = jnp.where(turn * width + lax.rem(place, width) == homes, 1.0, 0.0).astype(bf16)
    for row in range(2 * n_last):
        picked = nn(pick, final[row]).astype(bf16)
        for step in range(dp_size):
            line_out[step, row] = picked[step * width : (step + 1) * width]
    for step in range(dp_size):
        there = around(dp, step, dp_size)
        if step:
            back = dp_size - step
            send(line_out.at[step], line_in.at[back], line + step, line + back, (there, lat, lon))
            send(vec_now.at[2], vec_in.at[chips + lon_size + back], line + dp_size + step, line + dp_size + back, (there, lat, lon))
    move(1)
    summed = line_out[0].astype(f32)
    vec_total = vec_now[2]
    for step in range(1, dp_size):
        await_arrival(line_in.at[step], line + step)
        summed = summed + line_in[step].astype(f32)
        await_arrival(vec_in.at[chips + lon_size + step], line + dp_size + step)
        vec_total = vec_total + vec_in[chips + lon_size + step]
    total_ref[...] = vec_total
    for home in range(plane):
        plane_out[home] = summed[:, per_home * home : per_home * (home + 1), :]
    row_a = core * n_half + chip * n_chip + lon * n_last
    row_b = core * n_half + n_side + lon * n_lon + chip * n_last
    me = lat * lon_size + lon
    for lat_step in range(lat_size):
        for lon_step in range(lon_size):
            there = (dp, around(lat, lat_step, lat_size), around(lon, lon_step, lon_size))
            home = there[1] * lon_size + there[2]
            slot = last + 2 * (lat_step * lon_size + lon_step)
            back = last + 2 * ((lat_size - lat_step) % lat_size * lon_size + (lon_size - lon_step) % lon_size)
            if lat_step == 0 and lon_step == 0:
                for side, row in enumerate((row_a, row_b)):
                    copy = pltpu.make_async_copy(
                        plane_out.at[me, pl.ds(side * n_last, n_last)],
                        mine_ref.at[pl.ds(row, n_last)],
                        keeps.at[1 + side],
                    )
                    copy.start()
                continue
            for side, row in enumerate((row_a, row_b)):
                send(
                    plane_out.at[home, pl.ds(side * n_last, n_last)],
                    mine_ref.at[pl.ds(row, n_last)],
                    slot + side,
                    back + side,
                    there,
                )
    for side, row in enumerate((row_a, row_b)):
        pltpu.make_async_copy(
            plane_out.at[me, pl.ds(side * n_last, n_last)],
            mine_ref.at[pl.ds(row, n_last)],
            keeps.at[1 + side],
        ).wait()
    for index in range(1, plane):
        for side in range(2):
            await_arrival(mine_ref.at[pl.ds(0, n_last)], last + 2 * index + side)
    for kind in range(2):
        for quad in range(1, 4):
            await_arrival(tokens_ref.at[quad, kind], moves + 4 * kind + quad)
    keep.wait()
    for copy in begun:
        copy.wait_send()


def reduce_call(grads, vecs, quads, homes, per_home, sizes):
    dp_size, lat_size, lon_size = sizes
    chips = lat_size // 2
    rows, buckets = grads.shape[:2]
    plane = lat_size * lon_size
    n_half, n_side = rows // 2, rows // 4
    n_chip, n_lon, n_last = n_side // chips, n_side // lon_size, n_side // (chips * lon_size)
    count = 2 + 2 * chips + lon_size + 2 * lon_size + chips + 2 * dp_size + 2 * plane + 8
    vmem = pltpu.VMEM
    return pl.pallas_call(
        functools.partial(reduce_kernel, sizes),
        out_shape=[
            jax.ShapeDtypeStruct((rows, per_home, 128), f32),
            jax.ShapeDtypeStruct(vecs.shape, f32),
            jax.ShapeDtypeStruct(quads.shape, quads.dtype),
        ],
        in_specs=[pl.BlockSpec(memory_space=pltpu.VMEM)] * 4,
        out_specs=[pl.BlockSpec(memory_space=pltpu.VMEM)] * 3,
        scratch_shapes=[
            vmem((n_half, buckets, 128), bf16),
            vmem((n_half, buckets, 128), bf16),
            vmem((n_half, buckets, 128), bf16),
            vmem((n_chip + n_lon, buckets, 128), bf16),
            vmem((2, max(n_chip, n_lon), buckets, 128), bf16),
            vmem((dp_size, 2 * n_last, plane * per_home, 128), bf16),
            vmem((dp_size, 2 * n_last, plane * per_home, 128), bf16),
            vmem((plane, 2 * n_last, per_home, 128), f32),
            vmem((8, 128), f32),
            vmem((chips + lon_size + dp_size,) + vecs.shape, f32),
            vmem((3,) + vecs.shape, f32),
            pltpu.SemaphoreType.DMA((count,)),
            pltpu.SemaphoreType.DMA((count,)),
            pltpu.SemaphoreType.DMA((3,)),
        ],
        compiler_params=pltpu.CompilerParams(
            collective_id=1, has_side_effects=True, vmem_limit_bytes=40 * 1024 * 1024
        ),
        name="reduce",
    )(grads, vecs, quads, homes)


def adam_kernel(steps_ref, buckets_ref, marks, grads_ref, master_ref, one_ref, two_ref, new_master, new_one, new_two):
    homes = master_ref.shape[0]
    tiles = master_ref.shape[1] // 128
    steps = jnp.full((homes, 128), steps_ref[0], jnp.int32).astype(f32)
    fix_one = 1.0 / (1.0 - jnp.exp(steps * math.log(beta_one)))
    fix_two = 1.0 / (1.0 - jnp.exp(steps * math.log(beta_two)))
    base = jnp.concatenate(
        [jnp.full((1, 128), buckets_ref[home], jnp.int32) for home in range(homes)], axis=0
    ) + lax.broadcasted_iota(jnp.int32, (homes, 128), 1)
    rates = [2.6 / math.sqrt(D), 8.0 / math.sqrt(D), 2.6 / math.sqrt(D), 4.0 / math.sqrt(D), 2.0 / math.sqrt(D), 3.0 / math.sqrt(FF), 1.0, 0.6]
    for tile in range(tiles):
        columns = slice(128 * tile, 128 * (tile + 1))
        index = base + 128 * tile
        rate = jnp.full((homes, 128), 0.1, f32)
        for number in range(7, -1, -1):
            rate = jnp.where(index < marks[number + 1], rates[number], rate)
        grad = grads_ref[tile]
        weights = master_ref[:, columns]
        first = beta_one * one_ref[:, columns] + (1.0 - beta_one) * grad
        second = beta_two * two_ref[:, columns] + (1.0 - beta_two) * grad * grad
        step = first * fix_one / (jnp.sqrt(second * fix_two) + eps_adam) + decay_rate * weights
        new_master[:, columns] = weights - rate * step
        new_one[:, columns] = first
        new_two[:, columns] = second


def adam_call(steps, bases, marks, grads, master, one, two):
    smem = pl.BlockSpec(memory_space=pltpu.SMEM)
    vmem = pl.BlockSpec(memory_space=pltpu.VMEM)

    def body(steps_ref, bases_ref, *refs):
        adam_kernel(steps_ref, bases_ref, marks, *refs)

    return pl.pallas_call(
        body,
        out_shape=[jax.ShapeDtypeStruct(master.shape, f32)] * 3,
        in_specs=[smem, smem, vmem, vmem, vmem, vmem],
        out_specs=[vmem] * 3,
        name="adam",
    )(steps, bases, grads, master, one, two)


def quads_out(block):
    slots, levels = block.shape[:2]
    split = block.reshape(slots * levels, 2, HALF_LAT, 2, HALF_LON, D)
    return split.transpose(1, 3, 2, 4, 0, 5)[::-1, ::-1].reshape(4, -1, D)


def quads_back(quads, slots, levels):
    split = quads.reshape(2, 2, HALF_LAT, HALF_LON, slots * levels, D)[::-1, ::-1]
    return split.transpose(4, 0, 2, 1, 3, 5).reshape(slots, levels, WIN_LAT, WIN_LON, D)


def pad_qkv(weight):
    return jnp.pad(weight.reshape(D, 3, D), ((0, 0), (0, 0), (0, WIDE - D))).reshape(D, 3 * WIDE)


def cut_qkv(weight):
    return weight.reshape(D, 3, WIDE)[:, :, :D].reshape(D, 3 * D)


def per_device(
    inputs, cotangent, lead_counts, home_slots, master, moment_one, moment_two, step_count
):
    slots_here = inputs.shape[0]
    levels = inputs.shape[1]
    lat_size = lax.axis_size("lat")
    lat_place = lax.axis_index("lat")
    groups = lat_size + 1
    segment_marks = offsets(groups)
    dp_size, lon_size = lax.axis_size("dp"), lax.axis_size("lon")
    sizes = (dp_size, lat_size, lon_size)
    slots_mine, bucket_width = master.shape
    bucket_total = home_slots.shape[0]
    tiles = bucket_width // 128
    tiles_up = -(-tiles // 16) * 16
    own = jnp.pad(
        master.reshape(slots_mine, tiles, 128), ((0, 0), (0, tiles_up - tiles), (0, 0))
    ).astype(bf16)
    quads = jnp.stack([quads_out(inputs), quads_out(cotangent)], axis=1)
    copies, tok = gather_call(own, quads, sizes)
    home_device = home_slots // slots_mine
    home_lon = home_device % lon_size
    home_lat = home_device // lon_size % lat_size
    chips = lat_size // 2
    home_unit = jnp.where(
        home_lat % 2 == 0, home_lon * chips + home_lat // 2, home_lat // 2 * lon_size + home_lon
    )
    home_place = (home_device // (lon_size * lat_size) * 2 + home_lat % 2) * (chips * lon_size)
    home_place = (home_place + home_unit) * slots_mine + home_slots % slots_mine
    bucket_rows = jnp.take(copies.reshape(-1, tiles_up, 128), home_place, axis=0)[:, :tiles]
    qkv_one, out_one, qkv_two, out_two, up_weight, down_weight, earth_table, vectors = unpack(
        bucket_rows.reshape(-1), groups
    )
    earth_table = earth_table.astype(f32)
    vectors = vectors.astype(f32)
    slot_global = lax.axis_index("dp") * slots_here + jnp.arange(slots_here, dtype=jnp.int32)
    sample_match = (slot_global // LEADS)[:, None] == jnp.arange(
        lead_counts.shape[0], dtype=jnp.int32
    )[None, :]
    slot_counts = jnp.sum(jnp.where(sample_match, lead_counts[None, :], 0), axis=1)
    slot_gates = (slot_global % LEADS < slot_counts).astype(f32)
    gate = jnp.broadcast_to(slot_gates[:, None, None], (slots_here, levels, D)).reshape(-1, D)

    last = lat_place == lat_size - 1
    second = jnp.where(last, 0, lat_place + 1)
    halves = jnp.stack(
        [
            lax.dynamic_index_in_dim(earth_table, lat_place + 1, 0, keepdims=False)[:, :HALF_LAT],
            lax.dynamic_index_in_dim(earth_table, second, 0, keepdims=False)[:, HALF_LAT:],
        ]
    )
    full = jnp.einsum("uhabd,ced->behuac", halves, lon_table(), precision=lax.Precision.HIGHEST)
    full = full.reshape(2, HALF_LAT, 2, HALF_LON, HEADS, 2, HALF_LAT, 2, HALF_LON)
    full = full.transpose(0, 2, 1, 3, 4, 5, 7, 6, 8)
    sides = jnp.arange(2, dtype=jnp.int32)
    cross = (sides[:, None] != sides[None, :]) & last
    penalty = jnp.where(cross, penalty_value, 0.0)
    bias = (full + penalty[:, None, None, None, None, :, None, None, None]).reshape(AREA, LANES)

    pad_rows = ((0, WIDE - D), (0, 0))
    out_tok, dw1, do1, dw2, do2, dup, ddown, dbias, dvec = block_call(
        tok,
        gate,
        bias,
        pad_qkv(qkv_one),
        jnp.pad(out_one, pad_rows),
        pad_qkv(qkv_two),
        jnp.pad(out_two, pad_rows),
        up_weight,
        down_weight,
        vectors,
    )
    dfull = dbias.reshape(2, 2, HALF_LAT, HALF_LON, HEADS, 2, 2, HALF_LAT, HALF_LON)
    dfull = dfull.transpose(0, 2, 1, 3, 4, 5, 7, 6, 8)
    dfull = dfull.reshape(WIN_LAT, WIN_LON, HEADS, 2, HALF_LAT, WIN_LON)
    dhalves = jnp.einsum("behuac,ced->uhabd", dfull, lon_table(), precision=lax.Precision.HIGHEST)
    group_ids = jnp.arange(groups, dtype=jnp.int32)[:, None, None, None, None]
    grad_earth = jnp.concatenate(
        [
            jnp.where(group_ids == lat_place + 1, dhalves[0][None], 0.0),
            jnp.where(group_ids == second, dhalves[1][None], 0.0),
        ],
        axis=2,
    )
    grad_members = [
        cut_qkv(dw1),
        do1[:D],
        cut_qkv(dw2),
        do2[:D],
        dup,
        ddown,
        grad_earth,
        dvec,
    ]
    grad_flat = jnp.concatenate([member.reshape(-1) for member in grad_members])
    grad_flat = jnp.pad(grad_flat, (0, bucket_total * bucket_width - grad_flat.shape[0]))
    unit = 4 * chips * lon_size
    rows_up = -(-tiles // unit) * unit
    grad_rows = grad_flat.reshape(bucket_total, tiles, 128).transpose(1, 0, 2)
    grad_rows = jnp.pad(grad_rows, ((0, rows_up - tiles), (0, 0), (0, 0))).astype(bf16)
    my_grads, grad_vectors, tok_back = reduce_call(
        grad_rows, dvec, out_tok, home_slots[None, :], slots_mine, sizes
    )
    device_place = lax.axis_index(("dp", "lat", "lon"))
    slot_ids = device_place * slots_mine + jnp.arange(slots_mine, dtype=jnp.int32)
    owner_match = home_slots[None, :] == slot_ids[:, None]
    bucket_ids = jnp.sum(
        jnp.where(owner_match, jnp.arange(bucket_total, dtype=jnp.int32)[None, :], 0), axis=1
    )
    present = jnp.any(owner_match, axis=1)
    bases = jnp.where(present, bucket_ids * bucket_width, segment_marks[8])
    new_master, new_one, new_two = adam_call(
        step_count, bases, segment_marks, my_grads, master, moment_one, moment_two
    )
    result = quads_back(tok_back[:, 0], slots_here, levels)
    grad_inputs = quads_back(tok_back[:, 1], slots_here, levels).astype(f32)
    return (result, grad_inputs, grad_vectors + 0.0, new_master, new_one, new_two)


def solution(mesh):
    in_specs = (
        P("dp", None, "lat", "lon", None),
        P("dp", None, "lat", "lon", None),
        P(),
        P(),
        P(("dp", "lat", "lon"), None),
        P(("dp", "lat", "lon"), None),
        P(("dp", "lat", "lon"), None),
        P(),
    )
    out_specs = (
        P("dp", None, "lat", "lon", None),
        P("dp", None, "lat", "lon", None),
        P(),
        P(("dp", "lat", "lon"), None),
        P(("dp", "lat", "lon"), None),
        P(("dp", "lat", "lon"), None),
    )
    return jax.shard_map(
        per_device, mesh=mesh, in_specs=in_specs, out_specs=out_specs, check_vma=False
    )
```

```python
import functools
import math

import jax
import jax.numpy as jnp
import ml_dtypes
import numpy as np
from jax import lax
from jax.experimental import pallas as pl
from jax.experimental.pallas import tpu as pltpu
from jax.sharding import PartitionSpec as P

D = 192
FF = 768
HEADS = 6
HEAD_DIM = 32
LEVELS = 8
WIN_LAT = 6
WIN_LON = 12
LEADS = 4
HALF_LAT = WIN_LAT // 2
HALF_LON = WIN_LON // 2
QUAD = HALF_LAT * HALF_LON
AREA = WIN_LAT * WIN_LON
LANES = HEADS * AREA
WIDE = 256
SCALE = 1.0 / math.sqrt(HEAD_DIM)

beta_one = 0.6
beta_two = 0.45
eps_norm = 1e-05
eps_adam = 1e-08
decay_rate = 0.1
penalty_value = -1000000000.0
bf16 = jnp.bfloat16
f32 = jnp.float32


def offsets(groups):
    sizes_list = [
        3 * D * D,
        D * D,
        3 * D * D,
        D * D,
        D * FF,
        FF * D,
        groups * HEADS * WIN_LAT * WIN_LAT * (2 * WIN_LON - 1),
        9 * D,
    ]
    segment_marks = [0]
    for amount in sizes_list:
        segment_marks.append(segment_marks[-1] + amount)
    return segment_marks


def nn(left, right):
    return jnp.dot(left, right, preferred_element_type=f32)


def nt(left, right):
    return lax.dot_general(left, right, (((1,), (1,)), ((), ())), preferred_element_type=f32)


def tn(left, right):
    return lax.dot_general(left, right, (((0,), (0,)), ((), ())), preferred_element_type=f32)


def normed(values):
    center = values - jnp.sum(values, axis=-1, keepdims=True) * (1.0 / D)
    spread = jnp.sum(center * center, axis=-1, keepdims=True) * (1.0 / D)
    inverse = lax.rsqrt(spread + eps_norm)
    return center * inverse, inverse


def norm_back(grad, hat, inverse, gain):
    scaled = grad * gain
    mean_one = jnp.sum(scaled, axis=-1, keepdims=True) * (1.0 / D)
    mean_two = jnp.sum(scaled * hat, axis=-1, keepdims=True) * (1.0 / D)
    return inverse * (scaled - mean_one - hat * mean_two)


def row_fold(values):
    return jnp.sum(values.reshape(values.shape[0] // 8, 8, values.shape[1]), axis=0)


def head_masks(dtype):
    lane = lax.broadcasted_iota(jnp.int32, (1, WIDE), 1) // HEAD_DIM
    return [jnp.where(lane == head, 1.0, 0.0).astype(dtype) for head in range(HEADS)]


def spread_heads(values, masks):
    return jnp.concatenate([values * mask for mask in masks], axis=0)


def fold_heads(big, count):
    parts = [big[head * count : (head + 1) * count] for head in range(HEADS)]
    lane = lax.broadcasted_iota(jnp.int32, (count, 128), 1)
    low = parts[3][:, :128]
    for head in (2, 1, 0):
        low = jnp.where(lane < HEAD_DIM * (head + 1), parts[head][:, :128], low)
    high = jnp.where(lane < HEAD_DIM, parts[4][:, 128:], parts[5][:, 128:])
    return jnp.concatenate([low, high], axis=1)


def rounded(values):
    return values.astype(bf16).astype(f32)


GROUP = 64
GLANES = HEADS * GROUP
CHUNK = 288


def lanes_of(ref, start):
    row, lane = divmod(start, 128)
    here = ref[row : row + 1, :]
    if lane == 0:
        return here
    place = lax.broadcasted_iota(jnp.int32, (1, 128), 1)
    mixed = jnp.where(place >= lane, here, ref[row + 1 : row + 2, :])
    return pltpu.roll(mixed, 128 - lane, 1)


def tail_head(tail, head):
    place = lax.broadcasted_iota(jnp.int32, tail.shape, 1)
    return pltpu.roll(jnp.where(place >= 64, tail, head), 64, 1)


def head_head(first, second):
    place = lax.broadcasted_iota(jnp.int32, first.shape, 1)
    return jnp.where(place < 64, first, pltpu.roll(second, 64, 1))


def only_head(values):
    place = lax.broadcasted_iota(jnp.int32, values.shape, 1)
    return jnp.where(place < 64, values, 0.0)


def only_tail(values):
    place = lax.broadcasted_iota(jnp.int32, values.shape, 1)
    return pltpu.roll(jnp.where(place >= 64, values, 0.0), 64, 1)


EARTH_ROW = WIN_LAT * (2 * WIN_LON - 1)
EARTH_ROWS = HEADS * WIN_LAT


def earth_tables():
    entry = np.zeros((WIN_LON, AREA, 256), np.float32)
    place = np.zeros((WIN_LON, 40, LANES), np.float32)
    for column in range(WIN_LON):
        side, inner = divmod(column, HALF_LON)
        for key in range(AREA):
            key_up, rest = divmod(key, 2 * QUAD)
            key_side, rest = divmod(rest, QUAD)
            key_row, key_inner = divmod(rest, HALF_LON)
            row = key_up * HALF_LAT + key_row
            offset = column - (key_side * HALF_LON + key_inner) + WIN_LON - 1
            entry[column, key, row * (2 * WIN_LON - 1) + offset] = 1.0
        for head in range(HEADS):
            for row in range(WIN_LAT):
                up, low = divmod(row, HALF_LAT)
                lane = AREA * head + 2 * QUAD * up + QUAD * side + HALF_LON * low + inner
                place[column, head * WIN_LAT + row, lane] = 1.0
    return entry.astype(ml_dtypes.bfloat16), place.astype(ml_dtypes.bfloat16)


def block_kernel(
    sizes,
    home_ref,
    lead_ref,
    tok_ref,
    copies_ref,
    entry_ref,
    place_ref,
    out_ref,
    grads_ref,
    dvec_ref,
    flat_ref,
    mid_ref,
    earth_ref,
    gate_ref,
    bias_ref,
    dbias_ref,
    w1_ref,
    o1_ref,
    w2_ref,
    o2_ref,
    up_ref,
    down_ref,
    vec_ref,
    n1_ref,
    hat1_ref,
    inv1_ref,
    qkv_ref,
    probs_ref,
    att_ref,
    att1_ref,
    tok1_ref,
    n2_ref,
    hat2_ref,
    inv2_ref,
    mix2_ref,
    cprobs_ref,
    att2_ref,
    n3_ref,
    act_ref,
    gh_ref,
    delta3_ref,
    delta2_ref,
    delta1_ref,
    gmid_ref,
    glow_ref,
    gatt2_ref,
    gm2_ref,
    gm1_ref,
    vacc_ref,
):
    tokens = 4 * tok_ref.shape[2]
    count = tokens // AREA
    chunks = 4
    buckets, tiles, lat_size, slots_here = sizes
    lat = lax.axis_index("lat")
    is_last = lat == lat_size - 1
    marks = offsets(lat_size + 1)
    row_marks = [mark // 128 for mark in marks]

    for bucket in range(buckets):
        block = copies_ref[home_ref[bucket]].astype(f32)
        flat_ref[tiles * bucket : tiles * (bucket + 1), :] = block[:tiles]

    def take_pairs(base, parts, pairs):
        return [flat_ref[pl.ds(base + part, pairs, stride=parts), :] for part in range(parts)]

    def give_pairs(columns, rows, evens, odds):
        for column, (even, odd) in enumerate(zip(evens, odds)):
            mid_ref[column, pl.ds(0, rows // 2, stride=2), :] = even
            mid_ref[column, pl.ds(1, rows // 2, stride=2), :] = odd

    def load_qkv(base, ref):
        b = take_pairs(base, 9, D // 2)
        evens = [b[0], only_head(b[1]), tail_head(b[1], b[2]), only_tail(b[2]), b[3], only_head(b[4])]
        odds = [tail_head(b[4], b[5]), only_tail(b[5]), b[6], only_head(b[7]), tail_head(b[7], b[8]), only_tail(b[8])]
        give_pairs(6, D, evens, odds)
        for column in range(6):
            ref[:, 128 * column : 128 * (column + 1)] = mid_ref[column, pl.ds(0, D), :].astype(bf16)

    def load_square(base, rows, ref):
        b = take_pairs(base, 3, rows // 2)
        give_pairs(2, rows, [b[0], b[1]], [tail_head(b[1], b[2]), only_tail(b[2])])
        ref[0:rows, 0:128] = mid_ref[0, pl.ds(0, rows), :].astype(bf16)
        ref[0:rows, 128:D] = mid_ref[1, pl.ds(0, rows), :][:, : D - 128].astype(bf16)

    load_qkv(row_marks[0], w1_ref)
    load_square(row_marks[1], D, o1_ref)
    load_qkv(row_marks[2], w2_ref)
    load_square(row_marks[3], D, o2_ref)
    for ref in (o1_ref, o2_ref):
        ref[D:WIDE, :] = jnp.zeros((WIDE - D, D), bf16)
    for column in range(6):
        up_ref[:, 128 * column : 128 * (column + 1)] = flat_ref[
            pl.ds(row_marks[4] + column, D, stride=6), :
        ].astype(bf16)
    load_square(row_marks[5], FF, down_ref)
    for index in range(9):
        start = marks[7] + D * index
        vec_ref[index : index + 1, 0:128] = lanes_of(flat_ref, start)
        vec_ref[index : index + 1, 128:D] = lanes_of(flat_ref, start + 128)[:, : D - 128]

    def earth_places():
        group_one = lat + 1
        group_two = jnp.where(is_last, 0, lat + 1)
        for index in range(EARTH_ROWS):
            group = group_one if index % WIN_LAT < HALF_LAT else group_two
            start = marks[6] + EARTH_ROW * (EARTH_ROWS * group + index)
            row = start // 128
            yield index, row, start - 128 * row

    lane_place = lax.broadcasted_iota(jnp.int32, (1, 128), 1)
    earth_ref[...] = jnp.zeros_like(earth_ref)
    for index, row, lane in earth_places():
        rows = [flat_ref[pl.ds(row + step, 1), :] for step in range(3)]
        back = lax.rem(128 - lane, 128)
        first = pltpu.roll(jnp.where(lane_place >= lane, rows[0], rows[1]), back, 1)
        second = pltpu.roll(jnp.where(lane_place >= lane, rows[1], rows[2]), back, 1)
        earth_ref[index : index + 1, 0:128] = first
        earth_ref[index : index + 1, 128:256] = jnp.where(lane_place < EARTH_ROW - 128, second, 0.0)
    earth = earth_ref[...].astype(bf16)
    key_up = lax.broadcasted_iota(jnp.int32, (AREA, LANES), 0) // (2 * QUAD)
    query_up = lax.rem(lax.broadcasted_iota(jnp.int32, (AREA, LANES), 1), AREA) // (2 * QUAD)
    bias = jnp.where((key_up != query_up) & is_last, penalty_value, 0.0)
    for column in range(WIN_LON):
        bias = bias + nn(nt(entry_ref[column], earth).astype(bf16), place_ref[column])
    bias_ref[...] = bias

    for slot in range(slots_here):
        number = lax.axis_index("dp") * slots_here + slot
        live = lax.rem(number, LEADS) < lead_ref[number // LEADS]
        size = count // slots_here
        gate_ref[slot * size : (slot + 1) * size, :] = jnp.full((size, D), jnp.where(live, 1.0, 0.0), f32)

    def part(index):
        return pl.ds(pl.multiple_of(index * CHUNK, CHUNK), CHUNK)

    def vec(index):
        return vec_ref[index : index + 1, :]

    def gate_rows():
        gate = gate_ref[...]
        return jnp.broadcast_to(gate[None], (CHUNK // count, count, D)).reshape(CHUNK, D)

    vacc_ref[...] = jnp.zeros_like(vacc_ref)

    def note(index, values):
        vacc_ref[index] += row_fold(values)

    @pl.loop(0, chunks)
    def _(c):
        rows = part(c)
        hat, inverse = normed(tok_ref[c, 0].astype(f32))
        hat1_ref[rows, :] = hat
        inv1_ref[rows, :] = jnp.broadcast_to(inverse, (CHUNK, 128))
        low = (hat * vec(0) + vec(1)).astype(bf16)
        n1_ref[rows, :] = low
        mixed = rounded(nn(low, w1_ref[...]))
        for tile in range(6):
            qkv_ref[tile, rows, :] = mixed[:, 128 * tile : 128 * (tile + 1)]

    def window(ref, first, s):
        rows = pl.ds(s, AREA, stride=count)
        return jnp.concatenate([ref[first, rows, :], ref[first + 1, rows, :]], axis=1)

    def window_store(ref, first, s, values):
        rows = pl.ds(s, AREA, stride=count)
        ref[first, rows, :] = values[:, :128]
        ref[first + 1, rows, :] = values[:, 128:]

    @pl.loop(0, count)
    def _(s):
        masks = head_masks(f32)
        query = spread_heads(window(qkv_ref, 0, s), masks).astype(bf16)
        key = window(qkv_ref, 2, s).astype(bf16)
        value = window(qkv_ref, 4, s).astype(bf16)
        scores = nt(key, query) * SCALE + bias_ref[...]
        top = jnp.max(scores, axis=0, keepdims=True)
        exps = jnp.exp(scores - top)
        probs = exps * (1.0 / jnp.sum(exps, axis=0, keepdims=True))
        probs_ref[s] = probs
        out = fold_heads(tn(probs.astype(bf16), value), AREA)
        window_store(att_ref, 0, s, out)

    @pl.loop(0, chunks)
    def _(c):
        rows = part(c)
        att = jnp.concatenate([att_ref[0, rows, :], att_ref[1, rows, :]], axis=1).astype(bf16)
        att1_ref[rows, :] = att
        branch = nn(att, o1_ref[...]) + vec(2)
        tok = tok_ref[c, 0].astype(f32) + gate_rows() * branch
        tok1_ref[rows, :] = tok
        hat, inverse = normed(tok)
        hat2_ref[rows, :] = hat
        inv2_ref[rows, :] = jnp.broadcast_to(inverse, (CHUNK, 128))
        low = (hat * vec(3) + vec(4)).astype(bf16)
        n2_ref[rows, :] = low
        mix2_ref[rows, :] = nn(low, w2_ref[...]).astype(bf16)

    def column_masks():
        lane = lax.broadcasted_iota(jnp.int32, (8, GLANES), 1)
        place = (lane % GROUP) // 8
        return [place == index for index in range(GROUP // 8)]

    def squeeze_column(values, masks):
        out = values[:8]
        for index in range(1, GROUP // 8):
            out = jnp.where(masks[index], values[8 * index : 8 * index + 8], out)
        return out

    def widen_column(values, masks):
        return jnp.concatenate([jnp.where(mask, values, 0.0) for mask in masks], axis=0).astype(bf16)

    def group_rows(g):
        return pl.ds(pl.multiple_of(g * GROUP, GROUP), GROUP)

    @pl.loop(0, tokens // GROUP)
    def _(g):
        rows = group_rows(g)
        heads = head_masks(bf16)
        columns = column_masks()
        query = spread_heads(mix2_ref[rows, 0:WIDE], heads)
        key = mix2_ref[rows, WIDE : 2 * WIDE]
        value = mix2_ref[rows, 2 * WIDE : 3 * WIDE]
        scores = squeeze_column(nt(key, query), columns) * SCALE
        top = jnp.max(scores, axis=0, keepdims=True)
        exps = jnp.exp(scores - top)
        probs = exps * (1.0 / jnp.sum(exps, axis=0, keepdims=True))
        cprobs_ref[g] = probs
        out = fold_heads(tn(widen_column(probs, columns), value), GROUP)
        att2_ref[rows, :] = out.astype(bf16)

    root = math.sqrt(2.0 / math.pi)

    @pl.loop(0, chunks)
    def _(c):
        rows = part(c)
        gate = gate_rows()
        tok = tok1_ref[rows, :] + gate * (nn(att2_ref[rows, :], o2_ref[...]) + vec(5))
        hat, inverse = normed(tok)
        low = (hat * vec(6) + vec(7)).astype(bf16)
        n3_ref[rows, :] = low
        hidden = nn(low, up_ref[...])
        square = hidden * hidden
        bend = jnp.tanh(root * (hidden + 0.044715 * square * hidden))
        half = 0.5 * (1.0 + bend)
        act = (hidden * half).astype(bf16)
        act_ref[rows, :] = act
        out_ref[c, 0] = (tok + gate * (nn(act, down_ref[...]) + vec(8))).astype(bf16)
        slope = half + (0.5 * root) * hidden * (1.0 - bend * bend) * (
            1.0 + (3.0 * 0.044715) * square
        )
        after = tok_ref[c, 1].astype(f32)
        delta3 = (gate * after).astype(bf16)
        delta3_ref[rows, :] = delta3
        note(8, delta3.astype(f32))
        gh = (nt(delta3, down_ref[...]) * slope).astype(bf16)
        gh_ref[rows, :] = gh
        grad = nt(gh, up_ref[...])
        note(6, grad * hat)
        note(7, grad)
        mid = after + norm_back(grad, hat, inverse, vec(6))
        gmid_ref[rows, :] = mid
        delta2 = (gate * mid).astype(bf16)
        delta2_ref[rows, :] = delta2
        note(5, delta2.astype(f32))
        gatt2_ref[rows, :] = nt(delta2, o2_ref[...]).astype(bf16)

    @pl.loop(0, tokens // GROUP)
    def _(g):
        rows = group_rows(g)
        heads = head_masks(bf16)
        columns = column_masks()
        query = spread_heads(mix2_ref[rows, 0:WIDE], heads)
        key = mix2_ref[rows, WIDE : 2 * WIDE]
        value = mix2_ref[rows, 2 * WIDE : 3 * WIDE]
        grad = spread_heads(gatt2_ref[rows, :], heads)
        probs = cprobs_ref[g]
        slopes = squeeze_column(nt(value, grad), columns)
        slopes = probs * (slopes - jnp.sum(probs * slopes, axis=0, keepdims=True))
        wide = widen_column(slopes, columns)
        dquery = fold_heads(tn(wide, key), GROUP) * SCALE
        dkey = nn(wide, query) * SCALE
        dvalue = nn(widen_column(probs, columns), grad)
        gm2_ref[rows, 0:WIDE] = dquery.astype(bf16)
        gm2_ref[rows, WIDE : 2 * WIDE] = dkey.astype(bf16)
        gm2_ref[rows, 2 * WIDE : 3 * WIDE] = dvalue.astype(bf16)

    @pl.loop(0, chunks)
    def _(c):
        rows = part(c)
        grad = nt(gm2_ref[rows, :], w2_ref[...])
        hat = hat2_ref[rows, :]
        inverse = inv2_ref[rows, :][:, :1]
        note(3, grad * hat)
        note(4, grad)
        low = gmid_ref[rows, :] + norm_back(grad, hat, inverse, vec(3))
        glow_ref[rows, :] = low
        delta1 = (gate_rows() * low).astype(bf16)
        delta1_ref[rows, :] = delta1
        note(2, delta1.astype(f32))
        gatt = rounded(nt(delta1, o1_ref[...]))
        att_ref[0, rows, :] = gatt[:, :128]
        att_ref[1, rows, :] = gatt[:, 128:]

    dbias_ref[...] = jnp.zeros_like(dbias_ref)

    @pl.loop(0, count)
    def _(s):
        masks = head_masks(f32)
        query = spread_heads(window(qkv_ref, 0, s), masks).astype(bf16)
        key = window(qkv_ref, 2, s).astype(bf16)
        value = window(qkv_ref, 4, s).astype(bf16)
        grad = spread_heads(window(att_ref, 0, s), masks).astype(bf16)
        probs = probs_ref[s]
        slopes = nt(value, grad)
        slopes = probs * (slopes - jnp.sum(probs * slopes, axis=0, keepdims=True))
        low = slopes.astype(bf16)
        dbias_ref[...] += low.astype(f32)
        window_store(qkv_ref, 0, s, rounded(fold_heads(tn(low, key), AREA) * SCALE))
        window_store(qkv_ref, 2, s, rounded(nn(low, query) * SCALE))
        window_store(qkv_ref, 4, s, rounded(nn(probs.astype(bf16), grad)))

    @pl.loop(0, chunks)
    def _(c):
        rows = part(c)
        mixed = jnp.concatenate([qkv_ref[tile, rows, :] for tile in range(6)], axis=1).astype(bf16)
        gm1_ref[rows, :] = mixed
        grad = nt(mixed, w1_ref[...])
        hat = hat1_ref[rows, :]
        inverse = inv1_ref[rows, :][:, :1]
        note(0, grad * hat)
        note(1, grad)
        grad_in = glow_ref[rows, :] + norm_back(grad, hat, inverse, vec(0))
        out_ref[c, 1] = grad_in.astype(bf16)

    def keep_pairs(base, parts, blocks):
        for number, block in enumerate(blocks):
            flat_ref[pl.ds(base + number, block.shape[0], stride=parts), :] = block

    def split_pairs(columns, rows):
        evens = [mid_ref[column, pl.ds(0, rows // 2, stride=2), :] for column in range(columns)]
        odds = [mid_ref[column, pl.ds(1, rows // 2, stride=2), :] for column in range(columns)]
        return evens, odds

    def save_qkv(base, grad):
        for column in range(6):
            mid_ref[column, pl.ds(0, D), :] = grad[:, 128 * column : 128 * (column + 1)]
        e, o = split_pairs(6, D)
        blocks = [
            e[0],
            head_head(e[1], e[2]),
            tail_head(e[2], e[3]),
            e[4],
            head_head(e[5], o[0]),
            tail_head(o[0], o[1]),
            o[2],
            head_head(o[3], o[4]),
            tail_head(o[4], o[5]),
        ]
        keep_pairs(base, 9, blocks)

    def save_square(base, rows, grad):
        mid_ref[0, pl.ds(0, rows), :] = grad[:rows, :128]
        mid_ref[1, pl.ds(0, rows), 0 : D - 128] = grad[:rows, 128:]
        e, o = split_pairs(2, rows)
        keep_pairs(base, 3, [e[0], head_head(e[1], o[0]), tail_head(o[0], o[1])])

    save_qkv(row_marks[0], tn(n1_ref[...], gm1_ref[...]))
    save_square(row_marks[1], D, tn(att1_ref[...], delta1_ref[...]))
    save_qkv(row_marks[2], tn(n2_ref[...], gm2_ref[...]))
    save_square(row_marks[3], D, tn(att2_ref[...], delta2_ref[...]))
    grad_up = tn(n3_ref[...], gh_ref[...])
    for column in range(6):
        flat_ref[pl.ds(row_marks[4] + column, D, stride=6), :] = grad_up[
            :, 128 * column : 128 * (column + 1)
        ]
    save_square(row_marks[5], FF, tn(act_ref[...], delta3_ref[...]))

    rest = flat_ref.shape[0] - row_marks[6]
    flat_ref[row_marks[6] :, :] = jnp.zeros((rest, 128), f32)
    dbias = dbias_ref[...]
    high = dbias.astype(bf16)
    both = jnp.concatenate([high, (dbias - high.astype(f32)).astype(bf16)], axis=0)
    dearth = jnp.zeros((40, 256), f32)
    for column in range(WIN_LON):
        moved = nt(both, place_ref[column]).astype(bf16)
        entry = entry_ref[column]
        dearth = dearth + tn(moved[:AREA], entry) + tn(moved[AREA:], entry)
    for index, row, lane in earth_places():
        first = pltpu.roll(dearth[index : index + 1, :128], lane, 1)
        second = pltpu.roll(dearth[index : index + 1, 128:], lane, 1)
        tail = lane_place >= lane
        for step, values in enumerate(
            (
                jnp.where(tail, first, 0.0),
                jnp.where(tail, second, first),
                jnp.where(tail, 0.0, second),
            )
        ):
            flat_ref[pl.ds(row + step, 1), :] += values
    for index in range(9):
        total = jnp.sum(vacc_ref[index], axis=0, keepdims=True)
        dvec_ref[index : index + 1, :] = total
        start = marks[7] + D * index
        for values, size, begin in (
            (total[:, :128], 128, start),
            (jnp.concatenate([total[:, 128:], jnp.zeros((1, 256 - D), f32)], axis=1), D - 128, start + 128),
        ):
            row, lane = divmod(begin, 128)
            moved = pltpu.roll(values, lane, 1) if lane else values
            flat_ref[row : row + 1, :] += jnp.where(lane_place >= lane, moved, 0.0)
            if lane + size > 128:
                flat_ref[row + 1 : row + 2, :] += jnp.where(lane_place < lane, moved, 0.0)
    for tile in range(grads_ref.shape[0]):
        if tile < tiles:
            grads_ref[tile] = flat_ref[pl.ds(tile, buckets, stride=tiles), :].astype(bf16)
        else:
            grads_ref[tile] = jnp.zeros((buckets, 128), bf16)


def block_call(homes, leads, tok, copies, tiles, rows_up, lat_size, slots_here):
    tokens = 4 * tok.shape[2]
    count = tokens // AREA
    buckets = homes.shape[0]
    shape = jax.ShapeDtypeStruct
    outs = [
        shape(tok.shape, bf16),
        shape((rows_up, buckets, 128), bf16),
        shape((9, D), f32),
    ]
    vmem = pltpu.VMEM
    scratch = [
        vmem((buckets * tiles, 128), f32),
        vmem((6, FF, 128), f32),
        vmem((40, 256), f32),
        vmem((count, D), f32),
        vmem((AREA, LANES), f32),
        vmem((AREA, LANES), f32),
        vmem((D, 3 * WIDE), bf16),
        vmem((WIDE, D), bf16),
        vmem((D, 3 * WIDE), bf16),
        vmem((WIDE, D), bf16),
        vmem((D, FF), bf16),
        vmem((FF, D), bf16),
        vmem((16, D), f32),
        vmem((tokens, D), bf16),
        vmem((tokens, D), f32),
        vmem((tokens, 128), f32),
        vmem((6, tokens, 128), f32),
        vmem((count, AREA, LANES), f32),
        vmem((2, tokens, 128), f32),
        vmem((tokens, WIDE), bf16),
        vmem((tokens, D), f32),
        vmem((tokens, D), bf16),
        vmem((tokens, D), f32),
        vmem((tokens, 128), f32),
        vmem((tokens, 3 * WIDE), bf16),
        vmem((tokens // GROUP, 8, GLANES), f32),
        vmem((tokens, WIDE), bf16),
        vmem((tokens, D), bf16),
        vmem((tokens, FF), bf16),
        vmem((tokens, FF), bf16),
        vmem((tokens, D), bf16),
        vmem((tokens, D), bf16),
        vmem((tokens, D), bf16),
        vmem((tokens, D), f32),
        vmem((tokens, D), f32),
        vmem((tokens, WIDE), bf16),
        vmem((tokens, 3 * WIDE), bf16),
        vmem((tokens, 3 * WIDE), bf16),
        vmem((9, 8, D), f32),
    ]
    spec = pl.BlockSpec(memory_space=pltpu.VMEM)
    smem = pl.BlockSpec(memory_space=pltpu.SMEM)
    entry, place = earth_tables()
    return pl.pallas_call(
        functools.partial(block_kernel, (buckets, tiles, lat_size, slots_here)),
        out_shape=outs,
        in_specs=[smem, smem] + [spec] * 4,
        out_specs=[spec] * len(outs),
        scratch_shapes=scratch,
        compiler_params=pltpu.CompilerParams(vmem_limit_bytes=60 * 1024 * 1024),
        name="block",
    )(homes, leads, tok, copies, jnp.asarray(entry), jnp.asarray(place))


MESH = pl.DeviceIdType.MESH


def places():
    lat_size, lon_size, dp_size = lax.axis_size("lat"), lax.axis_size("lon"), lax.axis_size("dp")
    return (
        lax.axis_index("dp"),
        lax.axis_index("lat"),
        lax.axis_index("lon"),
        dp_size,
        lat_size,
        lon_size,
    )


def greet(targets):
    barrier = pltpu.get_barrier_semaphore()
    for target in targets:
        pl.semaphore_signal(barrier, inc=1, device_id=target, device_id_type=MESH)
    pl.semaphore_wait(barrier, len(targets))


def around(place, step, size):
    return lax.rem(place + step, size)


def neighbours(whole_plane):
    dp, lat, lon, dp_size, lat_size, lon_size = places()
    if whole_plane:
        steps = {(i, j) for i in range(lat_size) for j in range(lon_size)}
    else:
        steps = {(1, 0), (lat_size - 1, 0), (1, 1 % lon_size), (lat_size - 1, lon_size - 1)}
        steps |= {(2 * i, 0) for i in range(1, lat_size // 2)} | {(0, j) for j in range(lon_size)}
    steps.discard((0, 0))
    found = [(around(dp, step, dp_size), lat, lon) for step in range(1, dp_size)]
    return found + [
        (dp, around(lat, i, lat_size), around(lon, j, lon_size)) for i, j in sorted(steps)
    ]


def pairing(src, dst, sends, receives, send_slot, receive_slot, target):
    return pltpu.make_async_remote_copy(
        src_ref=src,
        dst_ref=dst,
        send_sem=sends.at[send_slot],
        recv_sem=receives.at[receive_slot],
        device_id=target,
        device_id_type=MESH,
    )


def gather_kernel(
    sizes, own_ref, quads_ref, all_ref, tokens_ref, sends, receives, keeps
):
    dp_size, lat_size, lon_size = sizes
    chips = lat_size // 2
    dp, lat, lon = lax.axis_index("dp"), lax.axis_index("lat"), lax.axis_index("lon")
    core, chip = lax.rem(lat, 2), lat // 2
    greet(neighbours(False))
    line = 0
    first = dp_size
    second = first + dp_size * max(chips, lon_size)
    cross = second + dp_size * max(chips, lon_size)
    moves = cross + dp_size

    def chip_at(step):
        return (dp, around(chip, step, chips) * 2 + core, lon)

    def lon_at(step):
        return (dp, lat, around(lon, step, lon_size))

    def run(mine):
        unit = lon * chips + chip if mine == 0 else chip * lon_size + lon
        one, two = (chips, lon_size) if mine == 0 else (lon_size, chips)
        one_at, two_at = (chip_at, lon_at) if mine == 0 else (lon_at, chip_at)
        place_two = lon if mine == 0 else chip
        begun = []

        def send(src, dst, slot, back, target):
            copy = pairing(src, dst, sends, receives, slot, back, target)
            copy.start()
            begun.append(copy)

        def await_arrival(dst, slot):
            pairing(dst, dst, sends, receives, slot, slot, chip_at(0)).wait_recv()

        own_copy = pltpu.make_async_copy(own_ref, all_ref.at[dp, mine, unit], keeps.at[0])
        own_copy.start()
        for step in range(1, dp_size):
            send(
                own_ref,
                all_ref.at[dp, mine, unit],
                line + step,
                line + dp_size - step,
                (around(dp, step, dp_size), lat, lon),
            )
        order = sorted(range(dp_size), key=lambda step: min(step, dp_size - step))
        chunk = [around(dp, step, dp_size) for step in order]
        for turn in range(dp_size + 2):
            if turn < dp_size:
                here = all_ref.at[chunk[turn], mine, unit]
                if turn:
                    await_arrival(here, line + order[turn])
                for step in range(1, one):
                    send(
                        here if turn else own_ref,
                        here,
                        first + order[turn] * one + step,
                        first + order[turn] * one + one - step,
                        one_at(step),
                    )
            if turn == 0:
                move_starts(send)
                own_copy.wait()
            if 0 <= turn - 1 < dp_size:
                back = turn - 1
                for step in range(1, one):
                    await_arrival(
                        all_ref.at[chunk[back], mine, unit], first + order[back] * one + step
                    )
                group = all_ref.at[chunk[back], mine, pl.ds(place_two * one, one)]
                for step in range(1, two):
                    send(
                        group,
                        group,
                        second + order[back] * two + step,
                        second + order[back] * two + two - step,
                        two_at(step),
                    )
            if 0 <= turn - 2 < dp_size:
                back = turn - 2
                group = all_ref.at[chunk[back], mine, pl.ds(place_two * one, one)]
                for step in range(1, two):
                    await_arrival(group, second + order[back] * two + step)
                whole = all_ref.at[chunk[back], mine]
                send(
                    whole, whole, cross + order[back], cross + order[back], (dp, chip * 2 + 1 - mine, lon)
                )
        for turn in range(dp_size):
            await_arrival(all_ref.at[chunk[turn], 1 - mine], cross + order[turn])
        for quad in range(1, 4):
            await_arrival(tokens_ref.at[quad], moves + quad)
        for copy in begun:
            copy.wait_send()

    def move_starts(send):
        for quad in range(1, 4):
            up, left = quad // 2, quad % 2
            target = (dp, around(lat, lat_size - up, lat_size), around(lon, lon_size - left, lon_size))
            send(quads_ref.at[quad], tokens_ref.at[quad], moves + quad, moves + quad, target)

    keep = pltpu.make_async_copy(quads_ref.at[0], tokens_ref.at[0], keeps.at[1])
    keep.start()
    for mine in range(2):

        @pl.when(core == mine)
        def _():
            run(mine)

    keep.wait()


def gather_call(own, quads, sizes):
    dp_size, lat_size, lon_size = sizes
    chips = lat_size // 2
    count = dp_size * (2 + 2 * max(chips, lon_size)) + 4
    return pl.pallas_call(
        functools.partial(gather_kernel, sizes),
        out_shape=[
            jax.ShapeDtypeStruct((dp_size, 2, chips * lon_size) + own.shape, own.dtype),
            jax.ShapeDtypeStruct(quads.shape, quads.dtype),
        ],
        in_specs=[pl.BlockSpec(memory_space=pltpu.VMEM)] * 2,
        out_specs=[pl.BlockSpec(memory_space=pltpu.VMEM)] * 2,
        scratch_shapes=[
            pltpu.SemaphoreType.DMA((count,)),
            pltpu.SemaphoreType.DMA((count,)),
            pltpu.SemaphoreType.DMA((2,)),
        ],
        compiler_params=pltpu.CompilerParams(
            collective_id=0, has_side_effects=True, vmem_limit_bytes=40 * 1024 * 1024
        ),
        name="gather",
    )(own, quads)


def reduce_kernel(
    sizes,
    grads_ref,
    vecs_ref,
    quads_ref,
    homes_ref,
    mine_ref,
    total_ref,
    tokens_ref,
    half_in,
    half,
    one_in,
    one,
    two_in,
    line_out,
    line_in,
    plane_out,
    plane_in,
    vec_in,
    vec_now,
    sends,
    receives,
    keeps,
):
    dp_size, lat_size, lon_size = sizes
    chips = lat_size // 2
    dp, lat, lon = lax.axis_index("dp"), lax.axis_index("lat"), lax.axis_index("lon")
    core, chip = lax.rem(lat, 2), lat // 2
    rows, buckets = grads_ref.shape[:2]
    n_half, n_side = rows // 2, rows // 4
    n_chip, n_lon, n_last = n_side // chips, n_side // lon_size, n_side // (chips * lon_size)
    plane = lat_size * lon_size
    per_home = plane_out.shape[2]
    greet(neighbours(True))
    begun = []

    def send(src, dst, slot, back, target):
        copy = pairing(src, dst, sends, receives, slot, back, target)
        copy.start()
        begun.append(copy)

    def await_arrival(dst, slot):
        pairing(dst, dst, sends, receives, slot, slot, (dp, lat, lon)).wait_recv()

    def chip_at(step):
        return (dp, around(chip, step, chips) * 2 + core, lon)

    def lon_at(step):
        return (dp, lat, around(lon, step, lon_size))

    cross = 0
    chip_one = 2
    lon_one = chip_one + 2 * chips
    lon_two = lon_one + lon_size
    chip_two = lon_two + 2 * lon_size
    line = chip_two + chips
    last = line + 2 * dp_size
    moves = last + 2 * plane

    partner = (dp, chip * 2 + 1 - core, lon)
    keep = pltpu.make_async_copy(quads_ref.at[0], tokens_ref.at[0], keeps.at[0])
    keep.start()
    send(grads_ref.at[pl.ds((1 - core) * n_half, n_half)], half_in, cross, cross, partner)
    send(vecs_ref, vec_in.at[0], cross + 1, cross + 1, partner)

    def move(kind):
        for quad in range(1, 4):
            down, right = quad // 2, quad % 2
            target = (dp, around(lat, down, lat_size), around(lon, right, lon_size))
            slot = moves + 4 * kind + quad
            send(quads_ref.at[quad, kind], tokens_ref.at[quad, kind], slot, slot, target)

    move(0)
    await_arrival(half_in, cross)
    half[...] = (grads_ref[pl.ds(core * n_half, n_half)].astype(f32) + half_in[...].astype(f32)).astype(bf16)
    await_arrival(vec_in.at[0], cross + 1)
    vec_now[0] = vecs_ref[...] + vec_in[0]

    for step in range(1, chips):
        there = around(chip, step, chips)
        back = chips - step
        send(half.at[pl.ds(there * n_chip, n_chip)], one_in.at[pl.ds(back * n_chip, n_chip)], chip_one + step, chip_one + back, chip_at(step))
        send(vec_now.at[0], vec_in.at[back], chip_one + chips + step, chip_one + chips + back, chip_at(step))
    for step in range(1, lon_size):
        there = around(lon, step, lon_size)
        back = lon_size - step
        send(
            half.at[pl.ds(n_side + there * n_lon, n_lon)],
            one_in.at[pl.ds(n_side + back * n_lon, n_lon)],
            lon_one + step,
            lon_one + back,
            lon_at(step),
        )
    total = half[pl.ds(chip * n_chip, n_chip)].astype(f32)
    vec_total = vec_now[0]
    for step in range(1, chips):
        await_arrival(one_in.at[pl.ds(step * n_chip, n_chip)], chip_one + step)
        total = total + one_in[pl.ds(step * n_chip, n_chip)].astype(f32)
        await_arrival(vec_in.at[step], chip_one + chips + step)
        vec_total = vec_total + vec_in[step]
    one[pl.ds(0, n_chip)] = total.astype(bf16)
    vec_now[1] = vec_total
    for step in range(1, lon_size):
        there = around(lon, step, lon_size)
        back = lon_size - step
        send(one.at[pl.ds(there * n_last, n_last)], two_in.at[0, pl.ds(back * n_last, n_last)], lon_two + step, lon_two + back, lon_at(step))
        send(vec_now.at[1], vec_in.at[chips + back], lon_two + lon_size + step, lon_two + lon_size + back, lon_at(step))
    total = half[pl.ds(n_side + lon * n_lon, n_lon)].astype(f32)
    for step in range(1, lon_size):
        await_arrival(one_in.at[pl.ds(n_side + step * n_lon, n_lon)], lon_one + step)
        total = total + one_in[pl.ds(n_side + step * n_lon, n_lon)].astype(f32)
    one[pl.ds(n_chip, n_lon)] = total.astype(bf16)
    for step in range(1, chips):
        there = around(chip, step, chips)
        back = chips - step
        send(
            one.at[pl.ds(n_chip + there * n_last, n_last)],
            two_in.at[1, pl.ds(back * n_last, n_last)],
            chip_two + step,
            chip_two + back,
            chip_at(step),
        )
    final_a = one[pl.ds(lon * n_last, n_last)].astype(f32)
    vec_total = vec_now[1]
    for step in range(1, lon_size):
        await_arrival(two_in.at[0, pl.ds(step * n_last, n_last)], lon_two + step)
        final_a = final_a + two_in[0, pl.ds(step * n_last, n_last)].astype(f32)
        await_arrival(vec_in.at[chips + step], lon_two + lon_size + step)
        vec_total = vec_total + vec_in[chips + step]
    vec_now[2] = vec_total
    final_b = one[pl.ds(n_chip + chip * n_last, n_last)].astype(f32)
    for step in range(1, chips):
        await_arrival(two_in.at[1, pl.ds(step * n_last, n_last)], chip_two + step)
        final_b = final_b + two_in[1, pl.ds(step * n_last, n_last)].astype(f32)
    final = jnp.concatenate([final_a, final_b], axis=0).astype(bf16)

    width = plane * per_home
    homes = homes_ref[...]
    place = lax.broadcasted_iota(jnp.int32, (dp_size * width, buckets), 0)
    turn = lax.rem(place // width + dp, dp_size)
    pick = jnp.where(turn * width + lax.rem(place, width) == homes, 1.0, 0.0).astype(bf16)
    for row in range(2 * n_last):
        picked = nn(pick, final[row]).astype(bf16)
        for step in range(dp_size):
            line_out[step, row] = picked[step * width : (step + 1) * width]
    for step in range(dp_size):
        there = around(dp, step, dp_size)
        if step:
            back = dp_size - step
            send(line_out.at[step], line_in.at[back], line + step, line + back, (there, lat, lon))
            send(vec_now.at[2], vec_in.at[chips + lon_size + back], line + dp_size + step, line + dp_size + back, (there, lat, lon))
    move(1)
    summed = line_out[0].astype(f32)
    vec_total = vec_now[2]
    for step in range(1, dp_size):
        await_arrival(line_in.at[step], line + step)
        summed = summed + line_in[step].astype(f32)
        await_arrival(vec_in.at[chips + lon_size + step], line + dp_size + step)
        vec_total = vec_total + vec_in[chips + lon_size + step]
    total_ref[...] = vec_total
    for home in range(plane):
        plane_out[home] = summed[:, per_home * home : per_home * (home + 1), :]
    row_a = core * n_half + chip * n_chip + lon * n_last
    row_b = core * n_half + n_side + lon * n_lon + chip * n_last
    me = lat * lon_size + lon
    for lat_step in range(lat_size):
        for lon_step in range(lon_size):
            there = (dp, around(lat, lat_step, lat_size), around(lon, lon_step, lon_size))
            home = there[1] * lon_size + there[2]
            slot = last + 2 * (lat_step * lon_size + lon_step)
            back = last + 2 * ((lat_size - lat_step) % lat_size * lon_size + (lon_size - lon_step) % lon_size)
            if lat_step == 0 and lon_step == 0:
                for side, row in enumerate((row_a, row_b)):
                    copy = pltpu.make_async_copy(
                        plane_out.at[me, pl.ds(side * n_last, n_last)],
                        mine_ref.at[pl.ds(row, n_last)],
                        keeps.at[1 + side],
                    )
                    copy.start()
                continue
            for side, row in enumerate((row_a, row_b)):
                send(
                    plane_out.at[home, pl.ds(side * n_last, n_last)],
                    mine_ref.at[pl.ds(row, n_last)],
                    slot + side,
                    back + side,
                    there,
                )
    for side, row in enumerate((row_a, row_b)):
        pltpu.make_async_copy(
            plane_out.at[me, pl.ds(side * n_last, n_last)],
            mine_ref.at[pl.ds(row, n_last)],
            keeps.at[1 + side],
        ).wait()
    for index in range(1, plane):
        for side in range(2):
            await_arrival(mine_ref.at[pl.ds(0, n_last)], last + 2 * index + side)
    for kind in range(2):
        for quad in range(1, 4):
            await_arrival(tokens_ref.at[quad, kind], moves + 4 * kind + quad)
    keep.wait()
    for copy in begun:
        copy.wait_send()


def reduce_call(grads, vecs, quads, homes, per_home, sizes):
    dp_size, lat_size, lon_size = sizes
    chips = lat_size // 2
    rows, buckets = grads.shape[:2]
    plane = lat_size * lon_size
    n_half, n_side = rows // 2, rows // 4
    n_chip, n_lon, n_last = n_side // chips, n_side // lon_size, n_side // (chips * lon_size)
    count = 2 + 2 * chips + lon_size + 2 * lon_size + chips + 2 * dp_size + 2 * plane + 8
    vmem = pltpu.VMEM
    return pl.pallas_call(
        functools.partial(reduce_kernel, sizes),
        out_shape=[
            jax.ShapeDtypeStruct((rows, per_home, 128), f32),
            jax.ShapeDtypeStruct(vecs.shape, f32),
            jax.ShapeDtypeStruct(quads.shape, quads.dtype),
        ],
        in_specs=[pl.BlockSpec(memory_space=pltpu.VMEM)] * 4,
        out_specs=[pl.BlockSpec(memory_space=pltpu.VMEM)] * 3,
        scratch_shapes=[
            vmem((n_half, buckets, 128), bf16),
            vmem((n_half, buckets, 128), bf16),
            vmem((n_half, buckets, 128), bf16),
            vmem((n_chip + n_lon, buckets, 128), bf16),
            vmem((2, max(n_chip, n_lon), buckets, 128), bf16),
            vmem((dp_size, 2 * n_last, plane * per_home, 128), bf16),
            vmem((dp_size, 2 * n_last, plane * per_home, 128), bf16),
            vmem((plane, 2 * n_last, per_home, 128), f32),
            vmem((8, 128), f32),
            vmem((chips + lon_size + dp_size,) + vecs.shape, f32),
            vmem((3,) + vecs.shape, f32),
            pltpu.SemaphoreType.DMA((count,)),
            pltpu.SemaphoreType.DMA((count,)),
            pltpu.SemaphoreType.DMA((3,)),
        ],
        compiler_params=pltpu.CompilerParams(
            collective_id=1, has_side_effects=True, vmem_limit_bytes=40 * 1024 * 1024
        ),
        name="reduce",
    )(grads, vecs, quads, homes)


def adam_kernel(steps_ref, buckets_ref, marks, grads_ref, master_ref, one_ref, two_ref, new_master, new_one, new_two):
    homes = master_ref.shape[0]
    tiles = master_ref.shape[1] // 128
    steps = jnp.full((homes, 128), steps_ref[0], jnp.int32).astype(f32)
    fix_one = 1.0 / (1.0 - jnp.exp(steps * math.log(beta_one)))
    fix_two = 1.0 / (1.0 - jnp.exp(steps * math.log(beta_two)))
    base = jnp.concatenate(
        [jnp.full((1, 128), buckets_ref[home], jnp.int32) for home in range(homes)], axis=0
    ) + lax.broadcasted_iota(jnp.int32, (homes, 128), 1)
    rates = [2.6 / math.sqrt(D), 8.0 / math.sqrt(D), 2.6 / math.sqrt(D), 4.0 / math.sqrt(D), 2.0 / math.sqrt(D), 3.0 / math.sqrt(FF), 1.0, 0.6]
    for tile in range(tiles):
        columns = slice(128 * tile, 128 * (tile + 1))
        index = base + 128 * tile
        rate = jnp.full((homes, 128), 0.1, f32)
        for number in range(7, -1, -1):
            rate = jnp.where(index < marks[number + 1], rates[number], rate)
        grad = grads_ref[tile]
        weights = master_ref[:, columns]
        first = beta_one * one_ref[:, columns] + (1.0 - beta_one) * grad
        second = beta_two * two_ref[:, columns] + (1.0 - beta_two) * grad * grad
        step = first * fix_one / (jnp.sqrt(second * fix_two) + eps_adam) + decay_rate * weights
        new_master[:, columns] = weights - rate * step
        new_one[:, columns] = first
        new_two[:, columns] = second


def adam_call(steps, bases, marks, grads, master, one, two):
    smem = pl.BlockSpec(memory_space=pltpu.SMEM)
    vmem = pl.BlockSpec(memory_space=pltpu.VMEM)

    def body(steps_ref, bases_ref, *refs):
        adam_kernel(steps_ref, bases_ref, marks, *refs)

    return pl.pallas_call(
        body,
        out_shape=[jax.ShapeDtypeStruct(master.shape, f32)] * 3,
        in_specs=[smem, smem, vmem, vmem, vmem, vmem],
        out_specs=[vmem] * 3,
        name="adam",
    )(steps, bases, grads, master, one, two)


def quads_out(block):
    slots, levels = block.shape[:2]
    split = block.reshape(slots * levels, 2, HALF_LAT, 2, HALF_LON, D)
    return split.transpose(1, 3, 2, 4, 0, 5)[::-1, ::-1].reshape(4, -1, D)


def quads_back(quads, slots, levels):
    split = quads.reshape(2, 2, HALF_LAT, HALF_LON, slots * levels, D)[::-1, ::-1]
    return split.transpose(4, 0, 2, 1, 3, 5).reshape(slots, levels, WIN_LAT, WIN_LON, D)


def per_device(
    inputs, cotangent, lead_counts, home_slots, master, moment_one, moment_two, step_count
):
    slots_here = inputs.shape[0]
    levels = inputs.shape[1]
    lat_size = lax.axis_size("lat")
    segment_marks = offsets(lat_size + 1)
    dp_size, lon_size = lax.axis_size("dp"), lax.axis_size("lon")
    sizes = (dp_size, lat_size, lon_size)
    slots_mine, bucket_width = master.shape
    bucket_total = home_slots.shape[0]
    tiles = bucket_width // 128
    tiles_up = -(-tiles // 16) * 16
    own = jnp.pad(
        master.reshape(slots_mine, tiles, 128), ((0, 0), (0, tiles_up - tiles), (0, 0))
    ).astype(bf16)
    quads = jnp.stack([quads_out(inputs), quads_out(cotangent)], axis=1)
    copies, tok = gather_call(own, quads, sizes)
    home_device = home_slots // slots_mine
    home_lon = home_device % lon_size
    home_lat = home_device // lon_size % lat_size
    chips = lat_size // 2
    home_unit = jnp.where(
        home_lat % 2 == 0, home_lon * chips + home_lat // 2, home_lat // 2 * lon_size + home_lon
    )
    home_place = (home_device // (lon_size * lat_size) * 2 + home_lat % 2) * (chips * lon_size)
    home_place = (home_place + home_unit) * slots_mine + home_slots % slots_mine
    unit = 4 * chips * lon_size
    rows_up = -(-tiles // unit) * unit
    out_tok, grad_rows, dvec = block_call(
        home_place,
        lead_counts,
        tok,
        copies.reshape(-1, tiles_up, 128),
        tiles,
        rows_up,
        lat_size,
        slots_here,
    )
    my_grads, grad_vectors, tok_back = reduce_call(
        grad_rows, dvec, out_tok, home_slots[None, :], slots_mine, sizes
    )
    device_place = lax.axis_index(("dp", "lat", "lon"))
    slot_ids = device_place * slots_mine + jnp.arange(slots_mine, dtype=jnp.int32)
    owner_match = home_slots[None, :] == slot_ids[:, None]
    bucket_ids = jnp.sum(
        jnp.where(owner_match, jnp.arange(bucket_total, dtype=jnp.int32)[None, :], 0), axis=1
    )
    present = jnp.any(owner_match, axis=1)
    bases = jnp.where(present, bucket_ids * bucket_width, segment_marks[8])
    new_master, new_one, new_two = adam_call(
        step_count, bases, segment_marks, my_grads, master, moment_one, moment_two
    )
    result = quads_back(tok_back[:, 0], slots_here, levels)
    grad_inputs = quads_back(tok_back[:, 1], slots_here, levels).astype(f32)
    return (result, grad_inputs, grad_vectors + 0.0, new_master, new_one, new_two)


def solution(mesh):
    in_specs = (
        P("dp", None, "lat", "lon", None),
        P("dp", None, "lat", "lon", None),
        P(),
        P(),
        P(("dp", "lat", "lon"), None),
        P(("dp", "lat", "lon"), None),
        P(("dp", "lat", "lon"), None),
        P(),
    )
    out_specs = (
        P("dp", None, "lat", "lon", None),
        P("dp", None, "lat", "lon", None),
        P(),
        P(("dp", "lat", "lon"), None),
        P(("dp", "lat", "lon"), None),
        P(("dp", "lat", "lon"), None),
    )
    return jax.shard_map(
        per_device, mesh=mesh, in_specs=in_specs, out_specs=out_specs, check_vma=False
    )
```

```python
import functools
import math

import jax
import jax.numpy as jnp
import ml_dtypes
import numpy as np
from jax import lax
from jax.experimental import pallas as pl
from jax.experimental.pallas import tpu as pltpu
from jax.sharding import PartitionSpec as P

D = 192
FF = 768
HEADS = 6
HEAD_DIM = 32
LEVELS = 8
WIN_LAT = 6
WIN_LON = 12
LEADS = 4
HALF_LAT = WIN_LAT // 2
HALF_LON = WIN_LON // 2
QUAD = HALF_LAT * HALF_LON
AREA = WIN_LAT * WIN_LON
LANES = HEADS * AREA
WIDE = 256
SCALE = 1.0 / math.sqrt(HEAD_DIM)

beta_one = 0.6
beta_two = 0.45
eps_norm = 1e-05
eps_adam = 1e-08
decay_rate = 0.1
penalty_value = -1000000000.0
bf16 = jnp.bfloat16
f32 = jnp.float32


def offsets(groups):
    sizes_list = [
        3 * D * D,
        D * D,
        3 * D * D,
        D * D,
        D * FF,
        FF * D,
        groups * HEADS * WIN_LAT * WIN_LAT * (2 * WIN_LON - 1),
        9 * D,
    ]
    segment_marks = [0]
    for amount in sizes_list:
        segment_marks.append(segment_marks[-1] + amount)
    return segment_marks


def nn(left, right):
    return jnp.dot(left, right, preferred_element_type=f32)


def nt(left, right):
    return lax.dot_general(left, right, (((1,), (1,)), ((), ())), preferred_element_type=f32)


def tn(left, right):
    return lax.dot_general(left, right, (((0,), (0,)), ((), ())), preferred_element_type=f32)


def normed(values):
    center = values - jnp.sum(values, axis=-1, keepdims=True) * (1.0 / D)
    spread = jnp.sum(center * center, axis=-1, keepdims=True) * (1.0 / D)
    inverse = lax.rsqrt(spread + eps_norm)
    return center * inverse, inverse


def norm_back(grad, hat, inverse, gain):
    scaled = grad * gain
    mean_one = jnp.sum(scaled, axis=-1, keepdims=True) * (1.0 / D)
    mean_two = jnp.sum(scaled * hat, axis=-1, keepdims=True) * (1.0 / D)
    return inverse * (scaled - mean_one - hat * mean_two)


def row_fold(values):
    return jnp.sum(values.reshape(values.shape[0] // 8, 8, values.shape[1]), axis=0)


def head_masks(dtype):
    lane = lax.broadcasted_iota(jnp.int32, (1, WIDE), 1) // HEAD_DIM
    return [jnp.where(lane == head, 1.0, 0.0).astype(dtype) for head in range(HEADS)]


def spread_heads(values, masks):
    return jnp.concatenate([values * mask for mask in masks], axis=0)


def fold_heads(big, count):
    parts = [big[head * count : (head + 1) * count] for head in range(HEADS)]
    lane = lax.broadcasted_iota(jnp.int32, (count, 128), 1)
    low = parts[3][:, :128]
    for head in (2, 1, 0):
        low = jnp.where(lane < HEAD_DIM * (head + 1), parts[head][:, :128], low)
    high = jnp.where(lane < HEAD_DIM, parts[4][:, 128:], parts[5][:, 128:])
    return jnp.concatenate([low, high], axis=1)


def rounded(values):
    return values.astype(bf16).astype(f32)


def soft_columns(scores):
    exps = jnp.exp(scores - jnp.max(scores, axis=0, keepdims=True))
    return exps * (1.0 / jnp.sum(exps, axis=0, keepdims=True))


def soft_back(probs, slopes):
    return probs * (slopes - jnp.sum(probs * slopes, axis=0, keepdims=True))


GROUP = 64
GLANES = HEADS * GROUP
CHUNK = 288


def lanes_of(ref, start):
    row, lane = divmod(start, 128)
    here = ref[row : row + 1, :]
    if lane == 0:
        return here
    place = lax.broadcasted_iota(jnp.int32, (1, 128), 1)
    mixed = jnp.where(place >= lane, here, ref[row + 1 : row + 2, :])
    return pltpu.roll(mixed, 128 - lane, 1)


def tail_head(tail, head):
    place = lax.broadcasted_iota(jnp.int32, tail.shape, 1)
    return pltpu.roll(jnp.where(place >= 64, tail, head), 64, 1)


def head_head(first, second):
    place = lax.broadcasted_iota(jnp.int32, first.shape, 1)
    return jnp.where(place < 64, first, pltpu.roll(second, 64, 1))


def only_head(values):
    place = lax.broadcasted_iota(jnp.int32, values.shape, 1)
    return jnp.where(place < 64, values, 0.0)


def only_tail(values):
    place = lax.broadcasted_iota(jnp.int32, values.shape, 1)
    return pltpu.roll(jnp.where(place >= 64, values, 0.0), 64, 1)


EARTH_ROW = WIN_LAT * (2 * WIN_LON - 1)
EARTH_ROWS = HEADS * WIN_LAT


def earth_tables():
    entry = np.zeros((WIN_LON, AREA, 256), np.float32)
    place = np.zeros((WIN_LON, 40, LANES), np.float32)
    for column in range(WIN_LON):
        side, inner = divmod(column, HALF_LON)
        for key in range(AREA):
            key_up, rest = divmod(key, 2 * QUAD)
            key_side, rest = divmod(rest, QUAD)
            key_row, key_inner = divmod(rest, HALF_LON)
            row = key_up * HALF_LAT + key_row
            offset = column - (key_side * HALF_LON + key_inner) + WIN_LON - 1
            entry[column, key, row * (2 * WIN_LON - 1) + offset] = 1.0
        for head in range(HEADS):
            for row in range(WIN_LAT):
                up, low = divmod(row, HALF_LAT)
                lane = AREA * head + 2 * QUAD * up + QUAD * side + HALF_LON * low + inner
                place[column, head * WIN_LAT + row, lane] = 1.0
    return entry.astype(ml_dtypes.bfloat16), place.astype(ml_dtypes.bfloat16)


def block_kernel(
    sizes,
    home_ref,
    lead_ref,
    tok_ref,
    copies_ref,
    entry_ref,
    place_ref,
    out_ref,
    grads_ref,
    dvec_ref,
    flat_ref,
    mid_ref,
    earth_ref,
    gate_ref,
    bias_ref,
    dbias_ref,
    w1_ref,
    o1_ref,
    w2_ref,
    o2_ref,
    up_ref,
    down_ref,
    vec_ref,
    n1_ref,
    hat1_ref,
    inv1_ref,
    qkv_ref,
    probs_ref,
    att_ref,
    att1_ref,
    tok1_ref,
    n2_ref,
    hat2_ref,
    inv2_ref,
    mix2_ref,
    cprobs_ref,
    att2_ref,
    n3_ref,
    act_ref,
    gh_ref,
    delta3_ref,
    delta2_ref,
    delta1_ref,
    gmid_ref,
    glow_ref,
    gatt2_ref,
    gm2_ref,
    gm1_ref,
    vacc_ref,
):
    tokens = 4 * tok_ref.shape[2]
    count = tokens // AREA
    chunks = 4
    buckets, tiles, lat_size, slots_here = sizes
    lat = lax.axis_index("lat")
    is_last = lat == lat_size - 1
    marks = offsets(lat_size + 1)
    row_marks = [mark // 128 for mark in marks]

    for bucket in range(buckets):
        block = copies_ref[home_ref[bucket]].astype(f32)
        flat_ref[tiles * bucket : tiles * (bucket + 1), :] = block[:tiles]

    def take_pairs(base, parts, pairs):
        return [flat_ref[pl.ds(base + part, pairs, stride=parts), :] for part in range(parts)]

    def give_pairs(columns, rows, evens, odds):
        for column, (even, odd) in enumerate(zip(evens, odds)):
            mid_ref[column, pl.ds(0, rows // 2, stride=2), :] = even
            mid_ref[column, pl.ds(1, rows // 2, stride=2), :] = odd

    def load_qkv(base, ref):
        b = take_pairs(base, 9, D // 2)
        evens = [b[0], only_head(b[1]), tail_head(b[1], b[2]), only_tail(b[2]), b[3], only_head(b[4])]
        odds = [tail_head(b[4], b[5]), only_tail(b[5]), b[6], only_head(b[7]), tail_head(b[7], b[8]), only_tail(b[8])]
        give_pairs(6, D, evens, odds)
        for column in range(6):
            ref[:, 128 * column : 128 * (column + 1)] = mid_ref[column, pl.ds(0, D), :].astype(bf16)

    def load_square(base, rows, ref):
        b = take_pairs(base, 3, rows // 2)
        give_pairs(2, rows, [b[0], b[1]], [tail_head(b[1], b[2]), only_tail(b[2])])
        ref[0:rows, 0:128] = mid_ref[0, pl.ds(0, rows), :].astype(bf16)
        ref[0:rows, 128:D] = mid_ref[1, pl.ds(0, rows), :][:, : D - 128].astype(bf16)

    load_qkv(row_marks[0], w1_ref)
    load_square(row_marks[1], D, o1_ref)
    load_qkv(row_marks[2], w2_ref)
    load_square(row_marks[3], D, o2_ref)
    for ref in (o1_ref, o2_ref):
        ref[D:WIDE, :] = jnp.zeros((WIDE - D, D), bf16)
    for column in range(6):
        up_ref[:, 128 * column : 128 * (column + 1)] = flat_ref[
            pl.ds(row_marks[4] + column, D, stride=6), :
        ].astype(bf16)
    load_square(row_marks[5], FF, down_ref)
    for index in range(9):
        start = marks[7] + D * index
        vec_ref[index : index + 1, 0:128] = lanes_of(flat_ref, start)
        vec_ref[index : index + 1, 128:D] = lanes_of(flat_ref, start + 128)[:, : D - 128]

    def earth_places():
        group_one = lat + 1
        group_two = jnp.where(is_last, 0, lat + 1)
        for index in range(EARTH_ROWS):
            group = group_one if index % WIN_LAT < HALF_LAT else group_two
            start = marks[6] + EARTH_ROW * (EARTH_ROWS * group + index)
            row = start // 128
            yield index, row, start - 128 * row

    lane_place = lax.broadcasted_iota(jnp.int32, (1, 128), 1)
    earth_ref[...] = jnp.zeros_like(earth_ref)
    for index, row, lane in earth_places():
        rows = [flat_ref[pl.ds(row + step, 1), :] for step in range(3)]
        back = lax.rem(128 - lane, 128)
        first = pltpu.roll(jnp.where(lane_place >= lane, rows[0], rows[1]), back, 1)
        second = pltpu.roll(jnp.where(lane_place >= lane, rows[1], rows[2]), back, 1)
        earth_ref[index : index + 1, 0:128] = first
        earth_ref[index : index + 1, 128:256] = jnp.where(lane_place < EARTH_ROW - 128, second, 0.0)
    earth = earth_ref[...].astype(bf16)
    key_up = lax.broadcasted_iota(jnp.int32, (AREA, LANES), 0) // (2 * QUAD)
    query_up = lax.rem(lax.broadcasted_iota(jnp.int32, (AREA, LANES), 1), AREA) // (2 * QUAD)
    bias = jnp.where((key_up != query_up) & is_last, penalty_value, 0.0)
    for column in range(WIN_LON):
        bias = bias + nn(nt(entry_ref[column], earth).astype(bf16), place_ref[column])
    bias_ref[...] = bias

    for slot in range(slots_here):
        number = lax.axis_index("dp") * slots_here + slot
        live = lax.rem(number, LEADS) < lead_ref[number // LEADS]
        size = count // slots_here
        gate_ref[slot * size : (slot + 1) * size, :] = jnp.full((size, D), jnp.where(live, 1.0, 0.0), f32)

    def part(index):
        return pl.ds(pl.multiple_of(index * CHUNK, CHUNK), CHUNK)

    def vec(index):
        return vec_ref[index : index + 1, :]

    def gate_rows():
        gate = gate_ref[...]
        return jnp.broadcast_to(gate[None], (CHUNK // count, count, D)).reshape(CHUNK, D)

    vacc_ref[...] = jnp.zeros_like(vacc_ref)

    def note(index, values):
        vacc_ref[index] += row_fold(values)

    @pl.loop(0, chunks)
    def _(c):
        rows = part(c)
        hat, inverse = normed(tok_ref[c, 0].astype(f32))
        hat1_ref[rows, :] = hat
        inv1_ref[rows, :] = jnp.broadcast_to(inverse, (CHUNK, 128))
        low = (hat * vec(0) + vec(1)).astype(bf16)
        n1_ref[rows, :] = low
        mixed = rounded(nn(low, w1_ref[...]))
        for tile in range(6):
            qkv_ref[tile, rows, :] = mixed[:, 128 * tile : 128 * (tile + 1)]

    def window(ref, first, s):
        rows = pl.ds(s, AREA, stride=count)
        return jnp.concatenate([ref[first, rows, :], ref[first + 1, rows, :]], axis=1)

    def window_store(ref, first, s, values):
        rows = pl.ds(s, AREA, stride=count)
        ref[first, rows, :] = values[:, :128]
        ref[first + 1, rows, :] = values[:, 128:]

    @pl.loop(0, count // 4)
    def _(block):
        masks = head_masks(f32)
        places = [block * 4 + step for step in range(4)]
        reads = [[window(qkv_ref, 2 * kind, s) for kind in range(3)] for s in places]
        raw = [
            nt(key.astype(bf16), spread_heads(query, masks).astype(bf16)) for query, key, _ in reads
        ]
        probs = [soft_columns(scores * SCALE + bias_ref[...]) for scores in raw]
        outs = [tn(prob.astype(bf16), read[2].astype(bf16)) for prob, read in zip(probs, reads)]
        for s, prob, out in zip(places, probs, outs):
            probs_ref[s] = prob
            window_store(att_ref, 0, s, fold_heads(out, AREA))

    @pl.loop(0, chunks)
    def _(c):
        rows = part(c)
        att = jnp.concatenate([att_ref[0, rows, :], att_ref[1, rows, :]], axis=1).astype(bf16)
        att1_ref[rows, :] = att
        branch = nn(att, o1_ref[...]) + vec(2)
        tok = tok_ref[c, 0].astype(f32) + gate_rows() * branch
        tok1_ref[rows, :] = tok
        hat, inverse = normed(tok)
        hat2_ref[rows, :] = hat
        inv2_ref[rows, :] = jnp.broadcast_to(inverse, (CHUNK, 128))
        low = (hat * vec(3) + vec(4)).astype(bf16)
        n2_ref[rows, :] = low
        mix2_ref[rows, :] = nn(low, w2_ref[...]).astype(bf16)

    def column_masks():
        lane = lax.broadcasted_iota(jnp.int32, (8, GLANES), 1)
        place = (lane % GROUP) // 8
        return [place == index for index in range(GROUP // 8)]

    def squeeze_column(values, masks):
        out = values[:8]
        for index in range(1, GROUP // 8):
            out = jnp.where(masks[index], values[8 * index : 8 * index + 8], out)
        return out

    def widen_column(values, masks):
        return jnp.concatenate([jnp.where(mask, values, 0.0) for mask in masks], axis=0).astype(bf16)

    def group_rows(g):
        return pl.ds(pl.multiple_of(g * GROUP, GROUP), GROUP)

    @pl.loop(0, tokens // GROUP // 6)
    def _(block):
        heads = head_masks(bf16)
        columns = column_masks()
        places = [block * 6 + step for step in range(6)]
        reads = [mix2_ref[group_rows(g), :] for g in places]
        raw = [
            nt(mixed[:, WIDE : 2 * WIDE], spread_heads(mixed[:, 0:WIDE], heads)) for mixed in reads
        ]
        probs = [soft_columns(squeeze_column(scores, columns) * SCALE) for scores in raw]
        outs = [
            tn(widen_column(prob, columns), mixed[:, 2 * WIDE :])
            for prob, mixed in zip(probs, reads)
        ]
        for g, prob, out in zip(places, probs, outs):
            cprobs_ref[g] = prob
            att2_ref[group_rows(g), :] = fold_heads(out, GROUP).astype(bf16)

    root = math.sqrt(2.0 / math.pi)

    @pl.loop(0, chunks)
    def _(c):
        rows = part(c)
        gate = gate_rows()
        tok = tok1_ref[rows, :] + gate * (nn(att2_ref[rows, :], o2_ref[...]) + vec(5))
        hat, inverse = normed(tok)
        low = (hat * vec(6) + vec(7)).astype(bf16)
        n3_ref[rows, :] = low
        hidden = nn(low, up_ref[...])
        square = hidden * hidden
        half = 0.5 * jnp.tanh(hidden * (root + (root * 0.044715) * square)) + 0.5
        wave = hidden * half
        act = wave.astype(bf16)
        act_ref[rows, :] = act
        out_ref[c, 0] = (tok + gate * (nn(act, down_ref[...]) + vec(8))).astype(bf16)
        slope = half + wave * (1.0 - half) * (2.0 * root + (6.0 * root * 0.044715) * square)
        after = tok_ref[c, 1].astype(f32)
        delta3 = (gate * after).astype(bf16)
        delta3_ref[rows, :] = delta3
        note(8, delta3.astype(f32))
        gh = (nt(delta3, down_ref[...]) * slope).astype(bf16)
        gh_ref[rows, :] = gh
        grad = nt(gh, up_ref[...])
        note(6, grad * hat)
        note(7, grad)
        mid = after + norm_back(grad, hat, inverse, vec(6))
        gmid_ref[rows, :] = mid
        delta2 = (gate * mid).astype(bf16)
        delta2_ref[rows, :] = delta2
        note(5, delta2.astype(f32))
        gatt2_ref[rows, :] = nt(delta2, o2_ref[...]).astype(bf16)

    @pl.loop(0, tokens // GROUP // 6)
    def _(block):
        heads = head_masks(bf16)
        columns = column_masks()
        places = [block * 6 + step for step in range(6)]
        reads = [
            (mix2_ref[group_rows(g), :], gatt2_ref[group_rows(g), :], cprobs_ref[g]) for g in places
        ]
        grads = [spread_heads(read[1], heads) for read in reads]
        raw = [nt(read[0][:, 2 * WIDE :], grad) for read, grad in zip(reads, grads)]
        dvalues = [nn(widen_column(read[2], columns), grad) for read, grad in zip(reads, grads)]
        lows = [
            widen_column(soft_back(read[2], squeeze_column(slopes, columns)), columns)
            for read, slopes in zip(reads, raw)
        ]
        dkeys = [
            nn(low, spread_heads(read[0][:, 0:WIDE], heads)) for read, low in zip(reads, lows)
        ]
        dqueries = [tn(low, read[0][:, WIDE : 2 * WIDE]) for read, low in zip(reads, lows)]
        for g, dquery, dkey, dvalue in zip(places, dqueries, dkeys, dvalues):
            rows = group_rows(g)
            gm2_ref[rows, 0:WIDE] = (fold_heads(dquery, GROUP) * SCALE).astype(bf16)
            gm2_ref[rows, WIDE : 2 * WIDE] = (dkey * SCALE).astype(bf16)
            gm2_ref[rows, 2 * WIDE : 3 * WIDE] = dvalue.astype(bf16)

    @pl.loop(0, chunks)
    def _(c):
        rows = part(c)
        grad = nt(gm2_ref[rows, :], w2_ref[...])
        hat = hat2_ref[rows, :]
        inverse = inv2_ref[rows, :][:, :1]
        note(3, grad * hat)
        note(4, grad)
        low = gmid_ref[rows, :] + norm_back(grad, hat, inverse, vec(3))
        glow_ref[rows, :] = low
        delta1 = (gate_rows() * low).astype(bf16)
        delta1_ref[rows, :] = delta1
        note(2, delta1.astype(f32))
        gatt = rounded(nt(delta1, o1_ref[...]))
        att_ref[0, rows, :] = gatt[:, :128]
        att_ref[1, rows, :] = gatt[:, 128:]

    dbias_ref[...] = jnp.zeros_like(dbias_ref)

    @pl.loop(0, count // 4)
    def _(block):
        masks = head_masks(f32)
        places = [block * 4 + step for step in range(4)]
        reads = [
            [window(qkv_ref, 2 * kind, s) for kind in range(3)]
            + [window(att_ref, 0, s), probs_ref[s]]
            for s in places
        ]
        grads = [spread_heads(read[3], masks).astype(bf16) for read in reads]
        raw = [nt(read[2].astype(bf16), grad) for read, grad in zip(reads, grads)]
        dvalues = [nn(read[4].astype(bf16), grad) for read, grad in zip(reads, grads)]
        lows = [soft_back(read[4], slopes).astype(bf16) for read, slopes in zip(reads, raw)]
        dkeys = [
            nn(low, spread_heads(read[0], masks).astype(bf16)) for read, low in zip(reads, lows)
        ]
        dqueries = [tn(low, read[1].astype(bf16)) for read, low in zip(reads, lows)]
        dbias_ref[...] += functools.reduce(jnp.add, [low.astype(f32) for low in lows])
        for s, dquery, dkey, dvalue in zip(places, dqueries, dkeys, dvalues):
            window_store(qkv_ref, 0, s, rounded(fold_heads(dquery, AREA) * SCALE))
            window_store(qkv_ref, 2, s, rounded(dkey * SCALE))
            window_store(qkv_ref, 4, s, rounded(dvalue))

    @pl.loop(0, chunks)
    def _(c):
        rows = part(c)
        mixed = jnp.concatenate([qkv_ref[tile, rows, :] for tile in range(6)], axis=1).astype(bf16)
        gm1_ref[rows, :] = mixed
        grad = nt(mixed, w1_ref[...])
        hat = hat1_ref[rows, :]
        inverse = inv1_ref[rows, :][:, :1]
        note(0, grad * hat)
        note(1, grad)
        grad_in = glow_ref[rows, :] + norm_back(grad, hat, inverse, vec(0))
        out_ref[c, 1] = grad_in.astype(bf16)

    def keep_pairs(base, parts, blocks):
        for number, block in enumerate(blocks):
            flat_ref[pl.ds(base + number, block.shape[0], stride=parts), :] = block

    def split_pairs(columns, rows):
        evens = [mid_ref[column, pl.ds(0, rows // 2, stride=2), :] for column in range(columns)]
        odds = [mid_ref[column, pl.ds(1, rows // 2, stride=2), :] for column in range(columns)]
        return evens, odds

    def save_qkv(base, grad):
        for column in range(6):
            mid_ref[column, pl.ds(0, D), :] = grad[:, 128 * column : 128 * (column + 1)]
        e, o = split_pairs(6, D)
        blocks = [
            e[0],
            head_head(e[1], e[2]),
            tail_head(e[2], e[3]),
            e[4],
            head_head(e[5], o[0]),
            tail_head(o[0], o[1]),
            o[2],
            head_head(o[3], o[4]),
            tail_head(o[4], o[5]),
        ]
        keep_pairs(base, 9, blocks)

    def save_square(base, rows, grad):
        mid_ref[0, pl.ds(0, rows), :] = grad[:rows, :128]
        mid_ref[1, pl.ds(0, rows), 0 : D - 128] = grad[:rows, 128:]
        e, o = split_pairs(2, rows)
        keep_pairs(base, 3, [e[0], head_head(e[1], o[0]), tail_head(o[0], o[1])])

    save_qkv(row_marks[0], tn(n1_ref[...], gm1_ref[...]))
    save_square(row_marks[1], D, tn(att1_ref[...], delta1_ref[...]))
    save_qkv(row_marks[2], tn(n2_ref[...], gm2_ref[...]))
    save_square(row_marks[3], D, tn(att2_ref[...], delta2_ref[...]))
    grad_up = tn(n3_ref[...], gh_ref[...])
    for column in range(6):
        flat_ref[pl.ds(row_marks[4] + column, D, stride=6), :] = grad_up[
            :, 128 * column : 128 * (column + 1)
        ]
    save_square(row_marks[5], FF, tn(act_ref[...], delta3_ref[...]))

    rest = flat_ref.shape[0] - row_marks[6]
    flat_ref[row_marks[6] :, :] = jnp.zeros((rest, 128), f32)
    dbias = dbias_ref[...]
    high = dbias.astype(bf16)
    both = jnp.concatenate([high, (dbias - high.astype(f32)).astype(bf16)], axis=0)
    dearth = jnp.zeros((40, 256), f32)
    for column in range(WIN_LON):
        moved = nt(both, place_ref[column]).astype(bf16)
        entry = entry_ref[column]
        dearth = dearth + tn(moved[:AREA], entry) + tn(moved[AREA:], entry)
    for index, row, lane in earth_places():
        first = pltpu.roll(dearth[index : index + 1, :128], lane, 1)
        second = pltpu.roll(dearth[index : index + 1, 128:], lane, 1)
        tail = lane_place >= lane
        for step, values in enumerate(
            (
                jnp.where(tail, first, 0.0),
                jnp.where(tail, second, first),
                jnp.where(tail, 0.0, second),
            )
        ):
            flat_ref[pl.ds(row + step, 1), :] += values
    for index in range(9):
        total = jnp.sum(vacc_ref[index], axis=0, keepdims=True)
        dvec_ref[index : index + 1, :] = total
        start = marks[7] + D * index
        for values, size, begin in (
            (total[:, :128], 128, start),
            (jnp.concatenate([total[:, 128:], jnp.zeros((1, 256 - D), f32)], axis=1), D - 128, start + 128),
        ):
            row, lane = divmod(begin, 128)
            moved = pltpu.roll(values, lane, 1) if lane else values
            flat_ref[row : row + 1, :] += jnp.where(lane_place >= lane, moved, 0.0)
            if lane + size > 128:
                flat_ref[row + 1 : row + 2, :] += jnp.where(lane_place < lane, moved, 0.0)
    for tile in range(grads_ref.shape[0]):
        if tile < tiles:
            grads_ref[tile] = flat_ref[pl.ds(tile, buckets, stride=tiles), :].astype(bf16)
        else:
            grads_ref[tile] = jnp.zeros((buckets, 128), bf16)


def block_call(homes, leads, tok, copies, tiles, rows_up, lat_size, slots_here):
    tokens = 4 * tok.shape[2]
    count = tokens // AREA
    buckets = homes.shape[0]
    shape = jax.ShapeDtypeStruct
    outs = [
        shape(tok.shape, bf16),
        shape((rows_up, buckets, 128), bf16),
        shape((9, D), f32),
    ]
    vmem = pltpu.VMEM
    scratch = [
        vmem((buckets * tiles, 128), f32),
        vmem((6, FF, 128), f32),
        vmem((40, 256), f32),
        vmem((count, D), f32),
        vmem((AREA, LANES), f32),
        vmem((AREA, LANES), f32),
        vmem((D, 3 * WIDE), bf16),
        vmem((WIDE, D), bf16),
        vmem((D, 3 * WIDE), bf16),
        vmem((WIDE, D), bf16),
        vmem((D, FF), bf16),
        vmem((FF, D), bf16),
        vmem((16, D), f32),
        vmem((tokens, D), bf16),
        vmem((tokens, D), f32),
        vmem((tokens, 128), f32),
        vmem((6, tokens, 128), f32),
        vmem((count, AREA, LANES), f32),
        vmem((2, tokens, 128), f32),
        vmem((tokens, WIDE), bf16),
        vmem((tokens, D), f32),
        vmem((tokens, D), bf16),
        vmem((tokens, D), f32),
        vmem((tokens, 128), f32),
        vmem((tokens, 3 * WIDE), bf16),
        vmem((tokens // GROUP, 8, GLANES), f32),
        vmem((tokens, WIDE), bf16),
        vmem((tokens, D), bf16),
        vmem((tokens, FF), bf16),
        vmem((tokens, FF), bf16),
        vmem((tokens, D), bf16),
        vmem((tokens, D), bf16),
        vmem((tokens, D), bf16),
        vmem((tokens, D), f32),
        vmem((tokens, D), f32),
        vmem((tokens, WIDE), bf16),
        vmem((tokens, 3 * WIDE), bf16),
        vmem((tokens, 3 * WIDE), bf16),
        vmem((9, 8, D), f32),
    ]
    spec = pl.BlockSpec(memory_space=pltpu.VMEM)
    smem = pl.BlockSpec(memory_space=pltpu.SMEM)
    entry, place = earth_tables()
    return pl.pallas_call(
        functools.partial(block_kernel, (buckets, tiles, lat_size, slots_here)),
        out_shape=outs,
        in_specs=[smem, smem] + [spec] * 4,
        out_specs=[spec] * len(outs),
        scratch_shapes=scratch,
        compiler_params=pltpu.CompilerParams(vmem_limit_bytes=60 * 1024 * 1024),
        name="block",
    )(homes, leads, tok, copies, jnp.asarray(entry), jnp.asarray(place))


MESH = pl.DeviceIdType.MESH


def places():
    lat_size, lon_size, dp_size = lax.axis_size("lat"), lax.axis_size("lon"), lax.axis_size("dp")
    return (
        lax.axis_index("dp"),
        lax.axis_index("lat"),
        lax.axis_index("lon"),
        dp_size,
        lat_size,
        lon_size,
    )


def greet(targets):
    barrier = pltpu.get_barrier_semaphore()
    for target in targets:
        pl.semaphore_signal(barrier, inc=1, device_id=target, device_id_type=MESH)
    pl.semaphore_wait(barrier, len(targets))


def around(place, step, size):
    return lax.rem(place + step, size)


def neighbours(whole_plane):
    dp, lat, lon, dp_size, lat_size, lon_size = places()
    if whole_plane:
        steps = {(i, j) for i in range(lat_size) for j in range(lon_size)}
    else:
        steps = {(1, 0), (lat_size - 1, 0), (1, 1 % lon_size), (lat_size - 1, lon_size - 1)}
        steps |= {(2 * i, 0) for i in range(1, lat_size // 2)} | {(0, j) for j in range(lon_size)}
    steps.discard((0, 0))
    found = [(around(dp, step, dp_size), lat, lon) for step in range(1, dp_size)]
    return found + [
        (dp, around(lat, i, lat_size), around(lon, j, lon_size)) for i, j in sorted(steps)
    ]


def pairing(src, dst, sends, receives, send_slot, receive_slot, target):
    return pltpu.make_async_remote_copy(
        src_ref=src,
        dst_ref=dst,
        send_sem=sends.at[send_slot],
        recv_sem=receives.at[receive_slot],
        device_id=target,
        device_id_type=MESH,
    )


def gather_kernel(
    sizes, own_ref, quads_ref, all_ref, tokens_ref, sends, receives, keeps
):
    dp_size, lat_size, lon_size = sizes
    chips = lat_size // 2
    dp, lat, lon = lax.axis_index("dp"), lax.axis_index("lat"), lax.axis_index("lon")
    core, chip = lax.rem(lat, 2), lat // 2
    greet(neighbours(False))
    line = 0
    first = dp_size
    second = first + dp_size * max(chips, lon_size)
    cross = second + dp_size * max(chips, lon_size)
    moves = cross + dp_size

    def chip_at(step):
        return (dp, around(chip, step, chips) * 2 + core, lon)

    def lon_at(step):
        return (dp, lat, around(lon, step, lon_size))

    def run(mine):
        unit = lon * chips + chip if mine == 0 else chip * lon_size + lon
        one, two = (chips, lon_size) if mine == 0 else (lon_size, chips)
        one_at, two_at = (chip_at, lon_at) if mine == 0 else (lon_at, chip_at)
        place_two = lon if mine == 0 else chip
        begun = []

        def send(src, dst, slot, back, target):
            copy = pairing(src, dst, sends, receives, slot, back, target)
            copy.start()
            begun.append(copy)

        def await_arrival(dst, slot):
            pairing(dst, dst, sends, receives, slot, slot, chip_at(0)).wait_recv()

        own_copy = pltpu.make_async_copy(own_ref, all_ref.at[dp, mine, unit], keeps.at[0])
        own_copy.start()
        for step in range(1, dp_size):
            send(
                own_ref,
                all_ref.at[dp, mine, unit],
                line + step,
                line + dp_size - step,
                (around(dp, step, dp_size), lat, lon),
            )
        order = sorted(range(dp_size), key=lambda step: min(step, dp_size - step))
        chunk = [around(dp, step, dp_size) for step in order]
        for turn in range(dp_size + 2):
            if turn < dp_size:
                here = all_ref.at[chunk[turn], mine, unit]
                if turn:
                    await_arrival(here, line + order[turn])
                for step in range(1, one):
                    send(
                        here if turn else own_ref,
                        here,
                        first + order[turn] * one + step,
                        first + order[turn] * one + one - step,
                        one_at(step),
                    )
            if turn == 0:
                move_starts(send)
                own_copy.wait()
            if 0 <= turn - 1 < dp_size:
                back = turn - 1
                for step in range(1, one):
                    await_arrival(
                        all_ref.at[chunk[back], mine, unit], first + order[back] * one + step
                    )
                group = all_ref.at[chunk[back], mine, pl.ds(place_two * one, one)]
                for step in range(1, two):
                    send(
                        group,
                        group,
                        second + order[back] * two + step,
                        second + order[back] * two + two - step,
                        two_at(step),
                    )
            if 0 <= turn - 2 < dp_size:
                back = turn - 2
                group = all_ref.at[chunk[back], mine, pl.ds(place_two * one, one)]
                for step in range(1, two):
                    await_arrival(group, second + order[back] * two + step)
                whole = all_ref.at[chunk[back], mine]
                send(
                    whole, whole, cross + order[back], cross + order[back], (dp, chip * 2 + 1 - mine, lon)
                )
        for turn in range(dp_size):
            await_arrival(all_ref.at[chunk[turn], 1 - mine], cross + order[turn])
        for quad in range(1, 4):
            await_arrival(tokens_ref.at[quad], moves + quad)
        for copy in begun:
            copy.wait_send()

    def move_starts(send):
        for quad in range(1, 4):
            up, left = quad // 2, quad % 2
            target = (dp, around(lat, lat_size - up, lat_size), around(lon, lon_size - left, lon_size))
            send(quads_ref.at[quad], tokens_ref.at[quad], moves + quad, moves + quad, target)

    keep = pltpu.make_async_copy(quads_ref.at[0], tokens_ref.at[0], keeps.at[1])
    keep.start()
    for mine in range(2):

        @pl.when(core == mine)
        def _():
            run(mine)

    keep.wait()


def gather_call(own, quads, sizes):
    dp_size, lat_size, lon_size = sizes
    chips = lat_size // 2
    count = dp_size * (2 + 2 * max(chips, lon_size)) + 4
    return pl.pallas_call(
        functools.partial(gather_kernel, sizes),
        out_shape=[
            jax.ShapeDtypeStruct((dp_size, 2, chips * lon_size) + own.shape, own.dtype),
            jax.ShapeDtypeStruct(quads.shape, quads.dtype),
        ],
        in_specs=[pl.BlockSpec(memory_space=pltpu.VMEM)] * 2,
        out_specs=[pl.BlockSpec(memory_space=pltpu.VMEM)] * 2,
        scratch_shapes=[
            pltpu.SemaphoreType.DMA((count,)),
            pltpu.SemaphoreType.DMA((count,)),
            pltpu.SemaphoreType.DMA((2,)),
        ],
        compiler_params=pltpu.CompilerParams(
            collective_id=0, has_side_effects=True, vmem_limit_bytes=40 * 1024 * 1024
        ),
        name="gather",
    )(own, quads)


def reduce_kernel(
    sizes,
    grads_ref,
    vecs_ref,
    quads_ref,
    homes_ref,
    mine_ref,
    total_ref,
    tokens_ref,
    half_in,
    half,
    one_in,
    one,
    two_in,
    line_out,
    line_in,
    plane_out,
    plane_in,
    vec_in,
    vec_now,
    sends,
    receives,
    keeps,
):
    dp_size, lat_size, lon_size = sizes
    chips = lat_size // 2
    dp, lat, lon = lax.axis_index("dp"), lax.axis_index("lat"), lax.axis_index("lon")
    core, chip = lax.rem(lat, 2), lat // 2
    rows, buckets = grads_ref.shape[:2]
    n_half, n_side = rows // 2, rows // 4
    n_chip, n_lon, n_last = n_side // chips, n_side // lon_size, n_side // (chips * lon_size)
    plane = lat_size * lon_size
    per_home = plane_out.shape[2]
    greet(neighbours(True))
    begun = []

    def send(src, dst, slot, back, target):
        copy = pairing(src, dst, sends, receives, slot, back, target)
        copy.start()
        begun.append(copy)

    def await_arrival(dst, slot):
        pairing(dst, dst, sends, receives, slot, slot, (dp, lat, lon)).wait_recv()

    def chip_at(step):
        return (dp, around(chip, step, chips) * 2 + core, lon)

    def lon_at(step):
        return (dp, lat, around(lon, step, lon_size))

    cross = 0
    chip_one = 2
    lon_one = chip_one + 2 * chips
    lon_two = lon_one + lon_size
    chip_two = lon_two + 2 * lon_size
    line = chip_two + chips
    last = line + 2 * dp_size
    moves = last + 2 * plane

    partner = (dp, chip * 2 + 1 - core, lon)
    keep = pltpu.make_async_copy(quads_ref.at[0], tokens_ref.at[0], keeps.at[0])
    keep.start()
    send(grads_ref.at[pl.ds((1 - core) * n_half, n_half)], half_in, cross, cross, partner)
    send(vecs_ref, vec_in.at[0], cross + 1, cross + 1, partner)

    def move(kind):
        for quad in range(1, 4):
            down, right = quad // 2, quad % 2
            target = (dp, around(lat, down, lat_size), around(lon, right, lon_size))
            slot = moves + 4 * kind + quad
            send(quads_ref.at[quad, kind], tokens_ref.at[quad, kind], slot, slot, target)

    move(0)
    await_arrival(half_in, cross)
    half[...] = (grads_ref[pl.ds(core * n_half, n_half)].astype(f32) + half_in[...].astype(f32)).astype(bf16)
    await_arrival(vec_in.at[0], cross + 1)
    vec_now[0] = vecs_ref[...] + vec_in[0]

    for step in range(1, chips):
        there = around(chip, step, chips)
        back = chips - step
        send(half.at[pl.ds(there * n_chip, n_chip)], one_in.at[pl.ds(back * n_chip, n_chip)], chip_one + step, chip_one + back, chip_at(step))
        send(vec_now.at[0], vec_in.at[back], chip_one + chips + step, chip_one + chips + back, chip_at(step))
    for step in range(1, lon_size):
        there = around(lon, step, lon_size)
        back = lon_size - step
        send(
            half.at[pl.ds(n_side + there * n_lon, n_lon)],
            one_in.at[pl.ds(n_side + back * n_lon, n_lon)],
            lon_one + step,
            lon_one + back,
            lon_at(step),
        )
    total = half[pl.ds(chip * n_chip, n_chip)].astype(f32)
    vec_total = vec_now[0]
    for step in range(1, chips):
        await_arrival(one_in.at[pl.ds(step * n_chip, n_chip)], chip_one + step)
        total = total + one_in[pl.ds(step * n_chip, n_chip)].astype(f32)
        await_arrival(vec_in.at[step], chip_one + chips + step)
        vec_total = vec_total + vec_in[step]
    one[pl.ds(0, n_chip)] = total.astype(bf16)
    vec_now[1] = vec_total
    for step in range(1, lon_size):
        there = around(lon, step, lon_size)
        back = lon_size - step
        send(one.at[pl.ds(there * n_last, n_last)], two_in.at[0, pl.ds(back * n_last, n_last)], lon_two + step, lon_two + back, lon_at(step))
        send(vec_now.at[1], vec_in.at[chips + back], lon_two + lon_size + step, lon_two + lon_size + back, lon_at(step))
    total = half[pl.ds(n_side + lon * n_lon, n_lon)].astype(f32)
    for step in range(1, lon_size):
        await_arrival(one_in.at[pl.ds(n_side + step * n_lon, n_lon)], lon_one + step)
        total = total + one_in[pl.ds(n_side + step * n_lon, n_lon)].astype(f32)
    one[pl.ds(n_chip, n_lon)] = total.astype(bf16)
    for step in range(1, chips):
        there = around(chip, step, chips)
        back = chips - step
        send(
            one.at[pl.ds(n_chip + there * n_last, n_last)],
            two_in.at[1, pl.ds(back * n_last, n_last)],
            chip_two + step,
            chip_two + back,
            chip_at(step),
        )
    final_a = one[pl.ds(lon * n_last, n_last)].astype(f32)
    vec_total = vec_now[1]
    for step in range(1, lon_size):
        await_arrival(two_in.at[0, pl.ds(step * n_last, n_last)], lon_two + step)
        final_a = final_a + two_in[0, pl.ds(step * n_last, n_last)].astype(f32)
        await_arrival(vec_in.at[chips + step], lon_two + lon_size + step)
        vec_total = vec_total + vec_in[chips + step]
    vec_now[2] = vec_total
    final_b = one[pl.ds(n_chip + chip * n_last, n_last)].astype(f32)
    for step in range(1, chips):
        await_arrival(two_in.at[1, pl.ds(step * n_last, n_last)], chip_two + step)
        final_b = final_b + two_in[1, pl.ds(step * n_last, n_last)].astype(f32)
    final = jnp.concatenate([final_a, final_b], axis=0).astype(bf16)

    width = plane * per_home
    homes = homes_ref[...]
    place = lax.broadcasted_iota(jnp.int32, (dp_size * width, buckets), 0)
    turn = lax.rem(place // width + dp, dp_size)
    pick = jnp.where(turn * width + lax.rem(place, width) == homes, 1.0, 0.0).astype(bf16)
    for row in range(2 * n_last):
        picked = nn(pick, final[row]).astype(bf16)
        for step in range(dp_size):
            line_out[step, row] = picked[step * width : (step + 1) * width]
    for step in range(dp_size):
        there = around(dp, step, dp_size)
        if step:
            back = dp_size - step
            send(line_out.at[step], line_in.at[back], line + step, line + back, (there, lat, lon))
            send(vec_now.at[2], vec_in.at[chips + lon_size + back], line + dp_size + step, line + dp_size + back, (there, lat, lon))
    move(1)
    summed = line_out[0].astype(f32)
    vec_total = vec_now[2]
    for step in range(1, dp_size):
        await_arrival(line_in.at[step], line + step)
        summed = summed + line_in[step].astype(f32)
        await_arrival(vec_in.at[chips + lon_size + step], line + dp_size + step)
        vec_total = vec_total + vec_in[chips + lon_size + step]
    total_ref[...] = vec_total
    for home in range(plane):
        plane_out[home] = summed[:, per_home * home : per_home * (home + 1), :]
    row_a = core * n_half + chip * n_chip + lon * n_last
    row_b = core * n_half + n_side + lon * n_lon + chip * n_last
    me = lat * lon_size + lon
    for lat_step in range(lat_size):
        for lon_step in range(lon_size):
            there = (dp, around(lat, lat_step, lat_size), around(lon, lon_step, lon_size))
            home = there[1] * lon_size + there[2]
            slot = last + 2 * (lat_step * lon_size + lon_step)
            back = last + 2 * ((lat_size - lat_step) % lat_size * lon_size + (lon_size - lon_step) % lon_size)
            if lat_step == 0 and lon_step == 0:
                for side, row in enumerate((row_a, row_b)):
                    copy = pltpu.make_async_copy(
                        plane_out.at[me, pl.ds(side * n_last, n_last)],
                        mine_ref.at[pl.ds(row, n_last)],
                        keeps.at[1 + side],
                    )
                    copy.start()
                continue
            for side, row in enumerate((row_a, row_b)):
                send(
                    plane_out.at[home, pl.ds(side * n_last, n_last)],
                    mine_ref.at[pl.ds(row, n_last)],
                    slot + side,
                    back + side,
                    there,
                )
    for side, row in enumerate((row_a, row_b)):
        pltpu.make_async_copy(
            plane_out.at[me, pl.ds(side * n_last, n_last)],
            mine_ref.at[pl.ds(row, n_last)],
            keeps.at[1 + side],
        ).wait()
    for index in range(1, plane):
        for side in range(2):
            await_arrival(mine_ref.at[pl.ds(0, n_last)], last + 2 * index + side)
    for kind in range(2):
        for quad in range(1, 4):
            await_arrival(tokens_ref.at[quad, kind], moves + 4 * kind + quad)
    keep.wait()
    for copy in begun:
        copy.wait_send()


def reduce_call(grads, vecs, quads, homes, per_home, sizes):
    dp_size, lat_size, lon_size = sizes
    chips = lat_size // 2
    rows, buckets = grads.shape[:2]
    plane = lat_size * lon_size
    n_half, n_side = rows // 2, rows // 4
    n_chip, n_lon, n_last = n_side // chips, n_side // lon_size, n_side // (chips * lon_size)
    count = 2 + 2 * chips + lon_size + 2 * lon_size + chips + 2 * dp_size + 2 * plane + 8
    vmem = pltpu.VMEM
    return pl.pallas_call(
        functools.partial(reduce_kernel, sizes),
        out_shape=[
            jax.ShapeDtypeStruct((rows, per_home, 128), f32),
            jax.ShapeDtypeStruct(vecs.shape, f32),
            jax.ShapeDtypeStruct(quads.shape, quads.dtype),
        ],
        in_specs=[pl.BlockSpec(memory_space=pltpu.VMEM)] * 4,
        out_specs=[pl.BlockSpec(memory_space=pltpu.VMEM)] * 3,
        scratch_shapes=[
            vmem((n_half, buckets, 128), bf16),
            vmem((n_half, buckets, 128), bf16),
            vmem((n_half, buckets, 128), bf16),
            vmem((n_chip + n_lon, buckets, 128), bf16),
            vmem((2, max(n_chip, n_lon), buckets, 128), bf16),
            vmem((dp_size, 2 * n_last, plane * per_home, 128), bf16),
            vmem((dp_size, 2 * n_last, plane * per_home, 128), bf16),
            vmem((plane, 2 * n_last, per_home, 128), f32),
            vmem((8, 128), f32),
            vmem((chips + lon_size + dp_size,) + vecs.shape, f32),
            vmem((3,) + vecs.shape, f32),
            pltpu.SemaphoreType.DMA((count,)),
            pltpu.SemaphoreType.DMA((count,)),
            pltpu.SemaphoreType.DMA((3,)),
        ],
        compiler_params=pltpu.CompilerParams(
            collective_id=1, has_side_effects=True, vmem_limit_bytes=40 * 1024 * 1024
        ),
        name="reduce",
    )(grads, vecs, quads, homes)


def adam_kernel(steps_ref, buckets_ref, marks, grads_ref, master_ref, one_ref, two_ref, new_master, new_one, new_two):
    homes = master_ref.shape[0]
    tiles = master_ref.shape[1] // 128
    steps = jnp.full((homes, 128), steps_ref[0], jnp.int32).astype(f32)
    fix_one = 1.0 / (1.0 - jnp.exp(steps * math.log(beta_one)))
    fix_two = 1.0 / (1.0 - jnp.exp(steps * math.log(beta_two)))
    base = jnp.concatenate(
        [jnp.full((1, 128), buckets_ref[home], jnp.int32) for home in range(homes)], axis=0
    ) + lax.broadcasted_iota(jnp.int32, (homes, 128), 1)
    rates = [2.6 / math.sqrt(D), 8.0 / math.sqrt(D), 2.6 / math.sqrt(D), 4.0 / math.sqrt(D), 2.0 / math.sqrt(D), 3.0 / math.sqrt(FF), 1.0, 0.6]
    for tile in range(tiles):
        columns = slice(128 * tile, 128 * (tile + 1))
        index = base + 128 * tile
        rate = jnp.full((homes, 128), 0.1, f32)
        for number in range(7, -1, -1):
            rate = jnp.where(index < marks[number + 1], rates[number], rate)
        grad = grads_ref[tile]
        weights = master_ref[:, columns]
        first = beta_one * one_ref[:, columns] + (1.0 - beta_one) * grad
        second = beta_two * two_ref[:, columns] + (1.0 - beta_two) * grad * grad
        step = first * fix_one / (jnp.sqrt(second * fix_two) + eps_adam) + decay_rate * weights
        new_master[:, columns] = weights - rate * step
        new_one[:, columns] = first
        new_two[:, columns] = second


def adam_call(steps, bases, marks, grads, master, one, two):
    smem = pl.BlockSpec(memory_space=pltpu.SMEM)
    vmem = pl.BlockSpec(memory_space=pltpu.VMEM)

    def body(steps_ref, bases_ref, *refs):
        adam_kernel(steps_ref, bases_ref, marks, *refs)

    return pl.pallas_call(
        body,
        out_shape=[jax.ShapeDtypeStruct(master.shape, f32)] * 3,
        in_specs=[smem, smem, vmem, vmem, vmem, vmem],
        out_specs=[vmem] * 3,
        name="adam",
    )(steps, bases, grads, master, one, two)


def quads_out(block):
    slots, levels = block.shape[:2]
    split = block.reshape(slots * levels, 2, HALF_LAT, 2, HALF_LON, D)
    return split.transpose(1, 3, 2, 4, 0, 5)[::-1, ::-1].reshape(4, -1, D)


def quads_back(quads, slots, levels):
    split = quads.reshape(2, 2, HALF_LAT, HALF_LON, slots * levels, D)[::-1, ::-1]
    return split.transpose(4, 0, 2, 1, 3, 5).reshape(slots, levels, WIN_LAT, WIN_LON, D)


def per_device(
    inputs, cotangent, lead_counts, home_slots, master, moment_one, moment_two, step_count
):
    slots_here = inputs.shape[0]
    levels = inputs.shape[1]
    lat_size = lax.axis_size("lat")
    segment_marks = offsets(lat_size + 1)
    dp_size, lon_size = lax.axis_size("dp"), lax.axis_size("lon")
    sizes = (dp_size, lat_size, lon_size)
    slots_mine, bucket_width = master.shape
    bucket_total = home_slots.shape[0]
    tiles = bucket_width // 128
    tiles_up = -(-tiles // 16) * 16
    own = jnp.pad(
        master.reshape(slots_mine, tiles, 128), ((0, 0), (0, tiles_up - tiles), (0, 0))
    ).astype(bf16)
    quads = jnp.stack([quads_out(inputs), quads_out(cotangent)], axis=1)
    copies, tok = gather_call(own, quads, sizes)
    home_device = home_slots // slots_mine
    home_lon = home_device % lon_size
    home_lat = home_device // lon_size % lat_size
    chips = lat_size // 2
    home_unit = jnp.where(
        home_lat % 2 == 0, home_lon * chips + home_lat // 2, home_lat // 2 * lon_size + home_lon
    )
    home_place = (home_device // (lon_size * lat_size) * 2 + home_lat % 2) * (chips * lon_size)
    home_place = (home_place + home_unit) * slots_mine + home_slots % slots_mine
    unit = 4 * chips * lon_size
    rows_up = -(-tiles // unit) * unit
    out_tok, grad_rows, dvec = block_call(
        home_place,
        lead_counts,
        tok,
        copies.reshape(-1, tiles_up, 128),
        tiles,
        rows_up,
        lat_size,
        slots_here,
    )
    my_grads, grad_vectors, tok_back = reduce_call(
        grad_rows, dvec, out_tok, home_slots[None, :], slots_mine, sizes
    )
    device_place = lax.axis_index(("dp", "lat", "lon"))
    slot_ids = device_place * slots_mine + jnp.arange(slots_mine, dtype=jnp.int32)
    owner_match = home_slots[None, :] == slot_ids[:, None]
    bucket_ids = jnp.sum(
        jnp.where(owner_match, jnp.arange(bucket_total, dtype=jnp.int32)[None, :], 0), axis=1
    )
    present = jnp.any(owner_match, axis=1)
    bases = jnp.where(present, bucket_ids * bucket_width, segment_marks[8])
    new_master, new_one, new_two = adam_call(
        step_count, bases, segment_marks, my_grads, master, moment_one, moment_two
    )
    result = quads_back(tok_back[:, 0], slots_here, levels)
    grad_inputs = quads_back(tok_back[:, 1], slots_here, levels).astype(f32)
    return (result, grad_inputs, grad_vectors + 0.0, new_master, new_one, new_two)


def solution(mesh):
    in_specs = (
        P("dp", None, "lat", "lon", None),
        P("dp", None, "lat", "lon", None),
        P(),
        P(),
        P(("dp", "lat", "lon"), None),
        P(("dp", "lat", "lon"), None),
        P(("dp", "lat", "lon"), None),
        P(),
    )
    out_specs = (
        P("dp", None, "lat", "lon", None),
        P("dp", None, "lat", "lon", None),
        P(),
        P(("dp", "lat", "lon"), None),
        P(("dp", "lat", "lon"), None),
        P(("dp", "lat", "lon"), None),
    )
    return jax.shard_map(
        per_device, mesh=mesh, in_specs=in_specs, out_specs=out_specs, check_vma=False
    )
```

```python
import functools
import math

import jax
import jax.numpy as jnp
import ml_dtypes
import numpy as np
from jax import lax
from jax.experimental import pallas as pl
from jax.experimental.pallas import tpu as pltpu
from jax.sharding import PartitionSpec as P

D = 192
FF = 768
HEADS = 6
HEAD_DIM = 32
LEVELS = 8
WIN_LAT = 6
WIN_LON = 12
LEADS = 4
HALF_LAT = WIN_LAT // 2
HALF_LON = WIN_LON // 2
QUAD = HALF_LAT * HALF_LON
AREA = WIN_LAT * WIN_LON
LANES = HEADS * AREA
WIDE = 256
SCALE = 1.0 / math.sqrt(HEAD_DIM)

beta_one = 0.6
beta_two = 0.45
eps_norm = 1e-05
eps_adam = 1e-08
decay_rate = 0.1
penalty_value = -1000000000.0
bf16 = jnp.bfloat16
f32 = jnp.float32


def offsets(groups):
    sizes_list = [
        3 * D * D,
        D * D,
        3 * D * D,
        D * D,
        D * FF,
        FF * D,
        groups * HEADS * WIN_LAT * WIN_LAT * (2 * WIN_LON - 1),
        9 * D,
    ]
    segment_marks = [0]
    for amount in sizes_list:
        segment_marks.append(segment_marks[-1] + amount)
    return segment_marks


def nn(left, right):
    return jnp.dot(left, right, preferred_element_type=f32)


def nt(left, right):
    return lax.dot_general(left, right, (((1,), (1,)), ((), ())), preferred_element_type=f32)


def tn(left, right):
    return lax.dot_general(left, right, (((0,), (0,)), ((), ())), preferred_element_type=f32)


def normed(values):
    center = values - jnp.sum(values, axis=-1, keepdims=True) * (1.0 / D)
    spread = jnp.sum(center * center, axis=-1, keepdims=True) * (1.0 / D)
    inverse = lax.rsqrt(spread + eps_norm)
    return center * inverse, inverse


def norm_back(grad, hat, inverse, gain):
    scaled = grad * gain
    mean_one = jnp.sum(scaled, axis=-1, keepdims=True) * (1.0 / D)
    mean_two = jnp.sum(scaled * hat, axis=-1, keepdims=True) * (1.0 / D)
    return inverse * (scaled - mean_one - hat * mean_two)


def row_fold(values):
    return jnp.sum(values.reshape(values.shape[0] // 8, 8, values.shape[1]), axis=0)


def head_masks(dtype):
    lane = lax.broadcasted_iota(jnp.int32, (1, WIDE), 1) // HEAD_DIM
    return [jnp.where(lane == head, 1.0, 0.0).astype(dtype) for head in range(HEADS)]


def spread_heads(values, masks):
    return jnp.concatenate([values * mask for mask in masks], axis=0)


def fold_heads(big, count):
    parts = [big[head * count : (head + 1) * count] for head in range(HEADS)]
    lane = lax.broadcasted_iota(jnp.int32, (count, 128), 1)
    low = parts[3][:, :128]
    for head in (2, 1, 0):
        low = jnp.where(lane < HEAD_DIM * (head + 1), parts[head][:, :128], low)
    high = jnp.where(lane < HEAD_DIM, parts[4][:, 128:], parts[5][:, 128:])
    return jnp.concatenate([low, high], axis=1)


def rounded(values):
    return values.astype(bf16).astype(f32)


def soft_columns(scores):
    exps = jnp.exp(scores - jnp.max(scores, axis=0, keepdims=True))
    return exps * (1.0 / jnp.sum(exps, axis=0, keepdims=True))


def soft_back(probs, slopes):
    return probs * (slopes - jnp.sum(probs * slopes, axis=0, keepdims=True))


GROUP = 64
GLANES = HEADS * GROUP
CHUNK = 288


def lanes_of(ref, start):
    row, lane = divmod(start, 128)
    here = ref[row : row + 1, :]
    if lane == 0:
        return here
    place = lax.broadcasted_iota(jnp.int32, (1, 128), 1)
    mixed = jnp.where(place >= lane, here, ref[row + 1 : row + 2, :])
    return pltpu.roll(mixed, 128 - lane, 1)


def tail_head(tail, head):
    place = lax.broadcasted_iota(jnp.int32, tail.shape, 1)
    return pltpu.roll(jnp.where(place >= 64, tail, head), 64, 1)


def head_head(first, second):
    place = lax.broadcasted_iota(jnp.int32, first.shape, 1)
    return jnp.where(place < 64, first, pltpu.roll(second, 64, 1))


def only_head(values):
    place = lax.broadcasted_iota(jnp.int32, values.shape, 1)
    return jnp.where(place < 64, values, 0.0)


def only_tail(values):
    place = lax.broadcasted_iota(jnp.int32, values.shape, 1)
    return pltpu.roll(jnp.where(place >= 64, values, 0.0), 64, 1)


EARTH_ROW = WIN_LAT * (2 * WIN_LON - 1)
EARTH_ROWS = HEADS * WIN_LAT


def earth_tables():
    entry = np.zeros((WIN_LON, AREA, 256), np.float32)
    place = np.zeros((WIN_LON, 40, LANES), np.float32)
    for column in range(WIN_LON):
        side, inner = divmod(column, HALF_LON)
        for key in range(AREA):
            key_up, rest = divmod(key, 2 * QUAD)
            key_side, rest = divmod(rest, QUAD)
            key_row, key_inner = divmod(rest, HALF_LON)
            row = key_up * HALF_LAT + key_row
            offset = column - (key_side * HALF_LON + key_inner) + WIN_LON - 1
            entry[column, key, row * (2 * WIN_LON - 1) + offset] = 1.0
        for head in range(HEADS):
            for row in range(WIN_LAT):
                up, low = divmod(row, HALF_LAT)
                lane = AREA * head + 2 * QUAD * up + QUAD * side + HALF_LON * low + inner
                place[column, head * WIN_LAT + row, lane] = 1.0
    return entry.astype(ml_dtypes.bfloat16), place.astype(ml_dtypes.bfloat16)


def block_kernel(
    sizes,
    home_ref,
    lead_ref,
    tok_ref,
    cotq_ref,
    copies_ref,
    entry_ref,
    place_ref,
    out_ref,
    grads_ref,
    dvec_ref,
    flat_ref,
    mid_ref,
    earth_ref,
    gate_ref,
    bias_ref,
    dbias_ref,
    w1_ref,
    o1_ref,
    w2_ref,
    o2_ref,
    up_ref,
    down_ref,
    vec_ref,
    n1_ref,
    hat1_ref,
    inv1_ref,
    qkv_ref,
    probs_ref,
    att_ref,
    att1_ref,
    tok1_ref,
    n2_ref,
    hat2_ref,
    inv2_ref,
    mix2_ref,
    cprobs_ref,
    att2_ref,
    n3_ref,
    act_ref,
    gh_ref,
    delta3_ref,
    delta2_ref,
    delta1_ref,
    gmid_ref,
    glow_ref,
    gatt2_ref,
    gm2_ref,
    gm1_ref,
    vacc_ref,
    cot_ref,
    move_sends,
    move_receives,
):
    tokens = 4 * tok_ref.shape[1]
    count = tokens // AREA
    chunks = 4
    buckets, tiles, lat_size, slots_here = sizes
    lat = lax.axis_index("lat")
    is_last = lat == lat_size - 1
    dp, lon = lax.axis_index("dp"), lax.axis_index("lon")
    lon_size = lax.axis_size("lon")
    targets = []
    barrier = pltpu.get_barrier_semaphore()
    for quad in range(1, 4):
        up, left = quad // 2, quad % 2
        target = (dp, around(lat, lat_size - up, lat_size), around(lon, lon_size - left, lon_size))
        source = (dp, around(lat, up, lat_size), around(lon, left, lon_size))
        targets.append(target)
        for other in (target, source):
            pl.semaphore_signal(barrier, inc=1, device_id=other, device_id_type=MESH)
    pl.semaphore_wait(barrier, 6)
    moves = [
        pltpu.make_async_remote_copy(
            src_ref=cotq_ref.at[quad],
            dst_ref=cot_ref.at[quad],
            send_sem=move_sends.at[quad],
            recv_sem=move_receives.at[quad],
            device_id=targets[quad - 1],
            device_id_type=MESH,
        )
        for quad in range(1, 4)
    ]
    for move in moves:
        move.start()
    cot_ref[0] = cotq_ref[0]
    marks = offsets(lat_size + 1)
    row_marks = [mark // 128 for mark in marks]

    for bucket in range(buckets):
        block = copies_ref[home_ref[bucket]].astype(f32)
        flat_ref[tiles * bucket : tiles * (bucket + 1), :] = block[:tiles]

    def take_pairs(base, parts, pairs):
        return [flat_ref[pl.ds(base + part, pairs, stride=parts), :] for part in range(parts)]

    def give_pairs(columns, rows, evens, odds):
        for column, (even, odd) in enumerate(zip(evens, odds)):
            mid_ref[column, pl.ds(0, rows // 2, stride=2), :] = even
            mid_ref[column, pl.ds(1, rows // 2, stride=2), :] = odd

    def load_qkv(base, ref):
        b = take_pairs(base, 9, D // 2)
        evens = [b[0], only_head(b[1]), tail_head(b[1], b[2]), only_tail(b[2]), b[3], only_head(b[4])]
        odds = [tail_head(b[4], b[5]), only_tail(b[5]), b[6], only_head(b[7]), tail_head(b[7], b[8]), only_tail(b[8])]
        give_pairs(6, D, evens, odds)
        for column in range(6):
            ref[:, 128 * column : 128 * (column + 1)] = mid_ref[column, pl.ds(0, D), :].astype(bf16)

    def load_square(base, rows, ref):
        b = take_pairs(base, 3, rows // 2)
        give_pairs(2, rows, [b[0], b[1]], [tail_head(b[1], b[2]), only_tail(b[2])])
        ref[0:rows, 0:128] = mid_ref[0, pl.ds(0, rows), :].astype(bf16)
        ref[0:rows, 128:D] = mid_ref[1, pl.ds(0, rows), :][:, : D - 128].astype(bf16)

    load_qkv(row_marks[0], w1_ref)
    load_square(row_marks[1], D, o1_ref)
    load_qkv(row_marks[2], w2_ref)
    load_square(row_marks[3], D, o2_ref)
    for ref in (o1_ref, o2_ref):
        ref[D:WIDE, :] = jnp.zeros((WIDE - D, D), bf16)
    for column in range(6):
        up_ref[:, 128 * column : 128 * (column + 1)] = flat_ref[
            pl.ds(row_marks[4] + column, D, stride=6), :
        ].astype(bf16)
    load_square(row_marks[5], FF, down_ref)
    for index in range(9):
        start = marks[7] + D * index
        vec_ref[index : index + 1, 0:128] = lanes_of(flat_ref, start)
        vec_ref[index : index + 1, 128:D] = lanes_of(flat_ref, start + 128)[:, : D - 128]

    def earth_places():
        group_one = lat + 1
        group_two = jnp.where(is_last, 0, lat + 1)
        for index in range(EARTH_ROWS):
            group = group_one if index % WIN_LAT < HALF_LAT else group_two
            start = marks[6] + EARTH_ROW * (EARTH_ROWS * group + index)
            row = start // 128
            yield index, row, start - 128 * row

    lane_place = lax.broadcasted_iota(jnp.int32, (1, 128), 1)
    earth_ref[...] = jnp.zeros_like(earth_ref)
    for index, row, lane in earth_places():
        rows = [flat_ref[pl.ds(row + step, 1), :] for step in range(3)]
        back = lax.rem(128 - lane, 128)
        first = pltpu.roll(jnp.where(lane_place >= lane, rows[0], rows[1]), back, 1)
        second = pltpu.roll(jnp.where(lane_place >= lane, rows[1], rows[2]), back, 1)
        earth_ref[index : index + 1, 0:128] = first
        earth_ref[index : index + 1, 128:256] = jnp.where(lane_place < EARTH_ROW - 128, second, 0.0)
    earth = earth_ref[...].astype(bf16)
    key_up = lax.broadcasted_iota(jnp.int32, (AREA, LANES), 0) // (2 * QUAD)
    query_up = lax.rem(lax.broadcasted_iota(jnp.int32, (AREA, LANES), 1), AREA) // (2 * QUAD)
    bias = jnp.where((key_up != query_up) & is_last, penalty_value, 0.0)
    for column in range(WIN_LON):
        bias = bias + nn(nt(entry_ref[column], earth).astype(bf16), place_ref[column])
    bias_ref[...] = bias

    for slot in range(slots_here):
        number = lax.axis_index("dp") * slots_here + slot
        live = lax.rem(number, LEADS) < lead_ref[number // LEADS]
        size = count // slots_here
        gate_ref[slot * size : (slot + 1) * size, :] = jnp.full((size, D), jnp.where(live, 1.0, 0.0), f32)

    def part(index):
        return pl.ds(pl.multiple_of(index * CHUNK, CHUNK), CHUNK)

    def vec(index):
        return vec_ref[index : index + 1, :]

    def gate_rows():
        gate = gate_ref[...]
        return jnp.broadcast_to(gate[None], (CHUNK // count, count, D)).reshape(CHUNK, D)

    vacc_ref[...] = jnp.zeros_like(vacc_ref)

    def note(index, values):
        vacc_ref[index] += row_fold(values)

    @pl.loop(0, chunks)
    def _(c):
        rows = part(c)
        hat, inverse = normed(tok_ref[c].astype(f32))
        hat1_ref[rows, :] = hat
        inv1_ref[rows, :] = jnp.broadcast_to(inverse, (CHUNK, 128))
        low = (hat * vec(0) + vec(1)).astype(bf16)
        n1_ref[rows, :] = low
        mixed = rounded(nn(low, w1_ref[...]))
        for tile in range(6):
            qkv_ref[tile, rows, :] = mixed[:, 128 * tile : 128 * (tile + 1)]

    def window(ref, first, s):
        rows = pl.ds(s, AREA, stride=count)
        return jnp.concatenate([ref[first, rows, :], ref[first + 1, rows, :]], axis=1)

    def window_store(ref, first, s, values):
        rows = pl.ds(s, AREA, stride=count)
        ref[first, rows, :] = values[:, :128]
        ref[first + 1, rows, :] = values[:, 128:]

    @pl.loop(0, count // 4)
    def _(block):
        masks = head_masks(f32)
        places = [block * 4 + step for step in range(4)]
        reads = [[window(qkv_ref, 2 * kind, s) for kind in range(3)] for s in places]
        raw = [
            nt(key.astype(bf16), spread_heads(query, masks).astype(bf16)) for query, key, _ in reads
        ]
        probs = [soft_columns(scores * SCALE + bias_ref[...]) for scores in raw]
        outs = [tn(prob.astype(bf16), read[2].astype(bf16)) for prob, read in zip(probs, reads)]
        for s, prob, out in zip(places, probs, outs):
            probs_ref[s] = prob
            window_store(att_ref, 0, s, fold_heads(out, AREA))

    @pl.loop(0, chunks)
    def _(c):
        rows = part(c)
        att = jnp.concatenate([att_ref[0, rows, :], att_ref[1, rows, :]], axis=1).astype(bf16)
        att1_ref[rows, :] = att
        branch = nn(att, o1_ref[...]) + vec(2)
        tok = tok_ref[c].astype(f32) + gate_rows() * branch
        tok1_ref[rows, :] = tok
        hat, inverse = normed(tok)
        hat2_ref[rows, :] = hat
        inv2_ref[rows, :] = jnp.broadcast_to(inverse, (CHUNK, 128))
        low = (hat * vec(3) + vec(4)).astype(bf16)
        n2_ref[rows, :] = low
        mix2_ref[rows, :] = nn(low, w2_ref[...]).astype(bf16)

    def column_masks():
        lane = lax.broadcasted_iota(jnp.int32, (8, GLANES), 1)
        place = (lane % GROUP) // 8
        return [place == index for index in range(GROUP // 8)]

    def squeeze_column(values, masks):
        out = values[:8]
        for index in range(1, GROUP // 8):
            out = jnp.where(masks[index], values[8 * index : 8 * index + 8], out)
        return out

    def widen_column(values, masks):
        return jnp.concatenate([jnp.where(mask, values, 0.0) for mask in masks], axis=0).astype(bf16)

    def group_rows(g):
        return pl.ds(pl.multiple_of(g * GROUP, GROUP), GROUP)

    @pl.loop(0, tokens // GROUP // 6)
    def _(block):
        heads = head_masks(bf16)
        columns = column_masks()
        places = [block * 6 + step for step in range(6)]
        reads = [mix2_ref[group_rows(g), :] for g in places]
        raw = [
            nt(mixed[:, WIDE : 2 * WIDE], spread_heads(mixed[:, 0:WIDE], heads)) for mixed in reads
        ]
        probs = [soft_columns(squeeze_column(scores, columns) * SCALE) for scores in raw]
        outs = [
            tn(widen_column(prob, columns), mixed[:, 2 * WIDE :])
            for prob, mixed in zip(probs, reads)
        ]
        for g, prob, out in zip(places, probs, outs):
            cprobs_ref[g] = prob
            att2_ref[group_rows(g), :] = fold_heads(out, GROUP).astype(bf16)

    root = math.sqrt(2.0 / math.pi)
    for move in moves:
        move.wait()

    @pl.loop(0, chunks)
    def _(c):
        rows = part(c)
        gate = gate_rows()
        tok = tok1_ref[rows, :] + gate * (nn(att2_ref[rows, :], o2_ref[...]) + vec(5))
        hat, inverse = normed(tok)
        low = (hat * vec(6) + vec(7)).astype(bf16)
        n3_ref[rows, :] = low
        hidden = nn(low, up_ref[...])
        square = hidden * hidden
        half = 0.5 * jnp.tanh(hidden * (root + (root * 0.044715) * square)) + 0.5
        wave = hidden * half
        act = wave.astype(bf16)
        act_ref[rows, :] = act
        out_ref[c, 0] = (tok + gate * (nn(act, down_ref[...]) + vec(8))).astype(bf16)
        slope = half + wave * (1.0 - half) * (2.0 * root + (6.0 * root * 0.044715) * square)
        after = cot_ref[c].astype(f32)
        delta3 = (gate * after).astype(bf16)
        delta3_ref[rows, :] = delta3
        note(8, delta3.astype(f32))
        gh = (nt(delta3, down_ref[...]) * slope).astype(bf16)
        gh_ref[rows, :] = gh
        grad = nt(gh, up_ref[...])
        note(6, grad * hat)
        note(7, grad)
        mid = after + norm_back(grad, hat, inverse, vec(6))
        gmid_ref[rows, :] = mid
        delta2 = (gate * mid).astype(bf16)
        delta2_ref[rows, :] = delta2
        note(5, delta2.astype(f32))
        gatt2_ref[rows, :] = nt(delta2, o2_ref[...]).astype(bf16)

    @pl.loop(0, tokens // GROUP // 6)
    def _(block):
        heads = head_masks(bf16)
        columns = column_masks()
        places = [block * 6 + step for step in range(6)]
        reads = [
            (mix2_ref[group_rows(g), :], gatt2_ref[group_rows(g), :], cprobs_ref[g]) for g in places
        ]
        grads = [spread_heads(read[1], heads) for read in reads]
        raw = [nt(read[0][:, 2 * WIDE :], grad) for read, grad in zip(reads, grads)]
        dvalues = [nn(widen_column(read[2], columns), grad) for read, grad in zip(reads, grads)]
        lows = [
            widen_column(soft_back(read[2], squeeze_column(slopes, columns)), columns)
            for read, slopes in zip(reads, raw)
        ]
        dkeys = [
            nn(low, spread_heads(read[0][:, 0:WIDE], heads)) for read, low in zip(reads, lows)
        ]
        dqueries = [tn(low, read[0][:, WIDE : 2 * WIDE]) for read, low in zip(reads, lows)]
        for g, dquery, dkey, dvalue in zip(places, dqueries, dkeys, dvalues):
            rows = group_rows(g)
            gm2_ref[rows, 0:WIDE] = (fold_heads(dquery, GROUP) * SCALE).astype(bf16)
            gm2_ref[rows, WIDE : 2 * WIDE] = (dkey * SCALE).astype(bf16)
            gm2_ref[rows, 2 * WIDE : 3 * WIDE] = dvalue.astype(bf16)

    @pl.loop(0, chunks)
    def _(c):
        rows = part(c)
        grad = nt(gm2_ref[rows, :], w2_ref[...])
        hat = hat2_ref[rows, :]
        inverse = inv2_ref[rows, :][:, :1]
        note(3, grad * hat)
        note(4, grad)
        low = gmid_ref[rows, :] + norm_back(grad, hat, inverse, vec(3))
        glow_ref[rows, :] = low
        delta1 = (gate_rows() * low).astype(bf16)
        delta1_ref[rows, :] = delta1
        note(2, delta1.astype(f32))
        gatt = rounded(nt(delta1, o1_ref[...]))
        att_ref[0, rows, :] = gatt[:, :128]
        att_ref[1, rows, :] = gatt[:, 128:]

    dbias_ref[...] = jnp.zeros_like(dbias_ref)

    @pl.loop(0, count // 4)
    def _(block):
        masks = head_masks(f32)
        places = [block * 4 + step for step in range(4)]
        reads = [
            [window(qkv_ref, 2 * kind, s) for kind in range(3)]
            + [window(att_ref, 0, s), probs_ref[s]]
            for s in places
        ]
        grads = [spread_heads(read[3], masks).astype(bf16) for read in reads]
        raw = [nt(read[2].astype(bf16), grad) for read, grad in zip(reads, grads)]
        dvalues = [nn(read[4].astype(bf16), grad) for read, grad in zip(reads, grads)]
        lows = [soft_back(read[4], slopes).astype(bf16) for read, slopes in zip(reads, raw)]
        dkeys = [
            nn(low, spread_heads(read[0], masks).astype(bf16)) for read, low in zip(reads, lows)
        ]
        dqueries = [tn(low, read[1].astype(bf16)) for read, low in zip(reads, lows)]
        dbias_ref[...] += functools.reduce(jnp.add, [low.astype(f32) for low in lows])
        for s, dquery, dkey, dvalue in zip(places, dqueries, dkeys, dvalues):
            window_store(qkv_ref, 0, s, rounded(fold_heads(dquery, AREA) * SCALE))
            window_store(qkv_ref, 2, s, rounded(dkey * SCALE))
            window_store(qkv_ref, 4, s, rounded(dvalue))

    @pl.loop(0, chunks)
    def _(c):
        rows = part(c)
        mixed = jnp.concatenate([qkv_ref[tile, rows, :] for tile in range(6)], axis=1).astype(bf16)
        gm1_ref[rows, :] = mixed
        grad = nt(mixed, w1_ref[...])
        hat = hat1_ref[rows, :]
        inverse = inv1_ref[rows, :][:, :1]
        note(0, grad * hat)
        note(1, grad)
        grad_in = glow_ref[rows, :] + norm_back(grad, hat, inverse, vec(0))
        out_ref[c, 1] = grad_in.astype(bf16)

    def keep_pairs(base, parts, blocks):
        for number, block in enumerate(blocks):
            flat_ref[pl.ds(base + number, block.shape[0], stride=parts), :] = block

    def split_pairs(columns, rows):
        evens = [mid_ref[column, pl.ds(0, rows // 2, stride=2), :] for column in range(columns)]
        odds = [mid_ref[column, pl.ds(1, rows // 2, stride=2), :] for column in range(columns)]
        return evens, odds

    def save_qkv(base, grad):
        for column in range(6):
            mid_ref[column, pl.ds(0, D), :] = grad[:, 128 * column : 128 * (column + 1)]
        e, o = split_pairs(6, D)
        blocks = [
            e[0],
            head_head(e[1], e[2]),
            tail_head(e[2], e[3]),
            e[4],
            head_head(e[5], o[0]),
            tail_head(o[0], o[1]),
            o[2],
            head_head(o[3], o[4]),
            tail_head(o[4], o[5]),
        ]
        keep_pairs(base, 9, blocks)

    def save_square(base, rows, grad):
        mid_ref[0, pl.ds(0, rows), :] = grad[:rows, :128]
        mid_ref[1, pl.ds(0, rows), 0 : D - 128] = grad[:rows, 128:]
        e, o = split_pairs(2, rows)
        keep_pairs(base, 3, [e[0], head_head(e[1], o[0]), tail_head(o[0], o[1])])

    save_qkv(row_marks[0], tn(n1_ref[...], gm1_ref[...]))
    save_square(row_marks[1], D, tn(att1_ref[...], delta1_ref[...]))
    save_qkv(row_marks[2], tn(n2_ref[...], gm2_ref[...]))
    save_square(row_marks[3], D, tn(att2_ref[...], delta2_ref[...]))
    grad_up = tn(n3_ref[...], gh_ref[...])
    for column in range(6):
        flat_ref[pl.ds(row_marks[4] + column, D, stride=6), :] = grad_up[
            :, 128 * column : 128 * (column + 1)
        ]
    save_square(row_marks[5], FF, tn(act_ref[...], delta3_ref[...]))

    rest = flat_ref.shape[0] - row_marks[6]
    flat_ref[row_marks[6] :, :] = jnp.zeros((rest, 128), f32)
    dbias = dbias_ref[...]
    high = dbias.astype(bf16)
    both = jnp.concatenate([high, (dbias - high.astype(f32)).astype(bf16)], axis=0)
    dearth = jnp.zeros((40, 256), f32)
    for column in range(WIN_LON):
        moved = nt(both, place_ref[column]).astype(bf16)
        entry = entry_ref[column]
        dearth = dearth + tn(moved[:AREA], entry) + tn(moved[AREA:], entry)
    for index, row, lane in earth_places():
        first = pltpu.roll(dearth[index : index + 1, :128], lane, 1)
        second = pltpu.roll(dearth[index : index + 1, 128:], lane, 1)
        tail = lane_place >= lane
        for step, values in enumerate(
            (
                jnp.where(tail, first, 0.0),
                jnp.where(tail, second, first),
                jnp.where(tail, 0.0, second),
            )
        ):
            flat_ref[pl.ds(row + step, 1), :] += values
    for index in range(9):
        total = jnp.sum(vacc_ref[index], axis=0, keepdims=True)
        dvec_ref[index : index + 1, :] = total
        start = marks[7] + D * index
        for values, size, begin in (
            (total[:, :128], 128, start),
            (jnp.concatenate([total[:, 128:], jnp.zeros((1, 256 - D), f32)], axis=1), D - 128, start + 128),
        ):
            row, lane = divmod(begin, 128)
            moved = pltpu.roll(values, lane, 1) if lane else values
            flat_ref[row : row + 1, :] += jnp.where(lane_place >= lane, moved, 0.0)
            if lane + size > 128:
                flat_ref[row + 1 : row + 2, :] += jnp.where(lane_place < lane, moved, 0.0)
    for tile in range(grads_ref.shape[0]):
        if tile < tiles:
            grads_ref[tile] = flat_ref[pl.ds(tile, buckets, stride=tiles), :].astype(bf16)
        else:
            grads_ref[tile] = jnp.zeros((buckets, 128), bf16)


def block_call(homes, leads, tok, cotq, copies, tiles, rows_up, lat_size, slots_here):
    tokens = 4 * tok.shape[1]
    count = tokens // AREA
    buckets = homes.shape[0]
    shape = jax.ShapeDtypeStruct
    outs = [
        shape((4, 2) + tok.shape[1:], bf16),
        shape((rows_up, buckets, 128), bf16),
        shape((9, D), f32),
    ]
    vmem = pltpu.VMEM
    scratch = [
        vmem((buckets * tiles, 128), f32),
        vmem((6, FF, 128), f32),
        vmem((40, 256), f32),
        vmem((count, D), f32),
        vmem((AREA, LANES), f32),
        vmem((AREA, LANES), f32),
        vmem((D, 3 * WIDE), bf16),
        vmem((WIDE, D), bf16),
        vmem((D, 3 * WIDE), bf16),
        vmem((WIDE, D), bf16),
        vmem((D, FF), bf16),
        vmem((FF, D), bf16),
        vmem((16, D), f32),
        vmem((tokens, D), bf16),
        vmem((tokens, D), f32),
        vmem((tokens, 128), f32),
        vmem((6, tokens, 128), f32),
        vmem((count, AREA, LANES), f32),
        vmem((2, tokens, 128), f32),
        vmem((tokens, WIDE), bf16),
        vmem((tokens, D), f32),
        vmem((tokens, D), bf16),
        vmem((tokens, D), f32),
        vmem((tokens, 128), f32),
        vmem((tokens, 3 * WIDE), bf16),
        vmem((tokens // GROUP, 8, GLANES), f32),
        vmem((tokens, WIDE), bf16),
        vmem((tokens, D), bf16),
        vmem((tokens, FF), bf16),
        vmem((tokens, FF), bf16),
        vmem((tokens, D), bf16),
        vmem((tokens, D), bf16),
        vmem((tokens, D), bf16),
        vmem((tokens, D), f32),
        vmem((tokens, D), f32),
        vmem((tokens, WIDE), bf16),
        vmem((tokens, 3 * WIDE), bf16),
        vmem((tokens, 3 * WIDE), bf16),
        vmem((9, 8, D), f32),
        vmem(tok.shape, bf16),
        pltpu.SemaphoreType.DMA((4,)),
        pltpu.SemaphoreType.DMA((4,)),
    ]
    spec = pl.BlockSpec(memory_space=pltpu.VMEM)
    smem = pl.BlockSpec(memory_space=pltpu.SMEM)
    entry, place = earth_tables()
    return pl.pallas_call(
        functools.partial(block_kernel, (buckets, tiles, lat_size, slots_here)),
        out_shape=outs,
        in_specs=[smem, smem] + [spec] * 5,
        out_specs=[spec] * len(outs),
        scratch_shapes=scratch,
        compiler_params=pltpu.CompilerParams(vmem_limit_bytes=60 * 1024 * 1024, collective_id=2, has_side_effects=True),
        name="block",
    )(homes, leads, tok, cotq, copies, jnp.asarray(entry), jnp.asarray(place))


MESH = pl.DeviceIdType.MESH


def places():
    lat_size, lon_size, dp_size = lax.axis_size("lat"), lax.axis_size("lon"), lax.axis_size("dp")
    return (
        lax.axis_index("dp"),
        lax.axis_index("lat"),
        lax.axis_index("lon"),
        dp_size,
        lat_size,
        lon_size,
    )


def greet(targets):
    barrier = pltpu.get_barrier_semaphore()
    for target in targets:
        pl.semaphore_signal(barrier, inc=1, device_id=target, device_id_type=MESH)
    pl.semaphore_wait(barrier, len(targets))


def around(place, step, size):
    return lax.rem(place + step, size)


def neighbours(whole_plane):
    dp, lat, lon, dp_size, lat_size, lon_size = places()
    if whole_plane:
        steps = {(i, j) for i in range(lat_size) for j in range(lon_size)}
    else:
        steps = {(1, 0), (lat_size - 1, 0), (1, 1 % lon_size), (lat_size - 1, lon_size - 1)}
        steps |= {(2 * i, 0) for i in range(1, lat_size // 2)} | {(0, j) for j in range(lon_size)}
    steps.discard((0, 0))
    found = [(around(dp, step, dp_size), lat, lon) for step in range(1, dp_size)]
    return found + [
        (dp, around(lat, i, lat_size), around(lon, j, lon_size)) for i, j in sorted(steps)
    ]


def pairing(src, dst, sends, receives, send_slot, receive_slot, target):
    return pltpu.make_async_remote_copy(
        src_ref=src,
        dst_ref=dst,
        send_sem=sends.at[send_slot],
        recv_sem=receives.at[receive_slot],
        device_id=target,
        device_id_type=MESH,
    )


def gather_kernel(
    sizes, own_ref, quads_ref, all_ref, tokens_ref, sends, receives, keeps
):
    dp_size, lat_size, lon_size = sizes
    chips = lat_size // 2
    dp, lat, lon = lax.axis_index("dp"), lax.axis_index("lat"), lax.axis_index("lon")
    core, chip = lax.rem(lat, 2), lat // 2
    greet(neighbours(False))
    line = 0
    first = dp_size
    second = first + dp_size * max(chips, lon_size)
    cross = second + dp_size * max(chips, lon_size)
    moves = cross + dp_size

    def chip_at(step):
        return (dp, around(chip, step, chips) * 2 + core, lon)

    def lon_at(step):
        return (dp, lat, around(lon, step, lon_size))

    def run(mine):
        unit = lon * chips + chip if mine == 0 else chip * lon_size + lon
        one, two = (chips, lon_size) if mine == 0 else (lon_size, chips)
        one_at, two_at = (chip_at, lon_at) if mine == 0 else (lon_at, chip_at)
        place_two = lon if mine == 0 else chip
        begun = []

        def send(src, dst, slot, back, target):
            copy = pairing(src, dst, sends, receives, slot, back, target)
            copy.start()
            begun.append(copy)

        def await_arrival(dst, slot):
            pairing(dst, dst, sends, receives, slot, slot, chip_at(0)).wait_recv()

        own_copy = pltpu.make_async_copy(own_ref, all_ref.at[dp, mine, unit], keeps.at[0])
        own_copy.start()
        for step in range(1, dp_size):
            send(
                own_ref,
                all_ref.at[dp, mine, unit],
                line + step,
                line + dp_size - step,
                (around(dp, step, dp_size), lat, lon),
            )
        order = sorted(range(dp_size), key=lambda step: min(step, dp_size - step))
        chunk = [around(dp, step, dp_size) for step in order]
        for turn in range(dp_size + 2):
            if turn < dp_size:
                here = all_ref.at[chunk[turn], mine, unit]
                if turn:
                    await_arrival(here, line + order[turn])
                for step in range(1, one):
                    send(
                        here if turn else own_ref,
                        here,
                        first + order[turn] * one + step,
                        first + order[turn] * one + one - step,
                        one_at(step),
                    )
            if turn == 0:
                move_starts(send)
                own_copy.wait()
            if 0 <= turn - 1 < dp_size:
                back = turn - 1
                for step in range(1, one):
                    await_arrival(
                        all_ref.at[chunk[back], mine, unit], first + order[back] * one + step
                    )
                group = all_ref.at[chunk[back], mine, pl.ds(place_two * one, one)]
                for step in range(1, two):
                    send(
                        group,
                        group,
                        second + order[back] * two + step,
                        second + order[back] * two + two - step,
                        two_at(step),
                    )
            if 0 <= turn - 2 < dp_size:
                back = turn - 2
                group = all_ref.at[chunk[back], mine, pl.ds(place_two * one, one)]
                for step in range(1, two):
                    await_arrival(group, second + order[back] * two + step)
                whole = all_ref.at[chunk[back], mine]
                send(
                    whole, whole, cross + order[back], cross + order[back], (dp, chip * 2 + 1 - mine, lon)
                )
        for turn in range(dp_size):
            await_arrival(all_ref.at[chunk[turn], 1 - mine], cross + order[turn])
        for quad in range(1, 4):
            await_arrival(tokens_ref.at[quad], moves + quad)
        for copy in begun:
            copy.wait_send()

    def move_starts(send):
        for quad in range(1, 4):
            up, left = quad // 2, quad % 2
            target = (dp, around(lat, lat_size - up, lat_size), around(lon, lon_size - left, lon_size))
            send(quads_ref.at[quad], tokens_ref.at[quad], moves + quad, moves + quad, target)

    keep = pltpu.make_async_copy(quads_ref.at[0], tokens_ref.at[0], keeps.at[1])
    keep.start()
    for mine in range(2):

        @pl.when(core == mine)
        def _():
            run(mine)

    keep.wait()


def gather_call(own, quads, sizes):
    dp_size, lat_size, lon_size = sizes
    chips = lat_size // 2
    count = dp_size * (2 + 2 * max(chips, lon_size)) + 4
    return pl.pallas_call(
        functools.partial(gather_kernel, sizes),
        out_shape=[
            jax.ShapeDtypeStruct((dp_size, 2, chips * lon_size) + own.shape, own.dtype),
            jax.ShapeDtypeStruct(quads.shape, quads.dtype),
        ],
        in_specs=[pl.BlockSpec(memory_space=pltpu.VMEM)] * 2,
        out_specs=[pl.BlockSpec(memory_space=pltpu.VMEM)] * 2,
        scratch_shapes=[
            pltpu.SemaphoreType.DMA((count,)),
            pltpu.SemaphoreType.DMA((count,)),
            pltpu.SemaphoreType.DMA((2,)),
        ],
        compiler_params=pltpu.CompilerParams(
            collective_id=0, has_side_effects=True, vmem_limit_bytes=40 * 1024 * 1024
        ),
        name="gather",
    )(own, quads)


def reduce_kernel(
    sizes,
    grads_ref,
    vecs_ref,
    quads_ref,
    homes_ref,
    mine_ref,
    total_ref,
    tokens_ref,
    half_in,
    half,
    one_in,
    one,
    two_in,
    line_out,
    line_in,
    plane_out,
    plane_in,
    vec_in,
    vec_now,
    sends,
    receives,
    keeps,
):
    dp_size, lat_size, lon_size = sizes
    chips = lat_size // 2
    dp, lat, lon = lax.axis_index("dp"), lax.axis_index("lat"), lax.axis_index("lon")
    core, chip = lax.rem(lat, 2), lat // 2
    rows, buckets = grads_ref.shape[:2]
    n_half, n_side = rows // 2, rows // 4
    n_chip, n_lon, n_last = n_side // chips, n_side // lon_size, n_side // (chips * lon_size)
    plane = lat_size * lon_size
    per_home = plane_out.shape[2]
    greet(neighbours(True))
    begun = []

    def send(src, dst, slot, back, target):
        copy = pairing(src, dst, sends, receives, slot, back, target)
        copy.start()
        begun.append(copy)

    def await_arrival(dst, slot):
        pairing(dst, dst, sends, receives, slot, slot, (dp, lat, lon)).wait_recv()

    def chip_at(step):
        return (dp, around(chip, step, chips) * 2 + core, lon)

    def lon_at(step):
        return (dp, lat, around(lon, step, lon_size))

    cross = 0
    chip_one = 2
    lon_one = chip_one + 2 * chips
    lon_two = lon_one + lon_size
    chip_two = lon_two + 2 * lon_size
    line = chip_two + chips
    last = line + 2 * dp_size
    moves = last + 2 * plane

    partner = (dp, chip * 2 + 1 - core, lon)
    keep = pltpu.make_async_copy(quads_ref.at[0], tokens_ref.at[0], keeps.at[0])
    keep.start()
    send(grads_ref.at[pl.ds((1 - core) * n_half, n_half)], half_in, cross, cross, partner)
    send(vecs_ref, vec_in.at[0], cross + 1, cross + 1, partner)

    def move(kind):
        for quad in range(1, 4):
            down, right = quad // 2, quad % 2
            target = (dp, around(lat, down, lat_size), around(lon, right, lon_size))
            slot = moves + 4 * kind + quad
            send(quads_ref.at[quad, kind], tokens_ref.at[quad, kind], slot, slot, target)

    move(0)
    await_arrival(half_in, cross)
    half[...] = (grads_ref[pl.ds(core * n_half, n_half)].astype(f32) + half_in[...].astype(f32)).astype(bf16)
    await_arrival(vec_in.at[0], cross + 1)
    vec_now[0] = vecs_ref[...] + vec_in[0]

    for step in range(1, chips):
        there = around(chip, step, chips)
        back = chips - step
        send(half.at[pl.ds(there * n_chip, n_chip)], one_in.at[pl.ds(back * n_chip, n_chip)], chip_one + step, chip_one + back, chip_at(step))
        send(vec_now.at[0], vec_in.at[back], chip_one + chips + step, chip_one + chips + back, chip_at(step))
    for step in range(1, lon_size):
        there = around(lon, step, lon_size)
        back = lon_size - step
        send(
            half.at[pl.ds(n_side + there * n_lon, n_lon)],
            one_in.at[pl.ds(n_side + back * n_lon, n_lon)],
            lon_one + step,
            lon_one + back,
            lon_at(step),
        )
    total = half[pl.ds(chip * n_chip, n_chip)].astype(f32)
    vec_total = vec_now[0]
    for step in range(1, chips):
        await_arrival(one_in.at[pl.ds(step * n_chip, n_chip)], chip_one + step)
        total = total + one_in[pl.ds(step * n_chip, n_chip)].astype(f32)
        await_arrival(vec_in.at[step], chip_one + chips + step)
        vec_total = vec_total + vec_in[step]
    one[pl.ds(0, n_chip)] = total.astype(bf16)
    vec_now[1] = vec_total
    for step in range(1, lon_size):
        there = around(lon, step, lon_size)
        back = lon_size - step
        send(one.at[pl.ds(there * n_last, n_last)], two_in.at[0, pl.ds(back * n_last, n_last)], lon_two + step, lon_two + back, lon_at(step))
        send(vec_now.at[1], vec_in.at[chips + back], lon_two + lon_size + step, lon_two + lon_size + back, lon_at(step))
    total = half[pl.ds(n_side + lon * n_lon, n_lon)].astype(f32)
    for step in range(1, lon_size):
        await_arrival(one_in.at[pl.ds(n_side + step * n_lon, n_lon)], lon_one + step)
        total = total + one_in[pl.ds(n_side + step * n_lon, n_lon)].astype(f32)
    one[pl.ds(n_chip, n_lon)] = total.astype(bf16)
    for step in range(1, chips):
        there = around(chip, step, chips)
        back = chips - step
        send(
            one.at[pl.ds(n_chip + there * n_last, n_last)],
            two_in.at[1, pl.ds(back * n_last, n_last)],
            chip_two + step,
            chip_two + back,
            chip_at(step),
        )
    final_a = one[pl.ds(lon * n_last, n_last)].astype(f32)
    vec_total = vec_now[1]
    for step in range(1, lon_size):
        await_arrival(two_in.at[0, pl.ds(step * n_last, n_last)], lon_two + step)
        final_a = final_a + two_in[0, pl.ds(step * n_last, n_last)].astype(f32)
        await_arrival(vec_in.at[chips + step], lon_two + lon_size + step)
        vec_total = vec_total + vec_in[chips + step]
    vec_now[2] = vec_total
    final_b = one[pl.ds(n_chip + chip * n_last, n_last)].astype(f32)
    for step in range(1, chips):
        await_arrival(two_in.at[1, pl.ds(step * n_last, n_last)], chip_two + step)
        final_b = final_b + two_in[1, pl.ds(step * n_last, n_last)].astype(f32)
    final = jnp.concatenate([final_a, final_b], axis=0).astype(bf16)

    width = plane * per_home
    homes = homes_ref[...]
    place = lax.broadcasted_iota(jnp.int32, (dp_size * width, buckets), 0)
    turn = lax.rem(place // width + dp, dp_size)
    pick = jnp.where(turn * width + lax.rem(place, width) == homes, 1.0, 0.0).astype(bf16)
    for row in range(2 * n_last):
        picked = nn(pick, final[row]).astype(bf16)
        for step in range(dp_size):
            line_out[step, row] = picked[step * width : (step + 1) * width]
    for step in range(dp_size):
        there = around(dp, step, dp_size)
        if step:
            back = dp_size - step
            send(line_out.at[step], line_in.at[back], line + step, line + back, (there, lat, lon))
            send(vec_now.at[2], vec_in.at[chips + lon_size + back], line + dp_size + step, line + dp_size + back, (there, lat, lon))
    move(1)
    summed = line_out[0].astype(f32)
    vec_total = vec_now[2]
    for step in range(1, dp_size):
        await_arrival(line_in.at[step], line + step)
        summed = summed + line_in[step].astype(f32)
        await_arrival(vec_in.at[chips + lon_size + step], line + dp_size + step)
        vec_total = vec_total + vec_in[chips + lon_size + step]
    total_ref[...] = vec_total
    for home in range(plane):
        plane_out[home] = summed[:, per_home * home : per_home * (home + 1), :]
    row_a = core * n_half + chip * n_chip + lon * n_last
    row_b = core * n_half + n_side + lon * n_lon + chip * n_last
    me = lat * lon_size + lon
    for lat_step in range(lat_size):
        for lon_step in range(lon_size):
            there = (dp, around(lat, lat_step, lat_size), around(lon, lon_step, lon_size))
            home = there[1] * lon_size + there[2]
            slot = last + 2 * (lat_step * lon_size + lon_step)
            back = last + 2 * ((lat_size - lat_step) % lat_size * lon_size + (lon_size - lon_step) % lon_size)
            if lat_step == 0 and lon_step == 0:
                for side, row in enumerate((row_a, row_b)):
                    copy = pltpu.make_async_copy(
                        plane_out.at[me, pl.ds(side * n_last, n_last)],
                        mine_ref.at[pl.ds(row, n_last)],
                        keeps.at[1 + side],
                    )
                    copy.start()
                continue
            for side, row in enumerate((row_a, row_b)):
                send(
                    plane_out.at[home, pl.ds(side * n_last, n_last)],
                    mine_ref.at[pl.ds(row, n_last)],
                    slot + side,
                    back + side,
                    there,
                )
    for side, row in enumerate((row_a, row_b)):
        pltpu.make_async_copy(
            plane_out.at[me, pl.ds(side * n_last, n_last)],
            mine_ref.at[pl.ds(row, n_last)],
            keeps.at[1 + side],
        ).wait()
    for index in range(1, plane):
        for side in range(2):
            await_arrival(mine_ref.at[pl.ds(0, n_last)], last + 2 * index + side)
    for kind in range(2):
        for quad in range(1, 4):
            await_arrival(tokens_ref.at[quad, kind], moves + 4 * kind + quad)
    keep.wait()
    for copy in begun:
        copy.wait_send()


def reduce_call(grads, vecs, quads, homes, per_home, sizes):
    dp_size, lat_size, lon_size = sizes
    chips = lat_size // 2
    rows, buckets = grads.shape[:2]
    plane = lat_size * lon_size
    n_half, n_side = rows // 2, rows // 4
    n_chip, n_lon, n_last = n_side // chips, n_side // lon_size, n_side // (chips * lon_size)
    count = 2 + 2 * chips + lon_size + 2 * lon_size + chips + 2 * dp_size + 2 * plane + 8
    vmem = pltpu.VMEM
    return pl.pallas_call(
        functools.partial(reduce_kernel, sizes),
        out_shape=[
            jax.ShapeDtypeStruct((rows, per_home, 128), f32),
            jax.ShapeDtypeStruct(vecs.shape, f32),
            jax.ShapeDtypeStruct(quads.shape, quads.dtype),
        ],
        in_specs=[pl.BlockSpec(memory_space=pltpu.VMEM)] * 4,
        out_specs=[pl.BlockSpec(memory_space=pltpu.VMEM)] * 3,
        scratch_shapes=[
            vmem((n_half, buckets, 128), bf16),
            vmem((n_half, buckets, 128), bf16),
            vmem((n_half, buckets, 128), bf16),
            vmem((n_chip + n_lon, buckets, 128), bf16),
            vmem((2, max(n_chip, n_lon), buckets, 128), bf16),
            vmem((dp_size, 2 * n_last, plane * per_home, 128), bf16),
            vmem((dp_size, 2 * n_last, plane * per_home, 128), bf16),
            vmem((plane, 2 * n_last, per_home, 128), f32),
            vmem((8, 128), f32),
            vmem((chips + lon_size + dp_size,) + vecs.shape, f32),
            vmem((3,) + vecs.shape, f32),
            pltpu.SemaphoreType.DMA((count,)),
            pltpu.SemaphoreType.DMA((count,)),
            pltpu.SemaphoreType.DMA((3,)),
        ],
        compiler_params=pltpu.CompilerParams(
            collective_id=1, has_side_effects=True, vmem_limit_bytes=40 * 1024 * 1024
        ),
        name="reduce",
    )(grads, vecs, quads, homes)


def adam_kernel(steps_ref, buckets_ref, marks, grads_ref, master_ref, one_ref, two_ref, new_master, new_one, new_two):
    homes = master_ref.shape[0]
    tiles = master_ref.shape[1] // 128
    steps = jnp.full((homes, 128), steps_ref[0], jnp.int32).astype(f32)
    fix_one = 1.0 / (1.0 - jnp.exp(steps * math.log(beta_one)))
    fix_two = 1.0 / (1.0 - jnp.exp(steps * math.log(beta_two)))
    base = jnp.concatenate(
        [jnp.full((1, 128), buckets_ref[home], jnp.int32) for home in range(homes)], axis=0
    ) + lax.broadcasted_iota(jnp.int32, (homes, 128), 1)
    rates = [2.6 / math.sqrt(D), 8.0 / math.sqrt(D), 2.6 / math.sqrt(D), 4.0 / math.sqrt(D), 2.0 / math.sqrt(D), 3.0 / math.sqrt(FF), 1.0, 0.6]
    for tile in range(tiles):
        columns = slice(128 * tile, 128 * (tile + 1))
        index = base + 128 * tile
        rate = jnp.full((homes, 128), 0.1, f32)
        for number in range(7, -1, -1):
            rate = jnp.where(index < marks[number + 1], rates[number], rate)
        grad = grads_ref[tile]
        weights = master_ref[:, columns]
        first = beta_one * one_ref[:, columns] + (1.0 - beta_one) * grad
        second = beta_two * two_ref[:, columns] + (1.0 - beta_two) * grad * grad
        step = first * fix_one / (jnp.sqrt(second * fix_two) + eps_adam) + decay_rate * weights
        new_master[:, columns] = weights - rate * step
        new_one[:, columns] = first
        new_two[:, columns] = second


def adam_call(steps, bases, marks, grads, master, one, two):
    smem = pl.BlockSpec(memory_space=pltpu.SMEM)
    vmem = pl.BlockSpec(memory_space=pltpu.VMEM)

    def body(steps_ref, bases_ref, *refs):
        adam_kernel(steps_ref, bases_ref, marks, *refs)

    return pl.pallas_call(
        body,
        out_shape=[jax.ShapeDtypeStruct(master.shape, f32)] * 3,
        in_specs=[smem, smem, vmem, vmem, vmem, vmem],
        out_specs=[vmem] * 3,
        name="adam",
    )(steps, bases, grads, master, one, two)


def quads_out(block):
    slots, levels = block.shape[:2]
    split = block.reshape(slots * levels, 2, HALF_LAT, 2, HALF_LON, D)
    return split.transpose(1, 3, 2, 4, 0, 5)[::-1, ::-1].reshape(4, -1, D)


def quads_back(quads, slots, levels):
    split = quads.reshape(2, 2, HALF_LAT, HALF_LON, slots * levels, D)[::-1, ::-1]
    return split.transpose(4, 0, 2, 1, 3, 5).reshape(slots, levels, WIN_LAT, WIN_LON, D)


def per_device(
    inputs, cotangent, lead_counts, home_slots, master, moment_one, moment_two, step_count
):
    slots_here = inputs.shape[0]
    levels = inputs.shape[1]
    lat_size = lax.axis_size("lat")
    segment_marks = offsets(lat_size + 1)
    dp_size, lon_size = lax.axis_size("dp"), lax.axis_size("lon")
    sizes = (dp_size, lat_size, lon_size)
    slots_mine, bucket_width = master.shape
    bucket_total = home_slots.shape[0]
    tiles = bucket_width // 128
    tiles_up = -(-tiles // 16) * 16
    own = jnp.pad(
        master.reshape(slots_mine, tiles, 128), ((0, 0), (0, tiles_up - tiles), (0, 0))
    ).astype(bf16)
    copies, tok = gather_call(own, quads_out(inputs), sizes)
    home_device = home_slots // slots_mine
    home_lon = home_device % lon_size
    home_lat = home_device // lon_size % lat_size
    chips = lat_size // 2
    home_unit = jnp.where(
        home_lat % 2 == 0, home_lon * chips + home_lat // 2, home_lat // 2 * lon_size + home_lon
    )
    home_place = (home_device // (lon_size * lat_size) * 2 + home_lat % 2) * (chips * lon_size)
    home_place = (home_place + home_unit) * slots_mine + home_slots % slots_mine
    unit = 4 * chips * lon_size
    rows_up = -(-tiles // unit) * unit
    out_tok, grad_rows, dvec = block_call(
        home_place,
        lead_counts,
        tok,
        quads_out(cotangent),
        copies.reshape(-1, tiles_up, 128),
        tiles,
        rows_up,
        lat_size,
        slots_here,
    )
    my_grads, grad_vectors, tok_back = reduce_call(
        grad_rows, dvec, out_tok, home_slots[None, :], slots_mine, sizes
    )
    device_place = lax.axis_index(("dp", "lat", "lon"))
    slot_ids = device_place * slots_mine + jnp.arange(slots_mine, dtype=jnp.int32)
    owner_match = home_slots[None, :] == slot_ids[:, None]
    bucket_ids = jnp.sum(
        jnp.where(owner_match, jnp.arange(bucket_total, dtype=jnp.int32)[None, :], 0), axis=1
    )
    present = jnp.any(owner_match, axis=1)
    bases = jnp.where(present, bucket_ids * bucket_width, segment_marks[8])
    new_master, new_one, new_two = adam_call(
        step_count, bases, segment_marks, my_grads, master, moment_one, moment_two
    )
    result = quads_back(tok_back[:, 0], slots_here, levels)
    grad_inputs = quads_back(tok_back[:, 1], slots_here, levels).astype(f32)
    return (result, grad_inputs, grad_vectors + 0.0, new_master, new_one, new_two)


def solution(mesh):
    in_specs = (
        P("dp", None, "lat", "lon", None),
        P("dp", None, "lat", "lon", None),
        P(),
        P(),
        P(("dp", "lat", "lon"), None),
        P(("dp", "lat", "lon"), None),
        P(("dp", "lat", "lon"), None),
        P(),
    )
    out_specs = (
        P("dp", None, "lat", "lon", None),
        P("dp", None, "lat", "lon", None),
        P(),
        P(("dp", "lat", "lon"), None),
        P(("dp", "lat", "lon"), None),
        P(("dp", "lat", "lon"), None),
    )
    return jax.shard_map(
        per_device, mesh=mesh, in_specs=in_specs, out_specs=out_specs, check_vma=False
    )
```

```python
import functools
import math

import jax
import jax.numpy as jnp
import ml_dtypes
import numpy as np
from jax import lax
from jax.experimental import pallas as pl
from jax.experimental.pallas import tpu as pltpu
from jax.sharding import PartitionSpec as P

D = 192
FF = 768
HEADS = 6
HEAD_DIM = 32
LEVELS = 8
WIN_LAT = 6
WIN_LON = 12
LEADS = 4
HALF_LAT = WIN_LAT // 2
HALF_LON = WIN_LON // 2
QUAD = HALF_LAT * HALF_LON
AREA = WIN_LAT * WIN_LON
LANES = HEADS * AREA
WIDE = 256
SCALE = 1.0 / math.sqrt(HEAD_DIM)

beta_one = 0.6
beta_two = 0.45
eps_norm = 1e-05
eps_adam = 1e-08
decay_rate = 0.1
penalty_value = -1000000000.0
bf16 = jnp.bfloat16
f32 = jnp.float32


def offsets(groups):
    sizes_list = [
        3 * D * D,
        D * D,
        3 * D * D,
        D * D,
        D * FF,
        FF * D,
        groups * HEADS * WIN_LAT * WIN_LAT * (2 * WIN_LON - 1),
        9 * D,
    ]
    segment_marks = [0]
    for amount in sizes_list:
        segment_marks.append(segment_marks[-1] + amount)
    return segment_marks


def nn(left, right):
    return jnp.dot(left, right, preferred_element_type=f32)


def nt(left, right):
    return lax.dot_general(left, right, (((1,), (1,)), ((), ())), preferred_element_type=f32)


def tn(left, right):
    return lax.dot_general(left, right, (((0,), (0,)), ((), ())), preferred_element_type=f32)


def normed(values):
    center = values - jnp.sum(values, axis=-1, keepdims=True) * (1.0 / D)
    spread = jnp.sum(center * center, axis=-1, keepdims=True) * (1.0 / D)
    inverse = lax.rsqrt(spread + eps_norm)
    return center * inverse, inverse


def norm_back(grad, hat, inverse, gain):
    scaled = grad * gain
    mean_one = jnp.sum(scaled, axis=-1, keepdims=True) * (1.0 / D)
    mean_two = jnp.sum(scaled * hat, axis=-1, keepdims=True) * (1.0 / D)
    return inverse * (scaled - mean_one - hat * mean_two)


def row_fold(values):
    return jnp.sum(values.reshape(values.shape[0] // 8, 8, values.shape[1]), axis=0)


def head_masks(dtype):
    lane = lax.broadcasted_iota(jnp.int32, (1, WIDE), 1) // HEAD_DIM
    return [jnp.where(lane == head, 1.0, 0.0).astype(dtype) for head in range(HEADS)]


def spread_heads(values, masks):
    return jnp.concatenate([values * mask for mask in masks], axis=0)


def fold_heads(big, count):
    parts = [big[head * count : (head + 1) * count] for head in range(HEADS)]
    lane = lax.broadcasted_iota(jnp.int32, (count, 128), 1)
    low = parts[3][:, :128]
    for head in (2, 1, 0):
        low = jnp.where(lane < HEAD_DIM * (head + 1), parts[head][:, :128], low)
    high = jnp.where(lane < HEAD_DIM, parts[4][:, 128:], parts[5][:, 128:])
    return jnp.concatenate([low, high], axis=1)


def rounded(values):
    return values.astype(bf16).astype(f32)


def soft_columns(scores):
    exps = jnp.exp(scores - jnp.max(scores, axis=0, keepdims=True))
    return exps * (1.0 / jnp.sum(exps, axis=0, keepdims=True))


def soft_back(probs, slopes):
    return probs * (slopes - jnp.sum(probs * slopes, axis=0, keepdims=True))


GROUP = 64
GLANES = HEADS * GROUP
CHUNK = 288


def lanes_of(ref, start):
    row, lane = divmod(start, 128)
    here = ref[row : row + 1, :]
    if lane == 0:
        return here
    place = lax.broadcasted_iota(jnp.int32, (1, 128), 1)
    mixed = jnp.where(place >= lane, here, ref[row + 1 : row + 2, :])
    return pltpu.roll(mixed, 128 - lane, 1)


def tail_head(tail, head):
    place = lax.broadcasted_iota(jnp.int32, tail.shape, 1)
    return pltpu.roll(jnp.where(place >= 64, tail, head), 64, 1)


def head_head(first, second):
    place = lax.broadcasted_iota(jnp.int32, first.shape, 1)
    return jnp.where(place < 64, first, pltpu.roll(second, 64, 1))


def only_head(values):
    place = lax.broadcasted_iota(jnp.int32, values.shape, 1)
    return jnp.where(place < 64, values, 0.0)


def only_tail(values):
    place = lax.broadcasted_iota(jnp.int32, values.shape, 1)
    return pltpu.roll(jnp.where(place >= 64, values, 0.0), 64, 1)


EARTH_ROW = WIN_LAT * (2 * WIN_LON - 1)
EARTH_ROWS = HEADS * WIN_LAT


def earth_tables():
    entry = np.zeros((WIN_LON, AREA, 256), np.float32)
    place = np.zeros((WIN_LON, 40, LANES), np.float32)
    for column in range(WIN_LON):
        side, inner = divmod(column, HALF_LON)
        for key in range(AREA):
            key_up, rest = divmod(key, 2 * QUAD)
            key_side, rest = divmod(rest, QUAD)
            key_row, key_inner = divmod(rest, HALF_LON)
            row = key_up * HALF_LAT + key_row
            offset = column - (key_side * HALF_LON + key_inner) + WIN_LON - 1
            entry[column, key, row * (2 * WIN_LON - 1) + offset] = 1.0
        for head in range(HEADS):
            for row in range(WIN_LAT):
                up, low = divmod(row, HALF_LAT)
                lane = AREA * head + 2 * QUAD * up + QUAD * side + HALF_LON * low + inner
                place[column, head * WIN_LAT + row, lane] = 1.0
    return entry.astype(ml_dtypes.bfloat16), place.astype(ml_dtypes.bfloat16)


MESH = pl.DeviceIdType.MESH


def places():
    lat_size, lon_size, dp_size = lax.axis_size("lat"), lax.axis_size("lon"), lax.axis_size("dp")
    return (
        lax.axis_index("dp"),
        lax.axis_index("lat"),
        lax.axis_index("lon"),
        dp_size,
        lat_size,
        lon_size,
    )


def greet(targets):
    barrier = pltpu.get_barrier_semaphore()
    for target in targets:
        pl.semaphore_signal(barrier, inc=1, device_id=target, device_id_type=MESH)
    pl.semaphore_wait(barrier, len(targets))


def around(place, step, size):
    return lax.rem(place + step, size)


def neighbours(whole_plane):
    dp, lat, lon, dp_size, lat_size, lon_size = places()
    if whole_plane:
        steps = {(i, j) for i in range(lat_size) for j in range(lon_size)}
    else:
        steps = {(1, 0), (lat_size - 1, 0), (1, 1 % lon_size), (lat_size - 1, lon_size - 1)}
        steps |= {(2 * i, 0) for i in range(1, lat_size // 2)} | {(0, j) for j in range(lon_size)}
    steps.discard((0, 0))
    found = [(around(dp, step, dp_size), lat, lon) for step in range(1, dp_size)]
    return found + [
        (dp, around(lat, i, lat_size), around(lon, j, lon_size)) for i, j in sorted(steps)
    ]


def pairing(src, dst, sends, receives, send_slot, receive_slot, target):
    return pltpu.make_async_remote_copy(
        src_ref=src,
        dst_ref=dst,
        send_sem=sends.at[send_slot],
        recv_sem=receives.at[receive_slot],
        device_id=target,
        device_id_type=MESH,
    )


def gather_slots(sizes, splits):
    dp_size, lat_size, lon_size = sizes
    return splits * dp_size * (2 * max(lat_size // 2, lon_size) + 2)


def gather_steps(sizes, own_ref, all_ref, sends, receives, keep_sem):
    splits, skew = SPLITS, SKEW
    dp_size, lat_size, lon_size = sizes
    chips = lat_size // 2
    dp, lat, lon = lax.axis_index("dp"), lax.axis_index("lat"), lax.axis_index("lon")
    chip = lat // 2
    wide = max(chips, lon_size)
    first = splits * dp_size
    second = first + splits * dp_size * wide
    cross = second + splits * dp_size * wide
    per = own_ref.shape[0] // splits
    order = sorted(range(dp_size), key=lambda step: min(step, dp_size - step))
    items = [(part, 0) for part in range(splits)]
    items += [(part, step) for part in range(splits) for step in order[1:]]

    def chip_at(step):
        return (dp, around(chip, step, chips) * 2 + lax.rem(lat, 2), lon)

    def lon_at(step):
        return (dp, lat, around(lon, step, lon_size))

    units = chips * lon_size

    def stretch(part, step, side, first, size):
        start = ((part * dp_size + around(dp, step, dp_size)) * 2 + side) * units + first
        return all_ref.at[pl.ds(start * per, size * per)]

    def run(mine, early_hook, late_hook):
        unit = lon * chips + chip if mine == 0 else chip * lon_size + lon
        one, two = (chips, lon_size) if mine == 0 else (lon_size, chips)
        one_at, two_at = (chip_at, lon_at) if mine == 0 else (lon_at, chip_at)
        place_two = lon if mine == 0 else chip
        partner = (dp, chip * 2 + 1 - mine, lon)
        begun = []

        def send(src, dst, slot, back, target):
            copy = pairing(src, dst, sends, receives, slot, back, target)
            copy.start()
            begun.append(copy)

        def arrive(dst, slot):
            pairing(dst, dst, sends, receives, slot, slot, partner).wait_recv()

        def own_part(part):
            return own_ref.at[pl.ds(part * per, per)]

        def chunk(part, step):
            return stretch(part, step, mine, unit, 1)

        def group(part, step):
            return stretch(part, step, mine, place_two * one, one)

        def whole(part, step, side):
            return stretch(part, step, side, 0, units)

        keeps = []
        for part in range(splits):
            keep = pltpu.make_async_copy(own_part(part), chunk(part, 0), keep_sem.at[part])
            keep.start()
            keeps.append(keep)

        def line(part):
            for step in order[1:]:
                target = (around(dp, step, dp_size), lat, lon)
                base = part * dp_size
                send(own_part(part), chunk(part, 0), base + step, base + dp_size - step, target)

        def stage_one(part, step):
            if step:
                arrive(chunk(part, step), part * dp_size + step)
            base = first + (part * dp_size + step) * wide
            src = chunk(part, step) if step else own_part(part)
            for far in range(1, one):
                send(src, chunk(part, step), base + far, base + one - far, one_at(far))

        def stage_two(part, step):
            base = first + (part * dp_size + step) * wide
            for far in range(1, one):
                arrive(chunk(part, step), base + far)
            if step == 0:
                keeps[part].wait()
            base = second + (part * dp_size + step) * wide
            for far in range(1, two):
                send(group(part, step), group(part, step), base + far, base + two - far, two_at(far))

        def stage_three(part, step):
            base = second + (part * dp_size + step) * wide
            for far in range(1, two):
                arrive(group(part, step), base + far)
            slot = cross + part * dp_size + step
            send(whole(part, step, mine), whole(part, step, mine), slot, slot, partner)

        for part in range(splits):
            line(part)
        for turn in range(len(items) + 2 * skew):
            for stage, place in ((stage_one, turn), (stage_two, turn - skew), (stage_three, turn - 2 * skew)):
                if 0 <= place < len(items):
                    stage(*items[place])
            if turn == 0:
                early_hook()
        late_hook()
        for part, step in items:
            arrive(whole(part, step, 1 - mine), cross + part * dp_size + step)
        for copy in begun:
            copy.wait_send()

    return run


def move_slots(sizes):
    dp_size, lat_size, lon_size = sizes
    spread = lat_size // 2 * lon_size
    moves = gather_slots(sizes, SPLITS)
    early = moves + 16
    late = early + 1 + spread + 2 * dp_size
    vectors = late + 1 + spread + 2 * dp_size
    hand = vectors + 1 + spread + dp_size
    return moves, early, late, vectors, hand, hand + lat_size * lon_size


SPLITS = 2
SKEW = 3


def block_kernel(
    shape_info,
    inside,
    home_ref,
    lead_ref,
    own_ref,
    quads_ref,
    entry_ref,
    place_ref,
    early_home_ref,
    late_home_ref,
    back_ref,
    grads_ref,
    total_ref,
    all_ref,
    tok_ref,
    res_ref,
    flat_ref,
    mid_ref,
    earth_ref,
    gate_ref,
    bias_ref,
    dbias_ref,
    w1_ref,
    o1_ref,
    w2_ref,
    o2_ref,
    up_ref,
    down_ref,
    vec_ref,
    n1_ref,
    hat1_ref,
    inv1_ref,
    qkv_ref,
    probs_ref,
    att_ref,
    att1_ref,
    tok1_ref,
    n2_ref,
    hat2_ref,
    inv2_ref,
    mix2_ref,
    cprobs_ref,
    att2_ref,
    n3_ref,
    act_ref,
    gh_ref,
    delta3_ref,
    delta2_ref,
    delta1_ref,
    gmid_ref,
    glow_ref,
    gatt2_ref,
    gm2_ref,
    gm1_ref,
    vacc_ref,
    sends,
    receives,
    keeps,
    *sum_refs,
):
    tokens = 4 * tok_ref.shape[2]
    count = tokens // AREA
    chunks = 4
    sizes, buckets, tiles, slots_here, early_span = shape_info
    dp_size, lat_size, lon_size = sizes
    chips = lat_size // 2
    spread = chips * lon_size
    dp, lat, lon = lax.axis_index("dp"), lax.axis_index("lat"), lax.axis_index("lon")
    core, chip = lax.rem(lat, 2), lat // 2
    is_last = lat == lat_size - 1
    moves, early_slots, late_slots, vector_slots, hand_slots, _ = move_slots(sizes)
    begun = []

    def send(src, dst, slot, back, target):
        copy = pairing(src, dst, sends, receives, slot, back, target)
        copy.start()
        begun.append(copy)

    def arrive(dst, slot):
        pairing(dst, dst, sends, receives, slot, slot, (dp, lat, lon)).wait_recv()

    def shift(kind, way, src, dst):
        for quad in range(1, 4):
            up, left = quad // 2, quad % 2
            target = (
                dp,
                around(lat, way * up % lat_size, lat_size),
                around(lon, way * left % lon_size, lon_size),
            )
            slot = moves + 4 * kind + quad
            send(src.at[quad, kind % 2], dst.at[quad, kind % 2], slot, slot, target)

    def shifted(kind, dst):
        for quad in range(1, 4):
            arrive(dst.at[quad, kind % 2], moves + 4 * kind + quad)

    def part(index):
        return pl.ds(pl.multiple_of(index * CHUNK, CHUNK), CHUNK)

    greet(neighbours(inside))
    keep_tokens = pltpu.make_async_copy(quads_ref.at[0], tok_ref.at[0], keeps.at[SPLITS])
    keep_tokens.start()

    def center_tokens():
        keep_tokens.wait()
        shifted(0, tok_ref)

        @pl.loop(0, chunks)
        def _(c):
            rows = part(c)
            hat, inverse = normed(tok_ref[c, 0].astype(f32))
            hat1_ref[rows, :] = hat
            inv1_ref[rows, :] = jnp.broadcast_to(inverse, (CHUNK, 128))

    gather = gather_steps(sizes, own_ref, all_ref, sends, receives, keeps)
    shift_first = functools.partial(shift, 0, -1, quads_ref, tok_ref)
    for mine in range(2):

        @pl.when(core == mine)
        def _():
            gather(mine, shift_first, center_tokens)
            for copy in begun:
                copy.wait_send()
            begun.clear()

    shift(1, -1, quads_ref, tok_ref)
    vacc_ref[...] = jnp.zeros_like(vacc_ref)
    marks = offsets(lat_size + 1)
    row_marks = [mark // 128 for mark in marks]

    for bucket in range(buckets):
        block = all_ref[home_ref[bucket]].astype(f32)
        flat_ref[tiles * bucket : tiles * (bucket + 1), :] = block[:tiles]

    def take_pairs(base, parts, pairs):
        return [flat_ref[pl.ds(base + part, pairs, stride=parts), :] for part in range(parts)]

    def give_pairs(columns, rows, evens, odds):
        for column, (even, odd) in enumerate(zip(evens, odds)):
            mid_ref[column, pl.ds(0, rows // 2, stride=2), :] = even
            mid_ref[column, pl.ds(1, rows // 2, stride=2), :] = odd

    def load_qkv(base, ref):
        b = take_pairs(base, 9, D // 2)
        evens = [b[0], only_head(b[1]), tail_head(b[1], b[2]), only_tail(b[2]), b[3], only_head(b[4])]
        odds = [tail_head(b[4], b[5]), only_tail(b[5]), b[6], only_head(b[7]), tail_head(b[7], b[8]), only_tail(b[8])]
        give_pairs(6, D, evens, odds)
        for column in range(6):
            ref[:, 128 * column : 128 * (column + 1)] = mid_ref[column, pl.ds(0, D), :].astype(bf16)

    def load_square(base, rows, ref):
        b = take_pairs(base, 3, rows // 2)
        give_pairs(2, rows, [b[0], b[1]], [tail_head(b[1], b[2]), only_tail(b[2])])
        ref[0:rows, 0:128] = mid_ref[0, pl.ds(0, rows), :].astype(bf16)
        ref[0:rows, 128:D] = mid_ref[1, pl.ds(0, rows), :][:, : D - 128].astype(bf16)

    load_qkv(row_marks[0], w1_ref)
    load_square(row_marks[1], D, o1_ref)
    load_qkv(row_marks[2], w2_ref)
    load_square(row_marks[3], D, o2_ref)
    for ref in (o1_ref, o2_ref):
        ref[D:WIDE, :] = jnp.zeros((WIDE - D, D), bf16)
    for column in range(6):
        up_ref[:, 128 * column : 128 * (column + 1)] = flat_ref[
            pl.ds(row_marks[4] + column, D, stride=6), :
        ].astype(bf16)
    load_square(row_marks[5], FF, down_ref)
    for index in range(9):
        start = marks[7] + D * index
        vec_ref[index : index + 1, 0:128] = lanes_of(flat_ref, start)
        vec_ref[index : index + 1, 128:D] = lanes_of(flat_ref, start + 128)[:, : D - 128]

    def earth_places():
        group_one = lat + 1
        group_two = jnp.where(is_last, 0, lat + 1)
        for index in range(EARTH_ROWS):
            group = group_one if index % WIN_LAT < HALF_LAT else group_two
            start = marks[6] + EARTH_ROW * (EARTH_ROWS * group + index)
            row = start // 128
            yield index, row, start - 128 * row

    lane_place = lax.broadcasted_iota(jnp.int32, (1, 128), 1)
    earth_ref[...] = jnp.zeros_like(earth_ref)
    for index, row, lane in earth_places():
        rows = [flat_ref[pl.ds(row + step, 1), :] for step in range(3)]
        back = lax.rem(128 - lane, 128)
        first = pltpu.roll(jnp.where(lane_place >= lane, rows[0], rows[1]), back, 1)
        second = pltpu.roll(jnp.where(lane_place >= lane, rows[1], rows[2]), back, 1)
        earth_ref[index : index + 1, 0:128] = first
        earth_ref[index : index + 1, 128:256] = jnp.where(lane_place < EARTH_ROW - 128, second, 0.0)
    earth = earth_ref[...].astype(bf16)
    key_up = lax.broadcasted_iota(jnp.int32, (AREA, LANES), 0) // (2 * QUAD)
    query_up = lax.rem(lax.broadcasted_iota(jnp.int32, (AREA, LANES), 1), AREA) // (2 * QUAD)
    bias = jnp.where((key_up != query_up) & is_last, penalty_value, 0.0)
    for column in range(WIN_LON):
        bias = bias + nn(nt(entry_ref[column], earth).astype(bf16), place_ref[column])
    bias_ref[...] = bias

    for slot in range(slots_here):
        number = lax.axis_index("dp") * slots_here + slot
        live = lax.rem(number, LEADS) < lead_ref[number // LEADS]
        size = count // slots_here
        gate_ref[slot * size : (slot + 1) * size, :] = jnp.full((size, D), jnp.where(live, 1.0, 0.0), f32)

    def vec(index):
        return vec_ref[index : index + 1, :]

    def gate_rows():
        gate = gate_ref[...]
        return jnp.broadcast_to(gate[None], (CHUNK // count, count, D)).reshape(CHUNK, D)

    def note(index, values):
        vacc_ref[index] += row_fold(values)

    @pl.loop(0, chunks)
    def _(c):
        rows = part(c)
        low = (hat1_ref[rows, :] * vec(0) + vec(1)).astype(bf16)
        n1_ref[rows, :] = low
        mixed = rounded(nn(low, w1_ref[...]))
        for tile in range(6):
            qkv_ref[tile, rows, :] = mixed[:, 128 * tile : 128 * (tile + 1)]

    def window(ref, first, s):
        rows = pl.ds(s, AREA, stride=count)
        return jnp.concatenate([ref[first, rows, :], ref[first + 1, rows, :]], axis=1)

    def window_store(ref, first, s, values):
        rows = pl.ds(s, AREA, stride=count)
        ref[first, rows, :] = values[:, :128]
        ref[first + 1, rows, :] = values[:, 128:]

    @pl.loop(0, count // 4)
    def _(block):
        masks = head_masks(f32)
        places = [block * 4 + step for step in range(4)]
        reads = [[window(qkv_ref, 2 * kind, s) for kind in range(3)] for s in places]
        raw = [
            nt(key.astype(bf16), spread_heads(query, masks).astype(bf16)) for query, key, _ in reads
        ]
        probs = [soft_columns(scores * SCALE + bias_ref[...]) for scores in raw]
        outs = [tn(prob.astype(bf16), read[2].astype(bf16)) for prob, read in zip(probs, reads)]
        for s, prob, out in zip(places, probs, outs):
            probs_ref[s] = prob
            window_store(att_ref, 0, s, fold_heads(out, AREA))

    @pl.loop(0, chunks)
    def _(c):
        rows = part(c)
        att = jnp.concatenate([att_ref[0, rows, :], att_ref[1, rows, :]], axis=1).astype(bf16)
        att1_ref[rows, :] = att
        branch = nn(att, o1_ref[...]) + vec(2)
        tok = tok_ref[c, 0].astype(f32) + gate_rows() * branch
        tok1_ref[rows, :] = tok
        hat, inverse = normed(tok)
        hat2_ref[rows, :] = hat
        inv2_ref[rows, :] = jnp.broadcast_to(inverse, (CHUNK, 128))
        low = (hat * vec(3) + vec(4)).astype(bf16)
        n2_ref[rows, :] = low
        mix2_ref[rows, :] = nn(low, w2_ref[...]).astype(bf16)

    def column_masks():
        lane = lax.broadcasted_iota(jnp.int32, (8, GLANES), 1)
        place = (lane % GROUP) // 8
        return [place == index for index in range(GROUP // 8)]

    def squeeze_column(values, masks):
        out = values[:8]
        for index in range(1, GROUP // 8):
            out = jnp.where(masks[index], values[8 * index : 8 * index + 8], out)
        return out

    def widen_column(values, masks):
        return jnp.concatenate([jnp.where(mask, values, 0.0) for mask in masks], axis=0).astype(bf16)

    def group_rows(g):
        return pl.ds(pl.multiple_of(g * GROUP, GROUP), GROUP)

    @pl.loop(0, tokens // GROUP // 6)
    def _(block):
        heads = head_masks(bf16)
        columns = column_masks()
        places = [block * 6 + step for step in range(6)]
        reads = [mix2_ref[group_rows(g), :] for g in places]
        raw = [
            nt(mixed[:, WIDE : 2 * WIDE], spread_heads(mixed[:, 0:WIDE], heads)) for mixed in reads
        ]
        probs = [soft_columns(squeeze_column(scores, columns) * SCALE) for scores in raw]
        outs = [
            tn(widen_column(prob, columns), mixed[:, 2 * WIDE :])
            for prob, mixed in zip(probs, reads)
        ]
        for g, prob, out in zip(places, probs, outs):
            cprobs_ref[g] = prob
            att2_ref[group_rows(g), :] = fold_heads(out, GROUP).astype(bf16)

    root = math.sqrt(2.0 / math.pi)
    shifted(1, tok_ref)

    @pl.loop(0, chunks)
    def _(c):
        rows = part(c)
        gate = gate_rows()
        tok = tok1_ref[rows, :] + gate * (nn(att2_ref[rows, :], o2_ref[...]) + vec(5))
        hat, inverse = normed(tok)
        low = (hat * vec(6) + vec(7)).astype(bf16)
        n3_ref[rows, :] = low
        hidden = nn(low, up_ref[...])
        square = hidden * hidden
        half = 0.5 * jnp.tanh(hidden * (root + (root * 0.044715) * square)) + 0.5
        wave = hidden * half
        act = wave.astype(bf16)
        act_ref[rows, :] = act
        res_ref[c, 0] = (tok + gate * (nn(act, down_ref[...]) + vec(8))).astype(bf16)
        slope = half + wave * (1.0 - half) * (2.0 * root + (6.0 * root * 0.044715) * square)
        after = tok_ref[c, 1].astype(f32)
        delta3 = (gate * after).astype(bf16)
        delta3_ref[rows, :] = delta3
        note(8, delta3.astype(f32))
        gh = (nt(delta3, down_ref[...]) * slope).astype(bf16)
        gh_ref[rows, :] = gh
        grad = nt(gh, up_ref[...])
        note(6, grad * hat)
        note(7, grad)
        mid = after + norm_back(grad, hat, inverse, vec(6))
        gmid_ref[rows, :] = mid
        delta2 = (gate * mid).astype(bf16)
        delta2_ref[rows, :] = delta2
        note(5, delta2.astype(f32))
        gatt2_ref[rows, :] = nt(delta2, o2_ref[...]).astype(bf16)

    shift(2, 1, res_ref, back_ref)

    @pl.loop(0, tokens // GROUP // 6)
    def _(block):
        heads = head_masks(bf16)
        columns = column_masks()
        places = [block * 6 + step for step in range(6)]
        reads = [
            (mix2_ref[group_rows(g), :], gatt2_ref[group_rows(g), :], cprobs_ref[g]) for g in places
        ]
        grads = [spread_heads(read[1], heads) for read in reads]
        raw = [nt(read[0][:, 2 * WIDE :], grad) for read, grad in zip(reads, grads)]
        dvalues = [nn(widen_column(read[2], columns), grad) for read, grad in zip(reads, grads)]
        lows = [
            widen_column(soft_back(read[2], squeeze_column(slopes, columns)), columns)
            for read, slopes in zip(reads, raw)
        ]
        dkeys = [
            nn(low, spread_heads(read[0][:, 0:WIDE], heads)) for read, low in zip(reads, lows)
        ]
        dqueries = [tn(low, read[0][:, WIDE : 2 * WIDE]) for read, low in zip(reads, lows)]
        for g, dquery, dkey, dvalue in zip(places, dqueries, dkeys, dvalues):
            rows = group_rows(g)
            gm2_ref[rows, 0:WIDE] = (fold_heads(dquery, GROUP) * SCALE).astype(bf16)
            gm2_ref[rows, WIDE : 2 * WIDE] = (dkey * SCALE).astype(bf16)
            gm2_ref[rows, 2 * WIDE : 3 * WIDE] = dvalue.astype(bf16)

    @pl.loop(0, chunks)
    def _(c):
        rows = part(c)
        grad = nt(gm2_ref[rows, :], w2_ref[...])
        hat = hat2_ref[rows, :]
        inverse = inv2_ref[rows, :][:, :1]
        note(3, grad * hat)
        note(4, grad)
        low = gmid_ref[rows, :] + norm_back(grad, hat, inverse, vec(3))
        glow_ref[rows, :] = low
        delta1 = (gate_rows() * low).astype(bf16)
        delta1_ref[rows, :] = delta1
        note(2, delta1.astype(f32))
        gatt = rounded(nt(delta1, o1_ref[...]))
        att_ref[0, rows, :] = gatt[:, :128]
        att_ref[1, rows, :] = gatt[:, 128:]

    def keep_pairs(base, parts, blocks):
        for number, block in enumerate(blocks):
            flat_ref[pl.ds(base + number, block.shape[0], stride=parts), :] = block

    def split_pairs(columns, rows):
        evens = [mid_ref[column, pl.ds(0, rows // 2, stride=2), :] for column in range(columns)]
        odds = [mid_ref[column, pl.ds(1, rows // 2, stride=2), :] for column in range(columns)]
        return evens, odds

    def save_qkv(base, grad):
        for column in range(6):
            mid_ref[column, pl.ds(0, D), :] = grad[:, 128 * column : 128 * (column + 1)]
        e, o = split_pairs(6, D)
        blocks = [
            e[0],
            head_head(e[1], e[2]),
            tail_head(e[2], e[3]),
            e[4],
            head_head(e[5], o[0]),
            tail_head(o[0], o[1]),
            o[2],
            head_head(o[3], o[4]),
            tail_head(o[4], o[5]),
        ]
        keep_pairs(base, 9, blocks)

    def save_square(base, rows, grad):
        mid_ref[0, pl.ds(0, rows), :] = grad[:rows, :128]
        mid_ref[1, pl.ds(0, rows), 0 : D - 128] = grad[:rows, 128:]
        e, o = split_pairs(2, rows)
        keep_pairs(base, 3, [e[0], head_head(e[1], o[0]), tail_head(o[0], o[1])])

    save_square(row_marks[1], D, tn(att1_ref[...], delta1_ref[...]))
    save_qkv(row_marks[2], tn(n2_ref[...], gm2_ref[...]))
    save_square(row_marks[3], D, tn(att2_ref[...], delta2_ref[...]))
    grad_up = tn(n3_ref[...], gh_ref[...])
    for column in range(6):
        flat_ref[pl.ds(row_marks[4] + column, D, stride=6), :] = grad_up[
            :, 128 * column : 128 * (column + 1)
        ]
    save_square(row_marks[5], FF, tn(act_ref[...], delta3_ref[...]))

    partner = (dp, chip * 2 + 1 - core, lon)
    place = chip * lon_size + lon

    def peers():
        for i in range(chips):
            for j in range(lon_size):
                if i or j:
                    back = (chips - i) % chips * lon_size + (lon_size - j) % lon_size
                    there = (around(chip, i, chips), around(lon, j, lon_size))
                    target = (dp, there[0] * 2 + core, there[1])
                    yield i * lon_size + j, back, there[0] * lon_size + there[1], target

    def line():
        for step in range(1, dp_size):
            there = around(dp, step, dp_size)
            yield step, dp_size - step, there, (there, lat, lon)

    def summing(base, grad, half_in, half, plane_in, mid, line_in, full):
        n_half = grad.shape[0] // 2
        n_place = n_half // spread
        n_line = n_place // dp_size

        def cross():
            send(grad.at[pl.ds((1 - core) * n_half, n_half)], half_in, base, base, partner)

        def plane():
            arrive(half_in, base)
            for first in range(0, n_half, 12):
                rows = pl.ds(first, 12)
                kept = grad[pl.ds(core * n_half + first, 12)].astype(f32)
                half[rows] = (kept + half_in[rows].astype(f32)).astype(bf16)
            for index, back, there, target in peers():
                send(
                    half.at[pl.ds(there * n_place, n_place)],
                    plane_in.at[back],
                    base + 1 + index,
                    base + 1 + back,
                    target,
                )

        def along():
            total = half[pl.ds(place * n_place, n_place)].astype(f32)
            for index in range(1, spread):
                arrive(plane_in.at[index], base + 1 + index)
                total = total + plane_in[index].astype(f32)
            mid[...] = total.astype(bf16)
            slots = base + 1 + spread
            for step, back, there, target in line():
                send(mid.at[pl.ds(there * n_line, n_line)], line_in.at[back], slots + step, slots + back, target)

        def share():
            slots = base + 1 + spread
            rows = pl.ds(dp * n_line, n_line)
            total = mid[rows].astype(f32)
            for step in range(1, dp_size):
                arrive(line_in.at[step], slots + step)
                total = total + line_in[step].astype(f32)
            full[rows] = total.astype(bf16)
            slots += dp_size
            for step, back, _, target in line():
                send(full.at[rows], full.at[rows], slots + step, slots + back, target)

        def done():
            slots = base + 1 + spread + dp_size
            for step, _, there, _ in line():
                arrive(full.at[pl.ds(there * n_line, n_line)], slots + step)

        return cross, plane, along, share, done

    bucket_low, bucket_high = early_span

    if inside:
        early_refs, late_refs = sum_refs[:7], sum_refs[7:14]
        hand_out, vec_sum, vec_in, vec_now = sum_refs[14:]
        early = summing(early_slots, *early_refs)
        late = summing(late_slots, *late_refs)

        def pack(grad, spans):
            for tile in range(grad.shape[0]):
                if tile < tiles:
                    rows = [
                        flat_ref[pl.ds(tile + tiles * first, last - first, stride=tiles), :]
                        for first, last in spans
                    ]
                    values = rows[0] if len(rows) == 1 else jnp.concatenate(rows, axis=0)
                    grad[tile] = values.astype(bf16)
                else:
                    grad[tile] = jnp.zeros(grad.shape[1:], bf16)

        pack(early_refs[0], [(bucket_low, bucket_high)])
        early[0]()
    else:
        (vec_sum,) = sum_refs

    dbias_ref[...] = jnp.zeros_like(dbias_ref)

    def window_back(block):
        masks = head_masks(f32)
        places = [block * 4 + step for step in range(4)]
        reads = [
            [window(qkv_ref, 2 * kind, s) for kind in range(3)]
            + [window(att_ref, 0, s), probs_ref[s]]
            for s in places
        ]
        grads = [spread_heads(read[3], masks).astype(bf16) for read in reads]
        raw = [nt(read[2].astype(bf16), grad) for read, grad in zip(reads, grads)]
        dvalues = [nn(read[4].astype(bf16), grad) for read, grad in zip(reads, grads)]
        lows = [soft_back(read[4], slopes).astype(bf16) for read, slopes in zip(reads, raw)]
        dkeys = [
            nn(low, spread_heads(read[0], masks).astype(bf16)) for read, low in zip(reads, lows)
        ]
        dqueries = [tn(low, read[1].astype(bf16)) for read, low in zip(reads, lows)]
        dbias_ref[...] += functools.reduce(jnp.add, [low.astype(f32) for low in lows])
        for s, dquery, dkey, dvalue in zip(places, dqueries, dkeys, dvalues):
            window_store(qkv_ref, 0, s, rounded(fold_heads(dquery, AREA) * SCALE))
            window_store(qkv_ref, 2, s, rounded(dkey * SCALE))
            window_store(qkv_ref, 4, s, rounded(dvalue))

    window_back(0)
    if inside:
        early[1]()

    @pl.loop(1, count // 4)
    def _(block):
        window_back(block)

    if inside:
        early[2]()

    @pl.loop(0, chunks)
    def _(c):
        rows = part(c)
        mixed = jnp.concatenate([qkv_ref[tile, rows, :] for tile in range(6)], axis=1).astype(bf16)
        gm1_ref[rows, :] = mixed
        grad = nt(mixed, w1_ref[...])
        hat = hat1_ref[rows, :]
        inverse = inv1_ref[rows, :][:, :1]
        note(0, grad * hat)
        note(1, grad)
        grad_in = glow_ref[rows, :] + norm_back(grad, hat, inverse, vec(0))
        res_ref[c, 1] = grad_in.astype(bf16)

    shift(3, 1, res_ref, back_ref)
    keep_back = pltpu.make_async_copy(res_ref.at[0], back_ref.at[0], keeps.at[SPLITS + 1 + 1])
    keep_back.start()
    if inside:
        early[3]()

    save_qkv(row_marks[0], tn(n1_ref[...], gm1_ref[...]))
    rest = flat_ref.shape[0] - row_marks[6]
    flat_ref[row_marks[6] :, :] = jnp.zeros((rest, 128), f32)
    dbias = dbias_ref[...]
    high = dbias.astype(bf16)
    both = jnp.concatenate([high, (dbias - high.astype(f32)).astype(bf16)], axis=0)
    dearth = jnp.zeros((40, 256), f32)
    for column in range(WIN_LON):
        moved = nt(both, place_ref[column]).astype(bf16)
        entry = entry_ref[column]
        dearth = dearth + tn(moved[:AREA], entry) + tn(moved[AREA:], entry)
    for index, row, lane in earth_places():
        first = pltpu.roll(dearth[index : index + 1, :128], lane, 1)
        second = pltpu.roll(dearth[index : index + 1, 128:], lane, 1)
        tail = lane_place >= lane
        for step, values in enumerate(
            (
                jnp.where(tail, first, 0.0),
                jnp.where(tail, second, first),
                jnp.where(tail, 0.0, second),
            )
        ):
            flat_ref[pl.ds(row + step, 1), :] += values
    for index in range(9):
        total = jnp.sum(vacc_ref[index], axis=0, keepdims=True)
        vec_sum[index : index + 1, :] = total
        start = marks[7] + D * index
        for values, size, begin in (
            (total[:, :128], 128, start),
            (jnp.concatenate([total[:, 128:], jnp.zeros((1, 256 - D), f32)], axis=1), D - 128, start + 128),
        ):
            row, lane = divmod(begin, 128)
            moved = pltpu.roll(values, lane, 1) if lane else values
            flat_ref[row : row + 1, :] += jnp.where(lane_place >= lane, moved, 0.0)
            if lane + size > 128:
                flat_ref[row + 1 : row + 2, :] += jnp.where(lane_place < lane, moved, 0.0)
    if inside:
        pack(late_refs[0], [(0, bucket_low), (bucket_high, buckets)])
        late[0]()
        send(vec_sum, vec_in.at[0], vector_slots, vector_slots, partner)
        late[1]()
        arrive(vec_in.at[0], vector_slots)
        vec_now[0] = vec_sum[...] + vec_in[0]
        for index, back, _, target in peers():
            send(vec_now.at[0], vec_in.at[back], vector_slots + 1 + index, vector_slots + 1 + back, target)
        late[2]()
        vec_total = vec_now[0]
        for index in range(1, spread):
            arrive(vec_in.at[index], vector_slots + 1 + index)
            vec_total = vec_total + vec_in[index]
        vec_now[1] = vec_total
        slots = vector_slots + 1 + spread
        for step, back, _, target in line():
            send(vec_now.at[1], vec_in.at[spread + back], slots + step, slots + back, target)
        late[3]()
        early[4]()
        for step in range(1, dp_size):
            arrive(vec_in.at[spread + step], slots + step)
            vec_total = vec_total + vec_in[spread + step]
        total_ref[...] = vec_total
        late[4]()
        homes = lat_size * lon_size
        per_home = grads_ref.shape[1]
        width = homes * per_home
        slot_ids = lax.broadcasted_iota(jnp.int32, (width, 1), 0) + dp * width
        early_pick = jnp.where(slot_ids == early_home_ref[...], 1.0, 0.0).astype(bf16)
        late_pick = jnp.where(slot_ids == late_home_ref[...], 1.0, 0.0).astype(bf16)
        for row in range(early_refs[6].shape[0]):
            owned = nn(early_pick, early_refs[6][row]) + nn(late_pick, late_refs[6][row])
            for home in range(homes):
                hand_out[home, row] = owned[per_home * home : per_home * (home + 1), :]
        n_rows = hand_out.shape[1]
        first = core * (n_rows * spread) + place * n_rows
        landing = grads_ref.at[pl.ds(first, n_rows)]
        me = lat * lon_size + lon
        keep_hand = pltpu.make_async_copy(hand_out.at[me], landing, keeps.at[SPLITS + 1])
        keep_hand.start()
        for i in range(lat_size):
            for j in range(lon_size):
                if i or j:
                    target = (dp, around(lat, i, lat_size), around(lon, j, lon_size))
                    back = (lat_size - i) % lat_size * lon_size + (lon_size - j) % lon_size
                    send(
                        hand_out.at[target[1] * lon_size + target[2]],
                        landing,
                        hand_slots + i * lon_size + j,
                        hand_slots + back,
                        target,
                    )
        keep_hand.wait()
        for index in range(1, homes):
            arrive(landing, hand_slots + index)
    else:
        total_ref[...] = vec_sum[...]
        for tile in range(tiles):
            grads_ref[tile] = flat_ref[pl.ds(tile, buckets, stride=tiles), :]
    shifted(2, back_ref)
    shifted(3, back_ref)
    keep_back.wait()
    for copy in begun:
        copy.wait_send()


def sum_rows(sizes, tiles):
    unit = sizes[0] * sizes[1] * sizes[2]
    rows = -(-tiles // unit) * unit
    return rows, rows <= 2 * tiles


def block_call(homes, leads, own, quads, places_in_all, tiles, sizes, slots_here):
    tokens = 4 * quads.shape[2]
    count = tokens // AREA
    buckets = homes.shape[0]
    per_home = own.shape[0]
    dp_size, lat_size, lon_size = sizes
    spread = lat_size // 2 * lon_size
    rows, inside = sum_rows(sizes, tiles)
    marks = offsets(lat_size + 1)
    width = tiles * 128
    low = -(-marks[1] // width)
    high = low + (marks[6] // width - low) // 16 * 16
    shape = jax.ShapeDtypeStruct
    outs = [
        shape(quads.shape, bf16),
        shape((rows, per_home, 128) if inside else (tiles, buckets, 128), f32),
        shape((9, D), f32),
    ]
    vmem = pltpu.VMEM
    scratch = [
        vmem((dp_size * lat_size * lon_size * per_home,) + own.shape[1:], bf16),
        vmem(quads.shape, bf16),
        vmem(quads.shape, bf16),
        vmem((buckets * tiles, 128), f32),
        vmem((6, FF, 128), f32),
        vmem((40, 256), f32),
        vmem((count, D), f32),
        vmem((AREA, LANES), f32),
        vmem((AREA, LANES), f32),
        vmem((D, 3 * WIDE), bf16),
        vmem((WIDE, D), bf16),
        vmem((D, 3 * WIDE), bf16),
        vmem((WIDE, D), bf16),
        vmem((D, FF), bf16),
        vmem((FF, D), bf16),
        vmem((16, D), f32),
        vmem((tokens, D), bf16),
        vmem((tokens, D), f32),
        vmem((tokens, 128), f32),
        vmem((6, tokens, 128), f32),
        vmem((count, AREA, LANES), f32),
        vmem((2, tokens, 128), f32),
        vmem((tokens, WIDE), bf16),
        vmem((tokens, D), f32),
        vmem((tokens, D), bf16),
        vmem((tokens, D), f32),
        vmem((tokens, 128), f32),
        vmem((tokens, 3 * WIDE), bf16),
        vmem((tokens // GROUP, 8, GLANES), f32),
        vmem((tokens, WIDE), bf16),
        vmem((tokens, D), bf16),
        vmem((tokens, FF), bf16),
        vmem((tokens, FF), bf16),
        vmem((tokens, D), bf16),
        vmem((tokens, D), bf16),
        vmem((tokens, D), bf16),
        vmem((tokens, D), f32),
        vmem((tokens, D), f32),
        vmem((tokens, WIDE), bf16),
        vmem((tokens, 3 * WIDE), bf16),
        vmem((tokens, 3 * WIDE), bf16),
        vmem((9, 8, D), f32),
        pltpu.SemaphoreType.DMA((move_slots(sizes)[-1],)),
        pltpu.SemaphoreType.DMA((move_slots(sizes)[-1],)),
        pltpu.SemaphoreType.DMA((SPLITS + 3,)),
    ]
    if inside:
        n_place = rows // 2 // spread
        for some in (high - low, buckets - (high - low)):
            scratch += [
                vmem((rows, some, 128), bf16),
                vmem((rows // 2, some, 128), bf16),
                vmem((rows // 2, some, 128), bf16),
                vmem((spread, n_place, some, 128), bf16),
                vmem((n_place, some, 128), bf16),
                vmem((dp_size, n_place // dp_size, some, 128), bf16),
                vmem((n_place, some, 128), bf16),
            ]
        scratch += [
            vmem((lat_size * lon_size, n_place, per_home, 128), f32),
            vmem((9, D), f32),
            vmem((spread + dp_size, 9, D), f32),
            vmem((2, 9, D), f32),
        ]
    else:
        scratch += [vmem((9, D), f32)]
    spec = pl.BlockSpec(memory_space=pltpu.VMEM)
    smem = pl.BlockSpec(memory_space=pltpu.SMEM)
    entry, place = earth_tables()
    return pl.pallas_call(
        functools.partial(block_kernel, (sizes, buckets, tiles, slots_here, (low, high)), inside),
        out_shape=outs,
        in_specs=[smem, smem, spec, pl.BlockSpec(memory_space=pl.ANY)] + [spec] * 4,
        out_specs=[spec] * len(outs),
        scratch_shapes=scratch,
        compiler_params=pltpu.CompilerParams(
            vmem_limit_bytes=62 * 1024 * 1024, collective_id=0, has_side_effects=True
        ),
        name="block",
    )(
        places_in_all,
        leads,
        own,
        quads,
        jnp.asarray(entry),
        jnp.asarray(place),
        homes[None, low:high],
        jnp.concatenate([homes[:low], homes[high:]])[None, :],
    )


def adam_kernel(steps_ref, buckets_ref, marks, grads_ref, master_ref, one_ref, two_ref, new_master, new_one, new_two):
    homes = master_ref.shape[0]
    tiles = master_ref.shape[1] // 128
    steps = jnp.full((homes, 128), steps_ref[0], jnp.int32).astype(f32)
    fix_one = 1.0 / (1.0 - jnp.exp(steps * math.log(beta_one)))
    fix_two = 1.0 / (1.0 - jnp.exp(steps * math.log(beta_two)))
    base = jnp.concatenate(
        [jnp.full((1, 128), buckets_ref[home], jnp.int32) for home in range(homes)], axis=0
    ) + lax.broadcasted_iota(jnp.int32, (homes, 128), 1)
    rates = [2.6 / math.sqrt(D), 8.0 / math.sqrt(D), 2.6 / math.sqrt(D), 4.0 / math.sqrt(D), 2.0 / math.sqrt(D), 3.0 / math.sqrt(FF), 1.0, 0.6]
    for tile in range(tiles):
        columns = slice(128 * tile, 128 * (tile + 1))
        index = base + 128 * tile
        rate = jnp.full((homes, 128), 0.1, f32)
        for number in range(7, -1, -1):
            rate = jnp.where(index < marks[number + 1], rates[number], rate)
        grad = grads_ref[tile]
        weights = master_ref[:, columns]
        first = beta_one * one_ref[:, columns] + (1.0 - beta_one) * grad
        second = beta_two * two_ref[:, columns] + (1.0 - beta_two) * grad * grad
        step = first * fix_one / (jnp.sqrt(second * fix_two) + eps_adam) + decay_rate * weights
        new_master[:, columns] = weights - rate * step
        new_one[:, columns] = first
        new_two[:, columns] = second


def adam_call(steps, bases, marks, grads, master, one, two):
    smem = pl.BlockSpec(memory_space=pltpu.SMEM)
    vmem = pl.BlockSpec(memory_space=pltpu.VMEM)

    def body(steps_ref, bases_ref, *refs):
        adam_kernel(steps_ref, bases_ref, marks, *refs)

    return pl.pallas_call(
        body,
        out_shape=[jax.ShapeDtypeStruct(master.shape, f32)] * 3,
        in_specs=[smem, smem, vmem, vmem, vmem, vmem],
        out_specs=[vmem] * 3,
        name="adam",
    )(steps, bases, grads, master, one, two)


def quads_out(block):
    slots, levels = block.shape[:2]
    split = block.reshape(slots * levels, 2, HALF_LAT, 2, HALF_LON, D)
    return split.transpose(1, 3, 2, 4, 0, 5)[::-1, ::-1].reshape(4, -1, D)


def quads_back(quads, slots, levels):
    split = quads.reshape(2, 2, HALF_LAT, HALF_LON, slots * levels, D)[::-1, ::-1]
    return split.transpose(4, 0, 2, 1, 3, 5).reshape(slots, levels, WIN_LAT, WIN_LON, D)


def per_device(
    inputs, cotangent, lead_counts, home_slots, master, moment_one, moment_two, step_count
):
    slots_here = inputs.shape[0]
    levels = inputs.shape[1]
    lat_size = lax.axis_size("lat")
    segment_marks = offsets(lat_size + 1)
    dp_size, lon_size = lax.axis_size("dp"), lax.axis_size("lon")
    sizes = (dp_size, lat_size, lon_size)
    slots_mine, bucket_width = master.shape
    bucket_total = home_slots.shape[0]
    tiles = bucket_width // 128
    tiles_up = -(-tiles // 16) * 16
    own = jnp.pad(
        master.reshape(slots_mine, tiles, 128), ((0, 0), (0, tiles_up - tiles), (0, 0))
    ).astype(bf16)
    home_device = home_slots // slots_mine
    home_lon = home_device % lon_size
    home_lat = home_device // lon_size % lat_size
    chips = lat_size // 2
    home_unit = jnp.where(
        home_lat % 2 == 0, home_lon * chips + home_lat // 2, home_lat // 2 * lon_size + home_lon
    )
    home_slot = home_slots % slots_mine
    per = slots_mine // SPLITS
    home_place = home_slot // per * dp_size + home_device // (lon_size * lat_size)
    home_place = (home_place * 2 + home_lat % 2) * (chips * lon_size) + home_unit
    home_place = home_place * per + home_slot % per
    quads = jnp.stack([quads_out(inputs), quads_out(cotangent)], axis=1)
    tok_back, grads, vectors = block_call(
        home_slots, lead_counts, own, quads, home_place, tiles, sizes, slots_here
    )
    axes = ("dp", "lat", "lon")
    if sum_rows(sizes, tiles)[1]:
        my_grads, grad_vectors = grads, vectors + 0.0
    else:
        spread = jnp.zeros((tiles, dp_size * lat_size * lon_size * slots_mine, 128), f32)
        spread = spread.at[:, home_slots].set(grads)
        my_grads = lax.psum_scatter(spread, axes, scatter_dimension=1, tiled=True)
        grad_vectors = lax.psum(vectors, axes)
    device_place = lax.axis_index(axes)
    slot_ids = device_place * slots_mine + jnp.arange(slots_mine, dtype=jnp.int32)
    owner_match = home_slots[None, :] == slot_ids[:, None]
    bucket_ids = jnp.sum(
        jnp.where(owner_match, jnp.arange(bucket_total, dtype=jnp.int32)[None, :], 0), axis=1
    )
    present = jnp.any(owner_match, axis=1)
    bases = jnp.where(present, bucket_ids * bucket_width, segment_marks[8])
    new_master, new_one, new_two = adam_call(
        step_count, bases, segment_marks, my_grads, master, moment_one, moment_two
    )
    result = quads_back(tok_back[:, 0], slots_here, levels)
    grad_inputs = quads_back(tok_back[:, 1], slots_here, levels).astype(f32)
    return (result, grad_inputs, grad_vectors, new_master, new_one, new_two)


def solution(mesh):
    in_specs = (
        P("dp", None, "lat", "lon", None),
        P("dp", None, "lat", "lon", None),
        P(),
        P(),
        P(("dp", "lat", "lon"), None),
        P(("dp", "lat", "lon"), None),
        P(("dp", "lat", "lon"), None),
        P(),
    )
    out_specs = (
        P("dp", None, "lat", "lon", None),
        P("dp", None, "lat", "lon", None),
        P(),
        P(("dp", "lat", "lon"), None),
        P(("dp", "lat", "lon"), None),
        P(("dp", "lat", "lon"), None),
    )
    return jax.shard_map(
        per_device, mesh=mesh, in_specs=in_specs, out_specs=out_specs, check_vma=False
    )
```

```python
import functools
import math

import jax
import jax.numpy as jnp
import ml_dtypes
import numpy as np
from jax import lax
from jax.experimental import pallas as pl
from jax.experimental.pallas import tpu as pltpu
from jax.sharding import PartitionSpec as P

D = 192
FF = 768
HEADS = 6
HEAD_DIM = 32
LEVELS = 8
WIN_LAT = 6
WIN_LON = 12
LEADS = 4
HALF_LAT = WIN_LAT // 2
HALF_LON = WIN_LON // 2
QUAD = HALF_LAT * HALF_LON
AREA = WIN_LAT * WIN_LON
LANES = HEADS * AREA
WIDE = 256
SCALE = 1.0 / math.sqrt(HEAD_DIM)

beta_one = 0.6
beta_two = 0.45
eps_norm = 1e-05
eps_adam = 1e-08
decay_rate = 0.1
penalty_value = -1000000000.0
bf16 = jnp.bfloat16
f32 = jnp.float32


def offsets(groups):
    sizes_list = [
        3 * D * D,
        D * D,
        3 * D * D,
        D * D,
        D * FF,
        FF * D,
        groups * HEADS * WIN_LAT * WIN_LAT * (2 * WIN_LON - 1),
        9 * D,
    ]
    segment_marks = [0]
    for amount in sizes_list:
        segment_marks.append(segment_marks[-1] + amount)
    return segment_marks


def nn(left, right):
    return jnp.dot(left, right, preferred_element_type=f32)


def nt(left, right):
    return lax.dot_general(left, right, (((1,), (1,)), ((), ())), preferred_element_type=f32)


def tn(left, right):
    return lax.dot_general(left, right, (((0,), (0,)), ((), ())), preferred_element_type=f32)


def normed(values):
    center = values - jnp.sum(values, axis=-1, keepdims=True) * (1.0 / D)
    spread = jnp.sum(center * center, axis=-1, keepdims=True) * (1.0 / D)
    inverse = lax.rsqrt(spread + eps_norm)
    return center * inverse, inverse


def norm_back(grad, hat, inverse, gain):
    scaled = grad * gain
    mean_one = jnp.sum(scaled, axis=-1, keepdims=True) * (1.0 / D)
    mean_two = jnp.sum(scaled * hat, axis=-1, keepdims=True) * (1.0 / D)
    return inverse * (scaled - mean_one - hat * mean_two)


def row_fold(values):
    return jnp.sum(values.reshape(values.shape[0] // 8, 8, values.shape[1]), axis=0)


def head_masks(dtype):
    lane = lax.broadcasted_iota(jnp.int32, (1, WIDE), 1) // HEAD_DIM
    return [jnp.where(lane == head, 1.0, 0.0).astype(dtype) for head in range(HEADS)]


def spread_heads(values, masks):
    return jnp.concatenate([values * mask for mask in masks], axis=0)


def fold_heads(big, count):
    parts = [big[head * count : (head + 1) * count] for head in range(HEADS)]
    lane = lax.broadcasted_iota(jnp.int32, (count, 128), 1)
    low = parts[3][:, :128]
    for head in (2, 1, 0):
        low = jnp.where(lane < HEAD_DIM * (head + 1), parts[head][:, :128], low)
    high = jnp.where(lane < HEAD_DIM, parts[4][:, 128:], parts[5][:, 128:])
    return jnp.concatenate([low, high], axis=1)


def rounded(values):
    return values.astype(bf16).astype(f32)


def soft_columns(scores):
    exps = jnp.exp(scores - jnp.max(scores, axis=0, keepdims=True))
    return exps * (1.0 / jnp.sum(exps, axis=0, keepdims=True))


def soft_back(probs, slopes):
    return probs * (slopes - jnp.sum(probs * slopes, axis=0, keepdims=True))


GROUP = 64
GLANES = HEADS * GROUP
CHUNK = 288


def lanes_of(ref, start):
    row, lane = divmod(start, 128)
    here = ref[row : row + 1, :]
    if lane == 0:
        return here
    place = lax.broadcasted_iota(jnp.int32, (1, 128), 1)
    mixed = jnp.where(place >= lane, here, ref[row + 1 : row + 2, :])
    return pltpu.roll(mixed, 128 - lane, 1)


def tail_head(tail, head):
    place = lax.broadcasted_iota(jnp.int32, tail.shape, 1)
    return pltpu.roll(jnp.where(place >= 64, tail, head), 64, 1)


def head_head(first, second):
    place = lax.broadcasted_iota(jnp.int32, first.shape, 1)
    return jnp.where(place < 64, first, pltpu.roll(second, 64, 1))


def only_head(values):
    place = lax.broadcasted_iota(jnp.int32, values.shape, 1)
    return jnp.where(place < 64, values, 0.0)


def only_tail(values):
    place = lax.broadcasted_iota(jnp.int32, values.shape, 1)
    return pltpu.roll(jnp.where(place >= 64, values, 0.0), 64, 1)


EARTH_ROW = WIN_LAT * (2 * WIN_LON - 1)
EARTH_ROWS = HEADS * WIN_LAT


def earth_tables():
    entry = np.zeros((WIN_LON, AREA, 256), np.float32)
    place = np.zeros((WIN_LON, 40, LANES), np.float32)
    for column in range(WIN_LON):
        side, inner = divmod(column, HALF_LON)
        for key in range(AREA):
            key_up, rest = divmod(key, 2 * QUAD)
            key_side, rest = divmod(rest, QUAD)
            key_row, key_inner = divmod(rest, HALF_LON)
            row = key_up * HALF_LAT + key_row
            offset = column - (key_side * HALF_LON + key_inner) + WIN_LON - 1
            entry[column, key, row * (2 * WIN_LON - 1) + offset] = 1.0
        for head in range(HEADS):
            for row in range(WIN_LAT):
                up, low = divmod(row, HALF_LAT)
                lane = AREA * head + 2 * QUAD * up + QUAD * side + HALF_LON * low + inner
                place[column, head * WIN_LAT + row, lane] = 1.0
    return entry.astype(ml_dtypes.bfloat16), place.astype(ml_dtypes.bfloat16)


MESH = pl.DeviceIdType.MESH


def places():
    lat_size, lon_size, dp_size = lax.axis_size("lat"), lax.axis_size("lon"), lax.axis_size("dp")
    return (
        lax.axis_index("dp"),
        lax.axis_index("lat"),
        lax.axis_index("lon"),
        dp_size,
        lat_size,
        lon_size,
    )


def greet(targets):
    barrier = pltpu.get_barrier_semaphore()
    for target in targets:
        pl.semaphore_signal(barrier, inc=1, device_id=target, device_id_type=MESH)


def greeted_wait(count):
    pl.semaphore_wait(pltpu.get_barrier_semaphore(), count)


def around(place, step, size):
    return lax.rem(place + step, size)


def neighbours(whole_plane):
    dp, lat, lon, dp_size, lat_size, lon_size = places()
    if whole_plane:
        steps = {(i, j) for i in range(lat_size) for j in range(lon_size)}
    else:
        steps = {(1, 0), (lat_size - 1, 0), (1, 1 % lon_size), (lat_size - 1, lon_size - 1)}
        steps |= {(2 * i, 0) for i in range(1, lat_size // 2)} | {(0, j) for j in range(lon_size)}
    steps.discard((0, 0))
    found = [(around(dp, step, dp_size), lat, lon) for step in range(1, dp_size)]
    return found + [
        (dp, around(lat, i, lat_size), around(lon, j, lon_size)) for i, j in sorted(steps)
    ]


def pairing(src, dst, sends, receives, send_slot, receive_slot, target):
    return pltpu.make_async_remote_copy(
        src_ref=src,
        dst_ref=dst,
        send_sem=sends.at[send_slot],
        recv_sem=receives.at[receive_slot],
        device_id=target,
        device_id_type=MESH,
    )


def gather_slots(sizes, splits):
    dp_size, lat_size, lon_size = sizes
    return splits * dp_size * (2 * max(lat_size // 2, lon_size) + 2)


def gather_steps(sizes, own_ref, all_ref, sends, receives, keep_sem):
    splits, skew = SPLITS, SKEW
    dp_size, lat_size, lon_size = sizes
    chips = lat_size // 2
    dp, lat, lon = lax.axis_index("dp"), lax.axis_index("lat"), lax.axis_index("lon")
    chip = lat // 2
    wide = max(chips, lon_size)
    first = splits * dp_size
    second = first + splits * dp_size * wide
    cross = second + splits * dp_size * wide
    per = own_ref.shape[0] // splits
    order = sorted(range(dp_size), key=lambda step: min(step, dp_size - step))
    items = [(part, 0) for part in range(splits)]
    items += [(part, step) for part in range(splits) for step in order[1:]]

    def chip_at(step):
        return (dp, around(chip, step, chips) * 2 + lax.rem(lat, 2), lon)

    def lon_at(step):
        return (dp, lat, around(lon, step, lon_size))

    units = chips * lon_size

    def stretch(part, step, side, first, size):
        start = ((part * dp_size + around(dp, step, dp_size)) * 2 + side) * units + first
        return all_ref.at[pl.ds(start * per, size * per)]

    def run(mine, hooks, late_hook):
        unit = lon * chips + chip if mine == 0 else chip * lon_size + lon
        one, two = (chips, lon_size) if mine == 0 else (lon_size, chips)
        one_at, two_at = (chip_at, lon_at) if mine == 0 else (lon_at, chip_at)
        place_two = lon if mine == 0 else chip
        partner = (dp, chip * 2 + 1 - mine, lon)
        begun = []

        def send(src, dst, slot, back, target):
            copy = pairing(src, dst, sends, receives, slot, back, target)
            copy.start()
            begun.append(copy)

        def arrive(dst, slot):
            pairing(dst, dst, sends, receives, slot, slot, partner).wait_recv()

        def own_part(part):
            return own_ref.at[pl.ds(part * per, per)]

        def chunk(part, step):
            return stretch(part, step, mine, unit, 1)

        def group(part, step):
            return stretch(part, step, mine, place_two * one, one)

        def whole(part, step, side):
            return stretch(part, step, side, 0, units)

        keeps = []
        for part in range(splits):
            keep = pltpu.make_async_copy(own_part(part), chunk(part, 0), keep_sem.at[part])
            keep.start()
            keeps.append(keep)

        def line(part):
            for step in order[1:]:
                target = (around(dp, step, dp_size), lat, lon)
                base = part * dp_size
                send(own_part(part), chunk(part, 0), base + step, base + dp_size - step, target)

        def stage_one(part, step):
            if step:
                arrive(chunk(part, step), part * dp_size + step)
            base = first + (part * dp_size + step) * wide
            src = chunk(part, step) if step else own_part(part)
            for far in range(1, one):
                send(src, chunk(part, step), base + far, base + one - far, one_at(far))

        def stage_two(part, step):
            base = first + (part * dp_size + step) * wide
            for far in range(1, one):
                arrive(chunk(part, step), base + far)
            if step == 0:
                keeps[part].wait()
            base = second + (part * dp_size + step) * wide
            for far in range(1, two):
                send(group(part, step), group(part, step), base + far, base + two - far, two_at(far))

        def stage_three(part, step):
            base = second + (part * dp_size + step) * wide
            for far in range(1, two):
                arrive(group(part, step), base + far)
            slot = cross + part * dp_size + step
            send(whole(part, step, mine), whole(part, step, mine), slot, slot, partner)

        for part in range(splits):
            line(part)
        for turn in range(len(items) + 2 * skew):
            for stage, place in ((stage_one, turn), (stage_two, turn - skew), (stage_three, turn - 2 * skew)):
                if 0 <= place < len(items):
                    stage(*items[place])
            if turn in hooks:
                hooks[turn]()
        late_hook()
        for part, step in items:
            arrive(whole(part, step, 1 - mine), cross + part * dp_size + step)
        for copy in begun:
            copy.wait_send()

    return run


def move_slots(sizes, slots):
    dp_size, lat_size, lon_size = sizes
    spread = lat_size // 2 * lon_size
    moves = gather_slots(sizes, SPLITS)
    early = moves + 16 * slots
    late = early + 1 + spread + 2 * dp_size
    vectors = late + 1 + spread + 2 * dp_size
    hand = vectors + 1 + spread + dp_size
    return moves, early, late, vectors, hand, hand + lat_size * lon_size


SPLITS = 2
SKEW = 3


def block_kernel(
    shape_info,
    inside,
    home_ref,
    lead_ref,
    homes_ref,
    master_ref,
    inputs_ref,
    cotangent_ref,
    entry_hbm,
    place_hbm,
    back_res_ref,
    back_in_ref,
    grads_ref,
    total_ref,
    spot_ref,
    weights_ref,
    entry_ref,
    place_ref,
    own_ref,
    all_ref,
    tok_ref,
    res_ref,
    flat_ref,
    mid_ref,
    earth_ref,
    gate_ref,
    bias_ref,
    dbias_ref,
    w1_ref,
    o1_ref,
    w2_ref,
    o2_ref,
    up_ref,
    down_ref,
    vec_ref,
    n1_ref,
    hat1_ref,
    inv1_ref,
    qkv_ref,
    probs_ref,
    att_ref,
    att1_ref,
    tok1_ref,
    n2_ref,
    hat2_ref,
    inv2_ref,
    mix2_ref,
    cprobs_ref,
    att2_ref,
    n3_ref,
    act_ref,
    gh_ref,
    delta3_ref,
    delta2_ref,
    delta1_ref,
    gmid_ref,
    glow_ref,
    gatt2_ref,
    gm2_ref,
    gm1_ref,
    vacc_ref,
    sends,
    receives,
    keeps,
    fetched,
    kept,
    *sum_refs,
):
    levels = tok_ref.shape[5]
    chunks = 4
    sizes, buckets, tiles, slots_here, early_span = shape_info
    count = slots_here * levels
    tokens = count * AREA
    dp_size, lat_size, lon_size = sizes
    chips = lat_size // 2
    spread = chips * lon_size
    dp, lat, lon = lax.axis_index("dp"), lax.axis_index("lat"), lax.axis_index("lon")
    core, chip = lax.rem(lat, 2), lat // 2
    is_last = lat == lat_size - 1
    moves, early_slots, late_slots, vector_slots, hand_slots, _ = move_slots(sizes, slots_here)
    begun = []

    def send(src, dst, slot, back, target):
        copy = pairing(src, dst, sends, receives, slot, back, target)
        copy.start()
        begun.append(copy)

    def arrive(dst, slot):
        pairing(dst, dst, sends, receives, slot, slot, (dp, lat, lon)).wait_recv()

    def pieces(kind, start):
        for quad in range(4):
            up, left = quad // 2, quad % 2
            way = 1 if kind > 1 else -1
            target = (
                dp,
                around(lat, way * up % lat_size, lat_size),
                around(lon, way * left % lon_size, lon_size),
            )
            grid = (inputs_ref, cotangent_ref, back_res_ref, back_in_ref)[kind]
            for slot in range(slots_here):
                on_grid = grid.at[
                    slot,
                    pl.ds(HALF_LAT * (1 - up), HALF_LAT),
                    pl.ds(HALF_LON * (1 - left), HALF_LON),
                ]
                quads = res_ref if kind > 1 else tok_ref
                in_quads = quads.at[quad, kind % 2, :, :, slot]
                src, dst = (in_quads, on_grid) if kind > 1 else (on_grid, in_quads)
                place = 4 * slots_here * kind + slots_here * quad + slot
                if quad == 0:
                    copy = pltpu.make_async_copy(src, dst, kept.at[kind * slots_here + slot])
                    copy.start() if start else copy.wait()
                elif start:
                    send(src, dst, moves + place, moves + place, target)
                else:
                    arrive(dst, moves + place)

    def shift(kind):
        pieces(kind, True)

    def shifted(kind):
        pieces(kind, False)

    def part(index):
        return pl.ds(pl.multiple_of(index * CHUNK, CHUNK), CHUNK)

    fetches = [
        pltpu.make_async_copy(source, target, fetched.at[index])
        for index, (source, target) in enumerate(
            (
                (master_ref, weights_ref),
                (entry_hbm, entry_ref),
                (place_hbm, place_ref),
            )
        )
    ]
    for fetch in fetches:
        fetch.start()
    def tokens_of(kind, c):
        return tok_ref[c, kind].astype(f32).reshape(CHUNK, D)

    def keep_tokens(kind, c, values):
        res_ref[c, kind] = values.reshape(res_ref.shape[2:]).astype(bf16)

    greeted = neighbours(inside)
    greet(greeted)

    per_home, own_rows = own_ref.shape[:2]
    flat_ref[pl.ds(0, per_home * own_rows), :] = jnp.zeros((per_home * own_rows, 128), f32)
    fetches[0].wait()
    for tile in range(tiles):
        flat_ref[pl.ds(tile, per_home, stride=own_rows), :] = weights_ref[
            :, 128 * tile : 128 * (tile + 1)
        ]
    for slot in range(per_home):
        own_ref[slot] = flat_ref[pl.ds(slot * own_rows, own_rows), :].astype(bf16)
    greeted_wait(len(greeted))

    def center_tokens():
        for bucket in range(buckets):
            home = home_ref[bucket]
            device, slot = home // per_home, lax.rem(home, per_home)
            home_lon = lax.rem(device, lon_size)
            home_lat = lax.rem(device // lon_size, lat_size)
            home_chip, home_core = home_lat // 2, lax.rem(home_lat, 2)
            unit = jnp.where(
                home_core == 0, home_lon * chips + home_chip, home_chip * lon_size + home_lon
            )
            per = per_home // SPLITS
            chunk = (slot // per) * dp_size + device // (lon_size * lat_size)
            spot_ref[bucket] = ((chunk * 2 + home_core) * spread + unit) * per + lax.rem(slot, per)
        shifted(0)

        @pl.loop(0, chunks)
        def _(c):
            rows = part(c)
            hat, inverse = normed(tokens_of(0, c))
            hat1_ref[rows, :] = hat
            inv1_ref[rows, :] = jnp.broadcast_to(inverse, (CHUNK, 128))

    gather = gather_steps(sizes, own_ref, all_ref, sends, receives, keeps)
    hooks = {0: functools.partial(shift, 0)}
    for mine in range(2):

        @pl.when(core == mine)
        def _():
            gather(mine, hooks, center_tokens)
            for copy in begun:
                copy.wait_send()
            begun.clear()

    shift(1)
    for fetch in fetches[1:]:
        fetch.wait()
    vacc_ref[...] = jnp.zeros_like(vacc_ref)
    marks = offsets(lat_size + 1)
    row_marks = [mark // 128 for mark in marks]

    for bucket in range(buckets):
        block = all_ref[spot_ref[bucket]].astype(f32)
        flat_ref[tiles * bucket : tiles * (bucket + 1), :] = block[:tiles]

    def take_pairs(base, parts, pairs):
        return [flat_ref[pl.ds(base + part, pairs, stride=parts), :] for part in range(parts)]

    def give_pairs(columns, rows, evens, odds):
        for column, (even, odd) in enumerate(zip(evens, odds)):
            mid_ref[column, pl.ds(0, rows // 2, stride=2), :] = even
            mid_ref[column, pl.ds(1, rows // 2, stride=2), :] = odd

    def load_qkv(base, ref):
        b = take_pairs(base, 9, D // 2)
        evens = [b[0], only_head(b[1]), tail_head(b[1], b[2]), only_tail(b[2]), b[3], only_head(b[4])]
        odds = [tail_head(b[4], b[5]), only_tail(b[5]), b[6], only_head(b[7]), tail_head(b[7], b[8]), only_tail(b[8])]
        give_pairs(6, D, evens, odds)
        for column in range(6):
            ref[:, 128 * column : 128 * (column + 1)] = mid_ref[column, pl.ds(0, D), :].astype(bf16)

    def load_square(base, rows, ref):
        b = take_pairs(base, 3, rows // 2)
        give_pairs(2, rows, [b[0], b[1]], [tail_head(b[1], b[2]), only_tail(b[2])])
        ref[0:rows, 0:128] = mid_ref[0, pl.ds(0, rows), :].astype(bf16)
        ref[0:rows, 128:D] = mid_ref[1, pl.ds(0, rows), :][:, : D - 128].astype(bf16)

    load_qkv(row_marks[0], w1_ref)
    load_square(row_marks[1], D, o1_ref)
    load_qkv(row_marks[2], w2_ref)
    load_square(row_marks[3], D, o2_ref)
    for ref in (o1_ref, o2_ref):
        ref[D:WIDE, :] = jnp.zeros((WIDE - D, D), bf16)
    for column in range(6):
        up_ref[:, 128 * column : 128 * (column + 1)] = flat_ref[
            pl.ds(row_marks[4] + column, D, stride=6), :
        ].astype(bf16)
    load_square(row_marks[5], FF, down_ref)
    for index in range(9):
        start = marks[7] + D * index
        vec_ref[index : index + 1, 0:128] = lanes_of(flat_ref, start)
        vec_ref[index : index + 1, 128:D] = lanes_of(flat_ref, start + 128)[:, : D - 128]

    def earth_places():
        group_one = lat + 1
        group_two = jnp.where(is_last, 0, lat + 1)
        for index in range(EARTH_ROWS):
            group = group_one if index % WIN_LAT < HALF_LAT else group_two
            start = marks[6] + EARTH_ROW * (EARTH_ROWS * group + index)
            row = start // 128
            yield index, row, start - 128 * row

    lane_place = lax.broadcasted_iota(jnp.int32, (1, 128), 1)
    earth_ref[...] = jnp.zeros_like(earth_ref)
    for index, row, lane in earth_places():
        rows = [flat_ref[pl.ds(row + step, 1), :] for step in range(3)]
        back = lax.rem(128 - lane, 128)
        first = pltpu.roll(jnp.where(lane_place >= lane, rows[0], rows[1]), back, 1)
        second = pltpu.roll(jnp.where(lane_place >= lane, rows[1], rows[2]), back, 1)
        earth_ref[index : index + 1, 0:128] = first
        earth_ref[index : index + 1, 128:256] = jnp.where(lane_place < EARTH_ROW - 128, second, 0.0)
    earth = earth_ref[...].astype(bf16)
    key_up = lax.broadcasted_iota(jnp.int32, (AREA, LANES), 0) // (2 * QUAD)
    query_up = lax.rem(lax.broadcasted_iota(jnp.int32, (AREA, LANES), 1), AREA) // (2 * QUAD)
    bias = jnp.where((key_up != query_up) & is_last, penalty_value, 0.0)
    for column in range(WIN_LON):
        bias = bias + nn(nt(entry_ref[column], earth).astype(bf16), place_ref[column])
    bias_ref[...] = bias

    for slot in range(slots_here):
        number = lax.axis_index("dp") * slots_here + slot
        live = lax.rem(number, LEADS) < lead_ref[number // LEADS]
        size = count // slots_here
        gate_ref[slot * size : (slot + 1) * size, :] = jnp.full((size, D), jnp.where(live, 1.0, 0.0), f32)

    def vec(index):
        return vec_ref[index : index + 1, :]

    def gate_rows():
        gate = gate_ref[...]
        return jnp.broadcast_to(gate[None], (CHUNK // count, count, D)).reshape(CHUNK, D)

    def note(index, values):
        vacc_ref[index] += row_fold(values)

    @pl.loop(0, chunks)
    def _(c):
        rows = part(c)
        low = (hat1_ref[rows, :] * vec(0) + vec(1)).astype(bf16)
        n1_ref[rows, :] = low
        mixed = rounded(nn(low, w1_ref[...]))
        for tile in range(6):
            qkv_ref[tile, rows, :] = mixed[:, 128 * tile : 128 * (tile + 1)]

    def window(ref, first, s):
        rows = pl.ds(s, AREA, stride=count)
        return jnp.concatenate([ref[first, rows, :], ref[first + 1, rows, :]], axis=1)

    def window_store(ref, first, s, values):
        rows = pl.ds(s, AREA, stride=count)
        ref[first, rows, :] = values[:, :128]
        ref[first + 1, rows, :] = values[:, 128:]

    @pl.loop(0, count // 4)
    def _(block):
        masks = head_masks(f32)
        places = [block * 4 + step for step in range(4)]
        reads = [[window(qkv_ref, 2 * kind, s) for kind in range(3)] for s in places]
        raw = [
            nt(key.astype(bf16), spread_heads(query, masks).astype(bf16)) for query, key, _ in reads
        ]
        probs = [soft_columns(scores * SCALE + bias_ref[...]) for scores in raw]
        outs = [tn(prob.astype(bf16), read[2].astype(bf16)) for prob, read in zip(probs, reads)]
        for s, prob, out in zip(places, probs, outs):
            probs_ref[s] = prob
            window_store(att_ref, 0, s, fold_heads(out, AREA))

    @pl.loop(0, chunks)
    def _(c):
        rows = part(c)
        att = jnp.concatenate([att_ref[0, rows, :], att_ref[1, rows, :]], axis=1).astype(bf16)
        att1_ref[rows, :] = att
        branch = nn(att, o1_ref[...]) + vec(2)
        tok = tokens_of(0, c) + gate_rows() * branch
        tok1_ref[rows, :] = tok
        hat, inverse = normed(tok)
        hat2_ref[rows, :] = hat
        inv2_ref[rows, :] = jnp.broadcast_to(inverse, (CHUNK, 128))
        low = (hat * vec(3) + vec(4)).astype(bf16)
        n2_ref[rows, :] = low
        mix2_ref[rows, :] = nn(low, w2_ref[...]).astype(bf16)

    def column_masks():
        lane = lax.broadcasted_iota(jnp.int32, (8, GLANES), 1)
        place = (lane % GROUP) // 8
        return [place == index for index in range(GROUP // 8)]

    def squeeze_column(values, masks):
        out = values[:8]
        for index in range(1, GROUP // 8):
            out = jnp.where(masks[index], values[8 * index : 8 * index + 8], out)
        return out

    def widen_column(values, masks):
        return jnp.concatenate([jnp.where(mask, values, 0.0) for mask in masks], axis=0).astype(bf16)

    def group_rows(g):
        return pl.ds(pl.multiple_of(g * GROUP, GROUP), GROUP)

    @pl.loop(0, tokens // GROUP // 6)
    def _(block):
        heads = head_masks(bf16)
        columns = column_masks()
        places = [block * 6 + step for step in range(6)]
        reads = [mix2_ref[group_rows(g), :] for g in places]
        raw = [
            nt(mixed[:, WIDE : 2 * WIDE], spread_heads(mixed[:, 0:WIDE], heads)) for mixed in reads
        ]
        probs = [soft_columns(squeeze_column(scores, columns) * SCALE) for scores in raw]
        outs = [
            tn(widen_column(prob, columns), mixed[:, 2 * WIDE :])
            for prob, mixed in zip(probs, reads)
        ]
        for g, prob, out in zip(places, probs, outs):
            cprobs_ref[g] = prob
            att2_ref[group_rows(g), :] = fold_heads(out, GROUP).astype(bf16)

    root = math.sqrt(2.0 / math.pi)
    shifted(1)

    @pl.loop(0, chunks)
    def _(c):
        rows = part(c)
        gate = gate_rows()
        tok = tok1_ref[rows, :] + gate * (nn(att2_ref[rows, :], o2_ref[...]) + vec(5))
        hat, inverse = normed(tok)
        low = (hat * vec(6) + vec(7)).astype(bf16)
        n3_ref[rows, :] = low
        hidden = nn(low, up_ref[...])
        square = hidden * hidden
        half = 0.5 * jnp.tanh(hidden * (root + (root * 0.044715) * square)) + 0.5
        wave = hidden * half
        act = wave.astype(bf16)
        act_ref[rows, :] = act
        keep_tokens(0, c, tok + gate * (nn(act, down_ref[...]) + vec(8)))
        slope = half + wave * (1.0 - half) * (2.0 * root + (6.0 * root * 0.044715) * square)
        after = tokens_of(1, c)
        delta3 = (gate * after).astype(bf16)
        delta3_ref[rows, :] = delta3
        note(8, delta3.astype(f32))
        gh = (nt(delta3, down_ref[...]) * slope).astype(bf16)
        gh_ref[rows, :] = gh
        grad = nt(gh, up_ref[...])
        note(6, grad * hat)
        note(7, grad)
        mid = after + norm_back(grad, hat, inverse, vec(6))
        gmid_ref[rows, :] = mid
        delta2 = (gate * mid).astype(bf16)
        delta2_ref[rows, :] = delta2
        note(5, delta2.astype(f32))
        gatt2_ref[rows, :] = nt(delta2, o2_ref[...]).astype(bf16)

    shift(2)

    @pl.loop(0, tokens // GROUP // 6)
    def _(block):
        heads = head_masks(bf16)
        columns = column_masks()
        places = [block * 6 + step for step in range(6)]
        reads = [
            (mix2_ref[group_rows(g), :], gatt2_ref[group_rows(g), :], cprobs_ref[g]) for g in places
        ]
        grads = [spread_heads(read[1], heads) for read in reads]
        raw = [nt(read[0][:, 2 * WIDE :], grad) for read, grad in zip(reads, grads)]
        dvalues = [nn(widen_column(read[2], columns), grad) for read, grad in zip(reads, grads)]
        lows = [
            widen_column(soft_back(read[2], squeeze_column(slopes, columns)), columns)
            for read, slopes in zip(reads, raw)
        ]
        dkeys = [
            nn(low, spread_heads(read[0][:, 0:WIDE], heads)) for read, low in zip(reads, lows)
        ]
        dqueries = [tn(low, read[0][:, WIDE : 2 * WIDE]) for read, low in zip(reads, lows)]
        for g, dquery, dkey, dvalue in zip(places, dqueries, dkeys, dvalues):
            rows = group_rows(g)
            gm2_ref[rows, 0:WIDE] = (fold_heads(dquery, GROUP) * SCALE).astype(bf16)
            gm2_ref[rows, WIDE : 2 * WIDE] = (dkey * SCALE).astype(bf16)
            gm2_ref[rows, 2 * WIDE : 3 * WIDE] = dvalue.astype(bf16)

    @pl.loop(0, chunks)
    def _(c):
        rows = part(c)
        grad = nt(gm2_ref[rows, :], w2_ref[...])
        hat = hat2_ref[rows, :]
        inverse = inv2_ref[rows, :][:, :1]
        note(3, grad * hat)
        note(4, grad)
        low = gmid_ref[rows, :] + norm_back(grad, hat, inverse, vec(3))
        glow_ref[rows, :] = low
        delta1 = (gate_rows() * low).astype(bf16)
        delta1_ref[rows, :] = delta1
        note(2, delta1.astype(f32))
        gatt = rounded(nt(delta1, o1_ref[...]))
        att_ref[0, rows, :] = gatt[:, :128]
        att_ref[1, rows, :] = gatt[:, 128:]

    def keep_pairs(base, parts, blocks):
        for number, block in enumerate(blocks):
            flat_ref[pl.ds(base + number, block.shape[0], stride=parts), :] = block

    def split_pairs(columns, rows):
        evens = [mid_ref[column, pl.ds(0, rows // 2, stride=2), :] for column in range(columns)]
        odds = [mid_ref[column, pl.ds(1, rows // 2, stride=2), :] for column in range(columns)]
        return evens, odds

    def save_qkv(base, grad):
        for column in range(6):
            mid_ref[column, pl.ds(0, D), :] = grad[:, 128 * column : 128 * (column + 1)]
        e, o = split_pairs(6, D)
        blocks = [
            e[0],
            head_head(e[1], e[2]),
            tail_head(e[2], e[3]),
            e[4],
            head_head(e[5], o[0]),
            tail_head(o[0], o[1]),
            o[2],
            head_head(o[3], o[4]),
            tail_head(o[4], o[5]),
        ]
        keep_pairs(base, 9, blocks)

    def save_square(base, rows, grad):
        mid_ref[0, pl.ds(0, rows), :] = grad[:rows, :128]
        mid_ref[1, pl.ds(0, rows), 0 : D - 128] = grad[:rows, 128:]
        e, o = split_pairs(2, rows)
        keep_pairs(base, 3, [e[0], head_head(e[1], o[0]), tail_head(o[0], o[1])])

    save_square(row_marks[1], D, tn(att1_ref[...], delta1_ref[...]))
    save_qkv(row_marks[2], tn(n2_ref[...], gm2_ref[...]))
    save_square(row_marks[3], D, tn(att2_ref[...], delta2_ref[...]))
    grad_up = tn(n3_ref[...], gh_ref[...])
    for column in range(6):
        flat_ref[pl.ds(row_marks[4] + column, D, stride=6), :] = grad_up[
            :, 128 * column : 128 * (column + 1)
        ]
    save_square(row_marks[5], FF, tn(act_ref[...], delta3_ref[...]))

    partner = (dp, chip * 2 + 1 - core, lon)
    place = chip * lon_size + lon

    def peers():
        for i in range(chips):
            for j in range(lon_size):
                if i or j:
                    back = (chips - i) % chips * lon_size + (lon_size - j) % lon_size
                    there = (around(chip, i, chips), around(lon, j, lon_size))
                    target = (dp, there[0] * 2 + core, there[1])
                    yield i * lon_size + j, back, there[0] * lon_size + there[1], target

    def line():
        for step in range(1, dp_size):
            there = around(dp, step, dp_size)
            yield step, dp_size - step, there, (there, lat, lon)

    def summing(base, grad, half_in, half, plane_in, mid, line_in, full):
        n_half = grad.shape[0] // 2
        n_place = n_half // spread
        n_line = n_place // dp_size

        def cross():
            send(grad.at[pl.ds((1 - core) * n_half, n_half)], half_in, base, base, partner)

        def plane():
            arrive(half_in, base)
            for first in range(0, n_half, 12):
                rows = pl.ds(first, 12)
                kept = grad[pl.ds(core * n_half + first, 12)].astype(f32)
                half[rows] = (kept + half_in[rows].astype(f32)).astype(bf16)
            for index, back, there, target in peers():
                send(
                    half.at[pl.ds(there * n_place, n_place)],
                    plane_in.at[back],
                    base + 1 + index,
                    base + 1 + back,
                    target,
                )

        def along():
            total = half[pl.ds(place * n_place, n_place)].astype(f32)
            for index in range(1, spread):
                arrive(plane_in.at[index], base + 1 + index)
                total = total + plane_in[index].astype(f32)
            mid[...] = total.astype(bf16)
            slots = base + 1 + spread
            for step, back, there, target in line():
                send(mid.at[pl.ds(there * n_line, n_line)], line_in.at[back], slots + step, slots + back, target)

        def share():
            slots = base + 1 + spread
            rows = pl.ds(dp * n_line, n_line)
            total = mid[rows].astype(f32)
            for step in range(1, dp_size):
                arrive(line_in.at[step], slots + step)
                total = total + line_in[step].astype(f32)
            full[rows] = total.astype(bf16)
            slots += dp_size
            for step, back, _, target in line():
                send(full.at[rows], full.at[rows], slots + step, slots + back, target)

        def done():
            slots = base + 1 + spread + dp_size
            for step, _, there, _ in line():
                arrive(full.at[pl.ds(there * n_line, n_line)], slots + step)

        return cross, plane, along, share, done

    bucket_low, bucket_high = early_span

    if inside:
        early_refs, late_refs = sum_refs[:7], sum_refs[7:14]
        hand_out, vec_sum, vec_in, vec_now = sum_refs[14:]
        early = summing(early_slots, *early_refs)
        late = summing(late_slots, *late_refs)

        def pack(grad, spans):
            for tile in range(grad.shape[0]):
                if tile < tiles:
                    rows = [
                        flat_ref[pl.ds(tile + tiles * first, last - first, stride=tiles), :]
                        for first, last in spans
                    ]
                    values = rows[0] if len(rows) == 1 else jnp.concatenate(rows, axis=0)
                    grad[tile] = values.astype(bf16)
                else:
                    grad[tile] = jnp.zeros(grad.shape[1:], bf16)

        pack(early_refs[0], [(bucket_low, bucket_high)])
        early[0]()
    else:
        (vec_sum,) = sum_refs

    dbias_ref[...] = jnp.zeros_like(dbias_ref)

    def window_back(block):
        masks = head_masks(f32)
        places = [block * 4 + step for step in range(4)]
        reads = [
            [window(qkv_ref, 2 * kind, s) for kind in range(3)]
            + [window(att_ref, 0, s), probs_ref[s]]
            for s in places
        ]
        grads = [spread_heads(read[3], masks).astype(bf16) for read in reads]
        raw = [nt(read[2].astype(bf16), grad) for read, grad in zip(reads, grads)]
        dvalues = [nn(read[4].astype(bf16), grad) for read, grad in zip(reads, grads)]
        lows = [soft_back(read[4], slopes).astype(bf16) for read, slopes in zip(reads, raw)]
        dkeys = [
            nn(low, spread_heads(read[0], masks).astype(bf16)) for read, low in zip(reads, lows)
        ]
        dqueries = [tn(low, read[1].astype(bf16)) for read, low in zip(reads, lows)]
        dbias_ref[...] += functools.reduce(jnp.add, [low.astype(f32) for low in lows])
        for s, dquery, dkey, dvalue in zip(places, dqueries, dkeys, dvalues):
            window_store(qkv_ref, 0, s, rounded(fold_heads(dquery, AREA) * SCALE))
            window_store(qkv_ref, 2, s, rounded(dkey * SCALE))
            window_store(qkv_ref, 4, s, rounded(dvalue))

    @pl.loop(0, 2)
    def _(block):
        window_back(block)

    if inside:
        early[1]()

    @pl.loop(2, count // 4)
    def _(block):
        window_back(block)

    @pl.loop(0, chunks)
    def _(c):
        rows = part(c)
        gm1_ref[rows, :] = jnp.concatenate(
            [qkv_ref[tile, rows, :] for tile in range(6)], axis=1
        ).astype(bf16)

    save_qkv(row_marks[0], tn(n1_ref[...], gm1_ref[...]))
    rest = flat_ref.shape[0] - row_marks[6]
    flat_ref[row_marks[6] :, :] = jnp.zeros((rest, 128), f32)
    dbias = dbias_ref[...]
    high = dbias.astype(bf16)
    both = jnp.concatenate([high, (dbias - high.astype(f32)).astype(bf16)], axis=0)
    dearth = jnp.zeros((40, 256), f32)
    for column in range(WIN_LON):
        moved = nt(both, place_ref[column]).astype(bf16)
        entry = entry_ref[column]
        dearth = dearth + tn(moved[:AREA], entry) + tn(moved[AREA:], entry)
    for index, row, lane in earth_places():
        first = pltpu.roll(dearth[index : index + 1, :128], lane, 1)
        second = pltpu.roll(dearth[index : index + 1, 128:], lane, 1)
        tail = lane_place >= lane
        for step, values in enumerate(
            (
                jnp.where(tail, first, 0.0),
                jnp.where(tail, second, first),
                jnp.where(tail, 0.0, second),
            )
        ):
            flat_ref[pl.ds(row + step, 1), :] += values
    if inside:
        pack(late_refs[0], [(0, bucket_low), (bucket_high, buckets)])
        late[0]()

    def input_grads(c):
        rows = part(c)
        mixed = gm1_ref[rows, :]
        grad = nt(mixed, w1_ref[...])
        hat = hat1_ref[rows, :]
        inverse = inv1_ref[rows, :][:, :1]
        note(0, grad * hat)
        note(1, grad)
        grad_in = glow_ref[rows, :] + norm_back(grad, hat, inverse, vec(0))
        keep_tokens(1, c, grad_in)

    @pl.loop(0, chunks // 2)
    def _(c):
        input_grads(c)

    if inside:
        early[2]()
        late[1]()

    @pl.loop(chunks // 2, chunks)
    def _(c):
        input_grads(c)

    for index in range(9):
        vec_sum[index : index + 1, :] = jnp.sum(vacc_ref[index], axis=0, keepdims=True)
    if inside:
        send(vec_sum, vec_in.at[0], vector_slots, vector_slots, partner)
        early[3]()
    shift(3)
    if inside:
        arrive(vec_in.at[0], vector_slots)
        vec_now[0] = vec_sum[...] + vec_in[0]
        for index, back, _, target in peers():
            send(vec_now.at[0], vec_in.at[back], vector_slots + 1 + index, vector_slots + 1 + back, target)
        late[2]()
        vec_total = vec_now[0]
        for index in range(1, spread):
            arrive(vec_in.at[index], vector_slots + 1 + index)
            vec_total = vec_total + vec_in[index]
        vec_now[1] = vec_total
        slots = vector_slots + 1 + spread
        for step, back, _, target in line():
            send(vec_now.at[1], vec_in.at[spread + back], slots + step, slots + back, target)
        late[3]()
        early[4]()
        for step in range(1, dp_size):
            arrive(vec_in.at[spread + step], slots + step)
            vec_total = vec_total + vec_in[spread + step]
        total_ref[...] = vec_total
        late[4]()
        homes = lat_size * lon_size
        width = homes * per_home
        slot_ids = lax.broadcasted_iota(jnp.int32, (width, 1), 0) + dp * width
        all_homes = homes_ref[...]
        early_homes = all_homes[:, bucket_low:bucket_high]
        late_homes = jnp.concatenate([all_homes[:, :bucket_low], all_homes[:, bucket_high:]], axis=1)
        early_pick = jnp.where(slot_ids == early_homes, 1.0, 0.0).astype(bf16)
        late_pick = jnp.where(slot_ids == late_homes, 1.0, 0.0).astype(bf16)
        for row in range(early_refs[6].shape[0]):
            owned = nn(early_pick, early_refs[6][row]) + nn(late_pick, late_refs[6][row])
            for home in range(homes):
                hand_out[home, row] = owned[per_home * home : per_home * (home + 1), :]
        n_rows = hand_out.shape[1]
        first = core * (n_rows * spread) + place * n_rows
        landing = grads_ref.at[pl.ds(first, n_rows)]
        me = lat * lon_size + lon
        keep_hand = pltpu.make_async_copy(hand_out.at[me], landing, keeps.at[SPLITS])
        keep_hand.start()
        for i in range(lat_size):
            for j in range(lon_size):
                if i or j:
                    target = (dp, around(lat, i, lat_size), around(lon, j, lon_size))
                    back = (lat_size - i) % lat_size * lon_size + (lon_size - j) % lon_size
                    send(
                        hand_out.at[target[1] * lon_size + target[2]],
                        landing,
                        hand_slots + i * lon_size + j,
                        hand_slots + back,
                        target,
                    )
        keep_hand.wait()
        for index in range(1, homes):
            arrive(landing, hand_slots + index)
    else:
        total_ref[...] = vec_sum[...]
        for tile in range(tiles):
            grads_ref[tile] = flat_ref[pl.ds(tile, buckets, stride=tiles), :]
    shifted(2)
    shifted(3)
    for copy in begun:
        copy.wait_send()


def sum_rows(sizes, tiles):
    unit = sizes[0] * sizes[1] * sizes[2]
    rows = -(-tiles // unit) * unit
    return rows, rows <= 2 * tiles


def block_call(homes, leads, master, inputs, cotangent, sizes):
    slots_here, levels = inputs.shape[0], inputs.shape[3]
    count = slots_here * levels
    tokens = count * AREA
    buckets = homes.shape[0]
    per_home, width = master.shape
    tiles = width // 128
    own_rows = -(-tiles // 16) * 16
    quads = (4, 2, HALF_LAT, HALF_LON, slots_here, levels, D)
    dp_size, lat_size, lon_size = sizes
    spread = lat_size // 2 * lon_size
    rows, inside = sum_rows(sizes, tiles)
    marks = offsets(lat_size + 1)
    low = -(-marks[1] // width)
    high = low + (marks[6] // width - low) // 16 * 16
    shape = jax.ShapeDtypeStruct
    outs = [
        shape(inputs.shape, bf16),
        shape(inputs.shape, bf16),
        shape((rows, per_home, 128) if inside else (tiles, buckets, 128), f32),
        shape((9, D), f32),
    ]
    vmem = pltpu.VMEM
    entry, place = earth_tables()
    scratch = [
        pltpu.SMEM((buckets,), jnp.int32),
        vmem(master.shape, f32),
        vmem(entry.shape, bf16),
        vmem(place.shape, bf16),
        vmem((per_home, own_rows, 128), bf16),
        vmem((dp_size * lat_size * lon_size * per_home, own_rows, 128), bf16),
        vmem(quads, bf16),
        vmem(quads, bf16),
        vmem((buckets * tiles, 128), f32),
        vmem((6, FF, 128), f32),
        vmem((40, 256), f32),
        vmem((count, D), f32),
        vmem((AREA, LANES), f32),
        vmem((AREA, LANES), f32),
        vmem((D, 3 * WIDE), bf16),
        vmem((WIDE, D), bf16),
        vmem((D, 3 * WIDE), bf16),
        vmem((WIDE, D), bf16),
        vmem((D, FF), bf16),
        vmem((FF, D), bf16),
        vmem((16, D), f32),
        vmem((tokens, D), bf16),
        vmem((tokens, D), f32),
        vmem((tokens, 128), f32),
        vmem((6, tokens, 128), f32),
        vmem((count, AREA, LANES), f32),
        vmem((2, tokens, 128), f32),
        vmem((tokens, WIDE), bf16),
        vmem((tokens, D), f32),
        vmem((tokens, D), bf16),
        vmem((tokens, D), f32),
        vmem((tokens, 128), f32),
        vmem((tokens, 3 * WIDE), bf16),
        vmem((tokens // GROUP, 8, GLANES), f32),
        vmem((tokens, WIDE), bf16),
        vmem((tokens, D), bf16),
        vmem((tokens, FF), bf16),
        vmem((tokens, FF), bf16),
        vmem((tokens, D), bf16),
        vmem((tokens, D), bf16),
        vmem((tokens, D), bf16),
        vmem((tokens, D), f32),
        vmem((tokens, D), f32),
        vmem((tokens, WIDE), bf16),
        vmem((tokens, 3 * WIDE), bf16),
        vmem((tokens, 3 * WIDE), bf16),
        vmem((9, 8, D), f32),
        pltpu.SemaphoreType.DMA((move_slots(sizes, slots_here)[-1],)),
        pltpu.SemaphoreType.DMA((move_slots(sizes, slots_here)[-1],)),
        pltpu.SemaphoreType.DMA((SPLITS + 1,)),
        pltpu.SemaphoreType.DMA((3,)),
        pltpu.SemaphoreType.DMA((4 * slots_here,)),
    ]
    if inside:
        n_place = rows // 2 // spread
        for some in (high - low, buckets - (high - low)):
            scratch += [
                vmem((rows, some, 128), bf16),
                vmem((rows // 2, some, 128), bf16),
                vmem((rows // 2, some, 128), bf16),
                vmem((spread, n_place, some, 128), bf16),
                vmem((n_place, some, 128), bf16),
                vmem((dp_size, n_place // dp_size, some, 128), bf16),
                vmem((n_place, some, 128), bf16),
            ]
        scratch += [
            vmem((lat_size * lon_size, n_place, per_home, 128), f32),
            vmem((9, D), f32),
            vmem((spread + dp_size, 9, D), f32),
            vmem((2, 9, D), f32),
        ]
    else:
        scratch += [vmem((9, D), f32)]
    spec = pl.BlockSpec(memory_space=pltpu.VMEM)
    smem = pl.BlockSpec(memory_space=pltpu.SMEM)
    hbm = pl.BlockSpec(memory_space=pl.ANY)
    return pl.pallas_call(
        functools.partial(block_kernel, (sizes, buckets, tiles, slots_here, (low, high)), inside),
        out_shape=outs,
        in_specs=[smem, smem, spec] + [hbm] * 5,
        out_specs=[hbm, hbm, spec, spec],
        scratch_shapes=scratch,
        compiler_params=pltpu.CompilerParams(
            vmem_limit_bytes=62 * 1024 * 1024, collective_id=0, has_side_effects=True
        ),
        name="block",
    )(
        homes,
        leads,
        homes[None, :],
        master,
        inputs,
        cotangent,
        jnp.asarray(entry),
        jnp.asarray(place),
    )


def finish_kernel(
    marks,
    steps_ref,
    homes_ref,
    grads_ref,
    vectors_ref,
    master_ref,
    one_ref,
    two_ref,
    back_res_ref,
    back_in_ref,
    result_ref,
    grad_inputs_ref,
    grad_vectors_ref,
    new_master,
    new_one,
    new_two,
    spare_ref,
):
    homes, width = master_ref.shape
    tiles = width // 128
    for slot in range(result_ref.shape[0]):
        result_ref[slot] = back_res_ref[slot]

        @pl.loop(0, WIN_LAT)
        def _(row):
            grad_inputs_ref[slot, row] = back_in_ref[slot, row].astype(f32)

    grad_vectors_ref[...] = vectors_ref[...]
    place = lax.axis_index("dp") * lax.axis_size("lat") + lax.axis_index("lat")
    place = (place * lax.axis_size("lon") + lax.axis_index("lon")) * homes
    slots = lax.broadcasted_iota(jnp.int32, (homes, 1), 0) + place
    match = homes_ref[...] == slots
    bucket = lax.broadcasted_iota(jnp.int32, match.shape, 1)
    held = jnp.max(jnp.where(match, bucket, -1), axis=1, keepdims=True)
    base = jnp.where(held >= 0, held * width, marks[8])

    top = marks[7] // 128
    spare_ref[...] = jnp.zeros_like(spare_ref)
    lanes = lax.broadcasted_iota(jnp.int32, (1, 128), 1)
    for index in range(9):
        vector = vectors_ref[index : index + 1, :]
        start = marks[7] + D * index
        tail = jnp.concatenate([vector[:, 128:], jnp.zeros((1, 256 - D), f32)], axis=1)
        for values, size, begin in ((vector[:, :128], 128, start), (tail, D - 128, start + 128)):
            row, lane = divmod(begin - 128 * top, 128)
            moved = pltpu.roll(values, lane, 1) if lane else values
            spare_ref[row : row + 1, :] += jnp.where(lanes >= lane, moved, 0.0)
            if lane + size > 128:
                spare_ref[row + 1 : row + 2, :] += jnp.where(lanes < lane, moved, 0.0)

    steps = jnp.full((homes, 128), steps_ref[0], jnp.int32).astype(f32)
    fix_one = 1.0 / (1.0 - jnp.exp(steps * math.log(beta_one)))
    fix_two = 1.0 / (1.0 - jnp.exp(steps * math.log(beta_two)))
    rates = [
        2.6 / math.sqrt(D),
        8.0 / math.sqrt(D),
        2.6 / math.sqrt(D),
        4.0 / math.sqrt(D),
        2.0 / math.sqrt(D),
        3.0 / math.sqrt(FF),
        1.0,
        0.6,
    ]
    spread = jnp.broadcast_to(base, (homes, 128)) + lax.broadcasted_iota(jnp.int32, (homes, 128), 1)
    for tile in range(tiles):
        columns = slice(128 * tile, 128 * (tile + 1))
        index = spread + 128 * tile
        rate = jnp.full((homes, 128), 0.1, f32)
        for number in range(7, -1, -1):
            rate = jnp.where(index < marks[number + 1], rates[number], rate)
        grad = grads_ref[tile]
        for owner in range(marks[7] // width, (marks[8] - 1) // width + 1):
            row = owner * tiles + tile - top
            if 0 <= row < spare_ref.shape[0]:
                grad = grad + jnp.where(held == owner, spare_ref[row : row + 1, :], 0.0)
        weights = master_ref[:, columns]
        first = beta_one * one_ref[:, columns] + (1.0 - beta_one) * grad
        second = beta_two * two_ref[:, columns] + (1.0 - beta_two) * grad * grad
        step = first * fix_one / (jnp.sqrt(second * fix_two) + eps_adam) + decay_rate * weights
        new_master[:, columns] = weights - rate * step
        new_one[:, columns] = first
        new_two[:, columns] = second


def finish_call(marks, steps, homes, grads, vectors, master, one, two, back_res, back_in):
    smem = pl.BlockSpec(memory_space=pltpu.SMEM)
    vmem = pl.BlockSpec(memory_space=pltpu.VMEM)
    grid = back_res.shape
    shape = jax.ShapeDtypeStruct
    return pl.pallas_call(
        functools.partial(finish_kernel, marks),
        out_shape=[shape(grid, bf16), shape(grid, f32), shape(vectors.shape, f32)]
        + [shape(master.shape, f32)] * 3,
        in_specs=[smem] + [vmem] * 8,
        out_specs=[vmem] * 6,
        scratch_shapes=[
            pltpu.VMEM((16, 128), f32),
        ],
        name="finish",
    )(steps, homes[None, :], grads, vectors, master, one, two, back_res, back_in)


def per_device(
    inputs, cotangent, lead_counts, home_slots, master, moment_one, moment_two, step_count
):
    axes = ("dp", "lat", "lon")
    sizes = tuple(lax.axis_size(axis) for axis in axes)
    slots_mine, bucket_width = master.shape
    tiles = bucket_width // 128
    order = (0, 2, 3, 1, 4)
    back_res, back_in, grads, vectors = block_call(
        home_slots, lead_counts, master, inputs.transpose(order), cotangent.transpose(order), sizes
    )
    if not sum_rows(sizes, tiles)[1]:
        spread = jnp.zeros((tiles, math.prod(sizes) * slots_mine, 128), f32)
        spread = spread.at[:, home_slots].set(grads)
        grads = lax.psum_scatter(spread, axes, scatter_dimension=1, tiled=True)
        vectors = lax.psum(vectors, axes)
    result, grad_inputs, grad_vectors, *new = finish_call(
        offsets(sizes[1] + 1),
        step_count,
        home_slots,
        grads,
        vectors,
        master,
        moment_one,
        moment_two,
        back_res,
        back_in,
    )
    order = (0, 3, 1, 2, 4)
    return (result.transpose(order), grad_inputs.transpose(order), grad_vectors, *new)


def solution(mesh):
    in_specs = (
        P("dp", None, "lat", "lon", None),
        P("dp", None, "lat", "lon", None),
        P(),
        P(),
        P(("dp", "lat", "lon"), None),
        P(("dp", "lat", "lon"), None),
        P(("dp", "lat", "lon"), None),
        P(),
    )
    out_specs = (
        P("dp", None, "lat", "lon", None),
        P("dp", None, "lat", "lon", None),
        P(),
        P(("dp", "lat", "lon"), None),
        P(("dp", "lat", "lon"), None),
        P(("dp", "lat", "lon"), None),
    )
    return jax.shard_map(
        per_device, mesh=mesh, in_specs=in_specs, out_specs=out_specs, check_vma=False
    )
```

```python
import functools
import math

import jax
import jax.numpy as jnp
import ml_dtypes
import numpy as np
from jax import lax
from jax.experimental import pallas as pl
from jax.experimental.pallas import tpu as pltpu
from jax.sharding import PartitionSpec as P

D = 192
FF = 768
HEADS = 6
HEAD_DIM = 32
LEVELS = 8
WIN_LAT = 6
WIN_LON = 12
LEADS = 4
HALF_LAT = WIN_LAT // 2
HALF_LON = WIN_LON // 2
QUAD = HALF_LAT * HALF_LON
AREA = WIN_LAT * WIN_LON
SIDE_HEADS = HEADS // 2
SIDE = SIDE_HEADS * HEAD_DIM
HEAD_ROWS = 80
LANES = 512
WIDE = 256
SCALE = 1.0 / math.sqrt(HEAD_DIM)

beta_one = 0.6
beta_two = 0.45
eps_norm = 1e-05
eps_adam = 1e-08
decay_rate = 0.1
penalty_value = -1000000000.0
bf16 = jnp.bfloat16
f32 = jnp.float32


def offsets(groups):
    sizes_list = [
        3 * D * D,
        D * D,
        3 * D * D,
        D * D,
        D * FF,
        FF * D,
        groups * HEADS * WIN_LAT * WIN_LAT * (2 * WIN_LON - 1),
        9 * D,
    ]
    segment_marks = [0]
    for amount in sizes_list:
        segment_marks.append(segment_marks[-1] + amount)
    return segment_marks


def nn(left, right):
    return jnp.dot(left, right, preferred_element_type=f32)


def nt(left, right):
    return lax.dot_general(left, right, (((1,), (1,)), ((), ())), preferred_element_type=f32)


def tn(left, right):
    return lax.dot_general(left, right, (((0,), (0,)), ((), ())), preferred_element_type=f32)


def normed(values):
    center = values - jnp.sum(values, axis=-1, keepdims=True) * (1.0 / D)
    spread = jnp.sum(center * center, axis=-1, keepdims=True) * (1.0 / D)
    inverse = lax.rsqrt(spread + eps_norm)
    return center * inverse, inverse


def norm_back(grad, hat, inverse, gain):
    scaled = grad * gain
    mean_one = jnp.sum(scaled, axis=-1, keepdims=True) * (1.0 / D)
    mean_two = jnp.sum(scaled * hat, axis=-1, keepdims=True) * (1.0 / D)
    return inverse * (scaled - mean_one - hat * mean_two)


def row_fold(values):
    return jnp.sum(values.reshape(values.shape[0] // 8, 8, values.shape[1]), axis=0)


def head_masks():
    lane = lax.broadcasted_iota(jnp.int32, (1, 128), 1) // HEAD_DIM
    return [jnp.where(lane == head, 1.0, 0.0).astype(bf16) for head in range(SIDE_HEADS)]


def spread_heads(values, masks):
    return jnp.concatenate([values * mask for mask in masks], axis=0)


def spread_window(values, masks):
    full = jnp.concatenate([values, jnp.zeros((HEAD_ROWS - AREA, 128), f32)], axis=0).astype(bf16)
    rest = jnp.zeros((LANES // 2 - SIDE_HEADS * HEAD_ROWS, 128), bf16)
    return jnp.concatenate([spread_heads(full, masks), rest], axis=0)


def fold_heads(big, step, count):
    lane = lax.broadcasted_iota(jnp.int32, (count, 128), 1)
    parts = [big[head * step : head * step + count] for head in range(SIDE_HEADS)]
    out = parts[-1]
    for head in range(SIDE_HEADS - 2, -1, -1):
        out = jnp.where(lane < HEAD_DIM * (head + 1), parts[head], out)
    return out


def rounded(values):
    return values.astype(bf16).astype(f32)


def soft_columns(scores):
    exps = jnp.exp(scores - jnp.max(scores, axis=0, keepdims=True))
    return exps * (1.0 / jnp.sum(exps, axis=0, keepdims=True))


def soft_back(probs, slopes):
    return probs * (slopes - jnp.sum(probs * slopes, axis=0, keepdims=True))


GROUP = 64
GLANES = SIDE_HEADS * GROUP
CHUNK = 288


def lanes_of(ref, start):
    row, lane = divmod(start, 128)
    here = ref[row : row + 1, :]
    if lane == 0:
        return here
    place = lax.broadcasted_iota(jnp.int32, (1, 128), 1)
    mixed = jnp.where(place >= lane, here, ref[row + 1 : row + 2, :])
    return pltpu.roll(mixed, 128 - lane, 1)


def lanes_from(first, second, lane, size):
    place = lax.broadcasted_iota(jnp.int32, first.shape, 1)
    if lane:
        first = pltpu.roll(jnp.where(place >= lane, first, second), 128 - lane, 1)
    return jnp.where(place < size, first, 0.0) if size < 128 else first


def lanes_join(first, begin, size, second):
    place = lax.broadcasted_iota(jnp.int32, first.shape, 1)
    moved = pltpu.roll(first, 128 - begin, 1) if begin else first
    return jnp.where(place < size, moved, pltpu.roll(second, size, 1))


EARTH_ROW = WIN_LAT * (2 * WIN_LON - 1)
EARTH_ROWS = HEADS * WIN_LAT


def earth_tables():
    entry = np.zeros((WIN_LON, AREA, 256), np.float32)
    place = np.zeros((WIN_LON, 40, LANES), np.float32)
    for column in range(WIN_LON):
        side, inner = divmod(column, HALF_LON)
        for key in range(AREA):
            key_up, rest = divmod(key, 2 * QUAD)
            key_side, rest = divmod(rest, QUAD)
            key_row, key_inner = divmod(rest, HALF_LON)
            row = key_up * HALF_LAT + key_row
            offset = column - (key_side * HALF_LON + key_inner) + WIN_LON - 1
            entry[column, key, row * (2 * WIN_LON - 1) + offset] = 1.0
        for head in range(HEADS):
            for row in range(WIN_LAT):
                up, low = divmod(row, HALF_LAT)
                lane = 2 * QUAD * up + QUAD * side + HALF_LON * low + inner
                lane += LANES // 2 * (head // SIDE_HEADS) + HEAD_ROWS * (head % SIDE_HEADS)
                place[column, head * WIN_LAT + row, lane] = 1.0
    return entry.astype(ml_dtypes.bfloat16), place.astype(ml_dtypes.bfloat16)


MESH = pl.DeviceIdType.MESH


def places():
    lat_size, lon_size, dp_size = lax.axis_size("lat"), lax.axis_size("lon"), lax.axis_size("dp")
    return (
        lax.axis_index("dp"),
        lax.axis_index("lat"),
        lax.axis_index("lon"),
        dp_size,
        lat_size,
        lon_size,
    )


def greet(targets):
    barrier = pltpu.get_barrier_semaphore()
    for target in targets:
        pl.semaphore_signal(barrier, inc=1, device_id=target, device_id_type=MESH)


def greeted_wait(count):
    pl.semaphore_wait(pltpu.get_barrier_semaphore(), count)


def split(value, size):
    if size & (size - 1) == 0:
        return lax.shift_right_logical(value, size.bit_length() - 1), value & (size - 1)
    return lax.div(value, size), lax.rem(value, size)


def around(place, step, size):
    return split(place + step, size)[1]


def neighbours(whole_plane):
    dp, lat, lon, dp_size, lat_size, lon_size = places()
    if whole_plane:
        steps = {(i, j) for i in range(lat_size) for j in range(lon_size)}
    else:
        steps = {(1, 0), (lat_size - 1, 0), (1, 1 % lon_size), (lat_size - 1, lon_size - 1)}
        steps |= {(2 * i, 0) for i in range(1, lat_size // 2)} | {(0, j) for j in range(lon_size)}
    steps.discard((0, 0))
    found = [(around(dp, step, dp_size), lat, lon) for step in range(1, dp_size)]
    return found + [
        (dp, around(lat, i, lat_size), around(lon, j, lon_size)) for i, j in sorted(steps)
    ]


def pairing(src, dst, sends, receives, send_slot, receive_slot, target):
    return pltpu.make_async_remote_copy(
        src_ref=src,
        dst_ref=dst,
        send_sem=sends.at[send_slot],
        recv_sem=receives.at[receive_slot],
        device_id=target,
        device_id_type=MESH,
    )


def gather_slots(sizes, splits):
    dp_size, lat_size, lon_size = sizes
    return splits * dp_size * (2 * max(lat_size // 2, lon_size) + 2)


def gather_steps(sizes, own_ref, all_ref, sends, receives, keep_sem):
    splits, skew = SPLITS, SKEW
    dp_size, lat_size, lon_size = sizes
    chips = lat_size // 2
    dp, lat, lon = lax.axis_index("dp"), lax.axis_index("lat"), lax.axis_index("lon")
    chip, core = split(lat, 2)
    wide = max(chips, lon_size)
    first = splits * dp_size
    second = first + splits * dp_size * wide
    cross = second + splits * dp_size * wide
    per = own_ref.shape[0] // splits
    order = sorted(range(dp_size), key=lambda step: min(step, dp_size - step))
    items = [(part, 0) for part in range(splits)]
    items += [(part, step) for part in range(splits) for step in order[1:]]

    def chip_at(step):
        return (dp, around(chip, step, chips) * 2 + core, lon)

    def lon_at(step):
        return (dp, lat, around(lon, step, lon_size))

    units = chips * lon_size

    def stretch(part, step, side, first, size):
        start = ((part * dp_size + around(dp, step, dp_size)) * 2 + side) * units + first
        return all_ref.at[pl.ds(start * per, size * per)]

    def run(mine, hooks, late_hook):
        unit = lon * chips + chip if mine == 0 else chip * lon_size + lon
        one, two = (chips, lon_size) if mine == 0 else (lon_size, chips)
        one_at, two_at = (chip_at, lon_at) if mine == 0 else (lon_at, chip_at)
        place_two = lon if mine == 0 else chip
        partner = (dp, chip * 2 + 1 - mine, lon)
        begun = []

        def send(src, dst, slot, back, target):
            copy = pairing(src, dst, sends, receives, slot, back, target)
            copy.start()
            begun.append(copy)

        def arrive(dst, slot):
            pairing(dst, dst, sends, receives, slot, slot, partner).wait_recv()

        def own_part(part):
            return own_ref.at[pl.ds(part * per, per)]

        def chunk(part, step):
            return stretch(part, step, mine, unit, 1)

        def group(part, step):
            return stretch(part, step, mine, place_two * one, one)

        def whole(part, step, side):
            return stretch(part, step, side, 0, units)

        keeps = []
        for part in range(splits):
            keep = pltpu.make_async_copy(own_part(part), chunk(part, 0), keep_sem.at[part])
            keep.start()
            keeps.append(keep)

        def line(part):
            for step in order[1:]:
                target = (around(dp, step, dp_size), lat, lon)
                base = part * dp_size
                send(own_part(part), chunk(part, 0), base + step, base + dp_size - step, target)

        def stage_one(part, step):
            if step:
                arrive(chunk(part, step), part * dp_size + step)
            base = first + (part * dp_size + step) * wide
            src = chunk(part, step) if step else own_part(part)
            for far in range(1, one):
                send(src, chunk(part, step), base + far, base + one - far, one_at(far))

        def stage_two(part, step):
            base = first + (part * dp_size + step) * wide
            for far in range(1, one):
                arrive(chunk(part, step), base + far)
            if step == 0:
                keeps[part].wait()
            base = second + (part * dp_size + step) * wide
            for far in range(1, two):
                send(group(part, step), group(part, step), base + far, base + two - far, two_at(far))

        def stage_three(part, step):
            base = second + (part * dp_size + step) * wide
            for far in range(1, two):
                arrive(group(part, step), base + far)
            slot = cross + part * dp_size + step
            send(whole(part, step, mine), whole(part, step, mine), slot, slot, partner)

        for part in range(splits):
            line(part)
        for turn in range(len(items) + 2 * skew):
            for stage, place in ((stage_one, turn), (stage_two, turn - skew), (stage_three, turn - 2 * skew)):
                if 0 <= place < len(items):
                    stage(*items[place])
            if turn in hooks:
                hooks[turn]()
        late_hook()
        for part, step in items:
            arrive(whole(part, step, 1 - mine), cross + part * dp_size + step)
        for copy in begun:
            copy.wait_send()

    return run


def move_slots(sizes, slots):
    dp_size, lat_size, lon_size = sizes
    spread = lat_size // 2 * lon_size
    moves = gather_slots(sizes, SPLITS)
    sums = moves + 16 * slots
    vectors = sums + 3 * (1 + spread + 2 * dp_size)
    hand = vectors + 1 + spread + dp_size
    return moves, sums, vectors, hand, hand + lat_size * lon_size


SPLITS = 2
SKEW = 3


def block_kernel(
    shape_info,
    inside,
    home_ref,
    lead_ref,
    homes_ref,
    master_ref,
    inputs_ref,
    cotangent_ref,
    entry_hbm,
    place_hbm,
    back_res_ref,
    back_in_ref,
    grads_ref,
    total_ref,
    spot_ref,
    weights_ref,
    entry_ref,
    place_ref,
    own_ref,
    all_ref,
    tok_ref,
    res_ref,
    flat_ref,
    mid_ref,
    earth_ref,
    gate_ref,
    bias_ref,
    dbias_ref,
    w1_ref,
    o1_ref,
    w2_ref,
    o2_ref,
    up_ref,
    down_ref,
    vec_ref,
    n1_ref,
    hat1_ref,
    inv1_ref,
    qkv_ref,
    probs_ref,
    att_ref,
    att1_ref,
    tok1_ref,
    n2_ref,
    hat2_ref,
    inv2_ref,
    mix2_ref,
    cprobs_ref,
    att2_ref,
    n3_ref,
    act_ref,
    gh_ref,
    delta3_ref,
    delta2_ref,
    delta1_ref,
    gmid_ref,
    glow_ref,
    gatt2_ref,
    gm2_ref,
    gm1_ref,
    vacc_ref,
    around_ref,
    sends,
    receives,
    keeps,
    fetched,
    kept,
    *sum_refs,
):
    levels = tok_ref.shape[5]
    chunks = 4
    sizes, buckets, tiles, slots_here, cuts = shape_info
    count = slots_here * levels
    tokens = count * AREA
    dp_size, lat_size, lon_size = sizes
    chips = lat_size // 2
    spread = chips * lon_size
    dp, lat, lon = lax.axis_index("dp"), lax.axis_index("lat"), lax.axis_index("lon")
    chip, core = split(lat, 2)
    is_last = lat == lat_size - 1
    moves, sum_slots, vector_slots, hand_slots, _ = move_slots(sizes, slots_here)
    begun = []

    def send(src, dst, slot, back, target):
        copy = pairing(src, dst, sends, receives, slot, back, target)
        copy.start()
        begun.append(copy)

    def arrive(dst, slot):
        pairing(dst, dst, sends, receives, slot, slot, (dp, lat, lon)).wait_recv()

    def pieces(kind, start, quads=range(4)):
        for quad in quads:
            up, left = quad // 2, quad % 2
            way = 1 if kind > 1 else -1
            target = (
                dp,
                around(lat, way * up % lat_size, lat_size),
                around(lon, way * left % lon_size, lon_size),
            )
            grid = (inputs_ref, cotangent_ref, back_res_ref, back_in_ref)[kind]
            for slot in range(slots_here):
                on_grid = grid.at[
                    slot,
                    pl.ds(HALF_LAT * (1 - up), HALF_LAT),
                    pl.ds(HALF_LON * (1 - left), HALF_LON),
                ]
                held = res_ref if kind > 1 else tok_ref
                in_quads = held.at[quad, kind % 2, :, :, slot]
                src, dst = (in_quads, on_grid) if kind > 1 else (on_grid, in_quads)
                place = 4 * slots_here * kind + slots_here * quad + slot
                if quad == 0:
                    copy = pltpu.make_async_copy(src, dst, kept.at[kind * slots_here + slot])
                    copy.start() if start else copy.wait()
                elif start:
                    send(src, dst, moves + place, moves + place, target)
                else:
                    arrive(dst, moves + place)

    def shift(kind, quads=range(4)):
        pieces(kind, True, quads)

    def shifted(kind):
        pieces(kind, False)

    def part(index):
        return pl.ds(pl.multiple_of(index * CHUNK, CHUNK), CHUNK)

    fetches = [
        pltpu.make_async_copy(source, target, fetched.at[index])
        for index, (source, target) in enumerate(
            (
                (master_ref, weights_ref),
                (entry_hbm, entry_ref),
                (place_hbm, place_ref),
            )
        )
    ]
    for fetch in fetches:
        fetch.start()
    def tokens_of(kind, c):
        return tok_ref[c, kind].astype(f32).reshape(CHUNK, D)

    def keep_tokens(kind, c, values):
        res_ref[c, kind] = values.reshape(res_ref.shape[2:]).astype(bf16)

    greeted = neighbours(inside)
    greet(greeted)

    per_home, own_rows = own_ref.shape[:2]
    flat_ref[pl.ds(0, per_home * own_rows), :] = jnp.zeros((per_home * own_rows, 128), f32)
    fetches[0].wait()
    for tile in range(tiles):
        flat_ref[pl.ds(tile, per_home, stride=own_rows), :] = weights_ref[
            :, 128 * tile : 128 * (tile + 1)
        ]
    for slot in range(per_home):
        own_ref[slot] = flat_ref[pl.ds(slot * own_rows, own_rows), :].astype(bf16)
    greeted_wait(len(greeted))

    def center_tokens():
        for bucket in range(buckets):
            home = home_ref[bucket]
            device, slot = split(home, per_home)
            rest, home_lon = split(device, lon_size)
            home_dp, home_lat = split(rest, lat_size)
            home_chip, home_core = split(home_lat, 2)
            unit = jnp.where(
                home_core == 0, home_lon * chips + home_chip, home_chip * lon_size + home_lon
            )
            side, inner = split(slot, per_home // SPLITS)
            chunk = (side * dp_size + home_dp) * 2 + home_core
            spot_ref[bucket] = (chunk * spread + unit) * (per_home // SPLITS) + inner
        shifted(0)

        @pl.loop(0, chunks)
        def _(c):
            rows = part(c)
            hat, inverse = normed(tokens_of(0, c))
            hat1_ref[rows, :] = hat
            inv1_ref[rows, :] = jnp.broadcast_to(inverse, (CHUNK, 128))

    gather = gather_steps(sizes, own_ref, all_ref, sends, receives, keeps)
    hooks = {0: functools.partial(shift, 0)}
    for mine in range(2):

        @pl.when(core == mine)
        def _():
            gather(mine, hooks, center_tokens)
            for copy in begun:
                copy.wait_send()
            begun.clear()

    shift(1)
    for fetch in fetches[1:]:
        fetch.wait()
    vacc_ref[...] = jnp.zeros_like(vacc_ref)
    marks = offsets(lat_size + 1)
    row_marks = [mark // 128 for mark in marks]

    for bucket in range(buckets):
        block = all_ref[spot_ref[bucket]].astype(f32)
        flat_ref[tiles * bucket : tiles * (bucket + 1), :] = block[:tiles]

    def take_pairs(base, parts, pairs):
        return [flat_ref[pl.ds(base + part, pairs, stride=parts), :] for part in range(parts)]

    def give_pairs(columns, rows, evens, odds):
        for column, (even, odd) in enumerate(zip(evens, odds)):
            mid_ref[column, pl.ds(0, rows // 2, stride=2), :] = even
            mid_ref[column, pl.ds(1, rows // 2, stride=2), :] = odd

    def load_qkv(base, ref):
        b = take_pairs(base, 9, D // 2)
        pieces = []
        for first in range(0, 9, 3):
            x, y, z = b[first : first + 3]
            pieces += [
                lanes_from(x, x, 0, SIDE),
                lanes_from(x, y, 96, SIDE),
                lanes_from(y, z, 64, SIDE),
                lanes_from(z, z, 32, SIDE),
            ]
        give_pairs(6, D, pieces[:6], pieces[6:])
        for column in range(6):
            ref[:, 128 * column : 128 * (column + 1)] = mid_ref[column, pl.ds(0, D), :].astype(bf16)

    def load_square(base, rows, ref, spans):
        b = take_pairs(base, 3, rows // 2)
        odds = [lanes_from(b[1], b[2], 64, 128), lanes_from(b[2], b[2], 64, D - 128)]
        give_pairs(2, rows, [b[0], b[1]], odds)
        for first, last, target in spans:
            size = last - first
            ref[target : target + size, 0:128] = mid_ref[0, pl.ds(first, size), :].astype(bf16)
            ref[target : target + size, 128:D] = mid_ref[1, pl.ds(first, size), :][
                :, : D - 128
            ].astype(bf16)

    sides = [(0, SIDE, 0), (SIDE, D, 128)]
    load_qkv(row_marks[0], w1_ref)
    load_square(row_marks[1], D, o1_ref, sides)
    load_qkv(row_marks[2], w2_ref)
    load_square(row_marks[3], D, o2_ref, sides)
    for ref in (o1_ref, o2_ref):
        for side in range(2):
            ref[128 * side + SIDE : 128 * (side + 1), :] = jnp.zeros((128 - SIDE, D), bf16)
    for column in range(6):
        up_ref[:, 128 * column : 128 * (column + 1)] = flat_ref[
            pl.ds(row_marks[4] + column, D, stride=6), :
        ].astype(bf16)
    load_square(row_marks[5], FF, down_ref, [(0, FF, 0)])
    for index in range(9):
        start = marks[7] + D * index
        vec_ref[index : index + 1, 0:128] = lanes_of(flat_ref, start)
        vec_ref[index : index + 1, 128:D] = lanes_of(flat_ref, start + 128)[:, : D - 128]

    def earth_places():
        group_one = lat + 1
        group_two = jnp.where(is_last, 0, lat + 1)
        for index in range(EARTH_ROWS):
            group = group_one if index % WIN_LAT < HALF_LAT else group_two
            start = marks[6] + EARTH_ROW * (EARTH_ROWS * group + index)
            yield (index,) + split(start, 128)

    lane_place = lax.broadcasted_iota(jnp.int32, (1, 128), 1)
    earth_ref[...] = jnp.zeros_like(earth_ref)
    for index, row, lane in earth_places():
        rows = [flat_ref[pl.ds(row + step, 1), :] for step in range(3)]
        back = (128 - lane) & 127
        first = pltpu.roll(jnp.where(lane_place >= lane, rows[0], rows[1]), back, 1)
        second = pltpu.roll(jnp.where(lane_place >= lane, rows[1], rows[2]), back, 1)
        earth_ref[index : index + 1, 0:128] = first
        earth_ref[index : index + 1, 128:256] = jnp.where(lane_place < EARTH_ROW - 128, second, 0.0)
    earth = earth_ref[...].astype(bf16)
    key_up = lax.broadcasted_iota(jnp.int32, (AREA, LANES), 0) // (2 * QUAD)
    query_up = lax.broadcasted_iota(jnp.int32, (AREA, LANES), 1) & (LANES // 2 - 1)
    query_up = lax.rem(query_up, HEAD_ROWS) // (2 * QUAD)
    bias = jnp.where((key_up != query_up) & is_last, penalty_value, 0.0)
    for column in range(WIN_LON):
        bias = bias + nn(nt(entry_ref[column], earth).astype(bf16), place_ref[column])
    bias_ref[...] = bias

    for slot in range(slots_here):
        number = lax.axis_index("dp") * slots_here + slot
        sample, lead = split(number, LEADS)
        live = lead < lead_ref[sample]
        size = count // slots_here
        gate_ref[slot * size : (slot + 1) * size, :] = jnp.full((size, D), jnp.where(live, 1.0, 0.0), f32)

    def vec(index):
        return vec_ref[index : index + 1, :]

    def gate_rows():
        gate = gate_ref[...]
        return jnp.broadcast_to(gate[None], (CHUNK // count, count, D)).reshape(CHUNK, D)

    def note(index, values):
        vacc_ref[index] += row_fold(values)

    def note_low(index, values):
        top = lax.broadcasted_iota(jnp.int32, (8, CHUNK), 0) == 0
        vacc_ref[index] += nn(jnp.where(top, 1.0, 0.0).astype(bf16), values)

    def first_mixed(c):
        rows = part(c)
        low = (hat1_ref[rows, :] * vec(0) + vec(1)).astype(bf16)
        n1_ref[rows, :] = low
        mixed = rounded(nn(low, w1_ref[...]))
        for tile in range(6):
            qkv_ref[tile, rows, :] = mixed[:, 128 * tile : 128 * (tile + 1)]

    for c in range(chunks):
        first_mixed(c)

    def window(ref, tile, s):
        return ref[tile, pl.ds(s, AREA, stride=count), :]

    def window_store(ref, tile, s, values):
        ref[tile, pl.ds(s, AREA, stride=count), :] = values

    halves = [slice(0, LANES // 2), slice(LANES // 2, LANES)]

    @pl.loop(0, count // 4)
    def _(block):
        masks = head_masks()
        places = [(block * 4 + step, side) for step in range(4) for side in range(2)]
        reads = [[window(qkv_ref, 2 * kind + side, s) for kind in range(3)] for s, side in places]
        raw = [
            nt(key.astype(bf16), spread_window(query, masks)) for query, key, _ in reads
        ]
        probs = [
            soft_columns(scores * SCALE + bias_ref[:, halves[side]])
            for scores, (_, side) in zip(raw, places)
        ]
        outs = [tn(prob.astype(bf16), read[2].astype(bf16)) for prob, read in zip(probs, reads)]
        for (s, side), prob, out in zip(places, probs, outs):
            probs_ref[s, :, halves[side]] = prob
            window_store(att_ref, side, s, fold_heads(out, HEAD_ROWS, AREA))

    def second_mixed(c):
        rows = part(c)
        att = jnp.concatenate([att_ref[0, rows, :], att_ref[1, rows, :]], axis=1).astype(bf16)
        att1_ref[rows, :] = att
        branch = nn(att, o1_ref[...]) + vec(2)
        tok = tokens_of(0, c) + gate_rows() * branch
        tok1_ref[rows, :] = tok
        hat, inverse = normed(tok)
        hat2_ref[rows, :] = hat
        inv2_ref[rows, :] = jnp.broadcast_to(inverse, (CHUNK, 128))
        low = (hat * vec(3) + vec(4)).astype(bf16)
        n2_ref[rows, :] = low
        mix2_ref[rows, :] = nn(low, w2_ref[...]).astype(bf16)

    for c in range(chunks):
        second_mixed(c)

    def column_masks():
        lane = lax.broadcasted_iota(jnp.int32, (8, GLANES), 1)
        place = lax.shift_right_logical(lane & (GROUP - 1), 3)
        return [place == index for index in range(GROUP // 8)]

    def squeeze_column(values, masks):
        out = values[:8]
        for index in range(1, GROUP // 8):
            out = jnp.where(masks[index], values[8 * index : 8 * index + 8], out)
        return out

    def widen_column(values, masks):
        return jnp.concatenate([jnp.where(mask, values, 0.0) for mask in masks], axis=0).astype(bf16)

    def group_rows(g):
        return pl.ds(pl.multiple_of(g * GROUP, GROUP), GROUP)

    def tile_of(ref, g, kind, side):
        first = WIDE * kind + 128 * side
        return ref[group_rows(g), first : first + 128]

    @pl.loop(0, tokens // GROUP // 6)
    def _(block):
        heads = head_masks()
        columns = column_masks()
        places = [(block * 6 + step, side) for step in range(6) for side in range(2)]
        reads = [[tile_of(mix2_ref, g, kind, side) for kind in range(3)] for g, side in places]
        raw = [nt(key, spread_heads(query, heads)) for query, key, _ in reads]
        probs = [soft_columns(squeeze_column(scores, columns) * SCALE) for scores in raw]
        outs = [tn(widen_column(prob, columns), read[2]) for prob, read in zip(probs, reads)]
        for (g, side), prob, out in zip(places, probs, outs):
            cprobs_ref[g, side] = prob
            att2_ref[group_rows(g), 128 * side : 128 * (side + 1)] = fold_heads(
                out, GROUP, GROUP
            ).astype(bf16)

    root = math.sqrt(2.0 / math.pi)
    shifted(1)

    @pl.loop(0, chunks)
    def _(c):
        rows = part(c)
        gate = gate_rows()
        tok = tok1_ref[rows, :] + gate * (nn(att2_ref[rows, :], o2_ref[...]) + vec(5))
        hat, inverse = normed(tok)
        low = (hat * vec(6) + vec(7)).astype(bf16)
        n3_ref[rows, :] = low
        hidden = nn(low, up_ref[...])
        square = hidden * hidden
        half = 0.5 * jnp.tanh(hidden * (root + (root * 0.044715) * square)) + 0.5
        wave = hidden * half
        act = wave.astype(bf16)
        act_ref[rows, :] = act
        keep_tokens(0, c, tok + gate * (nn(act, down_ref[...]) + vec(8)))
        slope = half + wave * (1.0 - half) * (2.0 * root + (6.0 * root * 0.044715) * square)
        after = tokens_of(1, c)
        delta3 = (gate * after).astype(bf16)
        delta3_ref[rows, :] = delta3
        note_low(8, delta3)
        gh = (nt(delta3, down_ref[...]) * slope).astype(bf16)
        gh_ref[rows, :] = gh
        grad = nt(gh, up_ref[...])
        note(6, grad * hat)
        note(7, grad)
        mid = after + norm_back(grad, hat, inverse, vec(6))
        gmid_ref[rows, :] = mid
        delta2 = (gate * mid).astype(bf16)
        delta2_ref[rows, :] = delta2
        note_low(5, delta2)
        gatt2_ref[rows, :] = nt(delta2, o2_ref[...]).astype(bf16)

    def keep_pairs(base, parts, blocks):
        for number, block in enumerate(blocks):
            flat_ref[pl.ds(base + number, block.shape[0], stride=parts), :] = block

    def split_pairs(columns, rows):
        evens = [mid_ref[column, pl.ds(0, rows // 2, stride=2), :] for column in range(columns)]
        odds = [mid_ref[column, pl.ds(1, rows // 2, stride=2), :] for column in range(columns)]
        return evens, odds

    def save_qkv(base, grad):
        for column in range(6):
            mid_ref[column, pl.ds(0, D), :] = grad[:, 128 * column : 128 * (column + 1)]
        e, o = split_pairs(6, D)
        pieces = e + o
        blocks = []
        for first in range(0, 12, 4):
            x, y, z, w = pieces[first : first + 4]
            blocks += [
                lanes_join(x, 0, 96, y),
                lanes_join(y, 32, 64, z),
                lanes_join(z, 64, 32, w),
            ]
        keep_pairs(base, 9, blocks)

    def save_square(base, rows, grad):
        mid_ref[0, pl.ds(0, rows), :] = grad[:, :128]
        mid_ref[1, pl.ds(0, rows), 0 : D - 128] = grad[:, 128:]
        e, o = split_pairs(2, rows)
        keep_pairs(
            base, 3, [e[0], lanes_join(e[1], 0, 64, o[0]), lanes_join(o[0], 64, 64, o[1])]
        )

    def used_rows(grad):
        return jnp.concatenate([grad[0:SIDE], grad[128 : 128 + SIDE]], axis=0)

    partner = (dp, chip * 2 + 1 - core, lon)
    place = chip * lon_size + lon

    def peers():
        for i in range(chips):
            for j in range(lon_size):
                if i or j:
                    back = (chips - i) % chips * lon_size + (lon_size - j) % lon_size
                    there = (around(chip, i, chips), around(lon, j, lon_size))
                    target = (dp, there[0] * 2 + core, there[1])
                    yield i * lon_size + j, back, there[0] * lon_size + there[1], target

    def line():
        for step in range(1, dp_size):
            there = around(dp, step, dp_size)
            yield step, dp_size - step, there, (there, lat, lon)

    def summing(base, grad, half_in, half, plane_in, mid, line_in, full):
        n_half = grad.shape[0] // 2
        n_place = n_half // spread
        n_line = n_place // dp_size

        def cross():
            send(grad.at[pl.ds((1 - core) * n_half, n_half)], half_in, base, base, partner)

        def plane():
            arrive(half_in, base)
            for first in range(0, n_half, 12):
                rows = pl.ds(first, 12)
                kept = grad[pl.ds(core * n_half + first, 12)].astype(f32)
                half[rows] = (kept + half_in[rows].astype(f32)).astype(bf16)
            for index, back, there, target in peers():
                send(
                    half.at[pl.ds(there * n_place, n_place)],
                    plane_in.at[back],
                    base + 1 + index,
                    base + 1 + back,
                    target,
                )

        def along():
            total = half[pl.ds(place * n_place, n_place)].astype(f32)
            for index in range(1, spread):
                arrive(plane_in.at[index], base + 1 + index)
                total = total + plane_in[index].astype(f32)
            mid[...] = total.astype(bf16)
            slots = base + 1 + spread
            for step, back, there, target in line():
                send(mid.at[pl.ds(there * n_line, n_line)], line_in.at[back], slots + step, slots + back, target)

        def share():
            slots = base + 1 + spread
            rows = pl.ds(dp * n_line, n_line)
            total = mid[rows].astype(f32)
            for step in range(1, dp_size):
                arrive(line_in.at[step], slots + step)
                total = total + line_in[step].astype(f32)
            full[rows] = total.astype(bf16)
            slots += dp_size
            for step, back, _, target in line():
                send(full.at[rows], full.at[rows], slots + step, slots + back, target)

        def done():
            slots = base + 1 + spread + dp_size
            for step, _, there, _ in line():
                arrive(full.at[pl.ds(there * n_line, n_line)], slots + step)

        return cross, plane, along, share, done

    spans = [[(cuts[1], cuts[2])], [(cuts[0], cuts[1])], [(0, cuts[0]), (cuts[2], buckets)]]
    if inside:
        sum_sets = [sum_refs[7 * number : 7 * (number + 1)] for number in range(3)]
        hand_out, vec_sum, vec_in, vec_now = sum_refs[21:]
        each = 1 + spread + 2 * dp_size
        soon, early, late = [
            summing(sum_slots + each * number, *refs) for number, refs in enumerate(sum_sets)
        ]

        def pack(number):
            grad = sum_sets[number][0]
            for tile in range(grad.shape[0]):
                if tile < tiles:
                    rows = [
                        flat_ref[pl.ds(tile + tiles * begin, end - begin, stride=tiles), :]
                        for begin, end in spans[number]
                    ]
                    values = rows[0] if len(rows) == 1 else jnp.concatenate(rows, axis=0)
                    grad[tile] = values.astype(bf16)
                else:
                    grad[tile] = jnp.zeros(grad.shape[1:], bf16)
    else:
        (vec_sum,) = sum_refs

    shift(2)

    grad_up = tn(n3_ref[...], gh_ref[...])
    for column in range(6):
        flat_ref[pl.ds(row_marks[4] + column, D, stride=6), :] = grad_up[
            :, 128 * column : 128 * (column + 1)
        ]
    save_square(row_marks[5], FF, tn(act_ref[...], delta3_ref[...]))
    if inside:
        pack(0)
        soon[0]()


    @pl.loop(0, tokens // GROUP // 6)
    def _(block):
        heads = head_masks()
        columns = column_masks()
        places = [(block * 6 + step, side) for step in range(6) for side in range(2)]
        reads = [
            [tile_of(mix2_ref, g, kind, side) for kind in range(3)]
            + [tile_of(gatt2_ref, g, 0, side), cprobs_ref[g, side]]
            for g, side in places
        ]
        grads = [spread_heads(read[3], heads) for read in reads]
        raw = [nt(read[2], grad) for read, grad in zip(reads, grads)]
        dvalues = [nn(widen_column(read[4], columns), grad) for read, grad in zip(reads, grads)]
        lows = [
            widen_column(soft_back(read[4], squeeze_column(slopes, columns)), columns)
            for read, slopes in zip(reads, raw)
        ]
        dkeys = [nn(low, spread_heads(read[0], heads)) for read, low in zip(reads, lows)]
        dqueries = [tn(low, read[1]) for read, low in zip(reads, lows)]
        for (g, side), dquery, dkey, dvalue in zip(places, dqueries, dkeys, dvalues):
            for kind, values in enumerate(
                (fold_heads(dquery, GROUP, GROUP) * SCALE, dkey * SCALE, dvalue)
            ):
                first = WIDE * kind + 128 * side
                gm2_ref[group_rows(g), first : first + 128] = values.astype(bf16)

    if inside:
        soon[1]()

    def second_back(c):
        rows = part(c)
        grad = nt(gm2_ref[rows, :], w2_ref[...])
        hat = hat2_ref[rows, :]
        inverse = inv2_ref[rows, :][:, :1]
        note(3, grad * hat)
        note(4, grad)
        low = gmid_ref[rows, :] + norm_back(grad, hat, inverse, vec(3))
        glow_ref[rows, :] = low
        delta1 = (gate_rows() * low).astype(bf16)
        delta1_ref[rows, :] = delta1
        note_low(2, delta1)
        gatt = rounded(nt(delta1, o1_ref[...]))
        att_ref[0, rows, :] = gatt[:, :128]
        att_ref[1, rows, :] = gatt[:, 128:]

    for c in range(chunks):
        second_back(c)

    save_square(row_marks[1], D, used_rows(tn(att1_ref[...], delta1_ref[...])))
    save_qkv(row_marks[2], tn(n2_ref[...], gm2_ref[...]))
    save_square(row_marks[3], D, used_rows(tn(att2_ref[...], delta2_ref[...])))

    if inside:
        pack(1)
        early[0]()
        soon[2]()

    dbias_ref[...] = jnp.zeros_like(dbias_ref)

    def window_back(block):
        masks = head_masks()
        places = [(block * 4 + step, side) for step in range(4) for side in range(2)]
        reads = [
            [window(qkv_ref, 2 * kind + side, s) for kind in range(3)]
            + [window(att_ref, side, s), probs_ref[s, :, halves[side]]]
            for s, side in places
        ]
        grads = [spread_window(read[3], masks) for read in reads]
        raw = [nt(read[2].astype(bf16), grad) for read, grad in zip(reads, grads)]
        dvalues = [nn(read[4].astype(bf16), grad) for read, grad in zip(reads, grads)]
        lows = [soft_back(read[4], slopes).astype(bf16) for read, slopes in zip(reads, raw)]
        dkeys = [nn(low, spread_window(read[0], masks)) for read, low in zip(reads, lows)]
        dqueries = [tn(low, read[1].astype(bf16)) for read, low in zip(reads, lows)]
        for side in range(2):
            dbias_ref[:, halves[side]] += functools.reduce(
                jnp.add, [low.astype(f32) for low, (_, there) in zip(lows, places) if there == side]
            )
        for (s, side), dquery, dkey, dvalue in zip(places, dqueries, dkeys, dvalues):
            dquery = fold_heads(dquery, HEAD_ROWS, AREA) * SCALE
            for kind, values in enumerate((dquery, dkey * SCALE, dvalue)):
                window_store(qkv_ref, 2 * kind + side, s, rounded(values))

    @pl.loop(0, 2)
    def _(block):
        window_back(block)

    if inside:
        early[1]()
        soon[3]()

    @pl.loop(2, count // 4)
    def _(block):
        window_back(block)

    @pl.loop(0, chunks)
    def _(c):
        rows = part(c)
        gm1_ref[rows, :] = jnp.concatenate(
            [qkv_ref[tile, rows, :] for tile in range(6)], axis=1
        ).astype(bf16)

    save_qkv(row_marks[0], tn(n1_ref[...], gm1_ref[...]))
    rest = flat_ref.shape[0] - row_marks[6]
    around_ref[...] = jnp.zeros_like(around_ref)
    dbias = dbias_ref[...].astype(bf16)
    moved = [nt(dbias, place_ref[column]).astype(bf16) for column in range(WIN_LON)]
    dearth = functools.reduce(
        jnp.add, [tn(moved[column], entry_ref[column]) for column in range(WIN_LON)]
    )
    for index, row, lane in earth_places():
        row = row - row_marks[6]
        first = pltpu.roll(dearth[index : index + 1, :128], lane, 1)
        second = pltpu.roll(dearth[index : index + 1, 128:], lane, 1)
        tail = lane_place >= lane
        for step, values in enumerate(
            (
                jnp.where(tail, first, 0.0),
                jnp.where(tail, second, first),
                jnp.where(tail, 0.0, second),
            )
        ):
            around_ref[index % 4, pl.ds(row + step, 1), :] += values
    flat_ref[row_marks[6] :, :] = functools.reduce(
        jnp.add, [around_ref[number, 0:rest, :] for number in range(4)]
    )
    if inside:
        early[2]()
        pack(2)
        late[0]()

    def input_grads(c):
        rows = part(c)
        mixed = gm1_ref[rows, :]
        grad = nt(mixed, w1_ref[...])
        hat = hat1_ref[rows, :]
        inverse = inv1_ref[rows, :][:, :1]
        note(0, grad * hat)
        note(1, grad)
        grad_in = glow_ref[rows, :] + norm_back(grad, hat, inverse, vec(0))
        keep_tokens(1, c, grad_in)

    @pl.loop(2, chunks)
    def _(c):
        input_grads(c)

    if inside:
        late[1]()

    @pl.loop(0, 2)
    def _(c):
        input_grads(1 - c)

    for index in range(9):
        vec_sum[index : index + 1, :] = jnp.sum(vacc_ref[index], axis=0, keepdims=True)
    if inside:
        send(vec_sum, vec_in.at[0], vector_slots, vector_slots, partner)
        early[3]()
        arrive(vec_in.at[0], vector_slots)
        vec_now[0] = vec_sum[...] + vec_in[0]
        for index, back, _, target in peers():
            send(vec_now.at[0], vec_in.at[back], vector_slots + 1 + index, vector_slots + 1 + back, target)
    shift(3)
    if inside:
        late[2]()
        vec_total = vec_now[0]
        for index in range(1, spread):
            arrive(vec_in.at[index], vector_slots + 1 + index)
            vec_total = vec_total + vec_in[index]
        vec_now[1] = vec_total
        slots = vector_slots + 1 + spread
        for step, back, _, target in line():
            send(vec_now.at[1], vec_in.at[spread + back], slots + step, slots + back, target)
        late[3]()
        soon[4]()
        early[4]()
        homes = lat_size * lon_size
        width = homes * per_home
        slot_ids = lax.broadcasted_iota(jnp.int32, (width, 1), 0) + dp * width
        all_homes = homes_ref[...]
        picks = []
        for some in spans:
            held = [all_homes[:, begin:end] for begin, end in some]
            held = held[0] if len(held) == 1 else jnp.concatenate(held, axis=1)
            picks.append(jnp.where(slot_ids == held, 1.0, 0.0).astype(bf16))
        n_rows = hand_out.shape[1]
        owned_first = [
            nn(picks[0], sum_sets[0][6][row]) + nn(picks[1], sum_sets[1][6][row])
            for row in range(n_rows)
        ]
        late[4]()
        for row in range(n_rows):
            owned = owned_first[row] + nn(picks[2], sum_sets[2][6][row])
            for home in range(homes):
                hand_out[home, row] = owned[per_home * home : per_home * (home + 1), :].astype(bf16)
        first = core * (n_rows * spread) + place * n_rows
        landing = grads_ref.at[pl.ds(first, n_rows)]
        me = lat * lon_size + lon
        keep_hand = pltpu.make_async_copy(hand_out.at[me], landing, keeps.at[SPLITS])
        keep_hand.start()
        for i in range(lat_size):
            for j in range(lon_size):
                if i or j:
                    target = (dp, around(lat, i, lat_size), around(lon, j, lon_size))
                    back = (lat_size - i) % lat_size * lon_size + (lon_size - j) % lon_size
                    send(
                        hand_out.at[target[1] * lon_size + target[2]],
                        landing,
                        hand_slots + i * lon_size + j,
                        hand_slots + back,
                        target,
                    )
        for step in range(1, dp_size):
            arrive(vec_in.at[spread + step], slots + step)
            vec_total = vec_total + vec_in[spread + step]
        total_ref[...] = vec_total
        keep_hand.wait()
        for index in range(1, homes):
            arrive(landing, hand_slots + index)
    else:
        total_ref[...] = vec_sum[...]
        for tile in range(tiles):
            grads_ref[tile] = flat_ref[pl.ds(tile, buckets, stride=tiles), :]
    shifted(2)
    shifted(3)
    for copy in begun:
        copy.wait_send()


def sum_rows(sizes, tiles):
    unit = sizes[0] * sizes[1] * sizes[2]
    rows = -(-tiles // unit) * unit
    return rows, rows <= 2 * tiles


def block_call(homes, leads, master, inputs, cotangent, sizes):
    slots_here, levels = inputs.shape[0], inputs.shape[3]
    count = slots_here * levels
    tokens = count * AREA
    buckets = homes.shape[0]
    per_home, width = master.shape
    tiles = width // 128
    own_rows = -(-tiles // 16) * 16
    quads = (4, 2, HALF_LAT, HALF_LON, slots_here, levels, D)
    dp_size, lat_size, lon_size = sizes
    spread = lat_size // 2 * lon_size
    rows, inside = sum_rows(sizes, tiles)
    marks = offsets(lat_size + 1)
    low = -(-marks[1] // width)
    mid = -(-marks[4] // width)
    high = marks[6] // width
    mid += (high - mid) % 8
    low += (mid - low) % 8
    cuts = (low, mid, high)
    shape = jax.ShapeDtypeStruct
    outs = [
        shape(inputs.shape, bf16),
        shape(inputs.shape, bf16),
        shape((rows, per_home, 128), bf16) if inside else shape((tiles, buckets, 128), f32),
        shape((9, D), f32),
    ]
    vmem = pltpu.VMEM
    entry, place = earth_tables()
    scratch = [
        pltpu.SMEM((buckets,), jnp.int32),
        vmem(master.shape, f32),
        vmem(entry.shape, bf16),
        vmem(place.shape, bf16),
        vmem((per_home, own_rows, 128), bf16),
        vmem((dp_size * lat_size * lon_size * per_home, own_rows, 128), bf16),
        vmem(quads, bf16),
        vmem(quads, bf16),
        vmem((buckets * tiles, 128), f32),
        vmem((6, FF, 128), f32),
        vmem((40, 256), f32),
        vmem((count, D), f32),
        vmem((AREA, LANES), f32),
        vmem((AREA, LANES), f32),
        vmem((D, 3 * WIDE), bf16),
        vmem((WIDE, D), bf16),
        vmem((D, 3 * WIDE), bf16),
        vmem((WIDE, D), bf16),
        vmem((D, FF), bf16),
        vmem((FF, D), bf16),
        vmem((16, D), f32),
        vmem((tokens, D), bf16),
        vmem((tokens, D), f32),
        vmem((tokens, 128), f32),
        vmem((6, tokens, 128), f32),
        vmem((count, AREA, LANES), f32),
        vmem((2, tokens, 128), f32),
        vmem((tokens, WIDE), bf16),
        vmem((tokens, D), f32),
        vmem((tokens, D), bf16),
        vmem((tokens, D), f32),
        vmem((tokens, 128), f32),
        vmem((tokens, 3 * WIDE), bf16),
        vmem((tokens // GROUP, 2, 8, GLANES), f32),
        vmem((tokens, WIDE), bf16),
        vmem((tokens, D), bf16),
        vmem((tokens, FF), bf16),
        vmem((tokens, FF), bf16),
        vmem((tokens, D), bf16),
        vmem((tokens, D), bf16),
        vmem((tokens, D), bf16),
        vmem((tokens, D), f32),
        vmem((tokens, D), f32),
        vmem((tokens, WIDE), bf16),
        vmem((tokens, 3 * WIDE), bf16),
        vmem((tokens, 3 * WIDE), bf16),
        vmem((9, 8, D), f32),
        vmem((4, buckets * tiles - marks[6] // 128, 128), f32),
        pltpu.SemaphoreType.DMA((move_slots(sizes, slots_here)[-1],)),
        pltpu.SemaphoreType.DMA((move_slots(sizes, slots_here)[-1],)),
        pltpu.SemaphoreType.DMA((SPLITS + 1,)),
        pltpu.SemaphoreType.DMA((3,)),
        pltpu.SemaphoreType.DMA((4 * slots_here,)),
    ]
    if inside:
        n_place = rows // 2 // spread
        for some in (high - mid, mid - low, buckets - (high - low)):
            scratch += [
                vmem((rows, some, 128), bf16),
                vmem((rows // 2, some, 128), bf16),
                vmem((rows // 2, some, 128), bf16),
                vmem((spread, n_place, some, 128), bf16),
                vmem((n_place, some, 128), bf16),
                vmem((dp_size, n_place // dp_size, some, 128), bf16),
                vmem((n_place, some, 128), bf16),
            ]
        scratch += [
            vmem((lat_size * lon_size, n_place, per_home, 128), bf16),
            vmem((9, D), f32),
            vmem((spread + dp_size, 9, D), f32),
            vmem((2, 9, D), f32),
        ]
    else:
        scratch += [vmem((9, D), f32)]
    spec = pl.BlockSpec(memory_space=pltpu.VMEM)
    smem = pl.BlockSpec(memory_space=pltpu.SMEM)
    hbm = pl.BlockSpec(memory_space=pl.ANY)
    return pl.pallas_call(
        functools.partial(block_kernel, (sizes, buckets, tiles, slots_here, cuts), inside),
        out_shape=outs,
        in_specs=[smem, smem, spec] + [hbm] * 5,
        out_specs=[hbm, hbm, spec, spec],
        scratch_shapes=scratch,
        compiler_params=pltpu.CompilerParams(
            vmem_limit_bytes=62 * 1024 * 1024, collective_id=0, has_side_effects=True
        ),
        name="block",
    )(
        homes,
        leads,
        homes[None, :],
        master,
        inputs,
        cotangent,
        jnp.asarray(entry),
        jnp.asarray(place),
    )


def finish_kernel(
    marks,
    steps_ref,
    homes_ref,
    grads_ref,
    vectors_ref,
    master_ref,
    one_ref,
    two_ref,
    back_res_ref,
    back_in_ref,
    result_ref,
    grad_inputs_ref,
    grad_vectors_ref,
    new_master,
    new_one,
    new_two,
    spare_ref,
):
    homes, width = master_ref.shape
    tiles = width // 128
    for slot in range(result_ref.shape[0]):
        result_ref[slot] = back_res_ref[slot]

        @pl.loop(0, WIN_LAT)
        def _(row):
            grad_inputs_ref[slot, row] = back_in_ref[slot, row].astype(f32)

    grad_vectors_ref[...] = vectors_ref[...]
    place = lax.axis_index("dp") * lax.axis_size("lat") + lax.axis_index("lat")
    place = (place * lax.axis_size("lon") + lax.axis_index("lon")) * homes
    slots = lax.broadcasted_iota(jnp.int32, (homes, 1), 0) + place
    match = homes_ref[...] == slots
    bucket = lax.broadcasted_iota(jnp.int32, match.shape, 1)
    held = jnp.max(jnp.where(match, bucket, -1), axis=1, keepdims=True)
    base = jnp.where(held >= 0, held * width, marks[8])

    top = marks[7] // 128
    spare_ref[...] = jnp.zeros_like(spare_ref)
    lanes = lax.broadcasted_iota(jnp.int32, (1, 128), 1)
    for index in range(9):
        vector = vectors_ref[index : index + 1, :]
        start = marks[7] + D * index
        tail = jnp.concatenate([vector[:, 128:], jnp.zeros((1, 256 - D), f32)], axis=1)
        for values, size, begin in ((vector[:, :128], 128, start), (tail, D - 128, start + 128)):
            row, lane = divmod(begin - 128 * top, 128)
            moved = pltpu.roll(values, lane, 1) if lane else values
            spare_ref[row : row + 1, :] += jnp.where(lanes >= lane, moved, 0.0)
            if lane + size > 128:
                spare_ref[row + 1 : row + 2, :] += jnp.where(lanes < lane, moved, 0.0)

    steps = jnp.full((homes, 128), steps_ref[0], jnp.int32).astype(f32)
    fix_one = 1.0 / (1.0 - jnp.exp(steps * math.log(beta_one)))
    fix_two = 1.0 / (1.0 - jnp.exp(steps * math.log(beta_two)))
    rates = [
        2.6 / math.sqrt(D),
        8.0 / math.sqrt(D),
        2.6 / math.sqrt(D),
        4.0 / math.sqrt(D),
        2.0 / math.sqrt(D),
        3.0 / math.sqrt(FF),
        1.0,
        0.6,
    ]
    spread = jnp.broadcast_to(base, (homes, 128)) + lax.broadcasted_iota(jnp.int32, (homes, 128), 1)
    for tile in range(tiles):
        columns = slice(128 * tile, 128 * (tile + 1))
        index = spread + 128 * tile
        rate = jnp.full((homes, 128), 0.1, f32)
        for number in range(7, -1, -1):
            rate = jnp.where(index < marks[number + 1], rates[number], rate)
        grad = grads_ref[tile].astype(f32)
        for owner in range(marks[7] // width, (marks[8] - 1) // width + 1):
            row = owner * tiles + tile - top
            if 0 <= row < spare_ref.shape[0]:
                grad = grad + jnp.where(held == owner, spare_ref[row : row + 1, :], 0.0)
        weights = master_ref[:, columns]
        first = beta_one * one_ref[:, columns] + (1.0 - beta_one) * grad
        second = beta_two * two_ref[:, columns] + (1.0 - beta_two) * grad * grad
        step = first * fix_one / (jnp.sqrt(second * fix_two) + eps_adam) + decay_rate * weights
        new_master[:, columns] = weights - rate * step
        new_one[:, columns] = first
        new_two[:, columns] = second


def finish_call(marks, steps, homes, grads, vectors, master, one, two, back_res, back_in):
    smem = pl.BlockSpec(memory_space=pltpu.SMEM)
    vmem = pl.BlockSpec(memory_space=pltpu.VMEM)
    grid = back_res.shape
    shape = jax.ShapeDtypeStruct
    return pl.pallas_call(
        functools.partial(finish_kernel, marks),
        out_shape=[shape(grid, bf16), shape(grid, f32), shape(vectors.shape, f32)]
        + [shape(master.shape, f32)] * 3,
        in_specs=[smem] + [vmem] * 8,
        out_specs=[vmem] * 6,
        scratch_shapes=[
            pltpu.VMEM((16, 128), f32),
        ],
        name="finish",
    )(steps, homes[None, :], grads, vectors, master, one, two, back_res, back_in)


def per_device(
    inputs, cotangent, lead_counts, home_slots, master, moment_one, moment_two, step_count
):
    axes = ("dp", "lat", "lon")
    sizes = tuple(lax.axis_size(axis) for axis in axes)
    slots_mine, bucket_width = master.shape
    tiles = bucket_width // 128
    order = (0, 2, 3, 1, 4)
    back_res, back_in, grads, vectors = block_call(
        home_slots, lead_counts, master, inputs.transpose(order), cotangent.transpose(order), sizes
    )
    if not sum_rows(sizes, tiles)[1]:
        spread = jnp.zeros((tiles, math.prod(sizes) * slots_mine, 128), f32)
        spread = spread.at[:, home_slots].set(grads)
        grads = lax.psum_scatter(spread, axes, scatter_dimension=1, tiled=True)
        vectors = lax.psum(vectors, axes)
    result, grad_inputs, grad_vectors, *new = finish_call(
        offsets(sizes[1] + 1),
        step_count,
        home_slots,
        grads,
        vectors,
        master,
        moment_one,
        moment_two,
        back_res,
        back_in,
    )
    order = (0, 3, 1, 2, 4)
    return (result.transpose(order), grad_inputs.transpose(order), grad_vectors, *new)


def solution(mesh):
    in_specs = (
        P("dp", None, "lat", "lon", None),
        P("dp", None, "lat", "lon", None),
        P(),
        P(),
        P(("dp", "lat", "lon"), None),
        P(("dp", "lat", "lon"), None),
        P(("dp", "lat", "lon"), None),
        P(),
    )
    out_specs = (
        P("dp", None, "lat", "lon", None),
        P("dp", None, "lat", "lon", None),
        P(),
        P(("dp", "lat", "lon"), None),
        P(("dp", "lat", "lon"), None),
        P(("dp", "lat", "lon"), None),
    )
    return jax.shard_map(
        per_device, mesh=mesh, in_specs=in_specs, out_specs=out_specs, check_vma=False
    )
```

```python
import functools
import math

import jax
import jax.numpy as jnp
import ml_dtypes
import numpy as np
from jax import lax
from jax.experimental import pallas as pl
from jax.experimental.pallas import tpu as pltpu
from jax.sharding import PartitionSpec as P

D = 192
FF = 768
HEADS = 6
HEAD_DIM = 32
LEVELS = 8
WIN_LAT = 6
WIN_LON = 12
LEADS = 4
HALF_LAT = WIN_LAT // 2
HALF_LON = WIN_LON // 2
QUAD = HALF_LAT * HALF_LON
AREA = WIN_LAT * WIN_LON
SIDE_HEADS = HEADS // 2
SIDE = SIDE_HEADS * HEAD_DIM
HEAD_ROWS = 80
LANES = 512
WIDE = 256
SCALE = 1.0 / math.sqrt(HEAD_DIM)

beta_one = 0.6
beta_two = 0.45
eps_norm = 1e-05
eps_adam = 1e-08
decay_rate = 0.1
penalty_value = -1000000000.0
bf16 = jnp.bfloat16
f32 = jnp.float32


def offsets(groups):
    sizes_list = [
        3 * D * D,
        D * D,
        3 * D * D,
        D * D,
        D * FF,
        FF * D,
        groups * HEADS * WIN_LAT * WIN_LAT * (2 * WIN_LON - 1),
        9 * D,
    ]
    segment_marks = [0]
    for amount in sizes_list:
        segment_marks.append(segment_marks[-1] + amount)
    return segment_marks


def nn(left, right):
    return jnp.dot(left, right, preferred_element_type=f32)


def nt(left, right):
    return lax.dot_general(left, right, (((1,), (1,)), ((), ())), preferred_element_type=f32)


def tn(left, right):
    return lax.dot_general(left, right, (((0,), (0,)), ((), ())), preferred_element_type=f32)


def normed(values):
    center = values - jnp.sum(values, axis=-1, keepdims=True) * (1.0 / D)
    spread = jnp.sum(center * center, axis=-1, keepdims=True) * (1.0 / D)
    inverse = lax.rsqrt(spread + eps_norm)
    return center * inverse, inverse


def norm_back(grad, hat, inverse, gain):
    scaled = grad * gain
    mean_one = jnp.sum(scaled, axis=-1, keepdims=True) * (1.0 / D)
    mean_two = jnp.sum(scaled * hat, axis=-1, keepdims=True) * (1.0 / D)
    return inverse * (scaled - mean_one - hat * mean_two)


def row_fold(values):
    return jnp.sum(values.reshape(values.shape[0] // 8, 8, values.shape[1]), axis=0)


def head_masks():
    lane = lax.broadcasted_iota(jnp.int32, (1, 128), 1) // HEAD_DIM
    return [jnp.where(lane == head, 1.0, 0.0).astype(bf16) for head in range(SIDE_HEADS)]


def spread_heads(values, masks):
    return jnp.concatenate([values * mask for mask in masks], axis=0)


def spread_window(values, masks):
    full = jnp.concatenate([values, jnp.zeros((HEAD_ROWS - AREA, 128), f32)], axis=0).astype(bf16)
    rest = jnp.zeros((LANES // 2 - SIDE_HEADS * HEAD_ROWS, 128), bf16)
    return jnp.concatenate([spread_heads(full, masks), rest], axis=0)


def fold_heads(big, step, count):
    lane = lax.broadcasted_iota(jnp.int32, (count, 128), 1)
    parts = [big[head * step : head * step + count] for head in range(SIDE_HEADS)]
    out = parts[-1]
    for head in range(SIDE_HEADS - 2, -1, -1):
        out = jnp.where(lane < HEAD_DIM * (head + 1), parts[head], out)
    return out


def rounded(values):
    return values.astype(bf16).astype(f32)


def soft_columns(scores):
    exps = jnp.exp(scores - jnp.max(scores, axis=0, keepdims=True))
    return exps * (1.0 / jnp.sum(exps, axis=0, keepdims=True))


def soft_back(probs, slopes):
    return probs * (slopes - jnp.sum(probs * slopes, axis=0, keepdims=True))


GROUP = 64
GLANES = SIDE_HEADS * GROUP
CHUNK = 288


def lanes_of(ref, start):
    row, lane = divmod(start, 128)
    here = ref[row : row + 1, :]
    if lane == 0:
        return here
    place = lax.broadcasted_iota(jnp.int32, (1, 128), 1)
    mixed = jnp.where(place >= lane, here, ref[row + 1 : row + 2, :])
    return pltpu.roll(mixed, 128 - lane, 1)


def lanes_from(first, second, lane, size):
    place = lax.broadcasted_iota(jnp.int32, first.shape, 1)
    if lane:
        first = pltpu.roll(jnp.where(place >= lane, first, second), 128 - lane, 1)
    return jnp.where(place < size, first, 0.0) if size < 128 else first


def lanes_join(first, begin, size, second):
    place = lax.broadcasted_iota(jnp.int32, first.shape, 1)
    moved = pltpu.roll(first, 128 - begin, 1) if begin else first
    return jnp.where(place < size, moved, pltpu.roll(second, size, 1))


EARTH_ROW = WIN_LAT * (2 * WIN_LON - 1)
EARTH_ROWS = HEADS * WIN_LAT


def earth_tables():
    entry = np.zeros((WIN_LON, AREA, 256), np.float32)
    place = np.zeros((WIN_LON, 40, LANES), np.float32)
    for column in range(WIN_LON):
        side, inner = divmod(column, HALF_LON)
        for key in range(AREA):
            key_up, rest = divmod(key, 2 * QUAD)
            key_side, rest = divmod(rest, QUAD)
            key_row, key_inner = divmod(rest, HALF_LON)
            row = key_up * HALF_LAT + key_row
            offset = column - (key_side * HALF_LON + key_inner) + WIN_LON - 1
            entry[column, key, row * (2 * WIN_LON - 1) + offset] = 1.0
        for head in range(HEADS):
            for row in range(WIN_LAT):
                up, low = divmod(row, HALF_LAT)
                lane = 2 * QUAD * up + QUAD * side + HALF_LON * low + inner
                lane += LANES // 2 * (head // SIDE_HEADS) + HEAD_ROWS * (head % SIDE_HEADS)
                place[column, head * WIN_LAT + row, lane] = 1.0
    return entry.astype(ml_dtypes.bfloat16), place.astype(ml_dtypes.bfloat16)


MESH = pl.DeviceIdType.MESH


def places():
    lat_size, lon_size, dp_size = lax.axis_size("lat"), lax.axis_size("lon"), lax.axis_size("dp")
    return (
        lax.axis_index("dp"),
        lax.axis_index("lat"),
        lax.axis_index("lon"),
        dp_size,
        lat_size,
        lon_size,
    )


def greet(targets):
    barrier = pltpu.get_barrier_semaphore()
    for target in targets:
        pl.semaphore_signal(barrier, inc=1, device_id=target, device_id_type=MESH)


def greeted_wait(count):
    pl.semaphore_wait(pltpu.get_barrier_semaphore(), count)


def split(value, size):
    if size & (size - 1) == 0:
        return lax.shift_right_logical(value, size.bit_length() - 1), value & (size - 1)
    return lax.div(value, size), lax.rem(value, size)


def around(place, step, size):
    return split(place + step, size)[1]


def neighbours(whole_plane):
    dp, lat, lon, dp_size, lat_size, lon_size = places()
    if whole_plane:
        steps = {(i, j) for i in range(lat_size) for j in range(lon_size)}
    else:
        steps = {(1, 0), (lat_size - 1, 0), (1, 1 % lon_size), (lat_size - 1, lon_size - 1)}
        steps |= {(2 * i, 0) for i in range(1, lat_size // 2)} | {(0, j) for j in range(lon_size)}
    steps.discard((0, 0))
    found = [(around(dp, step, dp_size), lat, lon) for step in range(1, dp_size)]
    return found + [
        (dp, around(lat, i, lat_size), around(lon, j, lon_size)) for i, j in sorted(steps)
    ]


def pairing(src, dst, sends, receives, send_slot, receive_slot, target):
    return pltpu.make_async_remote_copy(
        src_ref=src,
        dst_ref=dst,
        send_sem=sends.at[send_slot],
        recv_sem=receives.at[receive_slot],
        device_id=target,
        device_id_type=MESH,
    )


def gather_slots(sizes, splits):
    dp_size, lat_size, lon_size = sizes
    return splits * dp_size * (2 * max(lat_size // 2, lon_size) + 2)


def gather_steps(sizes, own_ref, all_ref, sends, receives, keep_sem):
    splits, skew = SPLITS, SKEW
    dp_size, lat_size, lon_size = sizes
    chips = lat_size // 2
    dp, lat, lon = lax.axis_index("dp"), lax.axis_index("lat"), lax.axis_index("lon")
    chip, core = split(lat, 2)
    wide = max(chips, lon_size)
    first = splits * dp_size
    second = first + splits * dp_size * wide
    cross = second + splits * dp_size * wide
    per = own_ref.shape[0] // splits
    order = sorted(range(dp_size), key=lambda step: min(step, dp_size - step))
    items = [(part, 0) for part in range(splits)]
    items += [(part, step) for part in range(splits) for step in order[1:]]

    def chip_at(step):
        return (dp, around(chip, step, chips) * 2 + core, lon)

    def lon_at(step):
        return (dp, lat, around(lon, step, lon_size))

    units = chips * lon_size

    def stretch(part, step, side, first, size):
        start = ((part * dp_size + around(dp, step, dp_size)) * 2 + side) * units + first
        return all_ref.at[pl.ds(start * per, size * per)]

    def run(mine, hooks, late_hook):
        unit = lon * chips + chip if mine == 0 else chip * lon_size + lon
        one, two = (chips, lon_size) if mine == 0 else (lon_size, chips)
        one_at, two_at = (chip_at, lon_at) if mine == 0 else (lon_at, chip_at)
        place_two = lon if mine == 0 else chip
        partner = (dp, chip * 2 + 1 - mine, lon)
        begun = []

        def send(src, dst, slot, back, target):
            copy = pairing(src, dst, sends, receives, slot, back, target)
            copy.start()
            begun.append(copy)

        def arrive(dst, slot):
            pairing(dst, dst, sends, receives, slot, slot, partner).wait_recv()

        def own_part(part):
            return own_ref.at[pl.ds(part * per, per)]

        def chunk(part, step):
            return stretch(part, step, mine, unit, 1)

        def group(part, step):
            return stretch(part, step, mine, place_two * one, one)

        def whole(part, step, side):
            return stretch(part, step, side, 0, units)

        keeps = []
        for part in range(splits):
            keep = pltpu.make_async_copy(own_part(part), chunk(part, 0), keep_sem.at[part])
            keep.start()
            keeps.append(keep)

        def line(part):
            for step in order[1:]:
                target = (around(dp, step, dp_size), lat, lon)
                base = part * dp_size
                send(own_part(part), chunk(part, 0), base + step, base + dp_size - step, target)

        def stage_one(part, step):
            if step:
                arrive(chunk(part, step), part * dp_size + step)
            base = first + (part * dp_size + step) * wide
            src = chunk(part, step) if step else own_part(part)
            for far in range(1, one):
                send(src, chunk(part, step), base + far, base + one - far, one_at(far))

        def stage_two(part, step):
            base = first + (part * dp_size + step) * wide
            for far in range(1, one):
                arrive(chunk(part, step), base + far)
            if step == 0:
                keeps[part].wait()
            base = second + (part * dp_size + step) * wide
            for far in range(1, two):
                send(group(part, step), group(part, step), base + far, base + two - far, two_at(far))

        def stage_three(part, step):
            base = second + (part * dp_size + step) * wide
            for far in range(1, two):
                arrive(group(part, step), base + far)
            slot = cross + part * dp_size + step
            send(whole(part, step, mine), whole(part, step, mine), slot, slot, partner)

        for part in range(splits):
            line(part)
        for turn in range(len(items) + 2 * skew):
            for stage, place in ((stage_one, turn), (stage_two, turn - skew), (stage_three, turn - 2 * skew)):
                if 0 <= place < len(items):
                    stage(*items[place])
            if turn in hooks:
                hooks[turn]()
        late_hook()
        for part, step in items:
            arrive(whole(part, step, 1 - mine), cross + part * dp_size + step)
        for copy in begun:
            copy.wait_send()

    return run


def move_slots(sizes, slots):
    dp_size, lat_size, lon_size = sizes
    spread = lat_size // 2 * lon_size
    moves = gather_slots(sizes, SPLITS)
    sums = moves + 16 * (slots + 1)
    vectors = sums + 3 * (1 + spread + 2 * dp_size)
    hand = vectors + 1 + spread + dp_size
    return moves, sums, vectors, hand, hand + lat_size * lon_size


SPLITS = 2
SKEW = 3


def block_kernel(
    shape_info,
    inside,
    home_ref,
    lead_ref,
    homes_ref,
    master_ref,
    inputs_ref,
    cotangent_ref,
    entry_hbm,
    place_hbm,
    back_res_ref,
    back_res_tail_ref,
    back_in_ref,
    back_in_tail_ref,
    grads_ref,
    total_ref,
    spot_ref,
    weights_ref,
    grid_ref,
    grid_tail_ref,
    entry_ref,
    place_ref,
    own_ref,
    all_ref,
    tok_ref,
    tok_tail_ref,
    res_ref,
    res_tail_ref,
    flat_ref,
    mid_ref,
    earth_ref,
    gate_ref,
    bias_ref,
    dbias_ref,
    w1_ref,
    o1_ref,
    w2_ref,
    o2_ref,
    up_ref,
    down_ref,
    vec_ref,
    n1_ref,
    hat1_ref,
    inv1_ref,
    qkv_ref,
    probs_ref,
    att_ref,
    att1_ref,
    tok1_ref,
    n2_ref,
    hat2_ref,
    inv2_ref,
    mix2_ref,
    cprobs_ref,
    att2_ref,
    n3_ref,
    act_ref,
    gh_ref,
    delta3_ref,
    delta2_ref,
    delta1_ref,
    gmid_ref,
    glow_ref,
    gatt2_ref,
    gm2_ref,
    gm1_ref,
    vacc_ref,
    around_ref,
    sends,
    receives,
    keeps,
    fetched,
    kept,
    *sum_refs,
):
    levels = tok_ref.shape[5]
    chunks = 4
    sizes, buckets, tiles, slots_here, cuts = shape_info
    count = slots_here * levels
    tokens = count * AREA
    dp_size, lat_size, lon_size = sizes
    chips = lat_size // 2
    spread = chips * lon_size
    dp, lat, lon = lax.axis_index("dp"), lax.axis_index("lat"), lax.axis_index("lon")
    chip, core = split(lat, 2)
    is_last = lat == lat_size - 1
    moves, sum_slots, vector_slots, hand_slots, _ = move_slots(sizes, slots_here)
    begun = []

    def send(src, dst, slot, back, target):
        copy = pairing(src, dst, sends, receives, slot, back, target)
        copy.start()
        begun.append(copy)

    def arrive(dst, slot):
        pairing(dst, dst, sends, receives, slot, slot, (dp, lat, lon)).wait_recv()

    def pieces(kind, start, quads=range(4)):
        for quad in quads:
            up, left = quad // 2, quad % 2
            way = 1 if kind > 1 else -1
            target = (
                dp,
                around(lat, way * up % lat_size, lat_size),
                around(lon, way * left % lon_size, lon_size),
            )
            grid, grid_tail = (
                (inputs_ref, grid_tail_ref.at[0]),
                (cotangent_ref, grid_tail_ref.at[1]),
                (back_res_ref, back_res_tail_ref),
                (back_in_ref, back_in_tail_ref),
            )[kind]
            held, held_tail = (res_ref, res_tail_ref) if kind > 1 else (tok_ref, tok_tail_ref)
            rows = pl.ds(HALF_LAT * (1 - up), HALF_LAT)
            columns = pl.ds(HALF_LON * (1 - left), HALF_LON)
            pairs = [(grid_tail.at[rows, columns], held_tail.at[quad, kind % 2])]
            for slot in range(slots_here):
                on_grid = grid.at[slot, rows, columns]
                on_grid = on_grid if kind > 1 else on_grid.at[:, :, :, pl.ds(0, 128)]
                pairs.append((on_grid, held.at[quad, kind % 2, :, :, slot]))
            for number, (on_grid, in_quads) in enumerate(pairs):
                src, dst = (in_quads, on_grid) if kind > 1 else (on_grid, in_quads)
                place = len(pairs) * (4 * kind + quad) + number
                if quad == 0:
                    copy = pltpu.make_async_copy(src, dst, kept.at[kind * len(pairs) + number])
                    copy.start() if start else copy.wait()
                elif start:
                    send(src, dst, moves + place, moves + place, target)
                else:
                    arrive(dst, moves + place)

    def shift(kind, quads=range(4)):
        pieces(kind, True, quads)

    def shifted(kind):
        pieces(kind, False)

    def part(index):
        return pl.ds(pl.multiple_of(index * CHUNK, CHUNK), CHUNK)

    fetches = [
        pltpu.make_async_copy(source, target, fetched.at[index])
        for index, (source, target) in enumerate(
            (
                (master_ref, weights_ref),
                (inputs_ref, grid_ref.at[0]),
                (cotangent_ref, grid_ref.at[1]),
                (entry_hbm, entry_ref),
                (place_hbm, place_ref),
            )
        )
    ]
    for fetch in fetches:
        fetch.start()
    def pack_tail(kind):
        @pl.loop(0, WIN_LAT)
        def _(row):
            tails = [
                grid_ref[kind, slot, row].astype(f32)[:, :, 128:].reshape(WIN_LON * levels, D - 128)
                for slot in range(2)
            ]
            grid_tail_ref[kind, row] = (
                jnp.concatenate(tails, axis=1).reshape(WIN_LON, levels, 128).astype(bf16)
            )

    def tokens_of(kind, c):
        top = tok_ref[c, kind].astype(f32).reshape(CHUNK, 128)
        tails = tok_tail_ref[c, kind].astype(f32).reshape(QUAD * levels, 128)
        both = [tails, pltpu.roll(tails, 64, 1)]
        both = jnp.concatenate([tail.reshape(QUAD, 1, levels, 128) for tail in both], axis=1)
        return jnp.concatenate([top, both.reshape(CHUNK, 128)[:, : D - 128]], axis=1)

    def keep_tokens(kind, c, values):
        res_ref[c, kind] = values[:, :128].reshape(res_ref.shape[2:]).astype(bf16)
        tails = values[:, 128:].reshape(QUAD, 2, levels, D - 128)
        tails = [tails[:, slot].reshape(QUAD * levels, D - 128) for slot in range(2)]
        tails = jnp.concatenate(tails, axis=1).reshape(res_tail_ref.shape[2:])
        res_tail_ref[c, kind] = tails.astype(bf16)

    greeted = neighbours(inside)
    greet(greeted)

    per_home, own_rows = own_ref.shape[:2]
    flat_ref[pl.ds(0, per_home * own_rows), :] = jnp.zeros((per_home * own_rows, 128), f32)
    fetches[0].wait()
    for tile in range(tiles):
        flat_ref[pl.ds(tile, per_home, stride=own_rows), :] = weights_ref[
            :, 128 * tile : 128 * (tile + 1)
        ]
    for slot in range(per_home):
        own_ref[slot] = flat_ref[pl.ds(slot * own_rows, own_rows), :].astype(bf16)
    fetches[1].wait()
    pack_tail(0)
    greeted_wait(len(greeted))

    def center_tokens():
        fetches[2].wait()
        pack_tail(1)
        for bucket in range(buckets):
            home = home_ref[bucket]
            device, slot = split(home, per_home)
            rest, home_lon = split(device, lon_size)
            home_dp, home_lat = split(rest, lat_size)
            home_chip, home_core = split(home_lat, 2)
            unit = jnp.where(
                home_core == 0, home_lon * chips + home_chip, home_chip * lon_size + home_lon
            )
            side, inner = split(slot, per_home // SPLITS)
            chunk = (side * dp_size + home_dp) * 2 + home_core
            spot_ref[bucket] = (chunk * spread + unit) * (per_home // SPLITS) + inner
        shifted(0)

        @pl.loop(0, chunks)
        def _(c):
            rows = part(c)
            hat, inverse = normed(tokens_of(0, c))
            hat1_ref[rows, :] = hat
            inv1_ref[rows, :] = jnp.broadcast_to(inverse, (CHUNK, 128))

    gather = gather_steps(sizes, own_ref, all_ref, sends, receives, keeps)
    hooks = {0: functools.partial(shift, 0)}
    for mine in range(2):

        @pl.when(core == mine)
        def _():
            gather(mine, hooks, center_tokens)
            for copy in begun:
                copy.wait_send()
            begun.clear()

    shift(1)
    for fetch in fetches[3:]:
        fetch.wait()
    vacc_ref[...] = jnp.zeros_like(vacc_ref)
    marks = offsets(lat_size + 1)
    row_marks = [mark // 128 for mark in marks]

    for bucket in range(buckets):
        block = all_ref[spot_ref[bucket]].astype(f32)
        flat_ref[tiles * bucket : tiles * (bucket + 1), :] = block[:tiles]

    def take_pairs(base, parts, pairs):
        return [flat_ref[pl.ds(base + part, pairs, stride=parts), :] for part in range(parts)]

    def give_pairs(columns, rows, evens, odds):
        for column, (even, odd) in enumerate(zip(evens, odds)):
            mid_ref[column, pl.ds(0, rows // 2, stride=2), :] = even
            mid_ref[column, pl.ds(1, rows // 2, stride=2), :] = odd

    def load_qkv(base, ref):
        b = take_pairs(base, 9, D // 2)
        pieces = []
        for first in range(0, 9, 3):
            x, y, z = b[first : first + 3]
            pieces += [
                lanes_from(x, x, 0, SIDE),
                lanes_from(x, y, 96, SIDE),
                lanes_from(y, z, 64, SIDE),
                lanes_from(z, z, 32, SIDE),
            ]
        give_pairs(6, D, pieces[:6], pieces[6:])
        for column in range(6):
            ref[:, 128 * column : 128 * (column + 1)] = mid_ref[column, pl.ds(0, D), :].astype(bf16)

    def load_square(base, rows, ref, spans):
        b = take_pairs(base, 3, rows // 2)
        odds = [lanes_from(b[1], b[2], 64, 128), lanes_from(b[2], b[2], 64, D - 128)]
        give_pairs(2, rows, [b[0], b[1]], odds)
        for first, last, target in spans:
            size = last - first
            ref[target : target + size, 0:128] = mid_ref[0, pl.ds(first, size), :].astype(bf16)
            ref[target : target + size, 128:D] = mid_ref[1, pl.ds(first, size), :][
                :, : D - 128
            ].astype(bf16)

    sides = [(0, SIDE, 0), (SIDE, D, 128)]
    load_qkv(row_marks[0], w1_ref)
    load_square(row_marks[1], D, o1_ref, sides)
    load_qkv(row_marks[2], w2_ref)
    load_square(row_marks[3], D, o2_ref, sides)
    for ref in (o1_ref, o2_ref):
        for side in range(2):
            ref[128 * side + SIDE : 128 * (side + 1), :] = jnp.zeros((128 - SIDE, D), bf16)
    for column in range(6):
        up_ref[:, 128 * column : 128 * (column + 1)] = flat_ref[
            pl.ds(row_marks[4] + column, D, stride=6), :
        ].astype(bf16)
    load_square(row_marks[5], FF, down_ref, [(0, FF, 0)])
    for index in range(9):
        start = marks[7] + D * index
        vec_ref[index : index + 1, 0:128] = lanes_of(flat_ref, start)
        vec_ref[index : index + 1, 128:D] = lanes_of(flat_ref, start + 128)[:, : D - 128]

    def earth_places():
        group_one = lat + 1
        group_two = jnp.where(is_last, 0, lat + 1)
        for index in range(EARTH_ROWS):
            group = group_one if index % WIN_LAT < HALF_LAT else group_two
            start = marks[6] + EARTH_ROW * (EARTH_ROWS * group + index)
            yield (index,) + split(start, 128)

    lane_place = lax.broadcasted_iota(jnp.int32, (1, 128), 1)
    earth_ref[...] = jnp.zeros_like(earth_ref)
    for index, row, lane in earth_places():
        rows = [flat_ref[pl.ds(row + step, 1), :] for step in range(3)]
        back = (128 - lane) & 127
        first = pltpu.roll(jnp.where(lane_place >= lane, rows[0], rows[1]), back, 1)
        second = pltpu.roll(jnp.where(lane_place >= lane, rows[1], rows[2]), back, 1)
        earth_ref[index : index + 1, 0:128] = first
        earth_ref[index : index + 1, 128:256] = jnp.where(lane_place < EARTH_ROW - 128, second, 0.0)
    earth = earth_ref[...].astype(bf16)
    key_up = lax.broadcasted_iota(jnp.int32, (AREA, LANES), 0) // (2 * QUAD)
    query_up = lax.broadcasted_iota(jnp.int32, (AREA, LANES), 1) & (LANES // 2 - 1)
    query_up = lax.rem(query_up, HEAD_ROWS) // (2 * QUAD)
    bias = jnp.where((key_up != query_up) & is_last, penalty_value, 0.0)
    for column in range(WIN_LON):
        bias = bias + nn(nt(entry_ref[column], earth).astype(bf16), place_ref[column])
    bias_ref[...] = bias

    for slot in range(slots_here):
        number = lax.axis_index("dp") * slots_here + slot
        sample, lead = split(number, LEADS)
        live = lead < lead_ref[sample]
        size = count // slots_here
        gate_ref[slot * size : (slot + 1) * size, :] = jnp.full((size, D), jnp.where(live, 1.0, 0.0), f32)

    def vec(index):
        return vec_ref[index : index + 1, :]

    def gate_rows():
        gate = gate_ref[...]
        return jnp.broadcast_to(gate[None], (CHUNK // count, count, D)).reshape(CHUNK, D)

    def note(index, values):
        vacc_ref[index] += row_fold(values)

    def note_low(index, values):
        top = lax.broadcasted_iota(jnp.int32, (8, CHUNK), 0) == 0
        vacc_ref[index] += nn(jnp.where(top, 1.0, 0.0).astype(bf16), values)

    def first_mixed(c):
        rows = part(c)
        low = (hat1_ref[rows, :] * vec(0) + vec(1)).astype(bf16)
        n1_ref[rows, :] = low
        mixed = rounded(nn(low, w1_ref[...]))
        for tile in range(6):
            qkv_ref[tile, rows, :] = mixed[:, 128 * tile : 128 * (tile + 1)]

    for c in range(chunks):
        first_mixed(c)

    def window(ref, tile, s):
        return ref[tile, pl.ds(s, AREA, stride=count), :]

    def window_store(ref, tile, s, values):
        ref[tile, pl.ds(s, AREA, stride=count), :] = values

    halves = [slice(0, LANES // 2), slice(LANES // 2, LANES)]

    @pl.loop(0, count // 4)
    def _(block):
        masks = head_masks()
        places = [(block * 4 + step, side) for step in range(4) for side in range(2)]
        reads = [[window(qkv_ref, 2 * kind + side, s) for kind in range(3)] for s, side in places]
        raw = [
            nt(key.astype(bf16), spread_window(query, masks)) for query, key, _ in reads
        ]
        probs = [
            soft_columns(scores * SCALE + bias_ref[:, halves[side]])
            for scores, (_, side) in zip(raw, places)
        ]
        outs = [tn(prob.astype(bf16), read[2].astype(bf16)) for prob, read in zip(probs, reads)]
        for (s, side), prob, out in zip(places, probs, outs):
            probs_ref[s, :, halves[side]] = prob
            window_store(att_ref, side, s, fold_heads(out, HEAD_ROWS, AREA))

    def second_mixed(c):
        rows = part(c)
        att = jnp.concatenate([att_ref[0, rows, :], att_ref[1, rows, :]], axis=1).astype(bf16)
        att1_ref[rows, :] = att
        branch = nn(att, o1_ref[...]) + vec(2)
        tok = tokens_of(0, c) + gate_rows() * branch
        tok1_ref[rows, :] = tok
        hat, inverse = normed(tok)
        hat2_ref[rows, :] = hat
        inv2_ref[rows, :] = jnp.broadcast_to(inverse, (CHUNK, 128))
        low = (hat * vec(3) + vec(4)).astype(bf16)
        n2_ref[rows, :] = low
        mix2_ref[rows, :] = nn(low, w2_ref[...]).astype(bf16)

    for c in range(chunks):
        second_mixed(c)

    def column_masks():
        lane = lax.broadcasted_iota(jnp.int32, (8, GLANES), 1)
        place = lax.shift_right_logical(lane & (GROUP - 1), 3)
        return [place == index for index in range(GROUP // 8)]

    def squeeze_column(values, masks):
        out = values[:8]
        for index in range(1, GROUP // 8):
            out = jnp.where(masks[index], values[8 * index : 8 * index + 8], out)
        return out

    def widen_column(values, masks):
        return jnp.concatenate([jnp.where(mask, values, 0.0) for mask in masks], axis=0).astype(bf16)

    def group_rows(g):
        return pl.ds(pl.multiple_of(g * GROUP, GROUP), GROUP)

    def tile_of(ref, g, kind, side):
        first = WIDE * kind + 128 * side
        return ref[group_rows(g), first : first + 128]

    @pl.loop(0, tokens // GROUP // 6)
    def _(block):
        heads = head_masks()
        columns = column_masks()
        places = [(block * 6 + step, side) for step in range(6) for side in range(2)]
        reads = [[tile_of(mix2_ref, g, kind, side) for kind in range(3)] for g, side in places]
        raw = [nt(key, spread_heads(query, heads)) for query, key, _ in reads]
        probs = [soft_columns(squeeze_column(scores, columns) * SCALE) for scores in raw]
        outs = [tn(widen_column(prob, columns), read[2]) for prob, read in zip(probs, reads)]
        for (g, side), prob, out in zip(places, probs, outs):
            cprobs_ref[g, side] = prob
            att2_ref[group_rows(g), 128 * side : 128 * (side + 1)] = fold_heads(
                out, GROUP, GROUP
            ).astype(bf16)

    root = math.sqrt(2.0 / math.pi)
    shifted(1)

    @pl.loop(0, chunks)
    def _(c):
        rows = part(c)
        gate = gate_rows()
        tok = tok1_ref[rows, :] + gate * (nn(att2_ref[rows, :], o2_ref[...]) + vec(5))
        hat, inverse = normed(tok)
        low = (hat * vec(6) + vec(7)).astype(bf16)
        n3_ref[rows, :] = low
        hidden = nn(low, up_ref[...])
        square = hidden * hidden
        half = 0.5 * jnp.tanh(hidden * (root + (root * 0.044715) * square)) + 0.5
        wave = hidden * half
        act = wave.astype(bf16)
        act_ref[rows, :] = act
        keep_tokens(0, c, tok + gate * (nn(act, down_ref[...]) + vec(8)))
        slope = half + wave * (1.0 - half) * (2.0 * root + (6.0 * root * 0.044715) * square)
        after = tokens_of(1, c)
        delta3 = (gate * after).astype(bf16)
        delta3_ref[rows, :] = delta3
        note_low(8, delta3)
        gh = (nt(delta3, down_ref[...]) * slope).astype(bf16)
        gh_ref[rows, :] = gh
        grad = nt(gh, up_ref[...])
        note(6, grad * hat)
        note(7, grad)
        mid = after + norm_back(grad, hat, inverse, vec(6))
        gmid_ref[rows, :] = mid
        delta2 = (gate * mid).astype(bf16)
        delta2_ref[rows, :] = delta2
        note_low(5, delta2)
        gatt2_ref[rows, :] = nt(delta2, o2_ref[...]).astype(bf16)

    def keep_pairs(base, parts, blocks):
        for number, block in enumerate(blocks):
            flat_ref[pl.ds(base + number, block.shape[0], stride=parts), :] = block

    def split_pairs(columns, rows):
        evens = [mid_ref[column, pl.ds(0, rows // 2, stride=2), :] for column in range(columns)]
        odds = [mid_ref[column, pl.ds(1, rows // 2, stride=2), :] for column in range(columns)]
        return evens, odds

    def save_qkv(base, grad):
        for column in range(6):
            mid_ref[column, pl.ds(0, D), :] = grad[:, 128 * column : 128 * (column + 1)]
        e, o = split_pairs(6, D)
        pieces = e + o
        blocks = []
        for first in range(0, 12, 4):
            x, y, z, w = pieces[first : first + 4]
            blocks += [
                lanes_join(x, 0, 96, y),
                lanes_join(y, 32, 64, z),
                lanes_join(z, 64, 32, w),
            ]
        keep_pairs(base, 9, blocks)

    def save_square(base, rows, grad):
        mid_ref[0, pl.ds(0, rows), :] = grad[:, :128]
        mid_ref[1, pl.ds(0, rows), 0 : D - 128] = grad[:, 128:]
        e, o = split_pairs(2, rows)
        keep_pairs(
            base, 3, [e[0], lanes_join(e[1], 0, 64, o[0]), lanes_join(o[0], 64, 64, o[1])]
        )

    def used_rows(grad):
        return jnp.concatenate([grad[0:SIDE], grad[128 : 128 + SIDE]], axis=0)

    partner = (dp, chip * 2 + 1 - core, lon)
    place = chip * lon_size + lon

    def peers():
        for i in range(chips):
            for j in range(lon_size):
                if i or j:
                    back = (chips - i) % chips * lon_size + (lon_size - j) % lon_size
                    there = (around(chip, i, chips), around(lon, j, lon_size))
                    target = (dp, there[0] * 2 + core, there[1])
                    yield i * lon_size + j, back, there[0] * lon_size + there[1], target

    def line():
        for step in range(1, dp_size):
            there = around(dp, step, dp_size)
            yield step, dp_size - step, there, (there, lat, lon)

    def summing(base, grad, half_in, half, plane_in, mid, line_in, full):
        n_half = grad.shape[0] // 2
        n_place = n_half // spread
        n_line = n_place // dp_size

        def cross():
            send(grad.at[pl.ds((1 - core) * n_half, n_half)], half_in, base, base, partner)

        def plane():
            arrive(half_in, base)
            for first in range(0, n_half, 12):
                rows = pl.ds(first, 12)
                kept = grad[pl.ds(core * n_half + first, 12)].astype(f32)
                half[rows] = (kept + half_in[rows].astype(f32)).astype(bf16)
            for index, back, there, target in peers():
                send(
                    half.at[pl.ds(there * n_place, n_place)],
                    plane_in.at[back],
                    base + 1 + index,
                    base + 1 + back,
                    target,
                )

        def along():
            total = half[pl.ds(place * n_place, n_place)].astype(f32)
            for index in range(1, spread):
                arrive(plane_in.at[index], base + 1 + index)
                total = total + plane_in[index].astype(f32)
            mid[...] = total.astype(bf16)
            slots = base + 1 + spread
            for step, back, there, target in line():
                send(mid.at[pl.ds(there * n_line, n_line)], line_in.at[back], slots + step, slots + back, target)

        def share():
            slots = base + 1 + spread
            rows = pl.ds(dp * n_line, n_line)
            total = mid[rows].astype(f32)
            for step in range(1, dp_size):
                arrive(line_in.at[step], slots + step)
                total = total + line_in[step].astype(f32)
            full[rows] = total.astype(bf16)
            slots += dp_size
            for step, back, _, target in line():
                send(full.at[rows], full.at[rows], slots + step, slots + back, target)

        def done():
            slots = base + 1 + spread + dp_size
            for step, _, there, _ in line():
                arrive(full.at[pl.ds(there * n_line, n_line)], slots + step)

        return cross, plane, along, share, done

    spans = [[(cuts[1], cuts[2])], [(cuts[0], cuts[1])], [(0, cuts[0]), (cuts[2], buckets)]]
    if inside:
        sum_sets = [sum_refs[7 * number : 7 * (number + 1)] for number in range(3)]
        hand_out, vec_sum, vec_in, vec_now = sum_refs[21:]
        each = 1 + spread + 2 * dp_size
        soon, early, late = [
            summing(sum_slots + each * number, *refs) for number, refs in enumerate(sum_sets)
        ]

        def pack(number):
            grad = sum_sets[number][0]
            for tile in range(grad.shape[0]):
                if tile < tiles:
                    rows = [
                        flat_ref[pl.ds(tile + tiles * begin, end - begin, stride=tiles), :]
                        for begin, end in spans[number]
                    ]
                    values = rows[0] if len(rows) == 1 else jnp.concatenate(rows, axis=0)
                    grad[tile] = values.astype(bf16)
                else:
                    grad[tile] = jnp.zeros(grad.shape[1:], bf16)
    else:
        (vec_sum,) = sum_refs

    shift(2)

    grad_up = tn(n3_ref[...], gh_ref[...])
    for column in range(6):
        flat_ref[pl.ds(row_marks[4] + column, D, stride=6), :] = grad_up[
            :, 128 * column : 128 * (column + 1)
        ]
    save_square(row_marks[5], FF, tn(act_ref[...], delta3_ref[...]))
    if inside:
        pack(0)
        soon[0]()


    @pl.loop(0, tokens // GROUP // 6)
    def _(block):
        heads = head_masks()
        columns = column_masks()
        places = [(block * 6 + step, side) for step in range(6) for side in range(2)]
        reads = [
            [tile_of(mix2_ref, g, kind, side) for kind in range(3)]
            + [tile_of(gatt2_ref, g, 0, side), cprobs_ref[g, side]]
            for g, side in places
        ]
        grads = [spread_heads(read[3], heads) for read in reads]
        raw = [nt(read[2], grad) for read, grad in zip(reads, grads)]
        dvalues = [nn(widen_column(read[4], columns), grad) for read, grad in zip(reads, grads)]
        lows = [
            widen_column(soft_back(read[4], squeeze_column(slopes, columns)), columns)
            for read, slopes in zip(reads, raw)
        ]
        dkeys = [nn(low, spread_heads(read[0], heads)) for read, low in zip(reads, lows)]
        dqueries = [tn(low, read[1]) for read, low in zip(reads, lows)]
        for (g, side), dquery, dkey, dvalue in zip(places, dqueries, dkeys, dvalues):
            for kind, values in enumerate(
                (fold_heads(dquery, GROUP, GROUP) * SCALE, dkey * SCALE, dvalue)
            ):
                first = WIDE * kind + 128 * side
                gm2_ref[group_rows(g), first : first + 128] = values.astype(bf16)

    if inside:
        soon[1]()

    def second_back(c):
        rows = part(c)
        grad = nt(gm2_ref[rows, :], w2_ref[...])
        hat = hat2_ref[rows, :]
        inverse = inv2_ref[rows, :][:, :1]
        note(3, grad * hat)
        note(4, grad)
        low = gmid_ref[rows, :] + norm_back(grad, hat, inverse, vec(3))
        glow_ref[rows, :] = low
        delta1 = (gate_rows() * low).astype(bf16)
        delta1_ref[rows, :] = delta1
        note_low(2, delta1)
        gatt = rounded(nt(delta1, o1_ref[...]))
        att_ref[0, rows, :] = gatt[:, :128]
        att_ref[1, rows, :] = gatt[:, 128:]

    for c in range(chunks):
        second_back(c)

    save_square(row_marks[1], D, used_rows(tn(att1_ref[...], delta1_ref[...])))
    save_qkv(row_marks[2], tn(n2_ref[...], gm2_ref[...]))
    save_square(row_marks[3], D, used_rows(tn(att2_ref[...], delta2_ref[...])))

    if inside:
        pack(1)
        early[0]()
        soon[2]()

    dbias_ref[...] = jnp.zeros_like(dbias_ref)

    def window_back(block):
        masks = head_masks()
        places = [(block * 4 + step, side) for step in range(4) for side in range(2)]
        reads = [
            [window(qkv_ref, 2 * kind + side, s) for kind in range(3)]
            + [window(att_ref, side, s), probs_ref[s, :, halves[side]]]
            for s, side in places
        ]
        grads = [spread_window(read[3], masks) for read in reads]
        raw = [nt(read[2].astype(bf16), grad) for read, grad in zip(reads, grads)]
        dvalues = [nn(read[4].astype(bf16), grad) for read, grad in zip(reads, grads)]
        lows = [soft_back(read[4], slopes).astype(bf16) for read, slopes in zip(reads, raw)]
        dkeys = [nn(low, spread_window(read[0], masks)) for read, low in zip(reads, lows)]
        dqueries = [tn(low, read[1].astype(bf16)) for read, low in zip(reads, lows)]
        for side in range(2):
            dbias_ref[:, halves[side]] += functools.reduce(
                jnp.add, [low.astype(f32) for low, (_, there) in zip(lows, places) if there == side]
            )
        for (s, side), dquery, dkey, dvalue in zip(places, dqueries, dkeys, dvalues):
            dquery = fold_heads(dquery, HEAD_ROWS, AREA) * SCALE
            for kind, values in enumerate((dquery, dkey * SCALE, dvalue)):
                window_store(qkv_ref, 2 * kind + side, s, rounded(values))

    @pl.loop(0, 2)
    def _(block):
        window_back(block)

    if inside:
        early[1]()
        soon[3]()

    @pl.loop(2, count // 4)
    def _(block):
        window_back(block)

    @pl.loop(0, chunks)
    def _(c):
        rows = part(c)
        gm1_ref[rows, :] = jnp.concatenate(
            [qkv_ref[tile, rows, :] for tile in range(6)], axis=1
        ).astype(bf16)

    save_qkv(row_marks[0], tn(n1_ref[...], gm1_ref[...]))
    rest = flat_ref.shape[0] - row_marks[6]
    around_ref[...] = jnp.zeros_like(around_ref)
    dbias = dbias_ref[...].astype(bf16)
    moved = [nt(dbias, place_ref[column]).astype(bf16) for column in range(WIN_LON)]
    dearth = functools.reduce(
        jnp.add, [tn(moved[column], entry_ref[column]) for column in range(WIN_LON)]
    )
    for index, row, lane in earth_places():
        row = row - row_marks[6]
        first = pltpu.roll(dearth[index : index + 1, :128], lane, 1)
        second = pltpu.roll(dearth[index : index + 1, 128:], lane, 1)
        tail = lane_place >= lane
        for step, values in enumerate(
            (
                jnp.where(tail, first, 0.0),
                jnp.where(tail, second, first),
                jnp.where(tail, 0.0, second),
            )
        ):
            around_ref[index % 4, pl.ds(row + step, 1), :] += values
    flat_ref[row_marks[6] :, :] = functools.reduce(
        jnp.add, [around_ref[number, 0:rest, :] for number in range(4)]
    )
    if inside:
        early[2]()
        pack(2)
        late[0]()

    def input_grads(c):
        rows = part(c)
        mixed = gm1_ref[rows, :]
        grad = nt(mixed, w1_ref[...])
        hat = hat1_ref[rows, :]
        inverse = inv1_ref[rows, :][:, :1]
        note(0, grad * hat)
        note(1, grad)
        grad_in = glow_ref[rows, :] + norm_back(grad, hat, inverse, vec(0))
        keep_tokens(1, c, grad_in)

    @pl.loop(2, chunks)
    def _(c):
        input_grads(c)

    if inside:
        late[1]()

    @pl.loop(0, 2)
    def _(c):
        input_grads(1 - c)

    for index in range(9):
        vec_sum[index : index + 1, :] = jnp.sum(vacc_ref[index], axis=0, keepdims=True)
    if inside:
        send(vec_sum, vec_in.at[0], vector_slots, vector_slots, partner)
        early[3]()
        arrive(vec_in.at[0], vector_slots)
        vec_now[0] = vec_sum[...] + vec_in[0]
        for index, back, _, target in peers():
            send(vec_now.at[0], vec_in.at[back], vector_slots + 1 + index, vector_slots + 1 + back, target)
    shift(3)
    if inside:
        late[2]()
        vec_total = vec_now[0]
        for index in range(1, spread):
            arrive(vec_in.at[index], vector_slots + 1 + index)
            vec_total = vec_total + vec_in[index]
        vec_now[1] = vec_total
        slots = vector_slots + 1 + spread
        for step, back, _, target in line():
            send(vec_now.at[1], vec_in.at[spread + back], slots + step, slots + back, target)
        late[3]()
        soon[4]()
        early[4]()
        homes = lat_size * lon_size
        width = homes * per_home
        slot_ids = lax.broadcasted_iota(jnp.int32, (width, 1), 0) + dp * width
        all_homes = homes_ref[...]
        picks = []
        for some in spans:
            held = [all_homes[:, begin:end] for begin, end in some]
            held = held[0] if len(held) == 1 else jnp.concatenate(held, axis=1)
            picks.append(jnp.where(slot_ids == held, 1.0, 0.0).astype(bf16))
        n_rows = hand_out.shape[1]
        owned_first = [
            nn(picks[0], sum_sets[0][6][row]) + nn(picks[1], sum_sets[1][6][row])
            for row in range(n_rows)
        ]
        late[4]()
        for row in range(n_rows):
            owned = owned_first[row] + nn(picks[2], sum_sets[2][6][row])
            for home in range(homes):
                hand_out[home, row] = owned[per_home * home : per_home * (home + 1), :].astype(bf16)
        first = core * (n_rows * spread) + place * n_rows
        landing = grads_ref.at[pl.ds(first, n_rows)]
        me = lat * lon_size + lon
        keep_hand = pltpu.make_async_copy(hand_out.at[me], landing, keeps.at[SPLITS])
        keep_hand.start()
        for i in range(lat_size):
            for j in range(lon_size):
                if i or j:
                    target = (dp, around(lat, i, lat_size), around(lon, j, lon_size))
                    back = (lat_size - i) % lat_size * lon_size + (lon_size - j) % lon_size
                    send(
                        hand_out.at[target[1] * lon_size + target[2]],
                        landing,
                        hand_slots + i * lon_size + j,
                        hand_slots + back,
                        target,
                    )
        for step in range(1, dp_size):
            arrive(vec_in.at[spread + step], slots + step)
            vec_total = vec_total + vec_in[spread + step]
        vec_in[0] = vec_total
        keep_total = pltpu.make_async_copy(vec_in.at[0], total_ref, keeps.at[0])
        keep_total.start()
        keep_hand.wait()
        keep_total.wait()
        for index in range(1, homes):
            arrive(landing, hand_slots + index)
    else:
        total_ref[...] = vec_sum[...]
        for tile in range(tiles):
            grads_ref[tile] = flat_ref[pl.ds(tile, buckets, stride=tiles), :]
    shifted(2)
    shifted(3)
    for copy in begun:
        copy.wait_send()


def sum_rows(sizes, tiles):
    unit = sizes[0] * sizes[1] * sizes[2]
    rows = -(-tiles // unit) * unit
    return rows, rows <= 2 * tiles


def block_call(homes, leads, master, inputs, cotangent, sizes):
    slots_here, levels = inputs.shape[0], inputs.shape[3]
    count = slots_here * levels
    tokens = count * AREA
    buckets = homes.shape[0]
    per_home, width = master.shape
    tiles = width // 128
    own_rows = -(-tiles // 16) * 16
    quads = (4, 2, HALF_LAT, HALF_LON, slots_here, levels, 128)
    tails = (4, 2, HALF_LAT, HALF_LON, levels, 128)
    assert slots_here == 2
    dp_size, lat_size, lon_size = sizes
    spread = lat_size // 2 * lon_size
    rows, inside = sum_rows(sizes, tiles)
    marks = offsets(lat_size + 1)
    low = -(-marks[1] // width)
    mid = -(-marks[4] // width)
    high = marks[6] // width
    mid += (high - mid) % 8
    low += (mid - low) % 8
    cuts = (low, mid, high)
    shape = jax.ShapeDtypeStruct
    outs = [
        shape(inputs.shape[:4] + (128,), bf16),
        shape(inputs.shape[1:4] + (128,), bf16),
        shape(inputs.shape[:4] + (128,), bf16),
        shape(inputs.shape[1:4] + (128,), bf16),
        shape((rows, per_home, 128), bf16) if inside else shape((tiles, buckets, 128), f32),
        shape((9, D), f32),
    ]
    vmem = pltpu.VMEM
    entry, place = earth_tables()
    scratch = [
        pltpu.SMEM((buckets,), jnp.int32),
        vmem(master.shape, f32),
        vmem((2,) + inputs.shape, bf16),
        vmem((2, WIN_LAT, WIN_LON, levels, 128), bf16),
        vmem(entry.shape, bf16),
        vmem(place.shape, bf16),
        vmem((per_home, own_rows, 128), bf16),
        vmem((dp_size * lat_size * lon_size * per_home, own_rows, 128), bf16),
        vmem(quads, bf16),
        vmem(tails, bf16),
        vmem(quads, bf16),
        vmem(tails, bf16),
        vmem((buckets * tiles, 128), f32),
        vmem((6, FF, 128), f32),
        vmem((40, 256), f32),
        vmem((count, D), f32),
        vmem((AREA, LANES), f32),
        vmem((AREA, LANES), f32),
        vmem((D, 3 * WIDE), bf16),
        vmem((WIDE, D), bf16),
        vmem((D, 3 * WIDE), bf16),
        vmem((WIDE, D), bf16),
        vmem((D, FF), bf16),
        vmem((FF, D), bf16),
        vmem((16, D), f32),
        vmem((tokens, D), bf16),
        vmem((tokens, D), f32),
        vmem((tokens, 128), f32),
        vmem((6, tokens, 128), f32),
        vmem((count, AREA, LANES), f32),
        vmem((2, tokens, 128), f32),
        vmem((tokens, WIDE), bf16),
        vmem((tokens, D), f32),
        vmem((tokens, D), bf16),
        vmem((tokens, D), f32),
        vmem((tokens, 128), f32),
        vmem((tokens, 3 * WIDE), bf16),
        vmem((tokens // GROUP, 2, 8, GLANES), f32),
        vmem((tokens, WIDE), bf16),
        vmem((tokens, D), bf16),
        vmem((tokens, FF), bf16),
        vmem((tokens, FF), bf16),
        vmem((tokens, D), bf16),
        vmem((tokens, D), bf16),
        vmem((tokens, D), bf16),
        vmem((tokens, D), f32),
        vmem((tokens, D), f32),
        vmem((tokens, WIDE), bf16),
        vmem((tokens, 3 * WIDE), bf16),
        vmem((tokens, 3 * WIDE), bf16),
        vmem((9, 8, D), f32),
        vmem((4, buckets * tiles - marks[6] // 128, 128), f32),
        pltpu.SemaphoreType.DMA((move_slots(sizes, slots_here)[-1],)),
        pltpu.SemaphoreType.DMA((move_slots(sizes, slots_here)[-1],)),
        pltpu.SemaphoreType.DMA((SPLITS + 1,)),
        pltpu.SemaphoreType.DMA((5,)),
        pltpu.SemaphoreType.DMA((4 * (slots_here + 1),)),
    ]
    if inside:
        n_place = rows // 2 // spread
        for some in (high - mid, mid - low, buckets - (high - low)):
            scratch += [
                vmem((rows, some, 128), bf16),
                vmem((rows // 2, some, 128), bf16),
                vmem((rows // 2, some, 128), bf16),
                vmem((spread, n_place, some, 128), bf16),
                vmem((n_place, some, 128), bf16),
                vmem((dp_size, n_place // dp_size, some, 128), bf16),
                vmem((n_place, some, 128), bf16),
            ]
        scratch += [
            vmem((lat_size * lon_size, n_place, per_home, 128), bf16),
            vmem((9, D), f32),
            vmem((spread + dp_size, 9, D), f32),
            vmem((2, 9, D), f32),
        ]
    else:
        scratch += [vmem((9, D), f32)]
    spec = pl.BlockSpec(memory_space=pltpu.VMEM)
    smem = pl.BlockSpec(memory_space=pltpu.SMEM)
    hbm = pl.BlockSpec(memory_space=pl.ANY)
    return pl.pallas_call(
        functools.partial(block_kernel, (sizes, buckets, tiles, slots_here, cuts), inside),
        out_shape=outs,
        in_specs=[smem, smem, spec] + [hbm] * 5,
        out_specs=[hbm] * 4 + [hbm if inside else spec] * 2,
        scratch_shapes=scratch,
        compiler_params=pltpu.CompilerParams(
            vmem_limit_bytes=62 * 1024 * 1024, collective_id=0, has_side_effects=True
        ),
        name="block",
    )(
        homes,
        leads,
        homes[None, :],
        master,
        inputs,
        cotangent,
        jnp.asarray(entry),
        jnp.asarray(place),
    )


def finish_kernel(marks, steps_ref, homes_ref, *refs):
    sources, targets = refs[:9], refs[9:15]
    held, made = refs[15:24], refs[24:29]
    spare_ref, incoming, outgoing = refs[29:]
    fetches = [
        pltpu.make_async_copy(src, dst, incoming.at[number])
        for number, (src, dst) in enumerate(zip(sources, held))
    ]
    for fetch in fetches:
        fetch.start()
    back_res_ref, back_res_tail_ref, back_in_ref, back_in_tail_ref = held[:4]
    grads_ref, vectors_ref, master_ref, one_ref, two_ref = held[4:]
    result_ref, grad_inputs_ref, new_master, new_one, new_two = made
    homes, width = master_ref.shape
    tiles = width // 128
    leaves = []

    def leave(src, dst):
        copy = pltpu.make_async_copy(src, dst, outgoing.at[len(leaves)])
        copy.start()
        leaves.append(copy)

    levels = result_ref.shape[3]
    for number, (top_ref, tail_ref, out_ref) in enumerate(
        (
            (back_res_ref, back_res_tail_ref, result_ref),
            (back_in_ref, back_in_tail_ref, grad_inputs_ref),
        )
    ):
        for fetch in fetches[2 * number : 2 * number + 2]:
            fetch.wait()
        for slot in range(out_ref.shape[0]):

            @pl.loop(0, WIN_LAT)
            def _(row):
                out_ref[slot, row, :, :, 0:128] = top_ref[slot, row].astype(out_ref.dtype)
                tail = tail_ref[row].astype(f32).reshape(WIN_LON * levels, 128)
                tail = (pltpu.roll(tail, 64, 1) if slot else tail)[:, : D - 128]
                out_ref[slot, row, :, :, 128:D] = tail.reshape(WIN_LON, levels, D - 128).astype(
                    out_ref.dtype
                )

            leave(out_ref.at[slot], targets[number].at[slot])
    for fetch in fetches[4:]:
        fetch.wait()
    leave(vectors_ref, targets[2])
    place = lax.axis_index("dp") * lax.axis_size("lat") + lax.axis_index("lat")
    place = (place * lax.axis_size("lon") + lax.axis_index("lon")) * homes
    slots = lax.broadcasted_iota(jnp.int32, (homes, 1), 0) + place
    match = homes_ref[...] == slots
    bucket = lax.broadcasted_iota(jnp.int32, match.shape, 1)
    held = jnp.max(jnp.where(match, bucket, -1), axis=1, keepdims=True)
    base = jnp.where(held >= 0, held * width, marks[8])

    top = marks[7] // 128
    spare_ref[...] = jnp.zeros_like(spare_ref)
    lanes = lax.broadcasted_iota(jnp.int32, (1, 128), 1)
    for index in range(9):
        vector = vectors_ref[index : index + 1, :]
        start = marks[7] + D * index
        tail = jnp.concatenate([vector[:, 128:], jnp.zeros((1, 256 - D), f32)], axis=1)
        for values, size, begin in ((vector[:, :128], 128, start), (tail, D - 128, start + 128)):
            row, lane = divmod(begin - 128 * top, 128)
            moved = pltpu.roll(values, lane, 1) if lane else values
            spare_ref[row : row + 1, :] += jnp.where(lanes >= lane, moved, 0.0)
            if lane + size > 128:
                spare_ref[row + 1 : row + 2, :] += jnp.where(lanes < lane, moved, 0.0)

    steps = jnp.full((homes, 128), steps_ref[0], jnp.int32).astype(f32)
    fix_one = 1.0 / (1.0 - jnp.exp(steps * math.log(beta_one)))
    fix_two = 1.0 / (1.0 - jnp.exp(steps * math.log(beta_two)))
    rates = [
        2.6 / math.sqrt(D),
        8.0 / math.sqrt(D),
        2.6 / math.sqrt(D),
        4.0 / math.sqrt(D),
        2.0 / math.sqrt(D),
        3.0 / math.sqrt(FF),
        1.0,
        0.6,
    ]
    spread = jnp.broadcast_to(base, (homes, 128)) + lax.broadcasted_iota(jnp.int32, (homes, 128), 1)
    for tile in range(tiles):
        columns = slice(128 * tile, 128 * (tile + 1))
        index = spread + 128 * tile
        rate = jnp.full((homes, 128), 0.1, f32)
        for number in range(7, -1, -1):
            rate = jnp.where(index < marks[number + 1], rates[number], rate)
        grad = grads_ref[tile].astype(f32)
        for owner in range(marks[7] // width, (marks[8] - 1) // width + 1):
            row = owner * tiles + tile - top
            if 0 <= row < spare_ref.shape[0]:
                grad = grad + jnp.where(held == owner, spare_ref[row : row + 1, :], 0.0)
        weights = master_ref[:, columns]
        first = beta_one * one_ref[:, columns] + (1.0 - beta_one) * grad
        second = beta_two * two_ref[:, columns] + (1.0 - beta_two) * grad * grad
        step = first * fix_one / (jnp.sqrt(second * fix_two) + eps_adam) + decay_rate * weights
        new_master[:, columns] = weights - rate * step
        new_one[:, columns] = first
        new_two[:, columns] = second
    for src, dst in zip(made[2:], targets[3:]):
        leave(src, dst)
    for copy in leaves:
        copy.wait()


def finish_call(marks, steps, homes, grads, vectors, master, one, two, backs):
    grid = backs[0].shape[:4] + (D,)
    shape = jax.ShapeDtypeStruct
    hbm = pl.BlockSpec(memory_space=pl.ANY)
    operands = [*backs, grads, vectors, master, one, two]
    outs = [shape(grid, bf16), shape(grid, f32), shape(vectors.shape, f32)]
    outs += [shape(master.shape, f32)] * 3
    made = outs[:2] + outs[3:]
    return pl.pallas_call(
        functools.partial(finish_kernel, marks),
        out_shape=outs,
        in_specs=[pl.BlockSpec(memory_space=pltpu.SMEM), pl.BlockSpec(memory_space=pltpu.VMEM)]
        + [hbm] * len(operands),
        out_specs=[hbm] * len(outs),
        scratch_shapes=[pltpu.VMEM(some.shape, some.dtype) for some in operands + made]
        + [
            pltpu.VMEM((16, 128), f32),
            pltpu.SemaphoreType.DMA((len(operands),)),
            pltpu.SemaphoreType.DMA((8,)),
        ],
        name="finish",
    )(steps, homes[None, :], *operands)


def per_device(
    inputs, cotangent, lead_counts, home_slots, master, moment_one, moment_two, step_count
):
    axes = ("dp", "lat", "lon")
    sizes = tuple(lax.axis_size(axis) for axis in axes)
    slots_mine, bucket_width = master.shape
    tiles = bucket_width // 128
    order = (0, 2, 3, 1, 4)
    *backs, grads, vectors = block_call(
        home_slots, lead_counts, master, inputs.transpose(order), cotangent.transpose(order), sizes
    )
    if not sum_rows(sizes, tiles)[1]:
        spread = jnp.zeros((tiles, math.prod(sizes) * slots_mine, 128), f32)
        spread = spread.at[:, home_slots].set(grads)
        grads = lax.psum_scatter(spread, axes, scatter_dimension=1, tiled=True)
        vectors = lax.psum(vectors, axes)
    result, grad_inputs, grad_vectors, *new = finish_call(
        offsets(sizes[1] + 1),
        step_count,
        home_slots,
        grads,
        vectors,
        master,
        moment_one,
        moment_two,
        backs,
    )
    order = (0, 3, 1, 2, 4)
    return (result.transpose(order), grad_inputs.transpose(order), grad_vectors, *new)


def solution(mesh):
    in_specs = (
        P("dp", None, "lat", "lon", None),
        P("dp", None, "lat", "lon", None),
        P(),
        P(),
        P(("dp", "lat", "lon"), None),
        P(("dp", "lat", "lon"), None),
        P(("dp", "lat", "lon"), None),
        P(),
    )
    out_specs = (
        P("dp", None, "lat", "lon", None),
        P("dp", None, "lat", "lon", None),
        P(),
        P(("dp", "lat", "lon"), None),
        P(("dp", "lat", "lon"), None),
        P(("dp", "lat", "lon"), None),
    )
    return jax.shard_map(
        per_device, mesh=mesh, in_specs=in_specs, out_specs=out_specs, check_vma=False
    )
```

```python
import functools
import math

import jax
import jax.numpy as jnp
import ml_dtypes
import numpy as np
from jax import lax
from jax.experimental import pallas as pl
from jax.experimental.pallas import tpu as pltpu
from jax.sharding import PartitionSpec as P

D = 192
FF = 768
HEADS = 6
HEAD_DIM = 32
LEVELS = 8
WIN_LAT = 6
WIN_LON = 12
LEADS = 4
HALF_LAT = WIN_LAT // 2
HALF_LON = WIN_LON // 2
QUAD = HALF_LAT * HALF_LON
AREA = WIN_LAT * WIN_LON
SIDE_HEADS = HEADS // 2
SIDE = SIDE_HEADS * HEAD_DIM
HEAD_ROWS = 80
LANES = 512
WIDE = 256
SCALE = 1.0 / math.sqrt(HEAD_DIM)

beta_one = 0.6
beta_two = 0.45
eps_norm = 1e-05
eps_adam = 1e-08
decay_rate = 0.1
penalty_value = -1000000000.0
bf16 = jnp.bfloat16
f32 = jnp.float32


def offsets(groups):
    sizes_list = [
        3 * D * D,
        D * D,
        3 * D * D,
        D * D,
        D * FF,
        FF * D,
        groups * HEADS * WIN_LAT * WIN_LAT * (2 * WIN_LON - 1),
        9 * D,
    ]
    segment_marks = [0]
    for amount in sizes_list:
        segment_marks.append(segment_marks[-1] + amount)
    return segment_marks


def nn(left, right):
    return jnp.dot(left, right, preferred_element_type=f32)


def nt(left, right):
    return lax.dot_general(left, right, (((1,), (1,)), ((), ())), preferred_element_type=f32)


def tn(left, right):
    return lax.dot_general(left, right, (((0,), (0,)), ((), ())), preferred_element_type=f32)


def normed(values):
    center = values - jnp.sum(values, axis=-1, keepdims=True) * (1.0 / D)
    spread = jnp.sum(center * center, axis=-1, keepdims=True) * (1.0 / D)
    inverse = lax.rsqrt(spread + eps_norm)
    return center * inverse, inverse


def norm_back(grad, hat, inverse, gain):
    scaled = grad * gain
    mean_one = jnp.sum(scaled, axis=-1, keepdims=True) * (1.0 / D)
    mean_two = jnp.sum(scaled * hat, axis=-1, keepdims=True) * (1.0 / D)
    return inverse * (scaled - mean_one - hat * mean_two)


def row_fold(values):
    return jnp.sum(values.reshape(values.shape[0] // 8, 8, values.shape[1]), axis=0)


def head_masks():
    lane = lax.broadcasted_iota(jnp.int32, (1, 128), 1) // HEAD_DIM
    return [jnp.where(lane == head, 1.0, 0.0).astype(bf16) for head in range(SIDE_HEADS)]


def spread_heads(values, masks):
    return jnp.concatenate([values * mask for mask in masks], axis=0)


def spread_window(values, masks):
    full = jnp.concatenate([values, jnp.zeros((HEAD_ROWS - AREA, 128), f32)], axis=0).astype(bf16)
    rest = jnp.zeros((LANES // 2 - SIDE_HEADS * HEAD_ROWS, 128), bf16)
    return jnp.concatenate([spread_heads(full, masks), rest], axis=0)


def fold_heads(big, step, count):
    lane = lax.broadcasted_iota(jnp.int32, (count, 128), 1)
    parts = [big[head * step : head * step + count] for head in range(SIDE_HEADS)]
    out = parts[-1]
    for head in range(SIDE_HEADS - 2, -1, -1):
        out = jnp.where(lane < HEAD_DIM * (head + 1), parts[head], out)
    return out


def rounded(values):
    return values.astype(bf16).astype(f32)


def soft_columns(scores):
    exps = jnp.exp(scores - jnp.max(scores, axis=0, keepdims=True))
    return exps * (1.0 / jnp.sum(exps, axis=0, keepdims=True))


def soft_back(probs, slopes):
    return probs * (slopes - jnp.sum(probs * slopes, axis=0, keepdims=True))


GROUP = 64
GLANES = SIDE_HEADS * GROUP
CHUNK = 288


def lanes_of(ref, start):
    row, lane = divmod(start, 128)
    here = ref[row : row + 1, :]
    if lane == 0:
        return here
    place = lax.broadcasted_iota(jnp.int32, (1, 128), 1)
    mixed = jnp.where(place >= lane, here, ref[row + 1 : row + 2, :])
    return pltpu.roll(mixed, 128 - lane, 1)


def lanes_from(first, second, lane, size):
    place = lax.broadcasted_iota(jnp.int32, first.shape, 1)
    if lane:
        first = pltpu.roll(jnp.where(place >= lane, first, second), 128 - lane, 1)
    return jnp.where(place < size, first, 0.0) if size < 128 else first


def lanes_join(first, begin, size, second):
    place = lax.broadcasted_iota(jnp.int32, first.shape, 1)
    moved = pltpu.roll(first, 128 - begin, 1) if begin else first
    return jnp.where(place < size, moved, pltpu.roll(second, size, 1))


EARTH_ROW = WIN_LAT * (2 * WIN_LON - 1)
EARTH_ROWS = HEADS * WIN_LAT


def earth_tables():
    entry = np.zeros((WIN_LON, AREA, 256), np.float32)
    place = np.zeros((WIN_LON, 40, LANES), np.float32)
    for column in range(WIN_LON):
        side, inner = divmod(column, HALF_LON)
        for key in range(AREA):
            key_up, rest = divmod(key, 2 * QUAD)
            key_side, rest = divmod(rest, QUAD)
            key_row, key_inner = divmod(rest, HALF_LON)
            row = key_up * HALF_LAT + key_row
            offset = column - (key_side * HALF_LON + key_inner) + WIN_LON - 1
            entry[column, key, row * (2 * WIN_LON - 1) + offset] = 1.0
        for head in range(HEADS):
            for row in range(WIN_LAT):
                up, low = divmod(row, HALF_LAT)
                lane = 2 * QUAD * up + QUAD * side + HALF_LON * low + inner
                lane += LANES // 2 * (head // SIDE_HEADS) + HEAD_ROWS * (head % SIDE_HEADS)
                place[column, head * WIN_LAT + row, lane] = 1.0
    return entry.astype(ml_dtypes.bfloat16), place.astype(ml_dtypes.bfloat16)


MESH = pl.DeviceIdType.MESH


def places():
    lat_size, lon_size, dp_size = lax.axis_size("lat"), lax.axis_size("lon"), lax.axis_size("dp")
    return (
        lax.axis_index("dp"),
        lax.axis_index("lat"),
        lax.axis_index("lon"),
        dp_size,
        lat_size,
        lon_size,
    )


def greet(targets):
    barrier = pltpu.get_barrier_semaphore()
    for target in targets:
        pl.semaphore_signal(barrier, inc=1, device_id=target, device_id_type=MESH)


def greeted_wait(count):
    pl.semaphore_wait(pltpu.get_barrier_semaphore(), count)


def split(value, size):
    if size & (size - 1) == 0:
        return lax.shift_right_logical(value, size.bit_length() - 1), value & (size - 1)
    return lax.div(value, size), lax.rem(value, size)


def around(place, step, size):
    return split(place + step, size)[1]


def neighbours(whole_plane):
    dp, lat, lon, dp_size, lat_size, lon_size = places()
    if whole_plane:
        steps = {(i, j) for i in range(lat_size) for j in range(lon_size)}
    else:
        steps = {(1, 0), (lat_size - 1, 0), (1, 1 % lon_size), (lat_size - 1, lon_size - 1)}
        steps |= {(2 * i, 0) for i in range(1, lat_size // 2)} | {(0, j) for j in range(lon_size)}
    steps.discard((0, 0))
    found = [(around(dp, step, dp_size), lat, lon) for step in range(1, dp_size)]
    return found + [
        (dp, around(lat, i, lat_size), around(lon, j, lon_size)) for i, j in sorted(steps)
    ]


def pairing(src, dst, sends, receives, send_slot, receive_slot, target):
    return pltpu.make_async_remote_copy(
        src_ref=src,
        dst_ref=dst,
        send_sem=sends.at[send_slot],
        recv_sem=receives.at[receive_slot],
        device_id=target,
        device_id_type=MESH,
    )


def gather_slots(sizes, splits):
    dp_size, lat_size, lon_size = sizes
    return splits * dp_size * (2 * max(lat_size // 2, lon_size) + 2)


def gather_steps(sizes, own_ref, all_ref, sends, receives, keep_sem):
    splits, skew = SPLITS, SKEW
    dp_size, lat_size, lon_size = sizes
    chips = lat_size // 2
    dp, lat, lon = lax.axis_index("dp"), lax.axis_index("lat"), lax.axis_index("lon")
    chip, core = split(lat, 2)
    wide = max(chips, lon_size)
    first = splits * dp_size
    second = first + splits * dp_size * wide
    cross = second + splits * dp_size * wide
    per = own_ref.shape[0] // splits
    order = sorted(range(dp_size), key=lambda step: min(step, dp_size - step))
    items = [(part, 0) for part in range(splits)]
    items += [(part, step) for part in range(splits) for step in order[1:]]

    def chip_at(step):
        return (dp, around(chip, step, chips) * 2 + core, lon)

    def lon_at(step):
        return (dp, lat, around(lon, step, lon_size))

    units = chips * lon_size

    def stretch(part, step, side, first, size):
        start = ((part * dp_size + around(dp, step, dp_size)) * 2 + side) * units + first
        return all_ref.at[pl.ds(start * per, size * per)]

    def run(mine, hooks, late_hook):
        unit = lon * chips + chip if mine == 0 else chip * lon_size + lon
        one, two = (chips, lon_size) if mine == 0 else (lon_size, chips)
        one_at, two_at = (chip_at, lon_at) if mine == 0 else (lon_at, chip_at)
        place_two = lon if mine == 0 else chip
        partner = (dp, chip * 2 + 1 - mine, lon)
        begun = []

        def send(src, dst, slot, back, target):
            copy = pairing(src, dst, sends, receives, slot, back, target)
            copy.start()
            begun.append(copy)

        def arrive(dst, slot):
            pairing(dst, dst, sends, receives, slot, slot, partner).wait_recv()

        def own_part(part):
            return own_ref.at[pl.ds(part * per, per)]

        def chunk(part, step):
            return stretch(part, step, mine, unit, 1)

        def group(part, step):
            return stretch(part, step, mine, place_two * one, one)

        def whole(part, step, side):
            return stretch(part, step, side, 0, units)

        keeps = []
        for part in range(splits):
            keep = pltpu.make_async_copy(own_part(part), chunk(part, 0), keep_sem.at[part])
            keep.start()
            keeps.append(keep)

        def line(part):
            for step in order[1:]:
                target = (around(dp, step, dp_size), lat, lon)
                base = part * dp_size
                send(own_part(part), chunk(part, 0), base + step, base + dp_size - step, target)

        def stage_one(part, step):
            if step:
                arrive(chunk(part, step), part * dp_size + step)
            base = first + (part * dp_size + step) * wide
            src = chunk(part, step) if step else own_part(part)
            for far in range(1, one):
                send(src, chunk(part, step), base + far, base + one - far, one_at(far))

        def stage_two(part, step):
            base = first + (part * dp_size + step) * wide
            for far in range(1, one):
                arrive(chunk(part, step), base + far)
            if step == 0:
                keeps[part].wait()
            base = second + (part * dp_size + step) * wide
            for far in range(1, two):
                send(group(part, step), group(part, step), base + far, base + two - far, two_at(far))

        def stage_three(part, step):
            base = second + (part * dp_size + step) * wide
            for far in range(1, two):
                arrive(group(part, step), base + far)
            slot = cross + part * dp_size + step
            send(whole(part, step, mine), whole(part, step, mine), slot, slot, partner)

        for part in range(splits):
            line(part)
        for turn in range(len(items) + 2 * skew):
            for stage, place in ((stage_one, turn), (stage_two, turn - skew), (stage_three, turn - 2 * skew)):
                if 0 <= place < len(items):
                    stage(*items[place])
            if turn in hooks:
                hooks[turn]()
        late_hook()
        for part, step in items:
            arrive(whole(part, step, 1 - mine), cross + part * dp_size + step)
        for copy in begun:
            copy.wait_send()

    return run


def move_slots(sizes, slots):
    dp_size, lat_size, lon_size = sizes
    spread = lat_size // 2 * lon_size
    moves = gather_slots(sizes, SPLITS)
    sums = moves + 16 * (slots + 1)
    vectors = sums + 3 * (1 + spread + 2 * dp_size)
    hand = vectors + 1 + spread + dp_size
    return moves, sums, vectors, hand, hand + lat_size * lon_size


SPLITS = 2
FF_STEP = 256
SKEW = 3


def block_kernel(
    shape_info,
    inside,
    home_ref,
    lead_ref,
    homes_ref,
    master_ref,
    inputs_ref,
    cotangent_ref,
    entry_hbm,
    place_hbm,
    back_res_ref,
    back_res_tail_ref,
    back_in_ref,
    back_in_tail_ref,
    grads_ref,
    total_ref,
    spot_ref,
    weights_ref,
    grid_ref,
    grid_tail_ref,
    entry_ref,
    place_ref,
    own_ref,
    all_ref,
    tok_ref,
    tok_tail_ref,
    res_ref,
    res_tail_ref,
    flat_ref,
    mid_ref,
    earth_ref,
    gate_ref,
    bias_ref,
    dbias_ref,
    w1_ref,
    o1_ref,
    w2_ref,
    o2_ref,
    up_ref,
    down_ref,
    vec_ref,
    n1_ref,
    hat1_ref,
    inv1_ref,
    qkv_ref,
    probs_ref,
    att_ref,
    att1_ref,
    tok1_ref,
    n2_ref,
    hat2_ref,
    inv2_ref,
    mix2_ref,
    cprobs_ref,
    att2_ref,
    n3_ref,
    act_ref,
    gh_ref,
    delta3_ref,
    delta2_ref,
    delta1_ref,
    gmid_ref,
    glow_ref,
    gatt2_ref,
    gm2_ref,
    gm1_ref,
    vacc_ref,
    around_ref,
    sends,
    receives,
    keeps,
    fetched,
    kept,
    *sum_refs,
):
    levels = tok_ref.shape[5]
    chunks = 4
    sizes, buckets, tiles, slots_here, cuts = shape_info
    count = slots_here * levels
    tokens = count * AREA
    dp_size, lat_size, lon_size = sizes
    chips = lat_size // 2
    spread = chips * lon_size
    dp, lat, lon = lax.axis_index("dp"), lax.axis_index("lat"), lax.axis_index("lon")
    chip, core = split(lat, 2)
    is_last = lat == lat_size - 1
    moves, sum_slots, vector_slots, hand_slots, _ = move_slots(sizes, slots_here)
    begun = []

    def send(src, dst, slot, back, target):
        copy = pairing(src, dst, sends, receives, slot, back, target)
        copy.start()
        begun.append(copy)

    def arrive(dst, slot):
        pairing(dst, dst, sends, receives, slot, slot, (dp, lat, lon)).wait_recv()

    def pieces(kind, start, quads=range(4)):
        for quad in quads:
            up, left = quad // 2, quad % 2
            way = 1 if kind > 1 else -1
            target = (
                dp,
                around(lat, way * up % lat_size, lat_size),
                around(lon, way * left % lon_size, lon_size),
            )
            grid, grid_tail = (
                (inputs_ref, grid_tail_ref.at[0]),
                (cotangent_ref, grid_tail_ref.at[1]),
                (back_res_ref, back_res_tail_ref),
                (back_in_ref, back_in_tail_ref),
            )[kind]
            held, held_tail = (res_ref, res_tail_ref) if kind > 1 else (tok_ref, tok_tail_ref)
            rows = pl.ds(HALF_LAT * (1 - up), HALF_LAT)
            columns = pl.ds(HALF_LON * (1 - left), HALF_LON)
            pairs = [(grid_tail.at[rows, columns], held_tail.at[quad, kind % 2])]
            for slot in range(slots_here):
                on_grid = grid.at[slot, rows, columns]
                on_grid = on_grid if kind > 1 else on_grid.at[:, :, :, pl.ds(0, 128)]
                pairs.append((on_grid, held.at[quad, kind % 2, :, :, slot]))
            for number, (on_grid, in_quads) in enumerate(pairs):
                src, dst = (in_quads, on_grid) if kind > 1 else (on_grid, in_quads)
                place = len(pairs) * (4 * kind + quad) + number
                if quad == 0:
                    copy = pltpu.make_async_copy(src, dst, kept.at[kind * len(pairs) + number])
                    copy.start() if start else copy.wait()
                elif start:
                    send(src, dst, moves + place, moves + place, target)
                else:
                    arrive(dst, moves + place)

    def shift(kind, quads=range(4)):
        pieces(kind, True, quads)

    def shifted(kind):
        pieces(kind, False)

    def part(index):
        return pl.ds(pl.multiple_of(index * CHUNK, CHUNK), CHUNK)

    fetches = [
        pltpu.make_async_copy(source, target, fetched.at[index])
        for index, (source, target) in enumerate(
            (
                (master_ref, weights_ref),
                (inputs_ref, grid_ref.at[0]),
                (cotangent_ref, grid_ref.at[1]),
                (entry_hbm, entry_ref),
                (place_hbm, place_ref),
            )
        )
    ]
    for fetch in fetches:
        fetch.start()
    def pack_tail(kind):
        @pl.loop(0, WIN_LAT)
        def _(row):
            tails = [
                grid_ref[kind, slot, row].astype(f32)[:, :, 128:].reshape(WIN_LON * levels, D - 128)
                for slot in range(2)
            ]
            grid_tail_ref[kind, row] = (
                jnp.concatenate(tails, axis=1).reshape(WIN_LON, levels, 128).astype(bf16)
            )

    def tokens_of(kind, c):
        top = tok_ref[c, kind].astype(f32).reshape(CHUNK, 128)
        tails = tok_tail_ref[c, kind].astype(f32).reshape(QUAD * levels, 128)
        both = [tails, pltpu.roll(tails, 64, 1)]
        both = jnp.concatenate([tail.reshape(QUAD, 1, levels, 128) for tail in both], axis=1)
        return jnp.concatenate([top, both.reshape(CHUNK, 128)[:, : D - 128]], axis=1)

    def keep_tokens(kind, c, values):
        res_ref[c, kind] = values[:, :128].reshape(res_ref.shape[2:]).astype(bf16)
        tails = values[:, 128:].reshape(QUAD, 2, levels, D - 128)
        tails = [tails[:, slot].reshape(QUAD * levels, D - 128) for slot in range(2)]
        tails = jnp.concatenate(tails, axis=1).reshape(res_tail_ref.shape[2:])
        res_tail_ref[c, kind] = tails.astype(bf16)

    greeted = neighbours(inside)
    greet(greeted)

    per_home, own_rows = own_ref.shape[:2]
    flat_ref[pl.ds(0, per_home * own_rows), :] = jnp.zeros((per_home * own_rows, 128), f32)
    fetches[0].wait()
    for tile in range(tiles):
        flat_ref[pl.ds(tile, per_home, stride=own_rows), :] = weights_ref[
            :, 128 * tile : 128 * (tile + 1)
        ]
    for slot in range(per_home):
        own_ref[slot] = flat_ref[pl.ds(slot * own_rows, own_rows), :].astype(bf16)
    fetches[1].wait()
    pack_tail(0)
    greeted_wait(len(greeted))

    def center_tokens():
        fetches[2].wait()
        pack_tail(1)
        for bucket in range(buckets):
            home = home_ref[bucket]
            device, slot = split(home, per_home)
            rest, home_lon = split(device, lon_size)
            home_dp, home_lat = split(rest, lat_size)
            home_chip, home_core = split(home_lat, 2)
            unit = jnp.where(
                home_core == 0, home_lon * chips + home_chip, home_chip * lon_size + home_lon
            )
            side, inner = split(slot, per_home // SPLITS)
            chunk = (side * dp_size + home_dp) * 2 + home_core
            spot_ref[bucket] = (chunk * spread + unit) * (per_home // SPLITS) + inner
        shifted(0)

        @pl.loop(0, chunks)
        def _(c):
            rows = part(c)
            hat, inverse = normed(tokens_of(0, c))
            hat1_ref[rows, :] = hat
            inv1_ref[rows, :] = jnp.broadcast_to(inverse, (CHUNK, 128))

    gather = gather_steps(sizes, own_ref, all_ref, sends, receives, keeps)
    hooks = {0: functools.partial(shift, 0)}
    for mine in range(2):

        @pl.when(core == mine)
        def _():
            gather(mine, hooks, center_tokens)
            for copy in begun:
                copy.wait_send()
            begun.clear()

    shift(1)
    for fetch in fetches[3:]:
        fetch.wait()
    vacc_ref[...] = jnp.zeros_like(vacc_ref)
    marks = offsets(lat_size + 1)
    row_marks = [mark // 128 for mark in marks]

    for bucket in range(buckets):
        block = all_ref[spot_ref[bucket]].astype(f32)
        flat_ref[tiles * bucket : tiles * (bucket + 1), :] = block[:tiles]

    def take_pairs(base, parts, pairs):
        return [flat_ref[pl.ds(base + part, pairs, stride=parts), :] for part in range(parts)]

    def give_pairs(columns, rows, evens, odds):
        for column, (even, odd) in enumerate(zip(evens, odds)):
            mid_ref[column, pl.ds(0, rows // 2, stride=2), :] = even
            mid_ref[column, pl.ds(1, rows // 2, stride=2), :] = odd

    def load_qkv(base, ref):
        b = take_pairs(base, 9, D // 2)
        pieces = []
        for first in range(0, 9, 3):
            x, y, z = b[first : first + 3]
            pieces += [
                lanes_from(x, x, 0, SIDE),
                lanes_from(x, y, 96, SIDE),
                lanes_from(y, z, 64, SIDE),
                lanes_from(z, z, 32, SIDE),
            ]
        give_pairs(6, D, pieces[:6], pieces[6:])
        for column in range(6):
            ref[:, 128 * column : 128 * (column + 1)] = mid_ref[column, pl.ds(0, D), :].astype(bf16)

    def load_square(base, rows, ref, spans):
        b = take_pairs(base, 3, rows // 2)
        odds = [lanes_from(b[1], b[2], 64, 128), lanes_from(b[2], b[2], 64, D - 128)]
        give_pairs(2, rows, [b[0], b[1]], odds)
        for first, last, target in spans:
            size = last - first
            ref[target : target + size, 0:128] = mid_ref[0, pl.ds(first, size), :].astype(bf16)
            ref[target : target + size, 128:D] = mid_ref[1, pl.ds(first, size), :][
                :, : D - 128
            ].astype(bf16)

    sides = [(0, SIDE, 0), (SIDE, D, 128)]
    load_qkv(row_marks[0], w1_ref)
    load_square(row_marks[1], D, o1_ref, sides)
    load_qkv(row_marks[2], w2_ref)
    load_square(row_marks[3], D, o2_ref, sides)
    for ref in (o1_ref, o2_ref):
        for side in range(2):
            ref[128 * side + SIDE : 128 * (side + 1), :] = jnp.zeros((128 - SIDE, D), bf16)
    for column in range(6):
        up_ref[:, 128 * column : 128 * (column + 1)] = flat_ref[
            pl.ds(row_marks[4] + column, D, stride=6), :
        ].astype(bf16)
    load_square(row_marks[5], FF, down_ref, [(0, FF, 0)])
    for index in range(9):
        start = marks[7] + D * index
        vec_ref[index : index + 1, 0:128] = lanes_of(flat_ref, start)
        vec_ref[index : index + 1, 128:D] = lanes_of(flat_ref, start + 128)[:, : D - 128]

    def earth_places():
        group_one = lat + 1
        group_two = jnp.where(is_last, 0, lat + 1)
        for index in range(EARTH_ROWS):
            group = group_one if index % WIN_LAT < HALF_LAT else group_two
            start = marks[6] + EARTH_ROW * (EARTH_ROWS * group + index)
            yield (index,) + split(start, 128)

    lane_place = lax.broadcasted_iota(jnp.int32, (1, 128), 1)
    earth_ref[...] = jnp.zeros_like(earth_ref)
    for index, row, lane in earth_places():
        rows = [flat_ref[pl.ds(row + step, 1), :] for step in range(3)]
        back = (128 - lane) & 127
        first = pltpu.roll(jnp.where(lane_place >= lane, rows[0], rows[1]), back, 1)
        second = pltpu.roll(jnp.where(lane_place >= lane, rows[1], rows[2]), back, 1)
        earth_ref[index : index + 1, 0:128] = first
        earth_ref[index : index + 1, 128:256] = jnp.where(lane_place < EARTH_ROW - 128, second, 0.0)
    earth = earth_ref[...].astype(bf16)
    key_up = lax.broadcasted_iota(jnp.int32, (AREA, LANES), 0) // (2 * QUAD)
    query_up = lax.broadcasted_iota(jnp.int32, (AREA, LANES), 1) & (LANES // 2 - 1)
    query_up = lax.rem(query_up, HEAD_ROWS) // (2 * QUAD)
    bias = jnp.where((key_up != query_up) & is_last, penalty_value, 0.0)
    for column in range(WIN_LON):
        bias = bias + nn(nt(entry_ref[column], earth).astype(bf16), place_ref[column])
    bias_ref[...] = bias

    for slot in range(slots_here):
        number = lax.axis_index("dp") * slots_here + slot
        sample, lead = split(number, LEADS)
        live = lead < lead_ref[sample]
        size = count // slots_here
        gate_ref[slot * size : (slot + 1) * size, :] = jnp.full((size, D), jnp.where(live, 1.0, 0.0), f32)

    def vec(index):
        return vec_ref[index : index + 1, :]

    def gate_rows():
        gate = gate_ref[...]
        return jnp.broadcast_to(gate[None], (CHUNK // count, count, D)).reshape(CHUNK, D)

    def note(index, values):
        vacc_ref[index] += row_fold(values)

    def note_low(index, values):
        top = lax.broadcasted_iota(jnp.int32, (8, CHUNK), 0) == 0
        vacc_ref[index] += nn(jnp.where(top, 1.0, 0.0).astype(bf16), values)

    def first_mixed(c):
        rows = part(c)
        low = (hat1_ref[rows, :] * vec(0) + vec(1)).astype(bf16)
        n1_ref[rows, :] = low
        mixed = rounded(nn(low, w1_ref[...]))
        for tile in range(6):
            qkv_ref[tile, rows, :] = mixed[:, 128 * tile : 128 * (tile + 1)]

    for c in range(chunks):
        first_mixed(c)

    def window(ref, tile, s):
        return ref[tile, pl.ds(s, AREA, stride=count), :]

    def window_store(ref, tile, s, values):
        ref[tile, pl.ds(s, AREA, stride=count), :] = values

    halves = [slice(0, LANES // 2), slice(LANES // 2, LANES)]

    @pl.loop(0, count // 4)
    def _(block):
        masks = head_masks()
        places = [(block * 4 + step, side) for step in range(4) for side in range(2)]
        reads = [[window(qkv_ref, 2 * kind + side, s) for kind in range(3)] for s, side in places]
        raw = [
            nt(key.astype(bf16), spread_window(query, masks)) for query, key, _ in reads
        ]
        probs = [
            soft_columns(scores * SCALE + bias_ref[:, halves[side]])
            for scores, (_, side) in zip(raw, places)
        ]
        outs = [tn(prob.astype(bf16), read[2].astype(bf16)) for prob, read in zip(probs, reads)]
        for (s, side), prob, out in zip(places, probs, outs):
            probs_ref[s, :, halves[side]] = prob
            window_store(att_ref, side, s, fold_heads(out, HEAD_ROWS, AREA))

    def second_mixed(c):
        rows = part(c)
        att = jnp.concatenate([att_ref[0, rows, :], att_ref[1, rows, :]], axis=1).astype(bf16)
        att1_ref[rows, :] = att
        branch = nn(att, o1_ref[...]) + vec(2)
        tok = tokens_of(0, c) + gate_rows() * branch
        tok1_ref[rows, :] = tok
        hat, inverse = normed(tok)
        hat2_ref[rows, :] = hat
        inv2_ref[rows, :] = jnp.broadcast_to(inverse, (CHUNK, 128))
        low = (hat * vec(3) + vec(4)).astype(bf16)
        n2_ref[rows, :] = low
        mix2_ref[rows, :] = nn(low, w2_ref[...]).astype(bf16)

    for c in range(chunks):
        second_mixed(c)

    def column_masks():
        lane = lax.broadcasted_iota(jnp.int32, (8, GLANES), 1)
        place = lax.shift_right_logical(lane & (GROUP - 1), 3)
        return [place == index for index in range(GROUP // 8)]

    def squeeze_column(values, masks):
        out = values[:8]
        for index in range(1, GROUP // 8):
            out = jnp.where(masks[index], values[8 * index : 8 * index + 8], out)
        return out

    def widen_column(values, masks):
        return jnp.concatenate([jnp.where(mask, values, 0.0) for mask in masks], axis=0).astype(bf16)

    def group_rows(g):
        return pl.ds(pl.multiple_of(g * GROUP, GROUP), GROUP)

    def tile_of(ref, g, kind, side):
        first = WIDE * kind + 128 * side
        return ref[group_rows(g), first : first + 128]

    @pl.loop(0, tokens // GROUP // 6)
    def _(block):
        heads = head_masks()
        columns = column_masks()
        places = [(block * 6 + step, side) for step in range(6) for side in range(2)]
        reads = [[tile_of(mix2_ref, g, kind, side) for kind in range(3)] for g, side in places]
        raw = [nt(key, spread_heads(query, heads)) for query, key, _ in reads]
        probs = [soft_columns(squeeze_column(scores, columns) * SCALE) for scores in raw]
        outs = [tn(widen_column(prob, columns), read[2]) for prob, read in zip(probs, reads)]
        for (g, side), prob, out in zip(places, probs, outs):
            cprobs_ref[g, side] = prob
            att2_ref[group_rows(g), 128 * side : 128 * (side + 1)] = fold_heads(
                out, GROUP, GROUP
            ).astype(bf16)

    root = math.sqrt(2.0 / math.pi)
    shifted(1)

    @pl.loop(0, chunks)
    def _(c):
        rows = part(c)
        gate = gate_rows()
        tok = tok1_ref[rows, :] + gate * (nn(att2_ref[rows, :], o2_ref[...]) + vec(5))
        hat, inverse = normed(tok)
        low = (hat * vec(6) + vec(7)).astype(bf16)
        n3_ref[rows, :] = low
        after = tokens_of(1, c)
        delta3 = (gate * after).astype(bf16)
        delta3_ref[rows, :] = delta3
        note_low(8, delta3)
        for first in range(0, FF, FF_STEP):
            columns = slice(first, first + FF_STEP)
            hidden = nn(low, up_ref[:, columns])
            square = hidden * hidden
            half = 0.5 * jnp.tanh(hidden * (root + (root * 0.044715) * square)) + 0.5
            wave = hidden * half
            act_ref[rows, columns] = wave.astype(bf16)
            slope = half + wave * (1.0 - half) * (2.0 * root + (6.0 * root * 0.044715) * square)
            gh_ref[rows, columns] = (nt(delta3, down_ref[columns, :]) * slope).astype(bf16)
        keep_tokens(0, c, tok + gate * (nn(act_ref[rows, :], down_ref[...]) + vec(8)))
        gh = gh_ref[rows, :]
        grad = nt(gh, up_ref[...])
        note(6, grad * hat)
        note(7, grad)
        mid = after + norm_back(grad, hat, inverse, vec(6))
        gmid_ref[rows, :] = mid
        delta2 = (gate * mid).astype(bf16)
        delta2_ref[rows, :] = delta2
        note_low(5, delta2)
        gatt2_ref[rows, :] = nt(delta2, o2_ref[...]).astype(bf16)

    def keep_pairs(base, parts, blocks):
        for number, block in enumerate(blocks):
            flat_ref[pl.ds(base + number, block.shape[0], stride=parts), :] = block

    def split_pairs(columns, rows):
        evens = [mid_ref[column, pl.ds(0, rows // 2, stride=2), :] for column in range(columns)]
        odds = [mid_ref[column, pl.ds(1, rows // 2, stride=2), :] for column in range(columns)]
        return evens, odds

    def save_qkv(base, grad):
        for column in range(6):
            mid_ref[column, pl.ds(0, D), :] = grad[:, 128 * column : 128 * (column + 1)]
        e, o = split_pairs(6, D)
        pieces = e + o
        blocks = []
        for first in range(0, 12, 4):
            x, y, z, w = pieces[first : first + 4]
            blocks += [
                lanes_join(x, 0, 96, y),
                lanes_join(y, 32, 64, z),
                lanes_join(z, 64, 32, w),
            ]
        keep_pairs(base, 9, blocks)

    def save_square(base, rows, grad):
        mid_ref[0, pl.ds(0, rows), :] = grad[:, :128]
        mid_ref[1, pl.ds(0, rows), 0 : D - 128] = grad[:, 128:]
        e, o = split_pairs(2, rows)
        keep_pairs(
            base, 3, [e[0], lanes_join(e[1], 0, 64, o[0]), lanes_join(o[0], 64, 64, o[1])]
        )

    def used_rows(grad):
        return jnp.concatenate([grad[0:SIDE], grad[128 : 128 + SIDE]], axis=0)

    partner = (dp, chip * 2 + 1 - core, lon)
    place = chip * lon_size + lon

    def peers():
        for i in range(chips):
            for j in range(lon_size):
                if i or j:
                    back = (chips - i) % chips * lon_size + (lon_size - j) % lon_size
                    there = (around(chip, i, chips), around(lon, j, lon_size))
                    target = (dp, there[0] * 2 + core, there[1])
                    yield i * lon_size + j, back, there[0] * lon_size + there[1], target

    def line():
        for step in range(1, dp_size):
            there = around(dp, step, dp_size)
            yield step, dp_size - step, there, (there, lat, lon)

    def summing(base, grad, half_in, half, plane_in, mid, line_in, full):
        n_half = grad.shape[0] // 2
        n_place = n_half // spread
        n_line = n_place // dp_size

        def cross():
            send(grad.at[pl.ds((1 - core) * n_half, n_half)], half_in, base, base, partner)

        def plane():
            arrive(half_in, base)
            for first in range(0, n_half, 12):
                rows = pl.ds(first, 12)
                kept = grad[pl.ds(core * n_half + first, 12)].astype(f32)
                half[rows] = (kept + half_in[rows].astype(f32)).astype(bf16)
            for index, back, there, target in peers():
                send(
                    half.at[pl.ds(there * n_place, n_place)],
                    plane_in.at[back],
                    base + 1 + index,
                    base + 1 + back,
                    target,
                )

        def along():
            total = half[pl.ds(place * n_place, n_place)].astype(f32)
            for index in range(1, spread):
                arrive(plane_in.at[index], base + 1 + index)
                total = total + plane_in[index].astype(f32)
            mid[...] = total.astype(bf16)
            slots = base + 1 + spread
            for step, back, there, target in line():
                send(mid.at[pl.ds(there * n_line, n_line)], line_in.at[back], slots + step, slots + back, target)

        def share():
            slots = base + 1 + spread
            rows = pl.ds(dp * n_line, n_line)
            total = mid[rows].astype(f32)
            for step in range(1, dp_size):
                arrive(line_in.at[step], slots + step)
                total = total + line_in[step].astype(f32)
            full[rows] = total.astype(bf16)
            slots += dp_size
            for step, back, _, target in line():
                send(full.at[rows], full.at[rows], slots + step, slots + back, target)

        def done():
            slots = base + 1 + spread + dp_size
            for step, _, there, _ in line():
                arrive(full.at[pl.ds(there * n_line, n_line)], slots + step)

        return cross, plane, along, share, done

    spans = [[(cuts[1], cuts[2])], [(cuts[0], cuts[1])], [(0, cuts[0]), (cuts[2], buckets)]]
    if inside:
        sum_sets = [sum_refs[7 * number : 7 * (number + 1)] for number in range(3)]
        hand_out, vec_sum, vec_in, vec_now = sum_refs[21:]
        each = 1 + spread + 2 * dp_size
        soon, early, late = [
            summing(sum_slots + each * number, *refs) for number, refs in enumerate(sum_sets)
        ]

        def pack(number):
            grad = sum_sets[number][0]
            for tile in range(grad.shape[0]):
                if tile < tiles:
                    rows = [
                        flat_ref[pl.ds(tile + tiles * begin, end - begin, stride=tiles), :]
                        for begin, end in spans[number]
                    ]
                    values = rows[0] if len(rows) == 1 else jnp.concatenate(rows, axis=0)
                    grad[tile] = values.astype(bf16)
                else:
                    grad[tile] = jnp.zeros(grad.shape[1:], bf16)
    else:
        (vec_sum,) = sum_refs

    shift(2)

    grad_up = tn(n3_ref[...], gh_ref[...])
    for column in range(6):
        flat_ref[pl.ds(row_marks[4] + column, D, stride=6), :] = grad_up[
            :, 128 * column : 128 * (column + 1)
        ]
    save_square(row_marks[5], FF, tn(act_ref[...], delta3_ref[...]))
    if inside:
        pack(0)
        soon[0]()


    @pl.loop(0, tokens // GROUP // 6)
    def _(block):
        heads = head_masks()
        columns = column_masks()
        places = [(block * 6 + step, side) for step in range(6) for side in range(2)]
        reads = [
            [tile_of(mix2_ref, g, kind, side) for kind in range(3)]
            + [tile_of(gatt2_ref, g, 0, side), cprobs_ref[g, side]]
            for g, side in places
        ]
        grads = [spread_heads(read[3], heads) for read in reads]
        raw = [nt(read[2], grad) for read, grad in zip(reads, grads)]
        dvalues = [nn(widen_column(read[4], columns), grad) for read, grad in zip(reads, grads)]
        lows = [
            widen_column(soft_back(read[4], squeeze_column(slopes, columns)), columns)
            for read, slopes in zip(reads, raw)
        ]
        dkeys = [nn(low, spread_heads(read[0], heads)) for read, low in zip(reads, lows)]
        dqueries = [tn(low, read[1]) for read, low in zip(reads, lows)]
        for (g, side), dquery, dkey, dvalue in zip(places, dqueries, dkeys, dvalues):
            for kind, values in enumerate(
                (fold_heads(dquery, GROUP, GROUP) * SCALE, dkey * SCALE, dvalue)
            ):
                first = WIDE * kind + 128 * side
                gm2_ref[group_rows(g), first : first + 128] = values.astype(bf16)

    if inside:
        soon[1]()

    def second_back(c):
        rows = part(c)
        grad = nt(gm2_ref[rows, :], w2_ref[...])
        hat = hat2_ref[rows, :]
        inverse = inv2_ref[rows, :][:, :1]
        note(3, grad * hat)
        note(4, grad)
        low = gmid_ref[rows, :] + norm_back(grad, hat, inverse, vec(3))
        glow_ref[rows, :] = low
        delta1 = (gate_rows() * low).astype(bf16)
        delta1_ref[rows, :] = delta1
        note_low(2, delta1)
        gatt = rounded(nt(delta1, o1_ref[...]))
        att_ref[0, rows, :] = gatt[:, :128]
        att_ref[1, rows, :] = gatt[:, 128:]

    for c in range(chunks):
        second_back(c)

    save_square(row_marks[1], D, used_rows(tn(att1_ref[...], delta1_ref[...])))
    save_qkv(row_marks[2], tn(n2_ref[...], gm2_ref[...]))
    save_square(row_marks[3], D, used_rows(tn(att2_ref[...], delta2_ref[...])))

    if inside:
        pack(1)
        early[0]()
        soon[2]()

    dbias_ref[...] = jnp.zeros_like(dbias_ref)

    def window_back(block):
        masks = head_masks()
        places = [(block * 4 + step, side) for step in range(4) for side in range(2)]
        reads = [
            [window(qkv_ref, 2 * kind + side, s) for kind in range(3)]
            + [window(att_ref, side, s), probs_ref[s, :, halves[side]]]
            for s, side in places
        ]
        grads = [spread_window(read[3], masks) for read in reads]
        raw = [nt(read[2].astype(bf16), grad) for read, grad in zip(reads, grads)]
        dvalues = [nn(read[4].astype(bf16), grad) for read, grad in zip(reads, grads)]
        lows = [soft_back(read[4], slopes).astype(bf16) for read, slopes in zip(reads, raw)]
        dkeys = [nn(low, spread_window(read[0], masks)) for read, low in zip(reads, lows)]
        dqueries = [tn(low, read[1].astype(bf16)) for read, low in zip(reads, lows)]
        for side in range(2):
            dbias_ref[:, halves[side]] += functools.reduce(
                jnp.add, [low.astype(f32) for low, (_, there) in zip(lows, places) if there == side]
            )
        for (s, side), dquery, dkey, dvalue in zip(places, dqueries, dkeys, dvalues):
            dquery = fold_heads(dquery, HEAD_ROWS, AREA) * SCALE
            for kind, values in enumerate((dquery, dkey * SCALE, dvalue)):
                window_store(qkv_ref, 2 * kind + side, s, rounded(values))

    @pl.loop(0, 2)
    def _(block):
        window_back(block)

    if inside:
        early[1]()
        soon[3]()

    @pl.loop(2, count // 4)
    def _(block):
        window_back(block)

    @pl.loop(0, chunks)
    def _(c):
        rows = part(c)
        gm1_ref[rows, :] = jnp.concatenate(
            [qkv_ref[tile, rows, :] for tile in range(6)], axis=1
        ).astype(bf16)

    save_qkv(row_marks[0], tn(n1_ref[...], gm1_ref[...]))
    rest = flat_ref.shape[0] - row_marks[6]
    around_ref[...] = jnp.zeros_like(around_ref)
    dbias = dbias_ref[...].astype(bf16)
    moved = [nt(dbias, place_ref[column]).astype(bf16) for column in range(WIN_LON)]
    dearth = functools.reduce(
        jnp.add, [tn(moved[column], entry_ref[column]) for column in range(WIN_LON)]
    )
    for index, row, lane in earth_places():
        row = row - row_marks[6]
        first = pltpu.roll(dearth[index : index + 1, :128], lane, 1)
        second = pltpu.roll(dearth[index : index + 1, 128:], lane, 1)
        tail = lane_place >= lane
        for step, values in enumerate(
            (
                jnp.where(tail, first, 0.0),
                jnp.where(tail, second, first),
                jnp.where(tail, 0.0, second),
            )
        ):
            around_ref[index % 4, pl.ds(row + step, 1), :] += values
    flat_ref[row_marks[6] :, :] = functools.reduce(
        jnp.add, [around_ref[number, 0:rest, :] for number in range(4)]
    )
    if inside:
        early[2]()
        pack(2)
        late[0]()

    def input_grads(c):
        rows = part(c)
        mixed = gm1_ref[rows, :]
        grad = nt(mixed, w1_ref[...])
        hat = hat1_ref[rows, :]
        inverse = inv1_ref[rows, :][:, :1]
        note(0, grad * hat)
        note(1, grad)
        grad_in = glow_ref[rows, :] + norm_back(grad, hat, inverse, vec(0))
        keep_tokens(1, c, grad_in)

    for c in (2, 3):
        input_grads(c)

    if inside:
        late[1]()

    for c in (1, 0):
        input_grads(c)

    for index in range(9):
        vec_sum[index : index + 1, :] = jnp.sum(vacc_ref[index], axis=0, keepdims=True)
    if inside:
        send(vec_sum, vec_in.at[0], vector_slots, vector_slots, partner)
        early[3]()
        arrive(vec_in.at[0], vector_slots)
        vec_now[0] = vec_sum[...] + vec_in[0]
        for index, back, _, target in peers():
            send(vec_now.at[0], vec_in.at[back], vector_slots + 1 + index, vector_slots + 1 + back, target)
    shift(3)
    if inside:
        late[2]()
        vec_total = vec_now[0]
        for index in range(1, spread):
            arrive(vec_in.at[index], vector_slots + 1 + index)
            vec_total = vec_total + vec_in[index]
        vec_now[1] = vec_total
        slots = vector_slots + 1 + spread
        for step, back, _, target in line():
            send(vec_now.at[1], vec_in.at[spread + back], slots + step, slots + back, target)
        late[3]()
        soon[4]()
        early[4]()
        homes = lat_size * lon_size
        width = homes * per_home
        slot_ids = lax.broadcasted_iota(jnp.int32, (width, 1), 0) + dp * width
        all_homes = homes_ref[...]
        picks = []
        for some in spans:
            held = [all_homes[:, begin:end] for begin, end in some]
            held = held[0] if len(held) == 1 else jnp.concatenate(held, axis=1)
            picks.append(jnp.where(slot_ids == held, 1.0, 0.0).astype(bf16))
        n_rows = hand_out.shape[1]
        owned_first = [
            nn(picks[0], sum_sets[0][6][row]) + nn(picks[1], sum_sets[1][6][row])
            for row in range(n_rows)
        ]
        late[4]()
        for row in range(n_rows):
            owned = owned_first[row] + nn(picks[2], sum_sets[2][6][row])
            for home in range(homes):
                hand_out[home, row] = owned[per_home * home : per_home * (home + 1), :].astype(bf16)
        first = core * (n_rows * spread) + place * n_rows
        landing = grads_ref.at[pl.ds(first, n_rows)]
        me = lat * lon_size + lon
        keep_hand = pltpu.make_async_copy(hand_out.at[me], landing, keeps.at[SPLITS])
        keep_hand.start()
        for i in range(lat_size):
            for j in range(lon_size):
                if i or j:
                    target = (dp, around(lat, i, lat_size), around(lon, j, lon_size))
                    back = (lat_size - i) % lat_size * lon_size + (lon_size - j) % lon_size
                    send(
                        hand_out.at[target[1] * lon_size + target[2]],
                        landing,
                        hand_slots + i * lon_size + j,
                        hand_slots + back,
                        target,
                    )
        for step in range(1, dp_size):
            arrive(vec_in.at[spread + step], slots + step)
            vec_total = vec_total + vec_in[spread + step]
        vec_in[0] = vec_total
        keep_total = pltpu.make_async_copy(vec_in.at[0], total_ref, keeps.at[0])
        keep_total.start()
        keep_hand.wait()
        keep_total.wait()
        for index in range(1, homes):
            arrive(landing, hand_slots + index)
    else:
        total_ref[...] = vec_sum[...]
        for tile in range(tiles):
            grads_ref[tile] = flat_ref[pl.ds(tile, buckets, stride=tiles), :]
    shifted(2)
    shifted(3)
    for copy in begun:
        copy.wait_send()


def sum_rows(sizes, tiles):
    unit = sizes[0] * sizes[1] * sizes[2]
    rows = -(-tiles // unit) * unit
    return rows, rows <= 2 * tiles


def block_call(homes, leads, master, inputs, cotangent, sizes):
    slots_here, levels = inputs.shape[0], inputs.shape[3]
    count = slots_here * levels
    tokens = count * AREA
    buckets = homes.shape[0]
    per_home, width = master.shape
    tiles = width // 128
    own_rows = -(-tiles // 16) * 16
    quads = (4, 2, HALF_LAT, HALF_LON, slots_here, levels, 128)
    tails = (4, 2, HALF_LAT, HALF_LON, levels, 128)
    assert slots_here == 2
    dp_size, lat_size, lon_size = sizes
    spread = lat_size // 2 * lon_size
    rows, inside = sum_rows(sizes, tiles)
    marks = offsets(lat_size + 1)
    low = -(-marks[1] // width)
    mid = -(-marks[4] // width)
    high = marks[6] // width
    mid += (high - mid) % 8
    low += (mid - low) % 8
    cuts = (low, mid, high)
    shape = jax.ShapeDtypeStruct
    outs = [
        shape(inputs.shape[:4] + (128,), bf16),
        shape(inputs.shape[1:4] + (128,), bf16),
        shape(inputs.shape[:4] + (128,), bf16),
        shape(inputs.shape[1:4] + (128,), bf16),
        shape((rows, per_home, 128), bf16) if inside else shape((tiles, buckets, 128), f32),
        shape((9, D), f32),
    ]
    vmem = pltpu.VMEM
    entry, place = earth_tables()
    scratch = [
        pltpu.SMEM((buckets,), jnp.int32),
        vmem(master.shape, f32),
        vmem((2,) + inputs.shape, bf16),
        vmem((2, WIN_LAT, WIN_LON, levels, 128), bf16),
        vmem(entry.shape, bf16),
        vmem(place.shape, bf16),
        vmem((per_home, own_rows, 128), bf16),
        vmem((dp_size * lat_size * lon_size * per_home, own_rows, 128), bf16),
        vmem(quads, bf16),
        vmem(tails, bf16),
        vmem(quads, bf16),
        vmem(tails, bf16),
        vmem((buckets * tiles, 128), f32),
        vmem((6, FF, 128), f32),
        vmem((40, 256), f32),
        vmem((count, D), f32),
        vmem((AREA, LANES), f32),
        vmem((AREA, LANES), f32),
        vmem((D, 3 * WIDE), bf16),
        vmem((WIDE, D), bf16),
        vmem((D, 3 * WIDE), bf16),
        vmem((WIDE, D), bf16),
        vmem((D, FF), bf16),
        vmem((FF, D), bf16),
        vmem((16, D), f32),
        vmem((tokens, D), bf16),
        vmem((tokens, D), f32),
        vmem((tokens, 128), f32),
        vmem((6, tokens, 128), f32),
        vmem((count, AREA, LANES), f32),
        vmem((2, tokens, 128), f32),
        vmem((tokens, WIDE), bf16),
        vmem((tokens, D), f32),
        vmem((tokens, D), bf16),
        vmem((tokens, D), f32),
        vmem((tokens, 128), f32),
        vmem((tokens, 3 * WIDE), bf16),
        vmem((tokens // GROUP, 2, 8, GLANES), f32),
        vmem((tokens, WIDE), bf16),
        vmem((tokens, D), bf16),
        vmem((tokens, FF), bf16),
        vmem((tokens, FF), bf16),
        vmem((tokens, D), bf16),
        vmem((tokens, D), bf16),
        vmem((tokens, D), bf16),
        vmem((tokens, D), f32),
        vmem((tokens, D), f32),
        vmem((tokens, WIDE), bf16),
        vmem((tokens, 3 * WIDE), bf16),
        vmem((tokens, 3 * WIDE), bf16),
        vmem((9, 8, D), f32),
        vmem((4, buckets * tiles - marks[6] // 128, 128), f32),
        pltpu.SemaphoreType.DMA((move_slots(sizes, slots_here)[-1],)),
        pltpu.SemaphoreType.DMA((move_slots(sizes, slots_here)[-1],)),
        pltpu.SemaphoreType.DMA((SPLITS + 1,)),
        pltpu.SemaphoreType.DMA((5,)),
        pltpu.SemaphoreType.DMA((4 * (slots_here + 1),)),
    ]
    if inside:
        n_place = rows // 2 // spread
        for some in (high - mid, mid - low, buckets - (high - low)):
            scratch += [
                vmem((rows, some, 128), bf16),
                vmem((rows // 2, some, 128), bf16),
                vmem((rows // 2, some, 128), bf16),
                vmem((spread, n_place, some, 128), bf16),
                vmem((n_place, some, 128), bf16),
                vmem((dp_size, n_place // dp_size, some, 128), bf16),
                vmem((n_place, some, 128), bf16),
            ]
        scratch += [
            vmem((lat_size * lon_size, n_place, per_home, 128), bf16),
            vmem((9, D), f32),
            vmem((spread + dp_size, 9, D), f32),
            vmem((2, 9, D), f32),
        ]
    else:
        scratch += [vmem((9, D), f32)]
    spec = pl.BlockSpec(memory_space=pltpu.VMEM)
    smem = pl.BlockSpec(memory_space=pltpu.SMEM)
    hbm = pl.BlockSpec(memory_space=pl.ANY)
    return pl.pallas_call(
        functools.partial(block_kernel, (sizes, buckets, tiles, slots_here, cuts), inside),
        out_shape=outs,
        in_specs=[smem, smem, spec] + [hbm] * 5,
        out_specs=[hbm] * 4 + [hbm if inside else spec] * 2,
        scratch_shapes=scratch,
        compiler_params=pltpu.CompilerParams(
            vmem_limit_bytes=62 * 1024 * 1024, collective_id=0, has_side_effects=True
        ),
        name="block",
    )(
        homes,
        leads,
        homes[None, :],
        master,
        inputs,
        cotangent,
        jnp.asarray(entry),
        jnp.asarray(place),
    )


def finish_kernel(marks, steps_ref, homes_ref, *refs):
    sources, targets = refs[:9], refs[9:15]
    held, made = refs[15:24], refs[24:29]
    spare_ref, incoming, outgoing = refs[29:]
    fetches = [
        pltpu.make_async_copy(src, dst, incoming.at[number])
        for number, (src, dst) in enumerate(zip(sources, held))
    ]
    for fetch in fetches:
        fetch.start()
    back_res_ref, back_res_tail_ref, back_in_ref, back_in_tail_ref = held[:4]
    grads_ref, vectors_ref, master_ref, one_ref, two_ref = held[4:]
    result_ref, grad_inputs_ref, new_master, new_one, new_two = made
    homes, width = master_ref.shape
    tiles = width // 128
    leaves = []

    def leave(src, dst):
        copy = pltpu.make_async_copy(src, dst, outgoing.at[len(leaves)])
        copy.start()
        leaves.append(copy)

    levels = result_ref.shape[3]
    for number, (top_ref, tail_ref, out_ref) in enumerate(
        (
            (back_res_ref, back_res_tail_ref, result_ref),
            (back_in_ref, back_in_tail_ref, grad_inputs_ref),
        )
    ):
        for fetch in fetches[2 * number : 2 * number + 2]:
            fetch.wait()
        for slot in range(out_ref.shape[0]):

            @pl.loop(0, WIN_LAT)
            def _(row):
                out_ref[slot, row, :, :, 0:128] = top_ref[slot, row].astype(out_ref.dtype)
                tail = tail_ref[row].astype(f32).reshape(WIN_LON * levels, 128)
                tail = (pltpu.roll(tail, 64, 1) if slot else tail)[:, : D - 128]
                out_ref[slot, row, :, :, 128:D] = tail.reshape(WIN_LON, levels, D - 128).astype(
                    out_ref.dtype
                )

            leave(out_ref.at[slot], targets[number].at[slot])
    for fetch in fetches[4:]:
        fetch.wait()
    leave(vectors_ref, targets[2])
    place = lax.axis_index("dp") * lax.axis_size("lat") + lax.axis_index("lat")
    place = (place * lax.axis_size("lon") + lax.axis_index("lon")) * homes
    slots = lax.broadcasted_iota(jnp.int32, (homes, 1), 0) + place
    match = homes_ref[...] == slots
    bucket = lax.broadcasted_iota(jnp.int32, match.shape, 1)
    held = jnp.max(jnp.where(match, bucket, -1), axis=1, keepdims=True)
    base = jnp.where(held >= 0, held * width, marks[8])

    top = marks[7] // 128
    spare_ref[...] = jnp.zeros_like(spare_ref)
    lanes = lax.broadcasted_iota(jnp.int32, (1, 128), 1)
    for index in range(9):
        vector = vectors_ref[index : index + 1, :]
        start = marks[7] + D * index
        tail = jnp.concatenate([vector[:, 128:], jnp.zeros((1, 256 - D), f32)], axis=1)
        for values, size, begin in ((vector[:, :128], 128, start), (tail, D - 128, start + 128)):
            row, lane = divmod(begin - 128 * top, 128)
            moved = pltpu.roll(values, lane, 1) if lane else values
            spare_ref[row : row + 1, :] += jnp.where(lanes >= lane, moved, 0.0)
            if lane + size > 128:
                spare_ref[row + 1 : row + 2, :] += jnp.where(lanes < lane, moved, 0.0)

    steps = jnp.full((homes, 128), steps_ref[0], jnp.int32).astype(f32)
    fix_one = 1.0 / (1.0 - jnp.exp(steps * math.log(beta_one)))
    fix_two = 1.0 / (1.0 - jnp.exp(steps * math.log(beta_two)))
    rates = [
        2.6 / math.sqrt(D),
        8.0 / math.sqrt(D),
        2.6 / math.sqrt(D),
        4.0 / math.sqrt(D),
        2.0 / math.sqrt(D),
        3.0 / math.sqrt(FF),
        1.0,
        0.6,
    ]
    spread = jnp.broadcast_to(base, (homes, 128)) + lax.broadcasted_iota(jnp.int32, (homes, 128), 1)
    for tile in range(tiles):
        columns = slice(128 * tile, 128 * (tile + 1))
        index = spread + 128 * tile
        rate = jnp.full((homes, 128), 0.1, f32)
        for number in range(7, -1, -1):
            rate = jnp.where(index < marks[number + 1], rates[number], rate)
        grad = grads_ref[tile].astype(f32)
        for owner in range(marks[7] // width, (marks[8] - 1) // width + 1):
            row = owner * tiles + tile - top
            if 0 <= row < spare_ref.shape[0]:
                grad = grad + jnp.where(held == owner, spare_ref[row : row + 1, :], 0.0)
        weights = master_ref[:, columns]
        first = beta_one * one_ref[:, columns] + (1.0 - beta_one) * grad
        second = beta_two * two_ref[:, columns] + (1.0 - beta_two) * grad * grad
        step = first * fix_one / (jnp.sqrt(second * fix_two) + eps_adam) + decay_rate * weights
        new_master[:, columns] = weights - rate * step
        new_one[:, columns] = first
        new_two[:, columns] = second
    for src, dst in zip(made[2:], targets[3:]):
        leave(src, dst)
    for copy in leaves:
        copy.wait()


def finish_call(marks, steps, homes, grads, vectors, master, one, two, backs):
    grid = backs[0].shape[:4] + (D,)
    shape = jax.ShapeDtypeStruct
    hbm = pl.BlockSpec(memory_space=pl.ANY)
    operands = [*backs, grads, vectors, master, one, two]
    outs = [shape(grid, bf16), shape(grid, f32), shape(vectors.shape, f32)]
    outs += [shape(master.shape, f32)] * 3
    made = outs[:2] + outs[3:]
    return pl.pallas_call(
        functools.partial(finish_kernel, marks),
        out_shape=outs,
        in_specs=[pl.BlockSpec(memory_space=pltpu.SMEM), pl.BlockSpec(memory_space=pltpu.VMEM)]
        + [hbm] * len(operands),
        out_specs=[hbm] * len(outs),
        scratch_shapes=[pltpu.VMEM(some.shape, some.dtype) for some in operands + made]
        + [
            pltpu.VMEM((16, 128), f32),
            pltpu.SemaphoreType.DMA((len(operands),)),
            pltpu.SemaphoreType.DMA((8,)),
        ],
        name="finish",
    )(steps, homes[None, :], *operands)


def per_device(
    inputs, cotangent, lead_counts, home_slots, master, moment_one, moment_two, step_count
):
    axes = ("dp", "lat", "lon")
    sizes = tuple(lax.axis_size(axis) for axis in axes)
    slots_mine, bucket_width = master.shape
    tiles = bucket_width // 128
    order = (0, 2, 3, 1, 4)
    *backs, grads, vectors = block_call(
        home_slots, lead_counts, master, inputs.transpose(order), cotangent.transpose(order), sizes
    )
    if not sum_rows(sizes, tiles)[1]:
        spread = jnp.zeros((tiles, math.prod(sizes) * slots_mine, 128), f32)
        spread = spread.at[:, home_slots].set(grads)
        grads = lax.psum_scatter(spread, axes, scatter_dimension=1, tiled=True)
        vectors = lax.psum(vectors, axes)
    result, grad_inputs, grad_vectors, *new = finish_call(
        offsets(sizes[1] + 1),
        step_count,
        home_slots,
        grads,
        vectors,
        master,
        moment_one,
        moment_two,
        backs,
    )
    order = (0, 3, 1, 2, 4)
    return (result.transpose(order), grad_inputs.transpose(order), grad_vectors, *new)


def solution(mesh):
    in_specs = (
        P("dp", None, "lat", "lon", None),
        P("dp", None, "lat", "lon", None),
        P(),
        P(),
        P(("dp", "lat", "lon"), None),
        P(("dp", "lat", "lon"), None),
        P(("dp", "lat", "lon"), None),
        P(),
    )
    out_specs = (
        P("dp", None, "lat", "lon", None),
        P("dp", None, "lat", "lon", None),
        P(),
        P(("dp", "lat", "lon"), None),
        P(("dp", "lat", "lon"), None),
        P(("dp", "lat", "lon"), None),
    )
    return jax.shard_map(
        per_device, mesh=mesh, in_specs=in_specs, out_specs=out_specs, check_vma=False
    )
```

```python
import functools
import math

import jax
import jax.numpy as jnp
import ml_dtypes
import numpy as np
from jax import lax
from jax.experimental import pallas as pl
from jax.experimental.pallas import tpu as pltpu
from jax.sharding import PartitionSpec as P

D = 192
FF = 768
HEADS = 6
HEAD_DIM = 32
LEVELS = 8
WIN_LAT = 6
WIN_LON = 12
LEADS = 4
HALF_LAT = WIN_LAT // 2
HALF_LON = WIN_LON // 2
QUAD = HALF_LAT * HALF_LON
AREA = WIN_LAT * WIN_LON
SIDE_HEADS = HEADS // 2
SIDE = SIDE_HEADS * HEAD_DIM
HEAD_ROWS = 80
LANES = 512
WIDE = 256
SCALE = 1.0 / math.sqrt(HEAD_DIM)

beta_one = 0.6
beta_two = 0.45
eps_norm = 1e-05
eps_adam = 1e-08
decay_rate = 0.1
penalty_value = -1000000000.0
bf16 = jnp.bfloat16
f32 = jnp.float32


def offsets(groups):
    sizes_list = [
        3 * D * D,
        D * D,
        3 * D * D,
        D * D,
        D * FF,
        FF * D,
        groups * HEADS * WIN_LAT * WIN_LAT * (2 * WIN_LON - 1),
        9 * D,
    ]
    segment_marks = [0]
    for amount in sizes_list:
        segment_marks.append(segment_marks[-1] + amount)
    return segment_marks


def nn(left, right):
    return jnp.dot(left, right, preferred_element_type=f32)


def nt(left, right):
    return lax.dot_general(left, right, (((1,), (1,)), ((), ())), preferred_element_type=f32)


def tn(left, right):
    return lax.dot_general(left, right, (((0,), (0,)), ((), ())), preferred_element_type=f32)


def normed(values):
    center = values - jnp.sum(values, axis=-1, keepdims=True) * (1.0 / D)
    spread = jnp.sum(center * center, axis=-1, keepdims=True) * (1.0 / D)
    inverse = lax.rsqrt(spread + eps_norm)
    return center * inverse, inverse


def norm_back(grad, hat, inverse, gain):
    scaled = grad * gain
    mean_one = jnp.sum(scaled, axis=-1, keepdims=True) * (1.0 / D)
    mean_two = jnp.sum(scaled * hat, axis=-1, keepdims=True) * (1.0 / D)
    return inverse * (scaled - mean_one - hat * mean_two)


def row_fold(values):
    return jnp.sum(values.reshape(values.shape[0] // 8, 8, values.shape[1]), axis=0)


def head_masks():
    lane = lax.broadcasted_iota(jnp.int32, (1, 128), 1) // HEAD_DIM
    return [jnp.where(lane == head, 1.0, 0.0).astype(bf16) for head in range(SIDE_HEADS)]


def spread_heads(values, masks):
    return jnp.concatenate([values * mask for mask in masks], axis=0)


def spread_window(values, masks):
    full = jnp.concatenate([values, jnp.zeros((HEAD_ROWS - AREA, 128), f32)], axis=0).astype(bf16)
    rest = jnp.zeros((LANES // 2 - SIDE_HEADS * HEAD_ROWS, 128), bf16)
    return jnp.concatenate([spread_heads(full, masks), rest], axis=0)


def fold_heads(big, step, count):
    lane = lax.broadcasted_iota(jnp.int32, (count, 128), 1)
    parts = [big[head * step : head * step + count] for head in range(SIDE_HEADS)]
    out = parts[-1]
    for head in range(SIDE_HEADS - 2, -1, -1):
        out = jnp.where(lane < HEAD_DIM * (head + 1), parts[head], out)
    return out


def rounded(values):
    return values.astype(bf16).astype(f32)


def soft_columns(scores):
    exps = jnp.exp(scores - jnp.max(scores, axis=0, keepdims=True))
    return exps * (1.0 / jnp.sum(exps, axis=0, keepdims=True))


def soft_back(probs, slopes):
    return probs * (slopes - jnp.sum(probs * slopes, axis=0, keepdims=True))


GROUP = 64
GLANES = SIDE_HEADS * GROUP
CHUNK = 288


def lanes_of(ref, start):
    row, lane = divmod(start, 128)
    here = ref[row : row + 1, :]
    if lane == 0:
        return here
    place = lax.broadcasted_iota(jnp.int32, (1, 128), 1)
    mixed = jnp.where(place >= lane, here, ref[row + 1 : row + 2, :])
    return pltpu.roll(mixed, 128 - lane, 1)


def lanes_from(first, second, lane, size):
    place = lax.broadcasted_iota(jnp.int32, first.shape, 1)
    if lane:
        first = pltpu.roll(jnp.where(place >= lane, first, second), 128 - lane, 1)
    return jnp.where(place < size, first, 0.0) if size < 128 else first


def lanes_join(first, begin, size, second):
    place = lax.broadcasted_iota(jnp.int32, first.shape, 1)
    moved = pltpu.roll(first, 128 - begin, 1) if begin else first
    return jnp.where(place < size, moved, pltpu.roll(second, size, 1))


EARTH_ROW = WIN_LAT * (2 * WIN_LON - 1)
EARTH_ROWS = HEADS * WIN_LAT


def earth_tables():
    entry = np.zeros((WIN_LON, AREA, 256), np.float32)
    place = np.zeros((WIN_LON, 40, LANES), np.float32)
    for column in range(WIN_LON):
        side, inner = divmod(column, HALF_LON)
        for key in range(AREA):
            key_up, rest = divmod(key, 2 * QUAD)
            key_side, rest = divmod(rest, QUAD)
            key_row, key_inner = divmod(rest, HALF_LON)
            row = key_up * HALF_LAT + key_row
            offset = column - (key_side * HALF_LON + key_inner) + WIN_LON - 1
            entry[column, key, row * (2 * WIN_LON - 1) + offset] = 1.0
        for head in range(HEADS):
            for row in range(WIN_LAT):
                up, low = divmod(row, HALF_LAT)
                lane = 2 * QUAD * up + QUAD * side + HALF_LON * low + inner
                lane += LANES // 2 * (head // SIDE_HEADS) + HEAD_ROWS * (head % SIDE_HEADS)
                place[column, head * WIN_LAT + row, lane] = 1.0
    return entry.astype(ml_dtypes.bfloat16), place.astype(ml_dtypes.bfloat16)


MESH = pl.DeviceIdType.MESH


def places():
    lat_size, lon_size, dp_size = lax.axis_size("lat"), lax.axis_size("lon"), lax.axis_size("dp")
    return (
        lax.axis_index("dp"),
        lax.axis_index("lat"),
        lax.axis_index("lon"),
        dp_size,
        lat_size,
        lon_size,
    )


def greet(targets):
    barrier = pltpu.get_barrier_semaphore()
    for target in targets:
        pl.semaphore_signal(barrier, inc=1, device_id=target, device_id_type=MESH)


def greeted_wait(count):
    pl.semaphore_wait(pltpu.get_barrier_semaphore(), count)


def split(value, size):
    if size & (size - 1) == 0:
        return lax.shift_right_logical(value, size.bit_length() - 1), value & (size - 1)
    return lax.div(value, size), lax.rem(value, size)


def around(place, step, size):
    return split(place + step, size)[1]


def neighbours(whole_plane):
    dp, lat, lon, dp_size, lat_size, lon_size = places()
    if whole_plane:
        steps = {(i, j) for i in range(lat_size) for j in range(lon_size)}
    else:
        steps = {(1, 0), (lat_size - 1, 0), (1, 1 % lon_size), (lat_size - 1, lon_size - 1)}
        steps |= {(2 * i, 0) for i in range(1, lat_size // 2)} | {(0, j) for j in range(lon_size)}
    steps.discard((0, 0))
    found = [(around(dp, step, dp_size), lat, lon) for step in range(1, dp_size)]
    return found + [
        (dp, around(lat, i, lat_size), around(lon, j, lon_size)) for i, j in sorted(steps)
    ]


def pairing(src, dst, sends, receives, send_slot, receive_slot, target):
    return pltpu.make_async_remote_copy(
        src_ref=src,
        dst_ref=dst,
        send_sem=sends.at[send_slot],
        recv_sem=receives.at[receive_slot],
        device_id=target,
        device_id_type=MESH,
    )


def gather_slots(sizes, splits):
    dp_size, lat_size, lon_size = sizes
    return splits * dp_size * (2 * max(lat_size // 2, lon_size) + 2)


def gather_steps(sizes, own_ref, all_ref, sends, receives, keep_sem):
    splits, skew = SPLITS, SKEW
    dp_size, lat_size, lon_size = sizes
    chips = lat_size // 2
    dp, lat, lon = lax.axis_index("dp"), lax.axis_index("lat"), lax.axis_index("lon")
    chip, core = split(lat, 2)
    wide = max(chips, lon_size)
    first = splits * dp_size
    second = first + splits * dp_size * wide
    cross = second + splits * dp_size * wide
    per = own_ref.shape[0] // splits
    order = sorted(range(dp_size), key=lambda step: min(step, dp_size - step))
    items = [(part, 0) for part in range(splits)]
    items += [(part, step) for part in range(splits) for step in order[1:]]

    def chip_at(step):
        return (dp, around(chip, step, chips) * 2 + core, lon)

    def lon_at(step):
        return (dp, lat, around(lon, step, lon_size))

    units = chips * lon_size

    def stretch(part, step, side, first, size):
        start = ((part * dp_size + around(dp, step, dp_size)) * 2 + side) * units + first
        return all_ref.at[pl.ds(start * per, size * per)]

    def run(mine, hooks, late_hook):
        unit = lon * chips + chip if mine == 0 else chip * lon_size + lon
        one, two = (chips, lon_size) if mine == 0 else (lon_size, chips)
        one_at, two_at = (chip_at, lon_at) if mine == 0 else (lon_at, chip_at)
        place_two = lon if mine == 0 else chip
        partner = (dp, chip * 2 + 1 - mine, lon)
        begun = []

        def send(src, dst, slot, back, target):
            copy = pairing(src, dst, sends, receives, slot, back, target)
            copy.start()
            begun.append(copy)

        def arrive(dst, slot):
            pairing(dst, dst, sends, receives, slot, slot, partner).wait_recv()

        def own_part(part):
            return own_ref.at[pl.ds(part * per, per)]

        def chunk(part, step):
            return stretch(part, step, mine, unit, 1)

        def group(part, step):
            return stretch(part, step, mine, place_two * one, one)

        def whole(part, step, side):
            return stretch(part, step, side, 0, units)

        keeps = []
        for part in range(splits):
            keep = pltpu.make_async_copy(own_part(part), chunk(part, 0), keep_sem.at[part])
            keep.start()
            keeps.append(keep)

        def line(part):
            for step in order[1:]:
                target = (around(dp, step, dp_size), lat, lon)
                base = part * dp_size
                send(own_part(part), chunk(part, 0), base + step, base + dp_size - step, target)

        def stage_one(part, step):
            if step:
                arrive(chunk(part, step), part * dp_size + step)
            base = first + (part * dp_size + step) * wide
            src = chunk(part, step) if step else own_part(part)
            for far in range(1, one):
                send(src, chunk(part, step), base + far, base + one - far, one_at(far))

        def stage_two(part, step):
            base = first + (part * dp_size + step) * wide
            for far in range(1, one):
                arrive(chunk(part, step), base + far)
            if step == 0:
                keeps[part].wait()
            base = second + (part * dp_size + step) * wide
            for far in range(1, two):
                send(group(part, step), group(part, step), base + far, base + two - far, two_at(far))

        def stage_three(part, step):
            base = second + (part * dp_size + step) * wide
            for far in range(1, two):
                arrive(group(part, step), base + far)
            slot = cross + part * dp_size + step
            send(whole(part, step, mine), whole(part, step, mine), slot, slot, partner)

        for part in range(splits):
            line(part)
        for turn in range(len(items) + 2 * skew):
            for stage, place in ((stage_one, turn), (stage_two, turn - skew), (stage_three, turn - 2 * skew)):
                if 0 <= place < len(items):
                    stage(*items[place])
            if turn in hooks:
                hooks[turn]()
        late_hook()
        for part, step in items:
            arrive(whole(part, step, 1 - mine), cross + part * dp_size + step)
        for copy in begun:
            copy.wait_send()

    return run


def move_slots(sizes, slots):
    dp_size, lat_size, lon_size = sizes
    spread = lat_size // 2 * lon_size
    moves = gather_slots(sizes, SPLITS)
    sums = moves + 16 * (slots + 1)
    vectors = sums + 3 * (1 + spread + 2 * dp_size)
    hand = vectors + 1 + spread + dp_size
    return moves, sums, vectors, hand, hand + lat_size * lon_size


SPLITS = 2
FF_STEP = 256
SKEW = 3


def block_kernel(
    shape_info,
    inside,
    home_ref,
    lead_ref,
    homes_ref,
    master_ref,
    inputs_ref,
    cotangent_ref,
    entry_hbm,
    place_hbm,
    back_res_ref,
    back_res_tail_ref,
    back_in_ref,
    back_in_tail_ref,
    grads_ref,
    total_ref,
    spot_ref,
    weights_ref,
    grid_ref,
    grid_tail_ref,
    entry_ref,
    place_ref,
    own_ref,
    all_ref,
    tok_ref,
    tok_tail_ref,
    res_ref,
    res_tail_ref,
    flat_ref,
    mid_ref,
    earth_ref,
    gate_ref,
    bias_ref,
    dbias_ref,
    w1_ref,
    o1_ref,
    w2_ref,
    o2_ref,
    up_ref,
    down_ref,
    vec_ref,
    n1_ref,
    hat1_ref,
    inv1_ref,
    qkv_ref,
    probs_ref,
    att_ref,
    att1_ref,
    tok1_ref,
    n2_ref,
    hat2_ref,
    inv2_ref,
    mix2_ref,
    cprobs_ref,
    att2_ref,
    n3_ref,
    act_ref,
    gh_ref,
    delta3_ref,
    delta2_ref,
    delta1_ref,
    gmid_ref,
    glow_ref,
    gatt2_ref,
    gm2_ref,
    gm1_ref,
    vacc_ref,
    around_ref,
    sends,
    receives,
    keeps,
    fetched,
    kept,
    *sum_refs,
):
    levels = tok_ref.shape[5]
    chunks = 4
    sizes, buckets, tiles, slots_here, cuts = shape_info
    count = slots_here * levels
    tokens = count * AREA
    dp_size, lat_size, lon_size = sizes
    chips = lat_size // 2
    spread = chips * lon_size
    dp, lat, lon = lax.axis_index("dp"), lax.axis_index("lat"), lax.axis_index("lon")
    chip, core = split(lat, 2)
    is_last = lat == lat_size - 1
    moves, sum_slots, vector_slots, hand_slots, _ = move_slots(sizes, slots_here)
    begun = []

    def send(src, dst, slot, back, target):
        copy = pairing(src, dst, sends, receives, slot, back, target)
        copy.start()
        begun.append(copy)

    def arrive(dst, slot):
        pairing(dst, dst, sends, receives, slot, slot, (dp, lat, lon)).wait_recv()

    def pieces(kind, start, quads=range(4)):
        for quad in quads:
            up, left = quad // 2, quad % 2
            way = 1 if kind > 1 else -1
            target = (
                dp,
                around(lat, way * up % lat_size, lat_size),
                around(lon, way * left % lon_size, lon_size),
            )
            grid, grid_tail = (
                (inputs_ref, grid_tail_ref.at[0]),
                (cotangent_ref, grid_tail_ref.at[1]),
                (back_res_ref, back_res_tail_ref),
                (back_in_ref, back_in_tail_ref),
            )[kind]
            held, held_tail = (res_ref, res_tail_ref) if kind > 1 else (tok_ref, tok_tail_ref)
            rows = pl.ds(HALF_LAT * (1 - up), HALF_LAT)
            columns = pl.ds(HALF_LON * (1 - left), HALF_LON)
            pairs = [(grid_tail.at[rows, columns], held_tail.at[quad, kind % 2])]
            for slot in range(slots_here):
                on_grid = grid.at[slot, rows, columns]
                on_grid = on_grid if kind > 1 else on_grid.at[:, :, :, pl.ds(0, 128)]
                pairs.append((on_grid, held.at[quad, kind % 2, :, :, slot]))
            for number, (on_grid, in_quads) in enumerate(pairs):
                src, dst = (in_quads, on_grid) if kind > 1 else (on_grid, in_quads)
                place = len(pairs) * (4 * kind + quad) + number
                if quad == 0:
                    copy = pltpu.make_async_copy(src, dst, kept.at[kind * len(pairs) + number])
                    copy.start() if start else copy.wait()
                elif start:
                    send(src, dst, moves + place, moves + place, target)
                else:
                    arrive(dst, moves + place)

    def shift(kind, quads=range(4)):
        pieces(kind, True, quads)

    def shifted(kind):
        pieces(kind, False)

    def part(index):
        return pl.ds(pl.multiple_of(index * CHUNK, CHUNK), CHUNK)

    fetches = [
        pltpu.make_async_copy(source, target, fetched.at[index])
        for index, (source, target) in enumerate(
            (
                (master_ref, weights_ref),
                (inputs_ref, grid_ref.at[0]),
                (cotangent_ref, grid_ref.at[1]),
                (entry_hbm, entry_ref),
                (place_hbm, place_ref),
            )
        )
    ]
    for fetch in fetches:
        fetch.start()
    def pack_tail(kind):
        @pl.loop(0, WIN_LAT)
        def _(row):
            tails = [
                grid_ref[kind, slot, row].astype(f32)[:, :, 128:].reshape(WIN_LON * levels, D - 128)
                for slot in range(2)
            ]
            grid_tail_ref[kind, row] = (
                jnp.concatenate(tails, axis=1).reshape(WIN_LON, levels, 128).astype(bf16)
            )

    def tokens_of(kind, c):
        top = tok_ref[c, kind].astype(f32).reshape(CHUNK, 128)
        tails = tok_tail_ref[c, kind].astype(f32).reshape(QUAD * levels, 128)
        both = [tails, pltpu.roll(tails, 64, 1)]
        both = jnp.concatenate([tail.reshape(QUAD, 1, levels, 128) for tail in both], axis=1)
        return jnp.concatenate([top, both.reshape(CHUNK, 128)[:, : D - 128]], axis=1)

    def keep_tokens(kind, c, values):
        res_ref[c, kind] = values[:, :128].reshape(res_ref.shape[2:]).astype(bf16)
        tails = values[:, 128:].reshape(QUAD, 2, levels, D - 128)
        tails = [tails[:, slot].reshape(QUAD * levels, D - 128) for slot in range(2)]
        tails = jnp.concatenate(tails, axis=1).reshape(res_tail_ref.shape[2:])
        res_tail_ref[c, kind] = tails.astype(bf16)

    greeted = neighbours(inside)
    greet(greeted)

    per_home, own_rows = own_ref.shape[:2]
    flat_ref[pl.ds(0, per_home * own_rows), :] = jnp.zeros((per_home * own_rows, 128), f32)
    fetches[0].wait()
    for tile in range(tiles):
        flat_ref[pl.ds(tile, per_home, stride=own_rows), :] = weights_ref[
            :, 128 * tile : 128 * (tile + 1)
        ]
    for slot in range(per_home):
        own_ref[slot] = flat_ref[pl.ds(slot * own_rows, own_rows), :].astype(bf16)
    fetches[1].wait()
    pack_tail(0)
    greeted_wait(len(greeted))

    def center_tokens():
        fetches[2].wait()
        pack_tail(1)
        for bucket in range(buckets):
            home = home_ref[bucket]
            device, slot = split(home, per_home)
            rest, home_lon = split(device, lon_size)
            home_dp, home_lat = split(rest, lat_size)
            home_chip, home_core = split(home_lat, 2)
            unit = jnp.where(
                home_core == 0, home_lon * chips + home_chip, home_chip * lon_size + home_lon
            )
            side, inner = split(slot, per_home // SPLITS)
            chunk = (side * dp_size + home_dp) * 2 + home_core
            spot_ref[bucket] = (chunk * spread + unit) * (per_home // SPLITS) + inner
        shifted(0)

        @pl.loop(0, chunks)
        def _(c):
            rows = part(c)
            hat, inverse = normed(tokens_of(0, c))
            hat1_ref[rows, :] = hat
            inv1_ref[rows, :] = jnp.broadcast_to(inverse, (CHUNK, 128))

    gather = gather_steps(sizes, own_ref, all_ref, sends, receives, keeps)
    hooks = {0: functools.partial(shift, 0)}
    for mine in range(2):

        @pl.when(core == mine)
        def _():
            gather(mine, hooks, center_tokens)
            for copy in begun:
                copy.wait_send()
            begun.clear()

    shift(1)
    for fetch in fetches[3:]:
        fetch.wait()
    vacc_ref[...] = jnp.zeros_like(vacc_ref)
    marks = offsets(lat_size + 1)
    row_marks = [mark // 128 for mark in marks]

    for bucket in range(buckets):
        block = all_ref[spot_ref[bucket]].astype(f32)
        flat_ref[tiles * bucket : tiles * (bucket + 1), :] = block[:tiles]

    def take_pairs(base, parts, pairs):
        return [flat_ref[pl.ds(base + part, pairs, stride=parts), :] for part in range(parts)]

    def give_pairs(columns, rows, evens, odds):
        for column, (even, odd) in enumerate(zip(evens, odds)):
            mid_ref[column, pl.ds(0, rows // 2, stride=2), :] = even
            mid_ref[column, pl.ds(1, rows // 2, stride=2), :] = odd

    def load_qkv(base, ref):
        b = take_pairs(base, 9, D // 2)
        pieces = []
        for first in range(0, 9, 3):
            x, y, z = b[first : first + 3]
            pieces += [
                lanes_from(x, x, 0, SIDE),
                lanes_from(x, y, 96, SIDE),
                lanes_from(y, z, 64, SIDE),
                lanes_from(z, z, 32, SIDE),
            ]
        give_pairs(6, D, pieces[:6], pieces[6:])
        for column in range(6):
            ref[:, 128 * column : 128 * (column + 1)] = mid_ref[column, pl.ds(0, D), :].astype(bf16)

    def load_square(base, rows, ref, spans):
        b = take_pairs(base, 3, rows // 2)
        odds = [lanes_from(b[1], b[2], 64, 128), lanes_from(b[2], b[2], 64, D - 128)]
        give_pairs(2, rows, [b[0], b[1]], odds)
        for first, last, target in spans:
            size = last - first
            ref[target : target + size, 0:128] = mid_ref[0, pl.ds(first, size), :].astype(bf16)
            ref[target : target + size, 128:D] = mid_ref[1, pl.ds(first, size), :][
                :, : D - 128
            ].astype(bf16)

    sides = [(0, SIDE, 0), (SIDE, D, 128)]
    load_qkv(row_marks[0], w1_ref)
    load_square(row_marks[1], D, o1_ref, sides)
    load_qkv(row_marks[2], w2_ref)
    load_square(row_marks[3], D, o2_ref, sides)
    for ref in (o1_ref, o2_ref):
        for side in range(2):
            ref[128 * side + SIDE : 128 * (side + 1), :] = jnp.zeros((128 - SIDE, D), bf16)
    for column in range(6):
        up_ref[:, 128 * column : 128 * (column + 1)] = flat_ref[
            pl.ds(row_marks[4] + column, D, stride=6), :
        ].astype(bf16)
    load_square(row_marks[5], FF, down_ref, [(0, FF, 0)])
    for index in range(9):
        start = marks[7] + D * index
        vec_ref[index : index + 1, 0:128] = lanes_of(flat_ref, start)
        vec_ref[index : index + 1, 128:D] = lanes_of(flat_ref, start + 128)[:, : D - 128]

    def earth_places():
        group_one = lat + 1
        group_two = jnp.where(is_last, 0, lat + 1)
        for index in range(EARTH_ROWS):
            group = group_one if index % WIN_LAT < HALF_LAT else group_two
            start = marks[6] + EARTH_ROW * (EARTH_ROWS * group + index)
            yield (index,) + split(start, 128)

    lane_place = lax.broadcasted_iota(jnp.int32, (1, 128), 1)
    earth_ref[...] = jnp.zeros_like(earth_ref)
    for index, row, lane in earth_places():
        rows = [flat_ref[pl.ds(row + step, 1), :] for step in range(3)]
        back = (128 - lane) & 127
        first = pltpu.roll(jnp.where(lane_place >= lane, rows[0], rows[1]), back, 1)
        second = pltpu.roll(jnp.where(lane_place >= lane, rows[1], rows[2]), back, 1)
        earth_ref[index : index + 1, 0:128] = first
        earth_ref[index : index + 1, 128:256] = jnp.where(lane_place < EARTH_ROW - 128, second, 0.0)
    earth = earth_ref[...].astype(bf16)
    key_up = lax.broadcasted_iota(jnp.int32, (AREA, LANES), 0) // (2 * QUAD)
    query_up = lax.broadcasted_iota(jnp.int32, (AREA, LANES), 1) & (LANES // 2 - 1)
    query_up = lax.rem(query_up, HEAD_ROWS) // (2 * QUAD)
    bias = jnp.where((key_up != query_up) & is_last, penalty_value, 0.0)
    chosen = [nt(entry_ref[column], earth).astype(bf16) for column in range(WIN_LON)]
    bias_ref[...] = functools.reduce(
        jnp.add, [nn(chosen[column], place_ref[column]) for column in range(WIN_LON)], bias
    )

    for slot in range(slots_here):
        number = lax.axis_index("dp") * slots_here + slot
        sample, lead = split(number, LEADS)
        live = lead < lead_ref[sample]
        size = count // slots_here
        gate_ref[slot * size : (slot + 1) * size, :] = jnp.full((size, D), jnp.where(live, 1.0, 0.0), f32)

    def vec(index):
        return vec_ref[index : index + 1, :]

    def gate_rows():
        gate = gate_ref[...]
        return jnp.broadcast_to(gate[None], (CHUNK // count, count, D)).reshape(CHUNK, D)

    def note(index, values):
        vacc_ref[index] += row_fold(values)

    def note_low(index, values):
        top = lax.broadcasted_iota(jnp.int32, (8, CHUNK), 0) == 0
        vacc_ref[index] += nn(jnp.where(top, 1.0, 0.0).astype(bf16), values)

    def first_mixed(c):
        rows = part(c)
        low = (hat1_ref[rows, :] * vec(0) + vec(1)).astype(bf16)
        n1_ref[rows, :] = low
        mixed = rounded(nn(low, w1_ref[...]))
        for tile in range(6):
            qkv_ref[tile, rows, :] = mixed[:, 128 * tile : 128 * (tile + 1)]

    for c in range(chunks):
        first_mixed(c)

    def window(ref, tile, s):
        return ref[tile, pl.ds(s, AREA, stride=count), :]

    def window_store(ref, tile, s, values):
        ref[tile, pl.ds(s, AREA, stride=count), :] = values

    halves = [slice(0, LANES // 2), slice(LANES // 2, LANES)]

    @pl.loop(0, count // 4)
    def _(block):
        masks = head_masks()
        places = [(block * 4 + step, side) for step in range(4) for side in range(2)]
        reads = [[window(qkv_ref, 2 * kind + side, s) for kind in range(3)] for s, side in places]
        raw = [
            nt(key.astype(bf16), spread_window(query, masks)) for query, key, _ in reads
        ]
        probs = [
            soft_columns(scores * SCALE + bias_ref[:, halves[side]])
            for scores, (_, side) in zip(raw, places)
        ]
        outs = [tn(prob.astype(bf16), read[2].astype(bf16)) for prob, read in zip(probs, reads)]
        for (s, side), prob, out in zip(places, probs, outs):
            probs_ref[s, :, halves[side]] = prob
            window_store(att_ref, side, s, fold_heads(out, HEAD_ROWS, AREA))

    def second_mixed(c):
        rows = part(c)
        att = jnp.concatenate([att_ref[0, rows, :], att_ref[1, rows, :]], axis=1).astype(bf16)
        att1_ref[rows, :] = att
        branch = nn(att, o1_ref[...]) + vec(2)
        tok = tokens_of(0, c) + gate_rows() * branch
        tok1_ref[rows, :] = tok
        hat, inverse = normed(tok)
        hat2_ref[rows, :] = hat
        inv2_ref[rows, :] = jnp.broadcast_to(inverse, (CHUNK, 128))
        low = (hat * vec(3) + vec(4)).astype(bf16)
        n2_ref[rows, :] = low
        mix2_ref[rows, :] = nn(low, w2_ref[...]).astype(bf16)

    for c in range(chunks):
        second_mixed(c)

    def column_masks():
        lane = lax.broadcasted_iota(jnp.int32, (8, GLANES), 1)
        place = lax.shift_right_logical(lane & (GROUP - 1), 3)
        return [place == index for index in range(GROUP // 8)]

    def squeeze_column(values, masks):
        out = values[:8]
        for index in range(1, GROUP // 8):
            out = jnp.where(masks[index], values[8 * index : 8 * index + 8], out)
        return out

    def widen_column(values, masks):
        return jnp.concatenate([jnp.where(mask, values, 0.0) for mask in masks], axis=0).astype(bf16)

    def group_rows(g):
        return pl.ds(pl.multiple_of(g * GROUP, GROUP), GROUP)

    def tile_of(ref, g, kind, side):
        first = WIDE * kind + 128 * side
        return ref[group_rows(g), first : first + 128]

    @pl.loop(0, tokens // GROUP // 6)
    def _(block):
        heads = head_masks()
        columns = column_masks()
        places = [(block * 6 + step, side) for step in range(6) for side in range(2)]
        reads = [[tile_of(mix2_ref, g, kind, side) for kind in range(3)] for g, side in places]
        raw = [nt(key, spread_heads(query, heads)) for query, key, _ in reads]
        probs = [soft_columns(squeeze_column(scores, columns) * SCALE) for scores in raw]
        outs = [tn(widen_column(prob, columns), read[2]) for prob, read in zip(probs, reads)]
        for (g, side), prob, out in zip(places, probs, outs):
            cprobs_ref[g, side] = prob
            att2_ref[group_rows(g), 128 * side : 128 * (side + 1)] = fold_heads(
                out, GROUP, GROUP
            ).astype(bf16)

    root = math.sqrt(2.0 / math.pi)
    shifted(1)

    def feed_forward(c):
        rows = part(c)
        gate = gate_rows()
        tok = tok1_ref[rows, :] + gate * (nn(att2_ref[rows, :], o2_ref[...]) + vec(5))
        hat, inverse = normed(tok)
        low = (hat * vec(6) + vec(7)).astype(bf16)
        n3_ref[rows, :] = low
        after = tokens_of(1, c)
        delta3 = (gate * after).astype(bf16)
        delta3_ref[rows, :] = delta3
        note_low(8, delta3)
        for first in range(0, FF, FF_STEP):
            columns = slice(first, first + FF_STEP)
            hidden = nn(low, up_ref[:, columns])
            square = hidden * hidden
            half = 0.5 * jnp.tanh(hidden * (root + (root * 0.044715) * square)) + 0.5
            wave = hidden * half
            act_ref[rows, columns] = wave.astype(bf16)
            slope = half + wave * (1.0 - half) * (2.0 * root + (6.0 * root * 0.044715) * square)
            gh_ref[rows, columns] = (nt(delta3, down_ref[columns, :]) * slope).astype(bf16)
        keep_tokens(0, c, tok + gate * (nn(act_ref[rows, :], down_ref[...]) + vec(8)))
        gh = gh_ref[rows, :]
        grad = nt(gh, up_ref[...])
        note(6, grad * hat)
        note(7, grad)
        mid = after + norm_back(grad, hat, inverse, vec(6))
        gmid_ref[rows, :] = mid
        delta2 = (gate * mid).astype(bf16)
        delta2_ref[rows, :] = delta2
        note_low(5, delta2)
        gatt2_ref[rows, :] = nt(delta2, o2_ref[...]).astype(bf16)

    for c in range(chunks):
        feed_forward(c)

    def keep_pairs(base, parts, blocks):
        for number, block in enumerate(blocks):
            flat_ref[pl.ds(base + number, block.shape[0], stride=parts), :] = block

    def split_pairs(columns, rows):
        evens = [mid_ref[column, pl.ds(0, rows // 2, stride=2), :] for column in range(columns)]
        odds = [mid_ref[column, pl.ds(1, rows // 2, stride=2), :] for column in range(columns)]
        return evens, odds

    def save_qkv(base, grad):
        for column in range(6):
            mid_ref[column, pl.ds(0, D), :] = grad[:, 128 * column : 128 * (column + 1)]
        e, o = split_pairs(6, D)
        pieces = e + o
        blocks = []
        for first in range(0, 12, 4):
            x, y, z, w = pieces[first : first + 4]
            blocks += [
                lanes_join(x, 0, 96, y),
                lanes_join(y, 32, 64, z),
                lanes_join(z, 64, 32, w),
            ]
        keep_pairs(base, 9, blocks)

    def save_square(base, rows, grad):
        mid_ref[0, pl.ds(0, rows), :] = grad[:, :128]
        mid_ref[1, pl.ds(0, rows), 0 : D - 128] = grad[:, 128:]
        e, o = split_pairs(2, rows)
        keep_pairs(
            base, 3, [e[0], lanes_join(e[1], 0, 64, o[0]), lanes_join(o[0], 64, 64, o[1])]
        )

    def used_rows(grad):
        return jnp.concatenate([grad[0:SIDE], grad[128 : 128 + SIDE]], axis=0)

    partner = (dp, chip * 2 + 1 - core, lon)
    place = chip * lon_size + lon

    def peers():
        for i in range(chips):
            for j in range(lon_size):
                if i or j:
                    back = (chips - i) % chips * lon_size + (lon_size - j) % lon_size
                    there = (around(chip, i, chips), around(lon, j, lon_size))
                    target = (dp, there[0] * 2 + core, there[1])
                    yield i * lon_size + j, back, there[0] * lon_size + there[1], target

    def line():
        for step in range(1, dp_size):
            there = around(dp, step, dp_size)
            yield step, dp_size - step, there, (there, lat, lon)

    def summing(base, grad, half_in, half, plane_in, mid, line_in, full):
        n_half = grad.shape[0] // 2
        n_place = n_half // spread
        n_line = n_place // dp_size

        def cross():
            send(grad.at[pl.ds((1 - core) * n_half, n_half)], half_in, base, base, partner)

        def plane():
            arrive(half_in, base)
            for first in range(0, n_half, 12):
                rows = pl.ds(first, 12)
                kept = grad[pl.ds(core * n_half + first, 12)].astype(f32)
                half[rows] = (kept + half_in[rows].astype(f32)).astype(bf16)
            for index, back, there, target in peers():
                send(
                    half.at[pl.ds(there * n_place, n_place)],
                    plane_in.at[back],
                    base + 1 + index,
                    base + 1 + back,
                    target,
                )

        def along():
            total = half[pl.ds(place * n_place, n_place)].astype(f32)
            for index in range(1, spread):
                arrive(plane_in.at[index], base + 1 + index)
                total = total + plane_in[index].astype(f32)
            mid[...] = total.astype(bf16)
            slots = base + 1 + spread
            for step, back, there, target in line():
                send(mid.at[pl.ds(there * n_line, n_line)], line_in.at[back], slots + step, slots + back, target)

        def share():
            slots = base + 1 + spread
            rows = pl.ds(dp * n_line, n_line)
            total = mid[rows].astype(f32)
            for step in range(1, dp_size):
                arrive(line_in.at[step], slots + step)
                total = total + line_in[step].astype(f32)
            full[rows] = total.astype(bf16)
            slots += dp_size
            for step, back, _, target in line():
                send(full.at[rows], full.at[rows], slots + step, slots + back, target)

        def done():
            slots = base + 1 + spread + dp_size
            for step, _, there, _ in line():
                arrive(full.at[pl.ds(there * n_line, n_line)], slots + step)

        return cross, plane, along, share, done

    spans = [[(cuts[1], cuts[2])], [(cuts[0], cuts[1])], [(0, cuts[0]), (cuts[2], buckets)]]
    if inside:
        sum_sets = [sum_refs[7 * number : 7 * (number + 1)] for number in range(3)]
        hand_out, vec_sum, vec_in, vec_now = sum_refs[21:]
        each = 1 + spread + 2 * dp_size
        soon, early, late = [
            summing(sum_slots + each * number, *refs) for number, refs in enumerate(sum_sets)
        ]

        def pack(number):
            grad = sum_sets[number][0]
            for tile in range(grad.shape[0]):
                if tile < tiles:
                    rows = [
                        flat_ref[pl.ds(tile + tiles * begin, end - begin, stride=tiles), :]
                        for begin, end in spans[number]
                    ]
                    values = rows[0] if len(rows) == 1 else jnp.concatenate(rows, axis=0)
                    grad[tile] = values.astype(bf16)
                else:
                    grad[tile] = jnp.zeros(grad.shape[1:], bf16)
    else:
        (vec_sum,) = sum_refs

    shift(2)

    grad_up = tn(n3_ref[...], gh_ref[...])
    for column in range(6):
        flat_ref[pl.ds(row_marks[4] + column, D, stride=6), :] = grad_up[
            :, 128 * column : 128 * (column + 1)
        ]
    save_square(row_marks[5], FF, tn(act_ref[...], delta3_ref[...]))
    if inside:
        pack(0)
        soon[0]()


    @pl.loop(0, tokens // GROUP // 6)
    def _(block):
        heads = head_masks()
        columns = column_masks()
        places = [(block * 6 + step, side) for step in range(6) for side in range(2)]
        reads = [
            [tile_of(mix2_ref, g, kind, side) for kind in range(3)]
            + [tile_of(gatt2_ref, g, 0, side), cprobs_ref[g, side]]
            for g, side in places
        ]
        grads = [spread_heads(read[3], heads) for read in reads]
        raw = [nt(read[2], grad) for read, grad in zip(reads, grads)]
        dvalues = [nn(widen_column(read[4], columns), grad) for read, grad in zip(reads, grads)]
        lows = [
            widen_column(soft_back(read[4], squeeze_column(slopes, columns)), columns)
            for read, slopes in zip(reads, raw)
        ]
        dkeys = [nn(low, spread_heads(read[0], heads)) for read, low in zip(reads, lows)]
        dqueries = [tn(low, read[1]) for read, low in zip(reads, lows)]
        for (g, side), dquery, dkey, dvalue in zip(places, dqueries, dkeys, dvalues):
            for kind, values in enumerate(
                (fold_heads(dquery, GROUP, GROUP) * SCALE, dkey * SCALE, dvalue)
            ):
                first = WIDE * kind + 128 * side
                gm2_ref[group_rows(g), first : first + 128] = values.astype(bf16)

    if inside:
        soon[1]()

    def second_back(c):
        rows = part(c)
        grad = nt(gm2_ref[rows, :], w2_ref[...])
        hat = hat2_ref[rows, :]
        inverse = inv2_ref[rows, :][:, :1]
        note(3, grad * hat)
        note(4, grad)
        low = gmid_ref[rows, :] + norm_back(grad, hat, inverse, vec(3))
        glow_ref[rows, :] = low
        delta1 = (gate_rows() * low).astype(bf16)
        delta1_ref[rows, :] = delta1
        note_low(2, delta1)
        gatt = rounded(nt(delta1, o1_ref[...]))
        att_ref[0, rows, :] = gatt[:, :128]
        att_ref[1, rows, :] = gatt[:, 128:]

    for c in range(chunks):
        second_back(c)

    save_square(row_marks[1], D, used_rows(tn(att1_ref[...], delta1_ref[...])))
    save_qkv(row_marks[2], tn(n2_ref[...], gm2_ref[...]))
    save_square(row_marks[3], D, used_rows(tn(att2_ref[...], delta2_ref[...])))

    if inside:
        pack(1)
        early[0]()
        soon[2]()

    dbias_ref[...] = jnp.zeros_like(dbias_ref)

    def window_back(block):
        masks = head_masks()
        places = [(block * 4 + step, side) for step in range(4) for side in range(2)]
        reads = [
            [window(qkv_ref, 2 * kind + side, s) for kind in range(3)]
            + [window(att_ref, side, s), probs_ref[s, :, halves[side]]]
            for s, side in places
        ]
        grads = [spread_window(read[3], masks) for read in reads]
        raw = [nt(read[2].astype(bf16), grad) for read, grad in zip(reads, grads)]
        dvalues = [nn(read[4].astype(bf16), grad) for read, grad in zip(reads, grads)]
        lows = [soft_back(read[4], slopes).astype(bf16) for read, slopes in zip(reads, raw)]
        dkeys = [nn(low, spread_window(read[0], masks)) for read, low in zip(reads, lows)]
        dqueries = [tn(low, read[1].astype(bf16)) for read, low in zip(reads, lows)]
        for side in range(2):
            dbias_ref[:, halves[side]] += functools.reduce(
                jnp.add, [low.astype(f32) for low, (_, there) in zip(lows, places) if there == side]
            )
        for (s, side), dquery, dkey, dvalue in zip(places, dqueries, dkeys, dvalues):
            dquery = fold_heads(dquery, HEAD_ROWS, AREA) * SCALE
            for kind, values in enumerate((dquery, dkey * SCALE, dvalue)):
                window_store(qkv_ref, 2 * kind + side, s, rounded(values))

    @pl.loop(0, 2)
    def _(block):
        window_back(block)

    if inside:
        early[1]()
        soon[3]()

    @pl.loop(2, count // 4)
    def _(block):
        window_back(block)

    @pl.loop(0, chunks)
    def _(c):
        rows = part(c)
        gm1_ref[rows, :] = jnp.concatenate(
            [qkv_ref[tile, rows, :] for tile in range(6)], axis=1
        ).astype(bf16)

    save_qkv(row_marks[0], tn(n1_ref[...], gm1_ref[...]))
    rest = flat_ref.shape[0] - row_marks[6]
    around_ref[...] = jnp.zeros_like(around_ref)
    dbias = dbias_ref[...].astype(bf16)
    moved = [nt(dbias, place_ref[column]).astype(bf16) for column in range(WIN_LON)]
    dearth = functools.reduce(
        jnp.add, [tn(moved[column], entry_ref[column]) for column in range(WIN_LON)]
    )
    for index, row, lane in earth_places():
        row = row - row_marks[6]
        first = pltpu.roll(dearth[index : index + 1, :128], lane, 1)
        second = pltpu.roll(dearth[index : index + 1, 128:], lane, 1)
        tail = lane_place >= lane
        for step, values in enumerate(
            (
                jnp.where(tail, first, 0.0),
                jnp.where(tail, second, first),
                jnp.where(tail, 0.0, second),
            )
        ):
            around_ref[index % 4, pl.ds(row + step, 1), :] += values
    flat_ref[row_marks[6] :, :] = functools.reduce(
        jnp.add, [around_ref[number, 0:rest, :] for number in range(4)]
    )
    if inside:
        early[2]()
        pack(2)
        late[0]()

    def input_grads(c):
        rows = part(c)
        mixed = gm1_ref[rows, :]
        grad = nt(mixed, w1_ref[...])
        hat = hat1_ref[rows, :]
        inverse = inv1_ref[rows, :][:, :1]
        note(0, grad * hat)
        note(1, grad)
        grad_in = glow_ref[rows, :] + norm_back(grad, hat, inverse, vec(0))
        keep_tokens(1, c, grad_in)

    for c in (2, 3):
        input_grads(c)

    if inside:
        late[1]()

    for c in (1, 0):
        input_grads(c)

    for index in range(9):
        vec_sum[index : index + 1, :] = jnp.sum(vacc_ref[index], axis=0, keepdims=True)
    if inside:
        send(vec_sum, vec_in.at[0], vector_slots, vector_slots, partner)
        early[3]()
        arrive(vec_in.at[0], vector_slots)
        vec_now[0] = vec_sum[...] + vec_in[0]
        for index, back, _, target in peers():
            send(vec_now.at[0], vec_in.at[back], vector_slots + 1 + index, vector_slots + 1 + back, target)
    shift(3)
    if inside:
        late[2]()
        vec_total = vec_now[0]
        for index in range(1, spread):
            arrive(vec_in.at[index], vector_slots + 1 + index)
            vec_total = vec_total + vec_in[index]
        vec_now[1] = vec_total
        slots = vector_slots + 1 + spread
        for step, back, _, target in line():
            send(vec_now.at[1], vec_in.at[spread + back], slots + step, slots + back, target)
        late[3]()
        soon[4]()
        early[4]()
        homes = lat_size * lon_size
        width = homes * per_home
        slot_ids = lax.broadcasted_iota(jnp.int32, (width, 1), 0) + dp * width
        all_homes = homes_ref[...]
        picks = []
        for some in spans:
            held = [all_homes[:, begin:end] for begin, end in some]
            held = held[0] if len(held) == 1 else jnp.concatenate(held, axis=1)
            picks.append(jnp.where(slot_ids == held, 1.0, 0.0).astype(bf16))
        n_rows = hand_out.shape[1]
        owned_first = [
            nn(picks[0], sum_sets[0][6][row]) + nn(picks[1], sum_sets[1][6][row])
            for row in range(n_rows)
        ]
        late[4]()
        for row in range(n_rows):
            owned = owned_first[row] + nn(picks[2], sum_sets[2][6][row])
            for home in range(homes):
                hand_out[home, row] = owned[per_home * home : per_home * (home + 1), :].astype(bf16)
        first = core * (n_rows * spread) + place * n_rows
        landing = grads_ref.at[pl.ds(first, n_rows)]
        me = lat * lon_size + lon
        keep_hand = pltpu.make_async_copy(hand_out.at[me], landing, keeps.at[SPLITS])
        keep_hand.start()
        for i in range(lat_size):
            for j in range(lon_size):
                if i or j:
                    target = (dp, around(lat, i, lat_size), around(lon, j, lon_size))
                    back = (lat_size - i) % lat_size * lon_size + (lon_size - j) % lon_size
                    send(
                        hand_out.at[target[1] * lon_size + target[2]],
                        landing,
                        hand_slots + i * lon_size + j,
                        hand_slots + back,
                        target,
                    )
        for step in range(1, dp_size):
            arrive(vec_in.at[spread + step], slots + step)
            vec_total = vec_total + vec_in[spread + step]
        vec_in[0] = vec_total
        keep_total = pltpu.make_async_copy(vec_in.at[0], total_ref, keeps.at[0])
        keep_total.start()
        keep_hand.wait()
        keep_total.wait()
        for index in range(1, homes):
            arrive(landing, hand_slots + index)
    else:
        total_ref[...] = vec_sum[...]
        for tile in range(tiles):
            grads_ref[tile] = flat_ref[pl.ds(tile, buckets, stride=tiles), :]
    shifted(2)
    shifted(3)
    for copy in begun:
        copy.wait_send()


def sum_rows(sizes, tiles):
    unit = sizes[0] * sizes[1] * sizes[2]
    rows = -(-tiles // unit) * unit
    return rows, rows <= 2 * tiles


def block_call(homes, leads, master, inputs, cotangent, sizes):
    slots_here, levels = inputs.shape[0], inputs.shape[3]
    count = slots_here * levels
    tokens = count * AREA
    buckets = homes.shape[0]
    per_home, width = master.shape
    tiles = width // 128
    own_rows = -(-tiles // 16) * 16
    quads = (4, 2, HALF_LAT, HALF_LON, slots_here, levels, 128)
    tails = (4, 2, HALF_LAT, HALF_LON, levels, 128)
    assert slots_here == 2
    dp_size, lat_size, lon_size = sizes
    spread = lat_size // 2 * lon_size
    rows, inside = sum_rows(sizes, tiles)
    marks = offsets(lat_size + 1)
    low = -(-marks[1] // width)
    mid = -(-marks[4] // width)
    high = marks[6] // width
    mid += (high - mid) % 8
    low += (mid - low) % 8
    cuts = (low, mid, high)
    shape = jax.ShapeDtypeStruct
    outs = [
        shape(inputs.shape[:4] + (128,), bf16),
        shape(inputs.shape[1:4] + (128,), bf16),
        shape(inputs.shape[:4] + (128,), bf16),
        shape(inputs.shape[1:4] + (128,), bf16),
        shape((rows, per_home, 128), bf16) if inside else shape((tiles, buckets, 128), f32),
        shape((9, D), f32),
    ]
    vmem = pltpu.VMEM
    entry, place = earth_tables()
    scratch = [
        pltpu.SMEM((buckets,), jnp.int32),
        vmem(master.shape, f32),
        vmem((2,) + inputs.shape, bf16),
        vmem((2, WIN_LAT, WIN_LON, levels, 128), bf16),
        vmem(entry.shape, bf16),
        vmem(place.shape, bf16),
        vmem((per_home, own_rows, 128), bf16),
        vmem((dp_size * lat_size * lon_size * per_home, own_rows, 128), bf16),
        vmem(quads, bf16),
        vmem(tails, bf16),
        vmem(quads, bf16),
        vmem(tails, bf16),
        vmem((buckets * tiles, 128), f32),
        vmem((6, FF, 128), f32),
        vmem((40, 256), f32),
        vmem((count, D), f32),
        vmem((AREA, LANES), f32),
        vmem((AREA, LANES), f32),
        vmem((D, 3 * WIDE), bf16),
        vmem((WIDE, D), bf16),
        vmem((D, 3 * WIDE), bf16),
        vmem((WIDE, D), bf16),
        vmem((D, FF), bf16),
        vmem((FF, D), bf16),
        vmem((16, D), f32),
        vmem((tokens, D), bf16),
        vmem((tokens, D), f32),
        vmem((tokens, 128), f32),
        vmem((6, tokens, 128), f32),
        vmem((count, AREA, LANES), f32),
        vmem((2, tokens, 128), f32),
        vmem((tokens, WIDE), bf16),
        vmem((tokens, D), f32),
        vmem((tokens, D), bf16),
        vmem((tokens, D), f32),
        vmem((tokens, 128), f32),
        vmem((tokens, 3 * WIDE), bf16),
        vmem((tokens // GROUP, 2, 8, GLANES), f32),
        vmem((tokens, WIDE), bf16),
        vmem((tokens, D), bf16),
        vmem((tokens, FF), bf16),
        vmem((tokens, FF), bf16),
        vmem((tokens, D), bf16),
        vmem((tokens, D), bf16),
        vmem((tokens, D), bf16),
        vmem((tokens, D), f32),
        vmem((tokens, D), f32),
        vmem((tokens, WIDE), bf16),
        vmem((tokens, 3 * WIDE), bf16),
        vmem((tokens, 3 * WIDE), bf16),
        vmem((9, 8, D), f32),
        vmem((4, buckets * tiles - marks[6] // 128, 128), f32),
        pltpu.SemaphoreType.DMA((move_slots(sizes, slots_here)[-1],)),
        pltpu.SemaphoreType.DMA((move_slots(sizes, slots_here)[-1],)),
        pltpu.SemaphoreType.DMA((SPLITS + 1,)),
        pltpu.SemaphoreType.DMA((5,)),
        pltpu.SemaphoreType.DMA((4 * (slots_here + 1),)),
    ]
    if inside:
        n_place = rows // 2 // spread
        for some in (high - mid, mid - low, buckets - (high - low)):
            scratch += [
                vmem((rows, some, 128), bf16),
                vmem((rows // 2, some, 128), bf16),
                vmem((rows // 2, some, 128), bf16),
                vmem((spread, n_place, some, 128), bf16),
                vmem((n_place, some, 128), bf16),
                vmem((dp_size, n_place // dp_size, some, 128), bf16),
                vmem((n_place, some, 128), bf16),
            ]
        scratch += [
            vmem((lat_size * lon_size, n_place, per_home, 128), bf16),
            vmem((9, D), f32),
            vmem((spread + dp_size, 9, D), f32),
            vmem((2, 9, D), f32),
        ]
    else:
        scratch += [vmem((9, D), f32)]
    spec = pl.BlockSpec(memory_space=pltpu.VMEM)
    smem = pl.BlockSpec(memory_space=pltpu.SMEM)
    hbm = pl.BlockSpec(memory_space=pl.ANY)
    return pl.pallas_call(
        functools.partial(block_kernel, (sizes, buckets, tiles, slots_here, cuts), inside),
        out_shape=outs,
        in_specs=[smem, smem, spec] + [hbm] * 5,
        out_specs=[hbm] * 4 + [hbm if inside else spec] * 2,
        scratch_shapes=scratch,
        compiler_params=pltpu.CompilerParams(
            vmem_limit_bytes=62 * 1024 * 1024, collective_id=0, has_side_effects=True
        ),
        name="block",
    )(
        homes,
        leads,
        homes[None, :],
        master,
        inputs,
        cotangent,
        jnp.asarray(entry),
        jnp.asarray(place),
    )


def finish_kernel(marks, steps_ref, homes_ref, *refs):
    sources, targets = refs[:9], refs[9:15]
    held, made = refs[15:24], refs[24:29]
    spare_ref, incoming, outgoing = refs[29:]
    fetches = [
        pltpu.make_async_copy(src, dst, incoming.at[number])
        for number, (src, dst) in enumerate(zip(sources, held))
    ]
    for fetch in fetches:
        fetch.start()
    back_res_ref, back_res_tail_ref, back_in_ref, back_in_tail_ref = held[:4]
    grads_ref, vectors_ref, master_ref, one_ref, two_ref = held[4:]
    result_ref, grad_inputs_ref, new_master, new_one, new_two = made
    homes, width = master_ref.shape
    tiles = width // 128
    leaves = []

    def leave(src, dst):
        copy = pltpu.make_async_copy(src, dst, outgoing.at[len(leaves)])
        copy.start()
        leaves.append(copy)

    levels = result_ref.shape[3]
    for number, (top_ref, tail_ref, out_ref) in enumerate(
        (
            (back_res_ref, back_res_tail_ref, result_ref),
            (back_in_ref, back_in_tail_ref, grad_inputs_ref),
        )
    ):
        for fetch in fetches[2 * number : 2 * number + 2]:
            fetch.wait()
        for slot in range(out_ref.shape[0]):

            @pl.loop(0, WIN_LAT)
            def _(row):
                out_ref[slot, row, :, :, 0:128] = top_ref[slot, row].astype(out_ref.dtype)
                tail = tail_ref[row].astype(f32).reshape(WIN_LON * levels, 128)
                tail = (pltpu.roll(tail, 64, 1) if slot else tail)[:, : D - 128]
                out_ref[slot, row, :, :, 128:D] = tail.reshape(WIN_LON, levels, D - 128).astype(
                    out_ref.dtype
                )

            leave(out_ref.at[slot], targets[number].at[slot])
    for fetch in fetches[4:]:
        fetch.wait()
    leave(vectors_ref, targets[2])
    place = lax.axis_index("dp") * lax.axis_size("lat") + lax.axis_index("lat")
    place = (place * lax.axis_size("lon") + lax.axis_index("lon")) * homes
    slots = lax.broadcasted_iota(jnp.int32, (homes, 1), 0) + place
    match = homes_ref[...] == slots
    bucket = lax.broadcasted_iota(jnp.int32, match.shape, 1)
    held = jnp.max(jnp.where(match, bucket, -1), axis=1, keepdims=True)
    base = jnp.where(held >= 0, held * width, marks[8])

    top = marks[7] // 128
    spare_ref[...] = jnp.zeros_like(spare_ref)
    lanes = lax.broadcasted_iota(jnp.int32, (1, 128), 1)
    for index in range(9):
        vector = vectors_ref[index : index + 1, :]
        start = marks[7] + D * index
        tail = jnp.concatenate([vector[:, 128:], jnp.zeros((1, 256 - D), f32)], axis=1)
        for values, size, begin in ((vector[:, :128], 128, start), (tail, D - 128, start + 128)):
            row, lane = divmod(begin - 128 * top, 128)
            moved = pltpu.roll(values, lane, 1) if lane else values
            spare_ref[row : row + 1, :] += jnp.where(lanes >= lane, moved, 0.0)
            if lane + size > 128:
                spare_ref[row + 1 : row + 2, :] += jnp.where(lanes < lane, moved, 0.0)

    steps = jnp.full((homes, 128), steps_ref[0], jnp.int32).astype(f32)
    fix_one = 1.0 / (1.0 - jnp.exp(steps * math.log(beta_one)))
    fix_two = 1.0 / (1.0 - jnp.exp(steps * math.log(beta_two)))
    rates = [
        2.6 / math.sqrt(D),
        8.0 / math.sqrt(D),
        2.6 / math.sqrt(D),
        4.0 / math.sqrt(D),
        2.0 / math.sqrt(D),
        3.0 / math.sqrt(FF),
        1.0,
        0.6,
    ]
    spread = jnp.broadcast_to(base, (homes, 128)) + lax.broadcasted_iota(jnp.int32, (homes, 128), 1)
    for tile in range(tiles):
        columns = slice(128 * tile, 128 * (tile + 1))
        index = spread + 128 * tile
        rate = jnp.full((homes, 128), 0.1, f32)
        for number in range(7, -1, -1):
            rate = jnp.where(index < marks[number + 1], rates[number], rate)
        grad = grads_ref[tile].astype(f32)
        for owner in range(marks[7] // width, (marks[8] - 1) // width + 1):
            row = owner * tiles + tile - top
            if 0 <= row < spare_ref.shape[0]:
                grad = grad + jnp.where(held == owner, spare_ref[row : row + 1, :], 0.0)
        weights = master_ref[:, columns]
        first = beta_one * one_ref[:, columns] + (1.0 - beta_one) * grad
        second = beta_two * two_ref[:, columns] + (1.0 - beta_two) * grad * grad
        step = first * fix_one / (jnp.sqrt(second * fix_two) + eps_adam) + decay_rate * weights
        new_master[:, columns] = weights - rate * step
        new_one[:, columns] = first
        new_two[:, columns] = second
    for src, dst in zip(made[2:], targets[3:]):
        leave(src, dst)
    for copy in leaves:
        copy.wait()


def finish_call(marks, steps, homes, grads, vectors, master, one, two, backs):
    grid = backs[0].shape[:4] + (D,)
    shape = jax.ShapeDtypeStruct
    hbm = pl.BlockSpec(memory_space=pl.ANY)
    operands = [*backs, grads, vectors, master, one, two]
    outs = [shape(grid, bf16), shape(grid, f32), shape(vectors.shape, f32)]
    outs += [shape(master.shape, f32)] * 3
    made = outs[:2] + outs[3:]
    return pl.pallas_call(
        functools.partial(finish_kernel, marks),
        out_shape=outs,
        in_specs=[pl.BlockSpec(memory_space=pltpu.SMEM), pl.BlockSpec(memory_space=pltpu.VMEM)]
        + [hbm] * len(operands),
        out_specs=[hbm] * len(outs),
        scratch_shapes=[pltpu.VMEM(some.shape, some.dtype) for some in operands + made]
        + [
            pltpu.VMEM((16, 128), f32),
            pltpu.SemaphoreType.DMA((len(operands),)),
            pltpu.SemaphoreType.DMA((8,)),
        ],
        name="finish",
    )(steps, homes[None, :], *operands)


def per_device(
    inputs, cotangent, lead_counts, home_slots, master, moment_one, moment_two, step_count
):
    axes = ("dp", "lat", "lon")
    sizes = tuple(lax.axis_size(axis) for axis in axes)
    slots_mine, bucket_width = master.shape
    tiles = bucket_width // 128
    order = (0, 2, 3, 1, 4)
    *backs, grads, vectors = block_call(
        home_slots, lead_counts, master, inputs.transpose(order), cotangent.transpose(order), sizes
    )
    if not sum_rows(sizes, tiles)[1]:
        spread = jnp.zeros((tiles, math.prod(sizes) * slots_mine, 128), f32)
        spread = spread.at[:, home_slots].set(grads)
        grads = lax.psum_scatter(spread, axes, scatter_dimension=1, tiled=True)
        vectors = lax.psum(vectors, axes)
    result, grad_inputs, grad_vectors, *new = finish_call(
        offsets(sizes[1] + 1),
        step_count,
        home_slots,
        grads,
        vectors,
        master,
        moment_one,
        moment_two,
        backs,
    )
    order = (0, 3, 1, 2, 4)
    return (result.transpose(order), grad_inputs.transpose(order), grad_vectors, *new)


def solution(mesh):
    in_specs = (
        P("dp", None, "lat", "lon", None),
        P("dp", None, "lat", "lon", None),
        P(),
        P(),
        P(("dp", "lat", "lon"), None),
        P(("dp", "lat", "lon"), None),
        P(("dp", "lat", "lon"), None),
        P(),
    )
    out_specs = (
        P("dp", None, "lat", "lon", None),
        P("dp", None, "lat", "lon", None),
        P(),
        P(("dp", "lat", "lon"), None),
        P(("dp", "lat", "lon"), None),
        P(("dp", "lat", "lon"), None),
    )
    return jax.shard_map(
        per_device, mesh=mesh, in_specs=in_specs, out_specs=out_specs, check_vma=False
    )
```

```python
import functools
import math

import jax
import jax.numpy as jnp
import ml_dtypes
import numpy as np
from jax import lax
from jax.experimental import pallas as pl
from jax.experimental.pallas import tpu as pltpu
from jax.sharding import PartitionSpec as P

D = 192
FF = 768
HEADS = 6
HEAD_DIM = 32
LEVELS = 8
WIN_LAT = 6
WIN_LON = 12
LEADS = 4
HALF_LAT = WIN_LAT // 2
HALF_LON = WIN_LON // 2
QUAD = HALF_LAT * HALF_LON
AREA = WIN_LAT * WIN_LON
SIDE_HEADS = HEADS // 2
SIDE = SIDE_HEADS * HEAD_DIM
HEAD_ROWS = 80
LANES = 512
WIDE = 256
SCALE = 1.0 / math.sqrt(HEAD_DIM)

beta_one = 0.6
beta_two = 0.45
eps_norm = 1e-05
eps_adam = 1e-08
decay_rate = 0.1
penalty_value = -1000000000.0
bf16 = jnp.bfloat16
f32 = jnp.float32


def offsets(groups):
    sizes_list = [
        3 * D * D,
        D * D,
        3 * D * D,
        D * D,
        D * FF,
        FF * D,
        groups * HEADS * WIN_LAT * WIN_LAT * (2 * WIN_LON - 1),
        9 * D,
    ]
    segment_marks = [0]
    for amount in sizes_list:
        segment_marks.append(segment_marks[-1] + amount)
    return segment_marks


def nn(left, right):
    return jnp.dot(left, right, preferred_element_type=f32)


def nt(left, right):
    return lax.dot_general(left, right, (((1,), (1,)), ((), ())), preferred_element_type=f32)


def tn(left, right):
    return lax.dot_general(left, right, (((0,), (0,)), ((), ())), preferred_element_type=f32)


def normed(values):
    center = values - jnp.sum(values, axis=-1, keepdims=True) * (1.0 / D)
    spread = jnp.sum(center * center, axis=-1, keepdims=True) * (1.0 / D)
    inverse = lax.rsqrt(spread + eps_norm)
    return center * inverse, inverse


def norm_back(grad, hat, inverse, gain):
    scaled = grad * gain
    mean_one = jnp.sum(scaled, axis=-1, keepdims=True) * (1.0 / D)
    mean_two = jnp.sum(scaled * hat, axis=-1, keepdims=True) * (1.0 / D)
    return inverse * (scaled - mean_one - hat * mean_two)


def row_fold(values):
    return jnp.sum(values.reshape(values.shape[0] // 8, 8, values.shape[1]), axis=0)


def head_masks():
    lane = lax.broadcasted_iota(jnp.int32, (1, 128), 1) // HEAD_DIM
    return [jnp.where(lane == head, 1.0, 0.0).astype(bf16) for head in range(SIDE_HEADS)]


def spread_heads(values, masks):
    return jnp.concatenate([values * mask for mask in masks], axis=0)


def spread_window(values, masks):
    full = jnp.concatenate([values, jnp.zeros((HEAD_ROWS - AREA, 128), f32)], axis=0).astype(bf16)
    rest = jnp.zeros((LANES // 2 - SIDE_HEADS * HEAD_ROWS, 128), bf16)
    return jnp.concatenate([spread_heads(full, masks), rest], axis=0)


def fold_heads(big, step, count):
    lane = lax.broadcasted_iota(jnp.int32, (count, 128), 1)
    parts = [big[head * step : head * step + count] for head in range(SIDE_HEADS)]
    out = parts[-1]
    for head in range(SIDE_HEADS - 2, -1, -1):
        out = jnp.where(lane < HEAD_DIM * (head + 1), parts[head], out)
    return out


def rounded(values):
    return values.astype(bf16).astype(f32)


def soft_columns(scores):
    exps = jnp.exp(scores - jnp.max(scores, axis=0, keepdims=True))
    return exps * (1.0 / jnp.sum(exps, axis=0, keepdims=True))


def soft_back(probs, slopes):
    return probs * (slopes - jnp.sum(probs * slopes, axis=0, keepdims=True))


GROUP = 64
GLANES = SIDE_HEADS * GROUP
CHUNK = 288


def lanes_of(ref, start):
    row, lane = divmod(start, 128)
    here = ref[row : row + 1, :]
    if lane == 0:
        return here
    place = lax.broadcasted_iota(jnp.int32, (1, 128), 1)
    mixed = jnp.where(place >= lane, here, ref[row + 1 : row + 2, :])
    return pltpu.roll(mixed, 128 - lane, 1)


def lanes_from(first, second, lane, size):
    place = lax.broadcasted_iota(jnp.int32, first.shape, 1)
    if lane:
        first = pltpu.roll(jnp.where(place >= lane, first, second), 128 - lane, 1)
    return jnp.where(place < size, first, 0.0) if size < 128 else first


def lanes_join(first, begin, size, second):
    place = lax.broadcasted_iota(jnp.int32, first.shape, 1)
    moved = pltpu.roll(first, 128 - begin, 1) if begin else first
    return jnp.where(place < size, moved, pltpu.roll(second, size, 1))


EARTH_ROW = WIN_LAT * (2 * WIN_LON - 1)
EARTH_ROWS = HEADS * WIN_LAT


def earth_tables():
    entry = np.zeros((WIN_LON, AREA, 256), np.float32)
    place = np.zeros((WIN_LON, 40, LANES), np.float32)
    for column in range(WIN_LON):
        side, inner = divmod(column, HALF_LON)
        for key in range(AREA):
            key_up, rest = divmod(key, 2 * QUAD)
            key_side, rest = divmod(rest, QUAD)
            key_row, key_inner = divmod(rest, HALF_LON)
            row = key_up * HALF_LAT + key_row
            offset = column - (key_side * HALF_LON + key_inner) + WIN_LON - 1
            entry[column, key, row * (2 * WIN_LON - 1) + offset] = 1.0
        for head in range(HEADS):
            for row in range(WIN_LAT):
                up, low = divmod(row, HALF_LAT)
                lane = 2 * QUAD * up + QUAD * side + HALF_LON * low + inner
                lane += LANES // 2 * (head // SIDE_HEADS) + HEAD_ROWS * (head % SIDE_HEADS)
                place[column, head * WIN_LAT + row, lane] = 1.0
    return entry.astype(ml_dtypes.bfloat16), place.astype(ml_dtypes.bfloat16)


MESH = pl.DeviceIdType.MESH


def places():
    lat_size, lon_size, dp_size = lax.axis_size("lat"), lax.axis_size("lon"), lax.axis_size("dp")
    return (
        lax.axis_index("dp"),
        lax.axis_index("lat"),
        lax.axis_index("lon"),
        dp_size,
        lat_size,
        lon_size,
    )


def greet(targets):
    barrier = pltpu.get_barrier_semaphore()
    for target in targets:
        pl.semaphore_signal(barrier, inc=1, device_id=target, device_id_type=MESH)


def greeted_wait(count):
    pl.semaphore_wait(pltpu.get_barrier_semaphore(), count)


def split(value, size):
    if size & (size - 1) == 0:
        return lax.shift_right_logical(value, size.bit_length() - 1), value & (size - 1)
    return lax.div(value, size), lax.rem(value, size)


def around(place, step, size):
    return split(place + step, size)[1]


def neighbours(whole_plane):
    dp, lat, lon, dp_size, lat_size, lon_size = places()
    if whole_plane:
        steps = {(i, j) for i in range(lat_size) for j in range(lon_size)}
    else:
        steps = {(1, 0), (lat_size - 1, 0), (1, 1 % lon_size), (lat_size - 1, lon_size - 1)}
        steps |= {(2 * i, 0) for i in range(1, lat_size // 2)} | {(0, j) for j in range(lon_size)}
    steps.discard((0, 0))
    found = [(around(dp, step, dp_size), lat, lon) for step in range(1, dp_size)]
    return found + [
        (dp, around(lat, i, lat_size), around(lon, j, lon_size)) for i, j in sorted(steps)
    ]


def pairing(src, dst, sends, receives, send_slot, receive_slot, target):
    return pltpu.make_async_remote_copy(
        src_ref=src,
        dst_ref=dst,
        send_sem=sends.at[send_slot],
        recv_sem=receives.at[receive_slot],
        device_id=target,
        device_id_type=MESH,
    )


def gather_slots(sizes, splits):
    dp_size, lat_size, lon_size = sizes
    return splits * dp_size * (2 * max(lat_size // 2, lon_size) + 2)


def gather_steps(sizes, own_ref, all_ref, sends, receives, keep_sem):
    splits, skew = SPLITS, SKEW
    dp_size, lat_size, lon_size = sizes
    chips = lat_size // 2
    dp, lat, lon = lax.axis_index("dp"), lax.axis_index("lat"), lax.axis_index("lon")
    chip, core = split(lat, 2)
    wide = max(chips, lon_size)
    first = splits * dp_size
    second = first + splits * dp_size * wide
    cross = second + splits * dp_size * wide
    per = own_ref.shape[0] // splits
    order = sorted(range(dp_size), key=lambda step: min(step, dp_size - step))
    items = [(part, 0) for part in range(splits)]
    items += [(part, step) for part in range(splits) for step in order[1:]]

    def chip_at(step):
        return (dp, around(chip, step, chips) * 2 + core, lon)

    def lon_at(step):
        return (dp, lat, around(lon, step, lon_size))

    units = chips * lon_size

    def stretch(part, step, side, first, size):
        start = ((part * dp_size + around(dp, step, dp_size)) * 2 + side) * units + first
        return all_ref.at[pl.ds(start * per, size * per)]

    def run(mine, hooks, late_hook):
        unit = lon * chips + chip if mine == 0 else chip * lon_size + lon
        one, two = (chips, lon_size) if mine == 0 else (lon_size, chips)
        one_at, two_at = (chip_at, lon_at) if mine == 0 else (lon_at, chip_at)
        place_two = lon if mine == 0 else chip
        partner = (dp, chip * 2 + 1 - mine, lon)
        begun = []

        def send(src, dst, slot, back, target):
            copy = pairing(src, dst, sends, receives, slot, back, target)
            copy.start()
            begun.append(copy)

        def arrive(dst, slot):
            pairing(dst, dst, sends, receives, slot, slot, partner).wait_recv()

        def own_part(part):
            return own_ref.at[pl.ds(part * per, per)]

        def chunk(part, step):
            return stretch(part, step, mine, unit, 1)

        def group(part, step):
            return stretch(part, step, mine, place_two * one, one)

        def whole(part, step, side):
            return stretch(part, step, side, 0, units)

        keeps = []
        for part in range(splits):
            keep = pltpu.make_async_copy(own_part(part), chunk(part, 0), keep_sem.at[part])
            keep.start()
            keeps.append(keep)

        def line(part):
            for step in order[1:]:
                target = (around(dp, step, dp_size), lat, lon)
                base = part * dp_size
                send(own_part(part), chunk(part, 0), base + step, base + dp_size - step, target)

        def stage_one(part, step):
            if step:
                arrive(chunk(part, step), part * dp_size + step)
            base = first + (part * dp_size + step) * wide
            src = chunk(part, step) if step else own_part(part)
            for far in range(1, one):
                send(src, chunk(part, step), base + far, base + one - far, one_at(far))

        def stage_two(part, step):
            base = first + (part * dp_size + step) * wide
            for far in range(1, one):
                arrive(chunk(part, step), base + far)
            if step == 0:
                keeps[part].wait()
            base = second + (part * dp_size + step) * wide
            for far in range(1, two):
                send(group(part, step), group(part, step), base + far, base + two - far, two_at(far))

        def stage_three(part, step):
            base = second + (part * dp_size + step) * wide
            for far in range(1, two):
                arrive(group(part, step), base + far)
            slot = cross + part * dp_size + step
            send(whole(part, step, mine), whole(part, step, mine), slot, slot, partner)

        for part in range(splits):
            line(part)
        for turn in range(len(items) + 2 * skew):
            for stage, place in ((stage_one, turn), (stage_two, turn - skew), (stage_three, turn - 2 * skew)):
                if 0 <= place < len(items):
                    stage(*items[place])
            if turn in hooks:
                hooks[turn]()
        late_hook()
        for part, step in items:
            arrive(whole(part, step, 1 - mine), cross + part * dp_size + step)
        for copy in begun:
            copy.wait_send()

    return run


def move_slots(sizes, slots):
    dp_size, lat_size, lon_size = sizes
    spread = lat_size // 2 * lon_size
    moves = gather_slots(sizes, SPLITS)
    sums = moves + 16 * (slots + 1)
    vectors = sums + 3 * (1 + spread + 2 * dp_size)
    hand = vectors + 1 + spread + dp_size
    return moves, sums, vectors, hand, hand + lat_size * lon_size


SPLITS = 2
FF_STEP = 256
SKEW = 3


def block_kernel(
    shape_info,
    inside,
    home_ref,
    lead_ref,
    homes_ref,
    master_ref,
    inputs_ref,
    cotangent_ref,
    entry_hbm,
    place_hbm,
    back_res_ref,
    back_res_tail_ref,
    back_in_ref,
    back_in_tail_ref,
    grads_ref,
    total_ref,
    spot_ref,
    weights_ref,
    grid_ref,
    grid_tail_ref,
    entry_ref,
    place_ref,
    own_ref,
    all_ref,
    tok_ref,
    tok_tail_ref,
    res_ref,
    res_tail_ref,
    flat_ref,
    mid_ref,
    earth_ref,
    gate_ref,
    bias_ref,
    dbias_ref,
    w1_ref,
    o1_ref,
    w2_ref,
    o2_ref,
    up_ref,
    down_ref,
    vec_ref,
    n1_ref,
    hat1_ref,
    inv1_ref,
    qkv_ref,
    probs_ref,
    att_ref,
    att1_ref,
    tok1_ref,
    n2_ref,
    hat2_ref,
    inv2_ref,
    mix2_ref,
    cprobs_ref,
    att2_ref,
    n3_ref,
    act_ref,
    gh_ref,
    delta3_ref,
    delta2_ref,
    delta1_ref,
    gmid_ref,
    glow_ref,
    gatt2_ref,
    gm2_ref,
    gm1_ref,
    vacc_ref,
    around_ref,
    sends,
    receives,
    keeps,
    fetched,
    kept,
    *sum_refs,
):
    levels = tok_ref.shape[5]
    chunks = 4
    sizes, buckets, tiles, slots_here, cuts = shape_info
    count = slots_here * levels
    tokens = count * AREA
    dp_size, lat_size, lon_size = sizes
    chips = lat_size // 2
    spread = chips * lon_size
    dp, lat, lon = lax.axis_index("dp"), lax.axis_index("lat"), lax.axis_index("lon")
    chip, core = split(lat, 2)
    is_last = lat == lat_size - 1
    moves, sum_slots, vector_slots, hand_slots, _ = move_slots(sizes, slots_here)
    begun = []

    def send(src, dst, slot, back, target):
        copy = pairing(src, dst, sends, receives, slot, back, target)
        copy.start()
        begun.append(copy)

    def arrive(dst, slot):
        pairing(dst, dst, sends, receives, slot, slot, (dp, lat, lon)).wait_recv()

    def pieces(kind, start, quads=range(4)):
        for quad in quads:
            up, left = quad // 2, quad % 2
            way = 1 if kind > 1 else -1
            target = (
                dp,
                around(lat, way * up % lat_size, lat_size),
                around(lon, way * left % lon_size, lon_size),
            )
            grid, grid_tail = (
                (inputs_ref, grid_tail_ref.at[0]),
                (cotangent_ref, grid_tail_ref.at[1]),
                (back_res_ref, back_res_tail_ref),
                (back_in_ref, back_in_tail_ref),
            )[kind]
            held, held_tail = (res_ref, res_tail_ref) if kind > 1 else (tok_ref, tok_tail_ref)
            rows = pl.ds(HALF_LAT * (1 - up), HALF_LAT)
            columns = pl.ds(HALF_LON * (1 - left), HALF_LON)
            pairs = [(grid_tail.at[rows, columns], held_tail.at[quad, kind % 2])]
            for slot in range(slots_here):
                on_grid = grid.at[slot, rows, columns]
                on_grid = on_grid if kind > 1 else on_grid.at[:, :, :, pl.ds(0, 128)]
                pairs.append((on_grid, held.at[quad, kind % 2, :, :, slot]))
            for number, (on_grid, in_quads) in enumerate(pairs):
                src, dst = (in_quads, on_grid) if kind > 1 else (on_grid, in_quads)
                place = len(pairs) * (4 * kind + quad) + number
                if quad == 0:
                    copy = pltpu.make_async_copy(src, dst, kept.at[kind * len(pairs) + number])
                    copy.start() if start else copy.wait()
                elif start:
                    send(src, dst, moves + place, moves + place, target)
                else:
                    arrive(dst, moves + place)

    def shift(kind, quads=range(4)):
        pieces(kind, True, quads)

    def shifted(kind):
        pieces(kind, False)

    def part(index):
        return pl.ds(pl.multiple_of(index * CHUNK, CHUNK), CHUNK)

    fetches = [
        pltpu.make_async_copy(source, target, fetched.at[index])
        for index, (source, target) in enumerate(
            (
                (master_ref, weights_ref),
                (inputs_ref, grid_ref.at[0]),
                (cotangent_ref, grid_ref.at[1]),
                (entry_hbm, entry_ref),
                (place_hbm, place_ref),
            )
        )
    ]
    for fetch in fetches:
        fetch.start()
    def pack_tail(kind):
        @pl.loop(0, WIN_LAT)
        def _(row):
            tails = [
                grid_ref[kind, slot, row].astype(f32)[:, :, 128:].reshape(WIN_LON * levels, D - 128)
                for slot in range(2)
            ]
            grid_tail_ref[kind, row] = (
                jnp.concatenate(tails, axis=1).reshape(WIN_LON, levels, 128).astype(bf16)
            )

    def tokens_of(kind, c):
        top = tok_ref[c, kind].astype(f32).reshape(CHUNK, 128)
        tails = tok_tail_ref[c, kind].astype(f32).reshape(QUAD * levels, 128)
        both = [tails, pltpu.roll(tails, 64, 1)]
        both = jnp.concatenate([tail.reshape(QUAD, 1, levels, 128) for tail in both], axis=1)
        return jnp.concatenate([top, both.reshape(CHUNK, 128)[:, : D - 128]], axis=1)

    def keep_tokens(kind, c, values):
        res_ref[c, kind] = values[:, :128].reshape(res_ref.shape[2:]).astype(bf16)
        tails = values[:, 128:].reshape(QUAD, 2, levels, D - 128)
        tails = [tails[:, slot].reshape(QUAD * levels, D - 128) for slot in range(2)]
        tails = jnp.concatenate(tails, axis=1).reshape(res_tail_ref.shape[2:])
        res_tail_ref[c, kind] = tails.astype(bf16)

    greeted = neighbours(inside)
    greet(greeted)

    per_home, own_rows = own_ref.shape[:2]
    flat_ref[pl.ds(0, per_home * own_rows), :] = jnp.zeros((per_home * own_rows, 128), f32)
    fetches[0].wait()
    for tile in range(tiles):
        flat_ref[pl.ds(tile, per_home, stride=own_rows), :] = weights_ref[
            :, 128 * tile : 128 * (tile + 1)
        ]
    for slot in range(per_home):
        own_ref[slot] = flat_ref[pl.ds(slot * own_rows, own_rows), :].astype(bf16)
    fetches[1].wait()
    pack_tail(0)
    greeted_wait(len(greeted))

    def center_tokens():
        fetches[2].wait()
        pack_tail(1)
        for bucket in range(buckets):
            home = home_ref[bucket]
            device, slot = split(home, per_home)
            rest, home_lon = split(device, lon_size)
            home_dp, home_lat = split(rest, lat_size)
            home_chip, home_core = split(home_lat, 2)
            unit = jnp.where(
                home_core == 0, home_lon * chips + home_chip, home_chip * lon_size + home_lon
            )
            side, inner = split(slot, per_home // SPLITS)
            chunk = (side * dp_size + home_dp) * 2 + home_core
            spot_ref[bucket] = (chunk * spread + unit) * (per_home // SPLITS) + inner
        shifted(0)

        @pl.loop(0, chunks)
        def _(c):
            rows = part(c)
            hat, inverse = normed(tokens_of(0, c))
            hat1_ref[rows, :] = hat
            inv1_ref[rows, :] = jnp.broadcast_to(inverse, (CHUNK, 128))

    gather = gather_steps(sizes, own_ref, all_ref, sends, receives, keeps)
    hooks = {0: functools.partial(shift, 0)}
    for mine in range(2):

        @pl.when(core == mine)
        def _():
            gather(mine, hooks, center_tokens)
            for copy in begun:
                copy.wait_send()
            begun.clear()

    shift(1)
    for fetch in fetches[3:]:
        fetch.wait()
    vacc_ref[...] = jnp.zeros_like(vacc_ref)
    marks = offsets(lat_size + 1)
    row_marks = [mark // 128 for mark in marks]

    for bucket in range(buckets):
        block = all_ref[spot_ref[bucket]].astype(f32)
        flat_ref[tiles * bucket : tiles * (bucket + 1), :] = block[:tiles]

    def take_pairs(base, parts, pairs):
        return [flat_ref[pl.ds(base + part, pairs, stride=parts), :] for part in range(parts)]

    def give_pairs(columns, rows, evens, odds):
        for column, (even, odd) in enumerate(zip(evens, odds)):
            mid_ref[column, pl.ds(0, rows // 2, stride=2), :] = even
            mid_ref[column, pl.ds(1, rows // 2, stride=2), :] = odd

    def load_qkv(base, ref):
        b = take_pairs(base, 9, D // 2)
        pieces = []
        for first in range(0, 9, 3):
            x, y, z = b[first : first + 3]
            pieces += [
                lanes_from(x, x, 0, SIDE),
                lanes_from(x, y, 96, SIDE),
                lanes_from(y, z, 64, SIDE),
                lanes_from(z, z, 32, SIDE),
            ]
        give_pairs(6, D, pieces[:6], pieces[6:])
        for column in range(6):
            ref[:, 128 * column : 128 * (column + 1)] = mid_ref[column, pl.ds(0, D), :].astype(bf16)

    def load_square(base, rows, ref, spans):
        b = take_pairs(base, 3, rows // 2)
        odds = [lanes_from(b[1], b[2], 64, 128), lanes_from(b[2], b[2], 64, D - 128)]
        give_pairs(2, rows, [b[0], b[1]], odds)
        for first, last, target in spans:
            size = last - first
            ref[target : target + size, 0:128] = mid_ref[0, pl.ds(first, size), :].astype(bf16)
            ref[target : target + size, 128:D] = mid_ref[1, pl.ds(first, size), :][
                :, : D - 128
            ].astype(bf16)

    sides = [(0, SIDE, 0), (SIDE, D, 128)]
    load_qkv(row_marks[0], w1_ref)
    load_square(row_marks[1], D, o1_ref, sides)
    load_qkv(row_marks[2], w2_ref)
    load_square(row_marks[3], D, o2_ref, sides)
    for ref in (o1_ref, o2_ref):
        for side in range(2):
            ref[128 * side + SIDE : 128 * (side + 1), :] = jnp.zeros((128 - SIDE, D), bf16)
    for column in range(6):
        up_ref[:, 128 * column : 128 * (column + 1)] = flat_ref[
            pl.ds(row_marks[4] + column, D, stride=6), :
        ].astype(bf16)
    load_square(row_marks[5], FF, down_ref, [(0, FF, 0)])
    for index in range(9):
        start = marks[7] + D * index
        vec_ref[index : index + 1, 0:128] = lanes_of(flat_ref, start)
        vec_ref[index : index + 1, 128:D] = lanes_of(flat_ref, start + 128)[:, : D - 128]

    def earth_places():
        group_one = lat + 1
        group_two = jnp.where(is_last, 0, lat + 1)
        for index in range(EARTH_ROWS):
            group = group_one if index % WIN_LAT < HALF_LAT else group_two
            start = marks[6] + EARTH_ROW * (EARTH_ROWS * group + index)
            yield (index,) + split(start, 128)

    lane_place = lax.broadcasted_iota(jnp.int32, (1, 128), 1)
    earth_ref[...] = jnp.zeros_like(earth_ref)
    for index, row, lane in earth_places():
        rows = [flat_ref[pl.ds(row + step, 1), :] for step in range(3)]
        back = (128 - lane) & 127
        first = pltpu.roll(jnp.where(lane_place >= lane, rows[0], rows[1]), back, 1)
        second = pltpu.roll(jnp.where(lane_place >= lane, rows[1], rows[2]), back, 1)
        earth_ref[index : index + 1, 0:128] = first
        earth_ref[index : index + 1, 128:256] = jnp.where(lane_place < EARTH_ROW - 128, second, 0.0)
    earth = earth_ref[...].astype(bf16)
    key_up = lax.broadcasted_iota(jnp.int32, (AREA, LANES), 0) // (2 * QUAD)
    query_up = lax.broadcasted_iota(jnp.int32, (AREA, LANES), 1) & (LANES // 2 - 1)
    query_up = lax.rem(query_up, HEAD_ROWS) // (2 * QUAD)
    bias = jnp.where((key_up != query_up) & is_last, penalty_value, 0.0)
    chosen = [nt(entry_ref[column], earth).astype(bf16) for column in range(WIN_LON)]
    bias_ref[...] = functools.reduce(
        jnp.add, [nn(chosen[column], place_ref[column]) for column in range(WIN_LON)], bias
    )

    for slot in range(slots_here):
        number = lax.axis_index("dp") * slots_here + slot
        sample, lead = split(number, LEADS)
        live = lead < lead_ref[sample]
        size = count // slots_here
        gate_ref[slot * size : (slot + 1) * size, :] = jnp.full((size, D), jnp.where(live, 1.0, 0.0), f32)

    def vec(index):
        return vec_ref[index : index + 1, :]

    def gate_rows():
        gate = gate_ref[...]
        return jnp.broadcast_to(gate[None], (CHUNK // count, count, D)).reshape(CHUNK, D)

    def note(index, values):
        vacc_ref[index] += row_fold(values)

    def note_low(index, values):
        top = lax.broadcasted_iota(jnp.int32, (8, CHUNK), 0) == 0
        vacc_ref[index] += nn(jnp.where(top, 1.0, 0.0).astype(bf16), values)

    def first_mixed(c):
        rows = part(c)
        low = (hat1_ref[rows, :] * vec(0) + vec(1)).astype(bf16)
        n1_ref[rows, :] = low
        mixed = rounded(nn(low, w1_ref[...]))
        for tile in range(6):
            qkv_ref[tile, rows, :] = mixed[:, 128 * tile : 128 * (tile + 1)]

    for c in range(chunks):
        first_mixed(c)

    def window(ref, tile, s):
        return ref[tile, pl.ds(s, AREA, stride=count), :]

    def window_store(ref, tile, s, values):
        ref[tile, pl.ds(s, AREA, stride=count), :] = values

    halves = [slice(0, LANES // 2), slice(LANES // 2, LANES)]

    @pl.loop(0, count // 4)
    def _(block):
        masks = head_masks()
        places = [(block * 4 + step, side) for step in range(4) for side in range(2)]
        reads = [[window(qkv_ref, 2 * kind + side, s) for kind in range(3)] for s, side in places]
        raw = [
            nt(key.astype(bf16), spread_window(query, masks)) for query, key, _ in reads
        ]
        probs = [
            soft_columns(scores * SCALE + bias_ref[:, halves[side]])
            for scores, (_, side) in zip(raw, places)
        ]
        outs = [tn(prob.astype(bf16), read[2].astype(bf16)) for prob, read in zip(probs, reads)]
        for (s, side), prob, out in zip(places, probs, outs):
            probs_ref[s, :, halves[side]] = prob
            window_store(att_ref, side, s, fold_heads(out, HEAD_ROWS, AREA))

    def second_mixed(c):
        rows = part(c)
        att = jnp.concatenate([att_ref[0, rows, :], att_ref[1, rows, :]], axis=1).astype(bf16)
        att1_ref[rows, :] = att
        branch = nn(att, o1_ref[...]) + vec(2)
        tok = tokens_of(0, c) + gate_rows() * branch
        tok1_ref[rows, :] = tok
        hat, inverse = normed(tok)
        hat2_ref[rows, :] = hat
        inv2_ref[rows, :] = jnp.broadcast_to(inverse, (CHUNK, 128))
        low = (hat * vec(3) + vec(4)).astype(bf16)
        n2_ref[rows, :] = low
        mix2_ref[rows, :] = nn(low, w2_ref[...]).astype(bf16)

    for c in range(chunks):
        second_mixed(c)

    def column_masks():
        lane = lax.broadcasted_iota(jnp.int32, (8, GLANES), 1)
        place = lax.shift_right_logical(lane & (GROUP - 1), 3)
        return [place == index for index in range(GROUP // 8)]

    def squeeze_column(values, masks):
        out = values[:8]
        for index in range(1, GROUP // 8):
            out = jnp.where(masks[index], values[8 * index : 8 * index + 8], out)
        return out

    def widen_column(values, masks):
        return jnp.concatenate([jnp.where(mask, values, 0.0) for mask in masks], axis=0).astype(bf16)

    def group_rows(g):
        return pl.ds(pl.multiple_of(g * GROUP, GROUP), GROUP)

    def tile_of(ref, g, kind, side):
        first = WIDE * kind + 128 * side
        return ref[group_rows(g), first : first + 128]

    @pl.loop(0, tokens // GROUP // 6)
    def _(block):
        heads = head_masks()
        columns = column_masks()
        places = [(block * 6 + step, side) for step in range(6) for side in range(2)]
        reads = [[tile_of(mix2_ref, g, kind, side) for kind in range(3)] for g, side in places]
        raw = [nt(key, spread_heads(query, heads)) for query, key, _ in reads]
        probs = [soft_columns(squeeze_column(scores, columns) * SCALE) for scores in raw]
        outs = [tn(widen_column(prob, columns), read[2]) for prob, read in zip(probs, reads)]
        for (g, side), prob, out in zip(places, probs, outs):
            cprobs_ref[g, side] = prob
            att2_ref[group_rows(g), 128 * side : 128 * (side + 1)] = fold_heads(
                out, GROUP, GROUP
            ).astype(bf16)

    root = math.sqrt(2.0 / math.pi)
    shifted(1)

    def feed_forward(c):
        rows = part(c)
        gate = gate_rows()
        tok = tok1_ref[rows, :] + gate * (nn(att2_ref[rows, :], o2_ref[...]) + vec(5))
        hat, inverse = normed(tok)
        low = (hat * vec(6) + vec(7)).astype(bf16)
        n3_ref[rows, :] = low
        after = tokens_of(1, c)
        delta3 = (gate * after).astype(bf16)
        delta3_ref[rows, :] = delta3
        note_low(8, delta3)
        for first in range(0, FF, FF_STEP):
            columns = slice(first, first + FF_STEP)
            hidden = nn(low, up_ref[:, columns])
            square = hidden * hidden
            half = 0.5 * jnp.tanh(hidden * (root + (root * 0.044715) * square)) + 0.5
            wave = hidden * half
            act_ref[rows, columns] = wave.astype(bf16)
            slope = half + wave * (1.0 - half) * (2.0 * root + (6.0 * root * 0.044715) * square)
            gh_ref[rows, columns] = (nt(delta3, down_ref[columns, :]) * slope).astype(bf16)
        keep_tokens(0, c, tok + gate * (nn(act_ref[rows, :], down_ref[...]) + vec(8)))
        gh = gh_ref[rows, :]
        grad = nt(gh, up_ref[...])
        note(6, grad * hat)
        note(7, grad)
        mid = after + norm_back(grad, hat, inverse, vec(6))
        gmid_ref[rows, :] = mid
        delta2 = (gate * mid).astype(bf16)
        delta2_ref[rows, :] = delta2
        note_low(5, delta2)
        gatt2_ref[rows, :] = nt(delta2, o2_ref[...]).astype(bf16)

    for c in range(chunks):
        feed_forward(c)

    def keep_pairs(base, parts, blocks):
        for number, block in enumerate(blocks):
            flat_ref[pl.ds(base + number, block.shape[0], stride=parts), :] = block

    def split_pairs(columns, rows):
        evens = [mid_ref[column, pl.ds(0, rows // 2, stride=2), :] for column in range(columns)]
        odds = [mid_ref[column, pl.ds(1, rows // 2, stride=2), :] for column in range(columns)]
        return evens, odds

    def save_qkv(base, grad):
        for column in range(6):
            mid_ref[column, pl.ds(0, D), :] = grad[:, 128 * column : 128 * (column + 1)]
        e, o = split_pairs(6, D)
        pieces = e + o
        blocks = []
        for first in range(0, 12, 4):
            x, y, z, w = pieces[first : first + 4]
            blocks += [
                lanes_join(x, 0, 96, y),
                lanes_join(y, 32, 64, z),
                lanes_join(z, 64, 32, w),
            ]
        keep_pairs(base, 9, blocks)

    def save_square(base, rows, grad):
        mid_ref[0, pl.ds(0, rows), :] = grad[:, :128]
        mid_ref[1, pl.ds(0, rows), 0 : D - 128] = grad[:, 128:]
        e, o = split_pairs(2, rows)
        keep_pairs(
            base, 3, [e[0], lanes_join(e[1], 0, 64, o[0]), lanes_join(o[0], 64, 64, o[1])]
        )

    def used_rows(grad):
        return jnp.concatenate([grad[0:SIDE], grad[128 : 128 + SIDE]], axis=0)

    partner = (dp, chip * 2 + 1 - core, lon)
    place = chip * lon_size + lon

    def peers():
        for i in range(chips):
            for j in range(lon_size):
                if i or j:
                    back = (chips - i) % chips * lon_size + (lon_size - j) % lon_size
                    there = (around(chip, i, chips), around(lon, j, lon_size))
                    target = (dp, there[0] * 2 + core, there[1])
                    yield i * lon_size + j, back, there[0] * lon_size + there[1], target

    def line():
        for step in range(1, dp_size):
            there = around(dp, step, dp_size)
            yield step, dp_size - step, there, (there, lat, lon)

    def summing(base, grad, half_in, half, plane_in, mid, line_in, full):
        n_half = grad.shape[0] // 2
        n_place = n_half // spread
        n_line = n_place // dp_size

        def cross():
            send(grad.at[pl.ds((1 - core) * n_half, n_half)], half_in, base, base, partner)

        def plane():
            arrive(half_in, base)
            for first in range(0, n_half, 12):
                rows = pl.ds(first, 12)
                kept = grad[pl.ds(core * n_half + first, 12)].astype(f32)
                half[rows] = (kept + half_in[rows].astype(f32)).astype(bf16)
            for index, back, there, target in peers():
                send(
                    half.at[pl.ds(there * n_place, n_place)],
                    plane_in.at[back],
                    base + 1 + index,
                    base + 1 + back,
                    target,
                )

        def along():
            total = half[pl.ds(place * n_place, n_place)].astype(f32)
            for index in range(1, spread):
                arrive(plane_in.at[index], base + 1 + index)
                total = total + plane_in[index].astype(f32)
            mid[...] = total.astype(bf16)
            slots = base + 1 + spread
            for step, back, there, target in line():
                send(mid.at[pl.ds(there * n_line, n_line)], line_in.at[back], slots + step, slots + back, target)

        def share():
            slots = base + 1 + spread
            rows = pl.ds(dp * n_line, n_line)
            total = mid[rows].astype(f32)
            for step in range(1, dp_size):
                arrive(line_in.at[step], slots + step)
                total = total + line_in[step].astype(f32)
            full[rows] = total.astype(bf16)
            slots += dp_size
            for step, back, _, target in line():
                send(full.at[rows], full.at[rows], slots + step, slots + back, target)

        def done():
            slots = base + 1 + spread + dp_size
            for step, _, there, _ in line():
                arrive(full.at[pl.ds(there * n_line, n_line)], slots + step)

        return cross, plane, along, share, done

    spans = [[(cuts[1], cuts[2])], [(cuts[0], cuts[1])], [(0, cuts[0]), (cuts[2], buckets)]]
    if inside:
        sum_sets = [sum_refs[7 * number : 7 * (number + 1)] for number in range(3)]
        hand_out, vec_sum, vec_in, vec_now = sum_refs[21:]
        each = 1 + spread + 2 * dp_size
        soon, early, late = [
            summing(sum_slots + each * number, *refs) for number, refs in enumerate(sum_sets)
        ]

        def pack(number):
            grad = sum_sets[number][0]
            for tile in range(grad.shape[0]):
                if tile < tiles:
                    rows = [
                        flat_ref[pl.ds(tile + tiles * begin, end - begin, stride=tiles), :]
                        for begin, end in spans[number]
                    ]
                    values = rows[0] if len(rows) == 1 else jnp.concatenate(rows, axis=0)
                    grad[tile] = values.astype(bf16)
                else:
                    grad[tile] = jnp.zeros(grad.shape[1:], bf16)
    else:
        (vec_sum,) = sum_refs

    shift(2)

    grad_up = tn(n3_ref[...], gh_ref[...])
    for column in range(6):
        flat_ref[pl.ds(row_marks[4] + column, D, stride=6), :] = grad_up[
            :, 128 * column : 128 * (column + 1)
        ]
    save_square(row_marks[5], FF, tn(act_ref[...], delta3_ref[...]))
    if inside:
        pack(0)
        soon[0]()


    @pl.loop(0, tokens // GROUP // 6)
    def _(block):
        heads = head_masks()
        columns = column_masks()
        places = [(block * 6 + step, side) for step in range(6) for side in range(2)]
        reads = [
            [tile_of(mix2_ref, g, kind, side) for kind in range(3)]
            + [tile_of(gatt2_ref, g, 0, side), cprobs_ref[g, side]]
            for g, side in places
        ]
        grads = [spread_heads(read[3], heads) for read in reads]
        raw = [nt(read[2], grad) for read, grad in zip(reads, grads)]
        dvalues = [nn(widen_column(read[4], columns), grad) for read, grad in zip(reads, grads)]
        lows = [
            widen_column(soft_back(read[4], squeeze_column(slopes, columns)), columns)
            for read, slopes in zip(reads, raw)
        ]
        dkeys = [nn(low, spread_heads(read[0], heads)) for read, low in zip(reads, lows)]
        dqueries = [tn(low, read[1]) for read, low in zip(reads, lows)]
        for (g, side), dquery, dkey, dvalue in zip(places, dqueries, dkeys, dvalues):
            for kind, values in enumerate(
                (fold_heads(dquery, GROUP, GROUP) * SCALE, dkey * SCALE, dvalue)
            ):
                first = WIDE * kind + 128 * side
                gm2_ref[group_rows(g), first : first + 128] = values.astype(bf16)

    if inside:
        soon[1]()

    def second_back(c):
        rows = part(c)
        grad = nt(gm2_ref[rows, :], w2_ref[...])
        hat = hat2_ref[rows, :]
        inverse = inv2_ref[rows, :][:, :1]
        note(3, grad * hat)
        note(4, grad)
        low = gmid_ref[rows, :] + norm_back(grad, hat, inverse, vec(3))
        glow_ref[rows, :] = low
        delta1 = (gate_rows() * low).astype(bf16)
        delta1_ref[rows, :] = delta1
        note_low(2, delta1)
        gatt = rounded(nt(delta1, o1_ref[...]))
        att_ref[0, rows, :] = gatt[:, :128]
        att_ref[1, rows, :] = gatt[:, 128:]

    for c in range(chunks):
        second_back(c)

    save_square(row_marks[1], D, used_rows(tn(att1_ref[...], delta1_ref[...])))
    save_qkv(row_marks[2], tn(n2_ref[...], gm2_ref[...]))
    save_square(row_marks[3], D, used_rows(tn(att2_ref[...], delta2_ref[...])))

    if inside:
        pack(1)
        early[0]()
        soon[2]()

    dbias_ref[...] = jnp.zeros_like(dbias_ref)

    def window_back(block):
        masks = head_masks()
        places = [(block * 4 + step, side) for step in range(4) for side in range(2)]
        reads = [
            [window(qkv_ref, 2 * kind + side, s) for kind in range(3)]
            + [window(att_ref, side, s), probs_ref[s, :, halves[side]]]
            for s, side in places
        ]
        grads = [spread_window(read[3], masks) for read in reads]
        raw = [nt(read[2].astype(bf16), grad) for read, grad in zip(reads, grads)]
        dvalues = [nn(read[4].astype(bf16), grad) for read, grad in zip(reads, grads)]
        lows = [soft_back(read[4], slopes).astype(bf16) for read, slopes in zip(reads, raw)]
        dkeys = [nn(low, spread_window(read[0], masks)) for read, low in zip(reads, lows)]
        dqueries = [tn(low, read[1].astype(bf16)) for read, low in zip(reads, lows)]
        for side in range(2):
            dbias_ref[:, halves[side]] += functools.reduce(
                jnp.add, [low.astype(f32) for low, (_, there) in zip(lows, places) if there == side]
            )
        for (s, side), dquery, dkey, dvalue in zip(places, dqueries, dkeys, dvalues):
            dquery = fold_heads(dquery, HEAD_ROWS, AREA) * SCALE
            for kind, values in enumerate((dquery, dkey * SCALE, dvalue)):
                window_store(qkv_ref, 2 * kind + side, s, rounded(values))

    @pl.loop(0, 2)
    def _(block):
        window_back(block)

    if inside:
        early[1]()
        soon[3]()

    @pl.loop(2, count // 4)
    def _(block):
        window_back(block)

    @pl.loop(0, chunks)
    def _(c):
        rows = part(c)
        gm1_ref[rows, :] = jnp.concatenate(
            [qkv_ref[tile, rows, :] for tile in range(6)], axis=1
        ).astype(bf16)

    save_qkv(row_marks[0], tn(n1_ref[...], gm1_ref[...]))
    rest = buckets * tiles - row_marks[6]
    around_ref[...] = jnp.zeros_like(around_ref)
    dbias = dbias_ref[...].astype(bf16)
    moved = [nt(dbias, place_ref[column]).astype(bf16) for column in range(WIN_LON)]
    dearth = functools.reduce(
        jnp.add, [tn(moved[column], entry_ref[column]) for column in range(WIN_LON)]
    )
    for index, row, lane in earth_places():
        row = row - row_marks[6]
        first = pltpu.roll(dearth[index : index + 1, :128], lane, 1)
        second = pltpu.roll(dearth[index : index + 1, 128:], lane, 1)
        tail = lane_place >= lane
        for step, values in enumerate(
            (
                jnp.where(tail, first, 0.0),
                jnp.where(tail, second, first),
                jnp.where(tail, 0.0, second),
            )
        ):
            around_ref[index % 4, pl.ds(row + step, 1), :] += values
    flat_ref[row_marks[6] : buckets * tiles, :] = functools.reduce(
        jnp.add, [around_ref[number, 0:rest, :] for number in range(4)]
    )
    if inside:
        early[2]()
        pack(2)
        late[0]()

    def input_grads(c):
        rows = part(c)
        mixed = gm1_ref[rows, :]
        grad = nt(mixed, w1_ref[...])
        hat = hat1_ref[rows, :]
        inverse = inv1_ref[rows, :][:, :1]
        note(0, grad * hat)
        note(1, grad)
        grad_in = glow_ref[rows, :] + norm_back(grad, hat, inverse, vec(0))
        keep_tokens(1, c, grad_in)

    for c in (2, 3):
        input_grads(c)

    if inside:
        late[1]()

    for c in (1, 0):
        input_grads(c)

    for index in range(9):
        vec_sum[index : index + 1, :] = jnp.sum(vacc_ref[index], axis=0, keepdims=True)
    if inside:
        send(vec_sum, vec_in.at[0], vector_slots, vector_slots, partner)
        early[3]()
        arrive(vec_in.at[0], vector_slots)
        vec_now[0] = vec_sum[...] + vec_in[0]
        for index, back, _, target in peers():
            send(vec_now.at[0], vec_in.at[back], vector_slots + 1 + index, vector_slots + 1 + back, target)
    shift(3)
    if inside:
        late[2]()
        vec_total = vec_now[0]
        for index in range(1, spread):
            arrive(vec_in.at[index], vector_slots + 1 + index)
            vec_total = vec_total + vec_in[index]
        vec_now[1] = vec_total
        slots = vector_slots + 1 + spread
        for step, back, _, target in line():
            send(vec_now.at[1], vec_in.at[spread + back], slots + step, slots + back, target)
        late[3]()
        soon[4]()
        early[4]()
        homes = lat_size * lon_size
        width = homes * per_home
        slot_ids = lax.broadcasted_iota(jnp.int32, (width, 1), 0) + dp * width
        all_homes = homes_ref[...]
        picks = []
        for some in spans:
            held = [all_homes[:, begin:end] for begin, end in some]
            held = held[0] if len(held) == 1 else jnp.concatenate(held, axis=1)
            picks.append(jnp.where(slot_ids == held, 1.0, 0.0).astype(bf16))
        n_rows = hand_out.shape[1]
        owned_first = [
            nn(picks[0], sum_sets[0][6][row]) + nn(picks[1], sum_sets[1][6][row])
            for row in range(n_rows)
        ]
        late[4]()
        for row in range(n_rows):
            owned = owned_first[row] + nn(picks[2], sum_sets[2][6][row])
            for home in range(homes):
                hand_out[home, row] = owned[per_home * home : per_home * (home + 1), :].astype(bf16)
        first = core * (n_rows * spread) + place * n_rows
        landing = grads_ref.at[pl.ds(first, n_rows)]
        me = lat * lon_size + lon
        keep_hand = pltpu.make_async_copy(hand_out.at[me], landing, keeps.at[SPLITS])
        keep_hand.start()
        for i in range(lat_size):
            for j in range(lon_size):
                if i or j:
                    target = (dp, around(lat, i, lat_size), around(lon, j, lon_size))
                    back = (lat_size - i) % lat_size * lon_size + (lon_size - j) % lon_size
                    send(
                        hand_out.at[target[1] * lon_size + target[2]],
                        landing,
                        hand_slots + i * lon_size + j,
                        hand_slots + back,
                        target,
                    )
        for step in range(1, dp_size):
            arrive(vec_in.at[spread + step], slots + step)
            vec_total = vec_total + vec_in[spread + step]
        vec_in[0] = vec_total
        keep_total = pltpu.make_async_copy(vec_in.at[0], total_ref, keeps.at[0])
        keep_total.start()
        keep_hand.wait()
        keep_total.wait()
        for index in range(1, homes):
            arrive(landing, hand_slots + index)
    else:
        total_ref[...] = vec_sum[...]
        for tile in range(tiles):
            grads_ref[tile] = flat_ref[pl.ds(tile, buckets, stride=tiles), :]
    shifted(2)
    shifted(3)
    for copy in begun:
        copy.wait_send()


def sum_rows(sizes, tiles):
    unit = sizes[0] * sizes[1] * sizes[2]
    rows = -(-tiles // unit) * unit
    return rows, rows <= 2 * tiles


def block_call(homes, leads, master, inputs, cotangent, sizes):
    slots_here, levels = inputs.shape[0], inputs.shape[3]
    count = slots_here * levels
    tokens = count * AREA
    buckets = homes.shape[0]
    per_home, width = master.shape
    tiles = width // 128
    own_rows = -(-tiles // 16) * 16
    quads = (4, 2, HALF_LAT, HALF_LON, slots_here, levels, 128)
    tails = (4, 2, HALF_LAT, HALF_LON, levels, 128)
    assert slots_here == 2
    dp_size, lat_size, lon_size = sizes
    spread = lat_size // 2 * lon_size
    rows, inside = sum_rows(sizes, tiles)
    marks = offsets(lat_size + 1)
    low = -(-marks[1] // width)
    mid = -(-marks[4] // width)
    high = marks[6] // width
    mid += (high - mid) % 8
    low += (mid - low) % 8
    cuts = (low, mid, high)
    shape = jax.ShapeDtypeStruct
    outs = [
        shape(inputs.shape[:4] + (128,), bf16),
        shape(inputs.shape[1:4] + (128,), bf16),
        shape(inputs.shape[:4] + (128,), bf16),
        shape(inputs.shape[1:4] + (128,), bf16),
        shape((rows, per_home, 128), bf16) if inside else shape((tiles, buckets, 128), f32),
        shape((9, D), f32),
    ]
    vmem = pltpu.VMEM
    entry, place = earth_tables()
    scratch = [
        pltpu.SMEM((buckets,), jnp.int32),
        vmem(master.shape, f32),
        vmem((2,) + inputs.shape, bf16),
        vmem((2, WIN_LAT, WIN_LON, levels, 128), bf16),
        vmem(entry.shape, bf16),
        vmem(place.shape, bf16),
        vmem((per_home, own_rows, 128), bf16),
        vmem((dp_size * lat_size * lon_size * per_home, own_rows, 128), bf16),
        vmem(quads, bf16),
        vmem(tails, bf16),
        vmem(quads, bf16),
        vmem(tails, bf16),
        vmem(((buckets + 8) * tiles, 128), f32),
        vmem((6, FF, 128), f32),
        vmem((40, 256), f32),
        vmem((count, D), f32),
        vmem((AREA, LANES), f32),
        vmem((AREA, LANES), f32),
        vmem((D, 3 * WIDE), bf16),
        vmem((WIDE, D), bf16),
        vmem((D, 3 * WIDE), bf16),
        vmem((WIDE, D), bf16),
        vmem((D, FF), bf16),
        vmem((FF, D), bf16),
        vmem((16, D), f32),
        vmem((tokens, D), bf16),
        vmem((tokens, D), f32),
        vmem((tokens, 128), f32),
        vmem((6, tokens, 128), f32),
        vmem((count, AREA, LANES), f32),
        vmem((2, tokens, 128), f32),
        vmem((tokens, WIDE), bf16),
        vmem((tokens, D), f32),
        vmem((tokens, D), bf16),
        vmem((tokens, D), f32),
        vmem((tokens, 128), f32),
        vmem((tokens, 3 * WIDE), bf16),
        vmem((tokens // GROUP, 2, 8, GLANES), f32),
        vmem((tokens, WIDE), bf16),
        vmem((tokens, D), bf16),
        vmem((tokens, FF), bf16),
        vmem((tokens, FF), bf16),
        vmem((tokens, D), bf16),
        vmem((tokens, D), bf16),
        vmem((tokens, D), bf16),
        vmem((tokens, D), f32),
        vmem((tokens, D), f32),
        vmem((tokens, WIDE), bf16),
        vmem((tokens, 3 * WIDE), bf16),
        vmem((tokens, 3 * WIDE), bf16),
        vmem((9, 8, D), f32),
        vmem((4, buckets * tiles - marks[6] // 128, 128), f32),
        pltpu.SemaphoreType.DMA((move_slots(sizes, slots_here)[-1],)),
        pltpu.SemaphoreType.DMA((move_slots(sizes, slots_here)[-1],)),
        pltpu.SemaphoreType.DMA((SPLITS + 1,)),
        pltpu.SemaphoreType.DMA((5,)),
        pltpu.SemaphoreType.DMA((4 * (slots_here + 1),)),
    ]
    if inside:
        n_place = rows // 2 // spread
        for some in (high - mid, mid - low, buckets - (high - low)):
            scratch += [
                vmem((rows, some, 128), bf16),
                vmem((rows // 2, some, 128), bf16),
                vmem((rows // 2, some, 128), bf16),
                vmem((spread, n_place, some, 128), bf16),
                vmem((n_place, some, 128), bf16),
                vmem((dp_size, n_place // dp_size, some, 128), bf16),
                vmem((n_place, some, 128), bf16),
            ]
        scratch += [
            vmem((lat_size * lon_size, n_place, per_home, 128), bf16),
            vmem((9, D), f32),
            vmem((spread + dp_size, 9, D), f32),
            vmem((2, 9, D), f32),
        ]
    else:
        scratch += [vmem((9, D), f32)]
    spec = pl.BlockSpec(memory_space=pltpu.VMEM)
    smem = pl.BlockSpec(memory_space=pltpu.SMEM)
    hbm = pl.BlockSpec(memory_space=pl.ANY)
    return pl.pallas_call(
        functools.partial(block_kernel, (sizes, buckets, tiles, slots_here, cuts), inside),
        out_shape=outs,
        in_specs=[smem, smem, spec] + [hbm] * 5,
        out_specs=[hbm] * 4 + [hbm if inside else spec] * 2,
        scratch_shapes=scratch,
        compiler_params=pltpu.CompilerParams(
            vmem_limit_bytes=62 * 1024 * 1024, collective_id=0, has_side_effects=True
        ),
        name="block",
    )(
        homes,
        leads,
        homes[None, :],
        master,
        inputs,
        cotangent,
        jnp.asarray(entry),
        jnp.asarray(place),
    )


def finish_kernel(marks, steps_ref, homes_ref, *refs):
    sources, targets = refs[:9], refs[9:15]
    held, made = refs[15:24], refs[24:29]
    spare_ref, incoming, outgoing = refs[29:]
    fetches = [
        pltpu.make_async_copy(src, dst, incoming.at[number])
        for number, (src, dst) in enumerate(zip(sources, held))
    ]
    for fetch in fetches:
        fetch.start()
    back_res_ref, back_res_tail_ref, back_in_ref, back_in_tail_ref = held[:4]
    grads_ref, vectors_ref, master_ref, one_ref, two_ref = held[4:]
    result_ref, grad_inputs_ref, new_master, new_one, new_two = made
    homes, width = master_ref.shape
    tiles = width // 128
    leaves = []

    def leave(src, dst):
        copy = pltpu.make_async_copy(src, dst, outgoing.at[len(leaves)])
        copy.start()
        leaves.append(copy)

    levels = result_ref.shape[3]
    for number, (top_ref, tail_ref, out_ref) in enumerate(
        (
            (back_res_ref, back_res_tail_ref, result_ref),
            (back_in_ref, back_in_tail_ref, grad_inputs_ref),
        )
    ):
        for fetch in fetches[2 * number : 2 * number + 2]:
            fetch.wait()
        for slot in range(out_ref.shape[0]):

            @pl.loop(0, WIN_LAT)
            def _(row):
                out_ref[slot, row, :, :, 0:128] = top_ref[slot, row].astype(out_ref.dtype)
                tail = tail_ref[row].astype(f32).reshape(WIN_LON * levels, 128)
                tail = (pltpu.roll(tail, 64, 1) if slot else tail)[:, : D - 128]
                out_ref[slot, row, :, :, 128:D] = tail.reshape(WIN_LON, levels, D - 128).astype(
                    out_ref.dtype
                )

            leave(out_ref.at[slot], targets[number].at[slot])
    for fetch in fetches[4:]:
        fetch.wait()
    leave(vectors_ref, targets[2])
    place = lax.axis_index("dp") * lax.axis_size("lat") + lax.axis_index("lat")
    place = (place * lax.axis_size("lon") + lax.axis_index("lon")) * homes
    slots = lax.broadcasted_iota(jnp.int32, (homes, 1), 0) + place
    match = homes_ref[...] == slots
    bucket = lax.broadcasted_iota(jnp.int32, match.shape, 1)
    held = jnp.max(jnp.where(match, bucket, -1), axis=1, keepdims=True)
    base = jnp.where(held >= 0, held * width, marks[8])

    top = marks[7] // 128
    spare_ref[...] = jnp.zeros_like(spare_ref)
    lanes = lax.broadcasted_iota(jnp.int32, (1, 128), 1)
    for index in range(9):
        vector = vectors_ref[index : index + 1, :]
        start = marks[7] + D * index
        tail = jnp.concatenate([vector[:, 128:], jnp.zeros((1, 256 - D), f32)], axis=1)
        for values, size, begin in ((vector[:, :128], 128, start), (tail, D - 128, start + 128)):
            row, lane = divmod(begin - 128 * top, 128)
            moved = pltpu.roll(values, lane, 1) if lane else values
            spare_ref[row : row + 1, :] += jnp.where(lanes >= lane, moved, 0.0)
            if lane + size > 128:
                spare_ref[row + 1 : row + 2, :] += jnp.where(lanes < lane, moved, 0.0)

    steps = jnp.full((homes, 128), steps_ref[0], jnp.int32).astype(f32)
    fix_one = 1.0 / (1.0 - jnp.exp(steps * math.log(beta_one)))
    fix_two = 1.0 / (1.0 - jnp.exp(steps * math.log(beta_two)))
    rates = [
        2.6 / math.sqrt(D),
        8.0 / math.sqrt(D),
        2.6 / math.sqrt(D),
        4.0 / math.sqrt(D),
        2.0 / math.sqrt(D),
        3.0 / math.sqrt(FF),
        1.0,
        0.6,
    ]
    spread = jnp.broadcast_to(base, (homes, 128)) + lax.broadcasted_iota(jnp.int32, (homes, 128), 1)
    for tile in range(tiles):
        columns = slice(128 * tile, 128 * (tile + 1))
        index = spread + 128 * tile
        rate = jnp.full((homes, 128), 0.1, f32)
        for number in range(7, -1, -1):
            rate = jnp.where(index < marks[number + 1], rates[number], rate)
        grad = grads_ref[tile].astype(f32)
        for owner in range(marks[7] // width, (marks[8] - 1) // width + 1):
            row = owner * tiles + tile - top
            if 0 <= row < spare_ref.shape[0]:
                grad = grad + jnp.where(held == owner, spare_ref[row : row + 1, :], 0.0)
        weights = master_ref[:, columns]
        first = beta_one * one_ref[:, columns] + (1.0 - beta_one) * grad
        second = beta_two * two_ref[:, columns] + (1.0 - beta_two) * grad * grad
        step = first * fix_one / (jnp.sqrt(second * fix_two) + eps_adam) + decay_rate * weights
        new_master[:, columns] = weights - rate * step
        new_one[:, columns] = first
        new_two[:, columns] = second
    for src, dst in zip(made[2:], targets[3:]):
        leave(src, dst)
    for copy in leaves:
        copy.wait()


def finish_call(marks, steps, homes, grads, vectors, master, one, two, backs):
    grid = backs[0].shape[:4] + (D,)
    shape = jax.ShapeDtypeStruct
    hbm = pl.BlockSpec(memory_space=pl.ANY)
    operands = [*backs, grads, vectors, master, one, two]
    outs = [shape(grid, bf16), shape(grid, f32), shape(vectors.shape, f32)]
    outs += [shape(master.shape, f32)] * 3
    made = outs[:2] + outs[3:]
    return pl.pallas_call(
        functools.partial(finish_kernel, marks),
        out_shape=outs,
        in_specs=[pl.BlockSpec(memory_space=pltpu.SMEM), pl.BlockSpec(memory_space=pltpu.VMEM)]
        + [hbm] * len(operands),
        out_specs=[hbm] * len(outs),
        scratch_shapes=[pltpu.VMEM(some.shape, some.dtype) for some in operands + made]
        + [
            pltpu.VMEM((16, 128), f32),
            pltpu.SemaphoreType.DMA((len(operands),)),
            pltpu.SemaphoreType.DMA((8,)),
        ],
        name="finish",
    )(steps, homes[None, :], *operands)


def per_device(
    inputs, cotangent, lead_counts, home_slots, master, moment_one, moment_two, step_count
):
    axes = ("dp", "lat", "lon")
    sizes = tuple(lax.axis_size(axis) for axis in axes)
    slots_mine, bucket_width = master.shape
    tiles = bucket_width // 128
    order = (0, 2, 3, 1, 4)
    *backs, grads, vectors = block_call(
        home_slots, lead_counts, master, inputs.transpose(order), cotangent.transpose(order), sizes
    )
    if not sum_rows(sizes, tiles)[1]:
        spread = jnp.zeros((tiles, math.prod(sizes) * slots_mine, 128), f32)
        spread = spread.at[:, home_slots].set(grads)
        grads = lax.psum_scatter(spread, axes, scatter_dimension=1, tiled=True)
        vectors = lax.psum(vectors, axes)
    result, grad_inputs, grad_vectors, *new = finish_call(
        offsets(sizes[1] + 1),
        step_count,
        home_slots,
        grads,
        vectors,
        master,
        moment_one,
        moment_two,
        backs,
    )
    order = (0, 3, 1, 2, 4)
    return (result.transpose(order), grad_inputs.transpose(order), grad_vectors, *new)


def solution(mesh):
    in_specs = (
        P("dp", None, "lat", "lon", None),
        P("dp", None, "lat", "lon", None),
        P(),
        P(),
        P(("dp", "lat", "lon"), None),
        P(("dp", "lat", "lon"), None),
        P(("dp", "lat", "lon"), None),
        P(),
    )
    out_specs = (
        P("dp", None, "lat", "lon", None),
        P("dp", None, "lat", "lon", None),
        P(),
        P(("dp", "lat", "lon"), None),
        P(("dp", "lat", "lon"), None),
        P(("dp", "lat", "lon"), None),
    )
    return jax.shard_map(
        per_device, mesh=mesh, in_specs=in_specs, out_specs=out_specs, check_vma=False
    )
```
